32 devices in a mesh: dp: 16 (over z, x, core), heads: 2 (over y).
Axes of the slice: x: 2, y: 2, z: 4, core: 2. Of those that a mesh axis runs over, the one named last changes fastest.
Arguments:
- images: bfloat16 [256, 196, 256], P(('dp', 'heads')), may hold values from -6 to 6
- cotangent: bfloat16 [256, 196, 256], P(('dp', 'heads')), may hold values from -6 to 6
- drop_masks: int32 [256, 2], P(('dp', 'heads')), may hold values 0 or 1
- group_master: float32 [2, 132608], P('heads', 'dp'), as said below
- group_m1: float32 [2, 132608], P('heads', 'dp'), as said below
- group_m2: float32 [2, 132608], P('heads', 'dp'), as said below
- shared_master: float32 [526848], P(('dp', 'heads')), as said below
- shared_m1: float32 [526848], P(('dp', 'heads')), as said below
- shared_m2: float32 [526848], P(('dp', 'heads')), as said below
Outputs:
- activations: float32 [256, 196, 256], P(('dp', 'heads'))
- input_grad: float32 [256, 196, 256], P(('dp', 'heads'))
- grad_norm: float32 [1], replicated
- group_grad: float32 [2, 132608], P('heads', 'dp')
- group_master_new: float32 [2, 132608], P('heads', 'dp')
- group_first: float32 [2, 132608], P('heads', 'dp')
- group_second: float32 [2, 132608], P('heads', 'dp')
- group_copy: bfloat16 [2, 132608], P('heads', 'dp')
- shared_grad: float32 [526848], P(('dp', 'heads'))
- shared_master_new: float32 [526848], P(('dp', 'heads'))
- shared_first: float32 [526848], P(('dp', 'heads'))
- shared_second: float32 [526848], P(('dp', 'heads'))
- shared_copy: bfloat16 [526848], P(('dp', 'heads'))
The draws below stay inside these ranges and needn't reach their ends.
Inputs may be any that keep to these rules, and one draw needn't show every extreme that they name: `group_master`: entries of either sign. `group_m1`: entries of either sign. `group_m2`: every entry positive. `shared_master`: entries of either sign. `shared_m1`: entries of either sign. `shared_m2`: every entry positive.
All inputs are finite; a program needn't handle non-finite values. No bound on the sum of `drop_masks` on one device may be relied on, other than what follows from the above.
Results may differ from the reference program's by a relative error of at most 0.011.
Values may be sent and summed in bfloat16 or wider, within the bound.
A program may use at most 128 MiB of HBM per device.

```python
import math
import jax
import jax.numpy as jnp
from jax import lax

D = 256
FF = 1024
SIDE = 14
SW = 7
STEP = 10
IMG_DEV = 8
HD = 32
HALF = 128
IMAGES = 256
GROUP_PARAMS = 132608
SHARED_PARAMS = 526848


def fill_segments(listing):
    overall = 0
    for length, amount_value in listing:
        overall = overall + length
    position = jnp.arange(overall)
    filled = jnp.zeros((overall,), jnp.float32)
    start_at = 0
    for length, amount_value in listing:
        inside = (position >= start_at) & (position < start_at + length)
        filled = jnp.where(inside, jnp.float32(amount_value), filled)
        start_at = start_at + length
    return filled


def group_layout(column):
    listing = [(D * 3 * HALF, D ** (-0.5), 0.0, 0.7), (2 * HALF, 0.3, 0.0, 1.5), (HALF * D, D ** (-0.5), 0.0, 1.4), (9 * HALF, 0.25, 0.0, 2.0), (HALF, 0.3, 0.0, 2.0)]
    return fill_segments([(record[0], record[column]) for record in listing])


def shared_layout(column):
    listing = [(D * FF, D ** (-0.5), 0.0, 0.7), (FF, 0.3, 0.0, 1.0), (FF * D, FF ** (-0.5), 0.0, 1.4), (D, 0.3, 0.0, 2.0), (D, 0.1, 1.0, 1.5), (D, 0.3, 0.0, 1.5), (D, 0.1, 1.0, 1.5), (D, 0.3, 0.0, 1.5), (D, 0.3, 0.0, 2.0)]
    return fill_segments([(record[0], record[column]) for record in listing])


def draw_group_master(key, part):
    normal_draw = jax.random.truncated_normal(key, -4.0, 4.0, (2, GROUP_PARAMS), jnp.float32)
    return group_layout(2)[None, :] + normal_draw * group_layout(1)[None, :]


def draw_group_m1(key, part):
    normal_draw = jax.random.truncated_normal(key, -4.0, 4.0, (2, GROUP_PARAMS), jnp.float32)
    return 0.1 / 0.9 * normal_draw * group_layout(3)[None, :]


def draw_group_m2(key, part):
    logs = jax.random.uniform(key, (2, GROUP_PARAMS), jnp.float32, math.log(0.5), math.log(8.0))
    sizing = group_layout(3)
    return 0.001 / 0.999 * (sizing * sizing)[None, :] * jnp.exp(logs)


def draw_shared_master(key, part):
    normal_draw = jax.random.truncated_normal(key, -4.0, 4.0, (SHARED_PARAMS,), jnp.float32)
    return shared_layout(2) + normal_draw * shared_layout(1)


def draw_shared_m1(key, part):
    normal_draw = jax.random.truncated_normal(key, -4.0, 4.0, (SHARED_PARAMS,), jnp.float32)
    return 0.1 / 0.9 * normal_draw * shared_layout(3)


def draw_shared_m2(key, part):
    logs = jax.random.uniform(key, (SHARED_PARAMS,), jnp.float32, math.log(0.5), math.log(8.0))
    sizing = shared_layout(3)
    return 0.001 / 0.999 * sizing * sizing * jnp.exp(logs)


def plant(drawn, rng, smallest, largest):
    place = [jax.random.randint(jax.random.fold_in(rng, axis), (), 0, length) for axis, length in enumerate(drawn.shape)]
    longest = drawn.shape.index(max(drawn.shape))
    beside = place[:longest] + [(place[longest] + 1) % drawn.shape[longest]] + place[longest + 1:]
    return drawn.at[tuple(place)].set(smallest).at[tuple(beside)].set(largest)


def levels(key, shape, pieces, smallest, largest):
    level = 1.0
    for dim, blocks in pieces:
        heights = jax.random.uniform(jax.random.fold_in(jax.random.fold_in(key, 6), dim), (blocks,), jnp.float32, smallest / len(pieces), largest / len(pieces))
        level = level * jnp.repeat(jnp.exp(heights), shape[dim] // blocks).reshape((-1,) + (1,) * (len(shape) - 1 - dim))
    return level


def bell_draw(own_key, dims, width, limit, cuts=(), dtype=jnp.bfloat16):
    result = jax.random.normal(own_key, dims, jnp.float32) * width
    if len(cuts) > 0:
        result = levels(own_key, dims, cuts, -0.22, 0.18) * result
    return jnp.clip(result, min=-limit, max=limit).astype(dtype)


def setup_inputs(seed: int = 0) -> dict:
    key_list = jax.random.split(jax.random.key(seed), 10)
    images = bell_draw(key_list[0], (IMAGES, SIDE * SIDE, D), 1.0, 6.0, ((0, 32),))
    cotangent = bell_draw(key_list[1], (IMAGES, SIDE * SIDE, D), 1.0, 6.0, ((0, 32),))
    drop_masks = plant((jax.random.randint(key_list[2], (IMAGES, 2), 0, 5) < 4).astype(jnp.int32), jax.random.fold_in(key_list[2], 1), 0, 1)
    group_master = draw_group_master(jax.random.fold_in(key_list[9], 71), 0)
    group_m1 = draw_group_m1(jax.random.fold_in(key_list[9], 71), 0)
    group_m2 = draw_group_m2(jax.random.fold_in(key_list[9], 71), 0)
    shared_master = draw_shared_master(jax.random.fold_in(key_list[9], 71), 0)
    shared_m1 = draw_shared_m1(jax.random.fold_in(key_list[9], 71), 0)
    shared_m2 = draw_shared_m2(jax.random.fold_in(key_list[9], 71), 0)
    return {"images": images, "cotangent": cotangent, "drop_masks": drop_masks, "group_master": group_master, "group_m1": group_m1, "group_m2": group_m2, "shared_master": shared_master, "shared_m1": shared_m1, "shared_m2": shared_m2}


@jax.custom_vjp
def low(v):
    return lax.optimization_barrier(v.astype(jnp.bfloat16)).astype(jnp.float32)

@jax.custom_vjp
def low_back(v):
    return v

def low_keep(v):
    return (low(v), None)

def low_pass(kept, grad):
    return (grad,)

def back_keep(v):
    return (v, None)

def back_low(kept, grad):
    return (low(grad),)
low.defvjp(low_keep, low_pass)
low_back.defvjp(back_keep, back_low)
eps_norm = 1e-05
keep_prob = 0.8
beta_one = 0.9
beta_two = 0.999
adam_eps = 1e-08
learn_rate = 0.04
decay_rate = 0.05
highest = lax.Precision.HIGHEST

def split_flat(flat, lengths):
    outcome = []
    offset = 0
    for length in lengths:
        outcome.append(flat[offset:offset + length])
        offset = offset + length
    return outcome

def shared_pieces(flat):
    parts = split_flat(flat, [D * FF, FF, FF * D, D, D, D, D, D, D])
    return (parts[0].reshape(D, FF), parts[1], parts[2].reshape(FF, D), parts[3], parts[4], parts[5], parts[6], parts[7], parts[8])

def group_pieces(flat):
    parts = split_flat(flat, [D * 3 * HALF, 2 * HALF, HALF * D, 9 * HALF, HALF])
    return (parts[0].reshape(D, 3 * HALF), parts[1], parts[2].reshape(HALF, D), parts[3].reshape(9, HALF), parts[4])

def layer_norm(values, gain, shift):
    center = values - lax.optimization_barrier(jnp.mean(values, axis=-1, keepdims=True))
    spread = lax.optimization_barrier(jnp.mean(center * center, axis=-1, keepdims=True))
    return center * lax.rsqrt(spread + eps_norm) * gain + shift

def lepe_conv(values, kernel, shift):
    padded = jnp.pad(values, ((0, 0), (0, 0), (1, 1), (1, 1), (0, 0)))
    summed = jnp.zeros_like(values) + shift
    for row_step in range(3):
        for col_step in range(3):
            summed = summed + kernel[row_step * 3 + col_step] * padded[:, :, row_step:row_step + SW, col_step:col_step + SIDE, :]
    return summed

def orient(grid, member):
    if member == 1:
        return jnp.swapaxes(grid, 1, 2)
    return grid

def stripe_branch(normed, params, member):
    triple_weight, pair_bias, out_weight, conv_kernel, conv_bias = params
    number = normed.shape[0]
    stripes = SIDE // SW
    zero_bias = jnp.zeros((HALF,), jnp.float32)
    bias_full = jnp.concatenate([pair_bias[:HALF], zero_bias, pair_bias[HALF:]])
    projected = jnp.einsum('ntd,de->nte', normed, triple_weight, precision=highest) + bias_full
    projected = low_back(low(projected))
    grid = orient(projected.reshape(number, SIDE, SIDE, 3 * HALF), member)
    parts = grid.reshape(number, stripes, SW * SIDE, 3, HALF // HD, HD)
    queries = parts[:, :, :, 0]
    key_part = parts[:, :, :, 1]
    value_part = parts[:, :, :, 2]
    scores = low_back(jnp.einsum('nsqhd,nskhd->nshqk', queries, key_part, precision=highest) * HD ** (-0.5))
    softmax_out = low(jax.nn.softmax(scores, axis=-1))
    attended = jnp.einsum('nshqk,nskhd->nsqhd', softmax_out, value_part, precision=highest)
    position_term = lepe_conv(value_part.reshape(number, stripes, SW, SIDE, HALF), conv_kernel, conv_bias)
    mixture = attended.reshape(number, stripes, SW, SIDE, HALF) + position_term
    mixture = orient(mixture.reshape(number, SIDE, SIDE, HALF), member).reshape(number, SIDE * SIDE, HALF)
    mixture = low_back(low(mixture))
    return jnp.einsum('nte,ed->ntd', mixture, out_weight, precision=highest)

def forward(values, weights, scale_one, scale_two):
    shared, groups = weights
    up_weight, up_bias, down_weight, down_bias, gain_one, shift_one, gain_two, shift_two, out_bias = shared
    normed = low(layer_norm(values, gain_one, shift_one))
    branch = stripe_branch(normed, groups[0], 0) + stripe_branch(normed, groups[1], 1)
    attended = low_back(branch) + out_bias
    middle = values + scale_one[:, None, None] * attended
    normed_two = low(layer_norm(middle, gain_two, shift_two))
    hidden = low_back(jnp.einsum('ntd,df->ntf', normed_two, up_weight, precision=highest) + up_bias)
    active = low(jax.nn.gelu(hidden, approximate=False))
    mlp_out = low_back(jnp.einsum('ntf,fd->ntd', active, down_weight, precision=highest)) + down_bias
    return middle + scale_two[:, None, None] * mlp_out

def adam_step(master, gradient, first, second, step):
    first_new = beta_one * first + (1.0 - beta_one) * gradient
    second_new = beta_two * second + (1.0 - beta_two) * gradient * gradient
    first_hat = first_new / (1.0 - jnp.power(jnp.float32(beta_one), step))
    second_hat = second_new / (1.0 - jnp.power(jnp.float32(beta_two), step))
    master_new = master - learn_rate * (first_hat / (jnp.sqrt(second_hat) + adam_eps) + decay_rate * master)
    return (master_new, first_new, second_new)

def reference(images, cotangent, drop_masks, group_master, group_m1, group_m2, shared_master, shared_m1, shared_m2):
    shared = shared_pieces(shared_master.astype(jnp.bfloat16).astype(jnp.float32))
    group_low = group_master.astype(jnp.bfloat16).astype(jnp.float32)
    groups = (group_pieces(group_low[0]), group_pieces(group_low[1]))
    weights = (shared, groups)
    per_block = 2 * IMG_DEV
    blocks = IMAGES // per_block
    tokens = SIDE * SIDE
    inputs = images.astype(jnp.float32).reshape(blocks, per_block, tokens, D)
    cotangents = cotangent.astype(jnp.float32).reshape(blocks, per_block, tokens, D)
    scales = (drop_masks.astype(jnp.float32) / keep_prob).reshape(blocks, per_block, 2)

    def one_block(summed, portion):
        values, backward_in, scale = portion

        def run_layer(layer_in, layer_weights):
            return forward(layer_in, layer_weights, scale[:, 0], scale[:, 1])
        output, pullback = jax.vjp(run_layer, values, weights)
        grad_values, grad_weights = pullback(backward_in)
        return (jax.tree.map(jnp.add, summed, grad_weights), (output, grad_values))
    start_zero = jax.tree.map(jnp.zeros_like, weights)
    gradients, (outputs, input_grads) = lax.scan(one_block, start_zero, (inputs, cotangents, scales))
    shared_raw = jnp.concatenate([member.reshape(-1) for member in gradients[0]])
    group_raw = jnp.stack([jnp.concatenate([member.reshape(-1) for member in gradients[1][which_group]]) for which_group in range(2)])
    grad_norm = jnp.sqrt(jnp.sum(group_raw * group_raw) + jnp.sum(shared_raw * shared_raw))
    threshold = math.sqrt(2 * GROUP_PARAMS + SHARED_PARAMS)
    factor = jnp.minimum(1.0, threshold / (grad_norm + 1e-06))
    group_grad = group_raw * factor
    shared_grad = shared_raw * factor
    step = jnp.float32(STEP)
    group_new, group_first, group_second = adam_step(group_master, group_grad, group_m1, group_m2, step)
    shared_new, shared_first, shared_second = adam_step(shared_master, shared_grad, shared_m1, shared_m2, step)
    return (outputs.reshape(IMAGES, tokens, D), input_grads.reshape(IMAGES, tokens, D), grad_norm.reshape(1), group_grad, group_new, group_first, group_second, group_new.astype(jnp.bfloat16), shared_grad, shared_new, shared_first, shared_second, shared_new.astype(jnp.bfloat16))
```

```python
from functools import partial
import math

import jax
import jax.numpy as jnp
from jax import lax
from jax.experimental import pallas as pl
from jax.experimental.pallas import tpu as pltpu
from jax.sharding import PartitionSpec as P

D = 256
FF = 1024
SIDE = 14
SW = 7
STEP = 10
HD = 32
HALF = 128
GROUP_PARAMS = 132608
SHARED_PARAMS = 526848
TOK = SIDE * SIDE
GRID = 16 * SIDE
STRIPE = 16 * SW
HEADS = HALF // HD
UNIT = 1024

eps_norm = 1e-05
keep_prob = 0.8
beta_one = 0.9
beta_two = 0.999
adam_eps = 1e-08
learn_rate = 0.04
decay_rate = 0.05

f32 = jnp.float32
bf16 = jnp.bfloat16


def window_rows(total, count):
    share = total // count
    most = max((share * k) % UNIT + share for k in range(count))
    return 16 * (-(-most // (2 * UNIT)))


def first_row(total, count, k):
    return (total // count * k) // UNIT * 8


def nn(a, b):
    return lax.dot_general(a, b, (((1,), (0,)), ((), ())), preferred_element_type=f32)


def nt(a, b):
    return lax.dot_general(a, b, (((1,), (1,)), ((), ())), preferred_element_type=f32)


def tn(a, b):
    return lax.dot_general(a, b, (((0,), (0,)), ((), ())), preferred_element_type=f32)


def norm_parts(values):
    center = values - jnp.mean(values, axis=-1, keepdims=True)
    inverse = lax.rsqrt(jnp.mean(center * center, axis=-1, keepdims=True) + eps_norm)
    return center * inverse, inverse


def norm_back(grad_after, unit, inverse, gain):
    scaled = grad_after * gain
    return inverse * (
        scaled
        - jnp.mean(scaled, axis=-1, keepdims=True)
        - unit * jnp.mean(scaled * unit, axis=-1, keepdims=True)
    )


def column_sum(values):
    return jnp.sum(values, axis=0, keepdims=True)


def head_masks(dtype):
    lane = lax.broadcasted_iota(jnp.int32, (1, HALF), 1) // HD
    return [(lane == h).astype(f32).astype(dtype) for h in range(HEADS)]


def spread_heads(values, masks):
    return jnp.concatenate([values * masks[h] for h in range(HEADS)], axis=0)


def pick_heads(stacked):
    lane = lax.broadcasted_iota(jnp.int32, (STRIPE, HALF), 1)
    picked = stacked[(HEADS - 1) * STRIPE :]
    for h in range(HEADS - 2, -1, -1):
        picked = jnp.where(lane < (h + 1) * HD, stacked[h * STRIPE : (h + 1) * STRIPE], picked)
    return picked


def row_shift(values, step):
    if step == 0:
        return values
    zero = jnp.zeros((16, HALF), f32)
    if step > 0:
        return jnp.concatenate([values[16:], zero], axis=0)
    return jnp.concatenate([zero, values[:-16]], axis=0)


def neighbours(values):
    return [pltpu.roll(values, 1, 0), values, pltpu.roll(values, STRIPE - 1, 0)]


def tile_sum(values):
    return jnp.sum(values.reshape(-1, 8, HALF), axis=0)


def place_matrices(pp_ref, ppt_ref):
    place = lax.broadcasted_iota(jnp.int32, (GRID, TOK), 0)
    token = lax.broadcasted_iota(jnp.int32, (GRID, TOK), 1)
    first, second = place // 16, place % 16
    inside = second < SIDE
    pp_ref[0] = (inside & (token == first * SIDE + second)).astype(f32).astype(bf16)
    pp_ref[1] = (inside & (token == second * SIDE + first)).astype(f32).astype(bf16)
    place = lax.broadcasted_iota(jnp.int32, (TOK, GRID), 1)
    token = lax.broadcasted_iota(jnp.int32, (TOK, GRID), 0)
    first, second = place // 16, place % 16
    inside = second < SIDE
    ppt_ref[0] = (inside & (token == first * SIDE + second)).astype(f32).astype(bf16)
    ppt_ref[1] = (inside & (token == second * SIDE + first)).astype(f32).astype(bf16)


def compute_kernel(
    n_dp,
    srows,
    grows,
    drop_ref,
    x_ref,
    co_ref,
    blocks_ref,
    out_ref,
    gin_ref,
    gblocks_ref,
    flat,
    gflat,
    pp_ref,
    ppt_ref,
    wq,
    ow,
    uw,
    dw,
    qbias,
    ubias,
    vecs,
    conv,
    a_wq,
    a_ow,
    a_uw,
    a_dwt,
    a_pb,
    a_ub,
    a_vec,
    a_conv,
    p_ref,
    qkv_ref,
):
    image = pl.program_id(0)
    n = 2 * n_dp

    @pl.when(image == 0)
    def _():
        place_matrices(pp_ref, ppt_ref)
        flat[...] = jnp.zeros_like(flat)
        gflat[...] = jnp.zeros_like(gflat)
        for k in range(n):
            at = first_row(SHARED_PARAMS, n, k)
            flat[at : at + srows] += blocks_ref[k, 0:srows].astype(f32)
            at = first_row(GROUP_PARAMS, n_dp, k // 2)
            gflat[k % 2, at : at + grows] += blocks_ref[k, srows : srows + grows].astype(f32)
        for c in range(8):
            cols = slice(c * 128, (c + 1) * 128)
            uw[:, cols] = flat[pl.ds(c, D, stride=8), :].astype(bf16)
            ubias[:, cols] = flat[2048 + c : 2049 + c, :]
        for c in range(2):
            cols = slice(c * 128, (c + 1) * 128)
            dw[:, cols] = flat[pl.ds(2056 + c, FF, stride=2), :].astype(bf16)
            for i in range(6):
                vecs[i : i + 1, cols] = flat[4104 + 2 * i + c : 4105 + 2 * i + c, :]
        for j in range(2):
            for c in range(3):
                cols = slice(j * 384 + c * 128, j * 384 + (c + 1) * 128)
                wq[:, cols] = gflat[j, pl.ds(c, D, stride=3), :].astype(bf16)
            for c in range(2):
                cols = slice(c * 128, (c + 1) * 128)
                ow[j * 128 : (j + 1) * 128, cols] = gflat[
                    j, pl.ds(770 + c, HALF, stride=2), :
                ].astype(bf16)
            qbias[:, j * 384 : j * 384 + 128] = gflat[j, 768:769, :]
            qbias[:, j * 384 + 128 : j * 384 + 256] = jnp.zeros((1, 128), f32)
            qbias[:, j * 384 + 256 : j * 384 + 384] = gflat[j, 769:770, :]
            conv[j, 0:10] = gflat[j, 1026:1036, :]
        for ref in (a_wq, a_ow, a_uw, a_dwt, a_pb, a_ub, a_vec, a_conv):
            ref[...] = jnp.zeros_like(ref)

    scale_one = drop_ref[image, 0].astype(f32) / keep_prob
    scale_two = drop_ref[image, 1].astype(f32) / keep_prob
    down_bias, gain_one, shift_one = vecs[0:1], vecs[1:2], vecs[2:3]
    gain_two, shift_two, out_bias = vecs[3:4], vecs[4:5], vecs[5:6]
    masks = head_masks(bf16)
    ones = jnp.ones((8, TOK), bf16)
    key_row = lax.broadcasted_iota(jnp.int32, (1, SW, 16, STRIPE), 2)
    scale = HD ** (-0.5)

    values = x_ref[0].astype(f32)
    unit_one, inverse_one = norm_parts(values)
    normed = (unit_one * gain_one + shift_one).astype(bf16)
    triple = (nn(normed, wq[...]) + qbias[...]).astype(bf16)
    heads_out = []
    for j in range(2):
        qkv_ref[j] = nn(pp_ref[j], triple[:, j * 384 : (j + 1) * 384]).astype(bf16)
        parts = []
        for s in range(2):
            rows = slice(s * STRIPE, (s + 1) * STRIPE)
            query = qkv_ref[j, rows, 0:128]
            keys = spread_heads(qkv_ref[j, rows, 128:256], masks)
            value = qkv_ref[j, rows, 256:384]
            scores = nt(keys, query).reshape(HEADS, SW, 16, STRIPE) * scale
            scores = jnp.where(key_row < SIDE, scores, -1e30)
            scores = scores.reshape(HEADS, STRIPE, STRIPE)
            weights = jnp.exp(scores - jnp.max(scores, axis=1, keepdims=True))
            probs = weights * (1.0 / jnp.sum(weights, axis=1, keepdims=True))
            probs = probs.reshape(HEADS * STRIPE, STRIPE)
            p_ref[2 * j + s] = probs
            attended = tn(probs.astype(bf16), spread_heads(value, masks))
            near = neighbours(value.astype(f32))
            total = attended + conv[j, 9:10]
            for a in range(3):
                part = near[0] * conv[j, 3 * a : 3 * a + 1]
                for b in range(1, 3):
                    part = part + near[b] * conv[j, 3 * a + b : 3 * a + b + 1]
                total = total + row_shift(part, a - 1)
            parts.append(total.astype(bf16))
        padded = jnp.concatenate(parts, axis=0)
        heads_out.append(nn(ppt_ref[j], padded).astype(bf16))
    heads_out = jnp.concatenate(heads_out, axis=1)
    branch = nn(heads_out, ow[...])
    middle = values + scale_one * (branch + out_bias)
    unit_two, inverse_two = norm_parts(middle)
    normed_two = (unit_two * gain_two + shift_two).astype(bf16)
    grad_output = co_ref[0].astype(f32)
    grad_mlp_f = scale_two * grad_output
    a_vec[0:1] += column_sum(grad_mlp_f)
    grad_mlp = grad_mlp_f.astype(bf16)
    mlp = None
    grad_normed_two = None
    for c in range(4):
        cols = slice(c * 256, (c + 1) * 256)
        hidden = nn(normed_two, uw[:, cols]) + ubias[:, cols]
        density = jnp.exp(hidden * hidden * -0.5) * (1.0 / math.sqrt(2.0 * math.pi))
        phi = 0.5 + 0.5 * lax.erf(hidden * math.sqrt(0.5))
        active = (hidden * phi).astype(bf16)
        part = nn(active, dw[cols, :])
        mlp = part if mlp is None else mlp + part
        a_dwt[:, cols] += tn(grad_mlp, active)
        grad_active = nt(grad_mlp, dw[cols, :])
        grad_hidden = (grad_active * (phi + hidden * density)).astype(bf16)
        a_ub[:, cols] += nn(ones, grad_hidden)
        a_uw[:, cols] += tn(normed_two, grad_hidden)
        part = nt(grad_hidden, uw[:, cols])
        grad_normed_two = part if grad_normed_two is None else grad_normed_two + part
    out_ref[0] = middle + scale_two * (mlp + down_bias)

    a_vec[3:4] += column_sum(grad_normed_two * unit_two)
    a_vec[4:5] += column_sum(grad_normed_two)
    grad_middle = grad_output + norm_back(grad_normed_two, unit_two, inverse_two, gain_two)
    grad_branch_f = scale_one * grad_middle
    a_vec[5:6] += column_sum(grad_branch_f)
    grad_branch = grad_branch_f.astype(bf16)
    a_ow[...] += tn(heads_out, grad_branch)
    grad_heads = nt(grad_branch, ow[...]).astype(bf16)
    grad_triple = []
    for j in range(2):
        padded = nn(pp_ref[j], grad_heads[:, j * 128 : (j + 1) * 128])
        parts = []
        for s in range(2):
            rows = slice(s * STRIPE, (s + 1) * STRIPE)
            query = qkv_ref[j, rows, 0:128]
            keys = spread_heads(qkv_ref[j, rows, 128:256], masks)
            value = qkv_ref[j, rows, 256:384]
            grad_f = padded[rows]
            grad = grad_f.astype(bf16)
            probs = p_ref[2 * j + s]
            grad_probs = nt(spread_heads(value, masks), grad)
            product = (probs * grad_probs).reshape(HEADS, STRIPE, STRIPE)
            inner = jnp.sum(product, axis=1, keepdims=True)
            probs_three = probs.reshape(HEADS, STRIPE, STRIPE)
            grad_scores = product - probs_three * inner
            grad_scores = grad_scores.reshape(HEADS * STRIPE, STRIPE).astype(bf16)
            grad_query = tn(grad_scores, keys) * scale
            grad_key = pick_heads(nn(grad_scores, query)) * scale
            grad_value = pick_heads(nn(probs.astype(bf16), grad))
            near = neighbours(grad_f)
            for a in range(3):
                part = near[2] * conv[j, 3 * a : 3 * a + 1]
                for b in range(1, 3):
                    part = part + near[2 - b] * conv[j, 3 * a + b : 3 * a + b + 1]
                grad_value = grad_value + row_shift(part, 1 - a)
            near = neighbours(value.astype(f32))
            for b in range(3):
                a_conv[j, b] += tile_sum(grad_f[16:] * near[b][:-16])
                a_conv[j, 3 + b] += tile_sum(grad_f * near[b])
                a_conv[j, 6 + b] += tile_sum(grad_f[:-16] * near[b][16:])
            a_conv[j, 9] += tile_sum(grad_f)
            parts.append(
                jnp.concatenate([grad_query, grad_key, grad_value], axis=1).astype(bf16)
            )
        both = jnp.concatenate(parts, axis=0)
        grad_triple.append(nn(ppt_ref[j], both).astype(bf16))
    grad_triple = jnp.concatenate(grad_triple, axis=1)
    a_pb[...] += nn(ones, grad_triple)
    a_wq[...] += tn(normed, grad_triple)
    grad_normed = nt(grad_triple, wq[...])
    a_vec[1:2] += column_sum(grad_normed * unit_one)
    a_vec[2:3] += column_sum(grad_normed)
    gin_ref[0] = grad_middle + norm_back(grad_normed, unit_one, inverse_one, gain_one)

    @pl.when(image == pl.num_programs(0) - 1)
    def _():
        for c in range(8):
            cols = slice(c * 128, (c + 1) * 128)
            flat[pl.ds(c, D, stride=8), :] = a_uw[:, cols]
            flat[2048 + c : 2049 + c, :] = a_ub[0:1, cols]
        for q in range(4):
            turned = a_dwt[:, q * 256 : (q + 1) * 256].T
            for c in range(2):
                flat[pl.ds(2056 + 512 * q + c, 256, stride=2), :] = turned[
                    :, c * 128 : (c + 1) * 128
                ]
        for c in range(2):
            cols = slice(c * 128, (c + 1) * 128)
            for i in range(6):
                flat[4104 + 2 * i + c : 4105 + 2 * i + c, :] = a_vec[i : i + 1, cols]
        for j in range(2):
            for c in range(3):
                cols = slice(j * 384 + c * 128, j * 384 + (c + 1) * 128)
                gflat[j, pl.ds(c, D, stride=3), :] = a_wq[:, cols]
            for c in range(2):
                cols = slice(c * 128, (c + 1) * 128)
                gflat[j, pl.ds(770 + c, HALF, stride=2), :] = a_ow[
                    j * 128 : (j + 1) * 128, cols
                ]
            gflat[j, 768:769, :] = a_pb[0:1, j * 384 : j * 384 + 128]
            gflat[j, 769:770, :] = a_pb[0:1, j * 384 + 256 : j * 384 + 384]
            for i in range(10):
                gflat[j, 1026 + i : 1027 + i, :] = column_sum(a_conv[j, i])
        for k in range(n):
            at = first_row(SHARED_PARAMS, n, k)
            gblocks_ref[k, 0:srows] = flat[at : at + srows].astype(bf16)
            at = first_row(GROUP_PARAMS, n_dp, k // 2)
            gblocks_ref[k, srows : srows + grows] = gflat[k % 2, at : at + grows].astype(bf16)


def compute(n_dp, srows, grows, drops, images, cotangent, blocks):
    n = 2 * n_dp
    count = images.shape[0]
    rows = srows + grows
    flat_rows = max(4120, first_row(SHARED_PARAMS, n, n - 1) + srows)
    gflat_rows = max(1040, first_row(GROUP_PARAMS, n_dp, n_dp - 1) + grows)
    one_image = lambda i: (i, 0, 0)
    whole = lambda i: (0, 0, 0)
    return pl.pallas_call(
        partial(compute_kernel, n_dp, srows, grows),
        grid=(count,),
        in_specs=[
            pl.BlockSpec(memory_space=pltpu.SMEM),
            pl.BlockSpec((1, TOK, D), one_image),
            pl.BlockSpec((1, TOK, D), one_image),
            pl.BlockSpec((n, rows, 128), whole, pipeline_mode=pl.Buffered(1)),
        ],
        out_specs=[
            pl.BlockSpec((1, TOK, D), one_image),
            pl.BlockSpec((1, TOK, D), one_image),
            pl.BlockSpec((n, rows, 128), whole, pipeline_mode=pl.Buffered(1)),
        ],
        out_shape=[
            jax.ShapeDtypeStruct((count, TOK, D), f32),
            jax.ShapeDtypeStruct((count, TOK, D), f32),
            jax.ShapeDtypeStruct((n, rows, 128), bf16),
        ],
        scratch_shapes=[
            pltpu.VMEM((flat_rows, 128), f32),
            pltpu.VMEM((2, gflat_rows, 128), f32),
            pltpu.VMEM((2, GRID, TOK), bf16),
            pltpu.VMEM((2, TOK, GRID), bf16),
            pltpu.VMEM((D, 768), bf16),
            pltpu.VMEM((D, D), bf16),
            pltpu.VMEM((D, FF), bf16),
            pltpu.VMEM((FF, D), bf16),
            pltpu.VMEM((1, 768), f32),
            pltpu.VMEM((1, FF), f32),
            pltpu.VMEM((8, D), f32),
            pltpu.VMEM((2, 16, 128), f32),
            pltpu.VMEM((D, 768), f32),
            pltpu.VMEM((D, D), f32),
            pltpu.VMEM((D, FF), f32),
            pltpu.VMEM((D, FF), f32),
            pltpu.VMEM((8, 768), f32),
            pltpu.VMEM((8, FF), f32),
            pltpu.VMEM((8, D), f32),
            pltpu.VMEM((2, 10, 8, 128), f32),
            pltpu.VMEM((4, HEADS * STRIPE, STRIPE), f32),
            pltpu.VMEM((2, GRID, 384), bf16),
        ],
        compiler_params=pltpu.CompilerParams(
            dimension_semantics=("arbitrary",), vmem_limit_bytes=56 * 1024 * 1024
        ),
        name="block",
    )(drops, images, cotangent, blocks)


def adam_step(master, gradient, first, second, step):
    first_new = beta_one * first + (1.0 - beta_one) * gradient
    second_new = beta_two * second + (1.0 - beta_two) * gradient * gradient
    first_hat = first_new / (1.0 - jnp.power(jnp.float32(beta_one), step))
    second_hat = second_new / (1.0 - jnp.power(jnp.float32(beta_two), step))
    master_new = master - learn_rate * (
        first_hat / (jnp.sqrt(second_hat) + adam_eps) + decay_rate * master
    )
    return (master_new, first_new, second_new)


def on_device(
    n_dp,
    images,
    cotangent,
    drop_masks,
    group_master,
    group_m1,
    group_m2,
    shared_master,
    shared_m1,
    shared_m2,
):
    n = 2 * n_dp
    srows = window_rows(SHARED_PARAMS, n)
    grows = window_rows(GROUP_PARAMS, n_dp)
    dp = lax.axis_index("dp")
    me = dp * 2 + lax.axis_index("heads")
    sshare, gshare = SHARED_PARAMS // n, GROUP_PARAMS // n_dp
    soff = lax.rem(me * sshare, UNIT)
    goff = lax.rem(dp * gshare, UNIT)
    sblock = lax.dynamic_update_slice(jnp.zeros((srows * 128,), f32), shared_master, (soff,))
    gblock = lax.dynamic_update_slice(jnp.zeros((grows * 128,), f32), group_master[0], (goff,))
    block = jnp.concatenate(
        [sblock.reshape(srows, 128), gblock.reshape(grows, 128)], axis=0
    ).astype(bf16)
    blocks = lax.all_gather(block, ("dp", "heads"), axis=0)
    output, input_grad, gblocks = compute(
        n_dp, srows, grows, drop_masks, images, cotangent, blocks
    )
    mine = lax.psum_scatter(gblocks, ("dp", "heads"), scatter_dimension=0).astype(f32)
    shared_share = lax.dynamic_slice(mine[:srows].reshape(-1), (soff,), (sshare,))
    group_share = lax.dynamic_slice(mine[srows:].reshape(-1), (goff,), (gshare,))
    group_share = group_share[None, :]
    squares = jnp.sum(group_share * group_share) + jnp.sum(shared_share * shared_share)
    grad_norm = jnp.sqrt(lax.psum(squares, ("dp", "heads")))
    threshold = math.sqrt(2 * GROUP_PARAMS + SHARED_PARAMS)
    factor = jnp.minimum(1.0, threshold / (grad_norm + 1e-06))
    group_grad = group_share * factor
    shared_grad = shared_share * factor
    step = jnp.float32(STEP)
    group_new, group_first, group_second = adam_step(
        group_master, group_grad, group_m1, group_m2, step
    )
    shared_new, shared_first, shared_second = adam_step(
        shared_master, shared_grad, shared_m1, shared_m2, step
    )
    return (
        output,
        input_grad,
        grad_norm.reshape(1),
        group_grad,
        group_new,
        group_first,
        group_second,
        group_new.astype(jnp.bfloat16),
        shared_grad,
        shared_new,
        shared_first,
        shared_second,
        shared_new.astype(jnp.bfloat16),
    )


def solution(mesh):
    both = P(("dp", "heads"))
    rows = P(("dp", "heads"), None, None)
    split = P("heads", "dp")
    in_specs = (rows, rows, P(("dp", "heads"), None), split, split, split, both, both, both)
    out_specs = (rows, rows, P(), split, split, split, split, split, both, both, both, both, both)
    return jax.shard_map(
        partial(on_device, mesh.shape["dp"]),
        mesh=mesh,
        in_specs=in_specs,
        out_specs=out_specs,
        check_vma=False,
    )
```

```python
from functools import partial
import math

import jax
import jax.numpy as jnp
from jax import lax
from jax.experimental import pallas as pl
from jax.experimental.pallas import tpu as pltpu
from jax.sharding import PartitionSpec as P

D = 256
FF = 1024
SIDE = 14
SW = 7
STEP = 10
HD = 32
HALF = 128
GROUP_PARAMS = 132608
SHARED_PARAMS = 526848
TOK = SIDE * SIDE
GRID = 16 * SIDE
STRIPE = 16 * SW
HEADS = HALF // HD
UNIT = 1024

eps_norm = 1e-05
keep_prob = 0.8
beta_one = 0.9
beta_two = 0.999
adam_eps = 1e-08
learn_rate = 0.04
decay_rate = 0.05

f32 = jnp.float32
bf16 = jnp.bfloat16


def window_rows(total, count):
    share = total // count
    most = max((share * k) % UNIT + share for k in range(count))
    return 16 * (-(-most // (2 * UNIT)))


def first_row(total, count, k):
    return (total // count * k) // UNIT * 8


HEADS_BIT = -1
FAST_BITS = 2


def exchange_orders(n_dp):
    bits = n_dp.bit_length() - 1
    far = list(range(bits - 1, 1, -1))
    near = [1] if bits > 1 else []
    core = [0] if bits > 0 else []
    return far + near + [HEADS_BIT] + core, far + [HEADS_BIT] + near + core


def place_of(order, k):
    dp, heads = k // 2, k % 2
    return sum(
        (heads if bit == HEADS_BIT else (dp >> bit) & 1) << t for t, bit in enumerate(order)
    )


def own_bits(order):
    dp, heads = lax.axis_index("dp"), lax.axis_index("heads")
    return [heads if bit == HEADS_BIT else (dp // (1 << bit)) % 2 for bit in order]


def partner(bit):
    if bit == HEADS_BIT:
        return {"heads": 1 - lax.axis_index("heads")}
    dp = lax.axis_index("dp")
    return {"dp": dp + (1 << bit) * (1 - 2 * ((dp // (1 << bit)) % 2))}


def half_rows(rows):
    first = 16 * (-(-rows // 32))
    return first, rows - first


def greet(devices):
    barrier = pltpu.get_barrier_semaphore()
    for device in devices:
        pl.semaphore_signal(barrier, inc=1, device_id=device)
    pl.semaphore_wait(barrier, len(devices))


def gather_kernel(orders, halves, own_ref, first_ref, second_ref, send_sem, recv_sem):
    greet([partner(bit) for bit in orders[0]])
    outs = (first_ref, second_ref)
    start = 0
    pending = []
    bits = [own_bits(order) for order in orders]
    for h in range(2):
        mine = sum(b * (1 << t) for t, b in enumerate(bits[h]))
        outs[h][mine] = own_ref[start : start + halves[h]].astype(bf16)
        start += halves[h]
        pending.append(None)
    for t in range(len(orders[0])):
        for h in range(2):
            if pending[h] is not None:
                pending[h].wait()
            base = sum(b * (1 << u) for u, b in enumerate(bits[h]) if u >= t)
            held = outs[h].at[pl.ds(base, 1 << t)]
            pending[h] = pltpu.make_async_remote_copy(
                src_ref=held,
                dst_ref=held,
                send_sem=send_sem.at[h, t],
                recv_sem=recv_sem.at[h, t],
                device_id=partner(orders[h][t]),
            )
            pending[h].start()
    for h in range(2):
        pending[h].wait()


def gather(n_dp, rows, own):
    n = 2 * n_dp
    orders = exchange_orders(n_dp)
    halves = half_rows(rows)
    stages = len(orders[0])
    return pl.pallas_call(
        partial(gather_kernel, orders, halves),
        in_specs=[pl.BlockSpec(memory_space=pltpu.VMEM)],
        out_specs=[pl.BlockSpec(memory_space=pltpu.VMEM)] * 2,
        out_shape=[jax.ShapeDtypeStruct((n, half, 128), bf16) for half in halves],
        scratch_shapes=[
            pltpu.SemaphoreType.DMA((2, stages)),
            pltpu.SemaphoreType.DMA((2, stages)),
        ],
        compiler_params=pltpu.CompilerParams(collective_id=0, has_side_effects=True),
        name="gather",
    )(own)


def group_peers(n_dp):
    dp, heads = lax.axis_index("dp"), lax.axis_index("heads")
    fast = min(1 << FAST_BITS, n_dp)
    low, high = dp % fast, dp // fast
    count = 2 * fast
    me = low * 2 + heads
    near = []
    for step in range(1, count):
        other = (me + step) % count
        near.append((other, {"dp": high * fast + other // 2, "heads": other % 2}))
    far = []
    for step in range(1, n_dp // fast):
        other = (high + step) % (n_dp // fast)
        far.append((other, {"dp": other * fast + low}))
    return (me, near), (high, far)


def all_share(me, peers, stat_ref, send_sem, recv_sem):
    copies = []
    for other, device in peers:
        copy = pltpu.make_async_remote_copy(
            src_ref=stat_ref.at[me],
            dst_ref=stat_ref.at[me],
            send_sem=send_sem.at[other],
            recv_sem=recv_sem.at[me],
            device_id=device,
        )
        copy.start()
        copies.append(copy)
    for other, device in peers:
        pltpu.make_async_remote_copy(
            src_ref=stat_ref.at[other],
            dst_ref=stat_ref.at[other],
            send_sem=send_sem.at[other],
            recv_sem=recv_sem.at[other],
            device_id=device,
        ).wait_recv()
    for copy in copies:
        copy.wait_send()
    return jnp.sum(stat_ref[...], axis=0)


def reduce_kernel(
    n_dp,
    srows,
    orders,
    halves,
    first_ref,
    second_ref,
    out_ref,
    norm_ref,
    acc_first,
    acc_second,
    out_first,
    out_second,
    in_first,
    in_second,
    near_stat,
    far_stat,
    send_sem,
    recv_sem,
    near_send,
    near_recv,
    far_send,
    far_recv,
):
    n = 2 * n_dp
    (near_me, near), (far_me, far) = group_peers(n_dp)
    greet([device for _, device in near] + [device for _, device in far])
    stages = len(orders[0])
    held = [first_ref, second_ref]
    accs = (acc_first, acc_second)
    outgoing = (out_first, out_second)
    incoming = (in_first, in_second)
    bits = [own_bits(order) for order in orders]
    pending = [None, None]
    start = [0, halves[0]]
    for t in range(stages - 1, -1, -1):
        count = 1 << t
        for h in range(2):
            source = held[h]
            if pending[h] is not None:
                pending[h].wait()
            arrived = 2 * count - 1
            keep, give = bits[h][t] * count, (1 - bits[h][t]) * count

            def value(i, at, h=h, source=source, arrived=arrived, last=pending[h] is None):
                got = source[at + i]
                if last:
                    return got
                return got + incoming[h][arrived + at + i].astype(f32)

            def fill(i, carry, h=h, give=give, count=count, value=value):
                outgoing[h][count - 1 + i] = value(i, give).astype(bf16)
                return carry

            lax.fori_loop(0, count, fill, 0)
            copy = pltpu.make_async_remote_copy(
                src_ref=outgoing[h].at[pl.ds(count - 1, count)],
                dst_ref=incoming[h].at[pl.ds(count - 1, count)],
                send_sem=send_sem.at[h, t],
                recv_sem=recv_sem.at[h, t],
                device_id=partner(orders[h][t]),
            )
            copy.start()
            pending[h] = copy

            def retain(i, carry, h=h, keep=keep, count=count, value=value):
                accs[h][count - 1 + i] = value(i, keep)
                return carry

            lax.fori_loop(0, count, retain, 0)
            held[h] = accs[h].at[pl.ds(count - 1, count)]
    dp = lax.axis_index("dp")
    me = dp * 2 + lax.axis_index("heads")
    sshare, gshare = SHARED_PARAMS // n, GROUP_PARAMS // n_dp
    soff = (me * sshare) % UNIT
    goff = (dp * gshare) % UNIT
    total = jnp.zeros((8, 128), f32)
    for h in range(2):
        pending[h].wait()
        value = held[h][0] + incoming[h][0].astype(f32)
        out_ref[start[h] : start[h] + halves[h]] = value
        row = lax.broadcasted_iota(jnp.int32, (halves[h], 128), 0) + start[h]
        place = row * 128 + lax.broadcasted_iota(jnp.int32, (halves[h], 128), 1)
        shared = (row < srows) & (place >= soff) & (place < soff + sshare)
        place = place - srows * 128
        grouped = (row >= srows) & (place >= goff) & (place < goff + gshare)
        own = jnp.where(shared | grouped, value, 0.0)
        total = total + jnp.sum((own * own).reshape(-1, 8, 128), axis=0)
    near_stat[near_me] = total
    far_stat[far_me] = all_share(near_me, near, near_stat, near_send, near_recv)
    total = all_share(far_me, far, far_stat, far_send, far_recv)
    total = jnp.sum(jnp.sum(total, axis=0, keepdims=True), axis=1, keepdims=True)
    norm = jnp.sqrt(total)
    norm_ref[...] = jnp.broadcast_to(norm, (8, 128))
    threshold = math.sqrt(2 * GROUP_PARAMS + SHARED_PARAMS)
    out_ref[...] = out_ref[...] * jnp.minimum(1.0, threshold / (norm + 1e-06))


def reduce(n_dp, srows, first, second):
    n = 2 * n_dp
    orders = exchange_orders(n_dp)
    halves = (first.shape[1], second.shape[1])
    stages = len(orders[0])
    fast = min(1 << FAST_BITS, n_dp)
    near, far = 2 * fast, n_dp // fast
    dma = pltpu.SemaphoreType.DMA
    return pl.pallas_call(
        partial(reduce_kernel, n_dp, srows, orders, halves),
        in_specs=[pl.BlockSpec(memory_space=pltpu.VMEM)] * 2,
        out_specs=[pl.BlockSpec(memory_space=pltpu.VMEM)] * 2,
        out_shape=[
            jax.ShapeDtypeStruct((sum(halves), 128), f32),
            jax.ShapeDtypeStruct((8, 128), f32),
        ],
        scratch_shapes=[pltpu.VMEM((n - 1, half, 128), f32) for half in halves]
        + [pltpu.VMEM((n - 1, half, 128), bf16) for half in halves] * 2
        + [
            pltpu.VMEM((near, 8, 128), f32),
            pltpu.VMEM((far, 8, 128), f32),
            dma((2, stages)),
            dma((2, stages)),
            dma((near,)),
            dma((near,)),
            dma((far,)),
            dma((far,)),
        ],
        compiler_params=pltpu.CompilerParams(
            collective_id=1, has_side_effects=True, vmem_limit_bytes=56 * 1024 * 1024
        ),
        name="reduce",
    )(first, second)


def window_parts(halves, rows):
    parts = []
    start = 0
    for h, size in enumerate(halves):
        low, high = max(rows[0], start), min(rows[1], start + size)
        if low < high:
            parts.append((h, low - start, high - start, low - rows[0], high - rows[0]))
        start += size
    return parts


def nn(a, b):
    return lax.dot_general(a, b, (((1,), (0,)), ((), ())), preferred_element_type=f32)


def nt(a, b):
    return lax.dot_general(a, b, (((1,), (1,)), ((), ())), preferred_element_type=f32)


def tn(a, b):
    return lax.dot_general(a, b, (((0,), (0,)), ((), ())), preferred_element_type=f32)


def norm_parts(values):
    center = values - jnp.mean(values, axis=-1, keepdims=True)
    inverse = lax.rsqrt(jnp.mean(center * center, axis=-1, keepdims=True) + eps_norm)
    return center * inverse, inverse


def norm_back(grad_after, unit, inverse, gain):
    scaled = grad_after * gain
    return inverse * (
        scaled
        - jnp.mean(scaled, axis=-1, keepdims=True)
        - unit * jnp.mean(scaled * unit, axis=-1, keepdims=True)
    )


def column_sum(values):
    return jnp.sum(values, axis=0, keepdims=True)


def head_masks(dtype):
    lane = lax.broadcasted_iota(jnp.int32, (1, HALF), 1) // HD
    return [(lane == h).astype(f32).astype(dtype) for h in range(HEADS)]


def spread_heads(values, masks):
    return jnp.concatenate([values * masks[h] for h in range(HEADS)], axis=0)


def pick_heads(stacked):
    lane = lax.broadcasted_iota(jnp.int32, (STRIPE, HALF), 1)
    picked = stacked[(HEADS - 1) * STRIPE :]
    for h in range(HEADS - 2, -1, -1):
        picked = jnp.where(lane < (h + 1) * HD, stacked[h * STRIPE : (h + 1) * STRIPE], picked)
    return picked


def row_shift(values, step):
    if step == 0:
        return values
    zero = jnp.zeros((16, HALF), f32)
    if step > 0:
        return jnp.concatenate([values[16:], zero], axis=0)
    return jnp.concatenate([zero, values[:-16]], axis=0)


def neighbours(values):
    return [pltpu.roll(values, 1, 0), values, pltpu.roll(values, STRIPE - 1, 0)]


def tile_sum(values):
    return jnp.sum(values.reshape(-1, 8, HALF), axis=0)


def place_matrices(pp_ref, ppt_ref):
    place = lax.broadcasted_iota(jnp.int32, (GRID, TOK), 0)
    token = lax.broadcasted_iota(jnp.int32, (GRID, TOK), 1)
    first, second = place // 16, place % 16
    inside = second < SIDE
    pp_ref[0] = (inside & (token == first * SIDE + second)).astype(f32).astype(bf16)
    pp_ref[1] = (inside & (token == second * SIDE + first)).astype(f32).astype(bf16)
    place = lax.broadcasted_iota(jnp.int32, (TOK, GRID), 1)
    token = lax.broadcasted_iota(jnp.int32, (TOK, GRID), 0)
    first, second = place // 16, place % 16
    inside = second < SIDE
    ppt_ref[0] = (inside & (token == first * SIDE + second)).astype(f32).astype(bf16)
    ppt_ref[1] = (inside & (token == second * SIDE + first)).astype(f32).astype(bf16)


def compute_kernel(
    n_dp,
    srows,
    grows,
    orders,
    halves,
    drop_ref,
    x_ref,
    co_ref,
    first_ref,
    second_ref,
    out_ref,
    gin_ref,
    gfirst_ref,
    gsecond_ref,
    flat,
    gflat,
    pp_ref,
    ppt_ref,
    wq,
    ow,
    uw,
    dw,
    qbias,
    ubias,
    vecs,
    conv,
    a_wq,
    a_ow,
    a_uw,
    a_dwt,
    a_pb,
    a_ub,
    a_vec,
    a_conv,
    p_ref,
    qkv_ref,
):
    image = pl.program_id(0)
    n = 2 * n_dp
    weights, gradients = (first_ref, second_ref), (gfirst_ref, gsecond_ref)
    shared_parts = window_parts(halves, (0, srows))
    group_parts = window_parts(halves, (srows, srows + grows))

    @pl.when(image == 0)
    def _():
        place_matrices(pp_ref, ppt_ref)
        flat[...] = jnp.zeros_like(flat)
        gflat[...] = jnp.zeros_like(gflat)
        for k in range(n):
            at = first_row(SHARED_PARAMS, n, k)
            for h, low, high, begin, end in shared_parts:
                window = weights[h][place_of(orders[h], k), low:high]
                flat[at + begin : at + end] += window.astype(f32)
            at = first_row(GROUP_PARAMS, n_dp, k // 2)
            for h, low, high, begin, end in group_parts:
                window = weights[h][place_of(orders[h], k), low:high]
                gflat[k % 2, at + begin : at + end] += window.astype(f32)
        for c in range(8):
            cols = slice(c * 128, (c + 1) * 128)
            uw[:, cols] = flat[pl.ds(c, D, stride=8), :].astype(bf16)
            ubias[:, cols] = flat[2048 + c : 2049 + c, :]
        for c in range(2):
            cols = slice(c * 128, (c + 1) * 128)
            dw[:, cols] = flat[pl.ds(2056 + c, FF, stride=2), :].astype(bf16)
            for i in range(6):
                vecs[i : i + 1, cols] = flat[4104 + 2 * i + c : 4105 + 2 * i + c, :]
        for j in range(2):
            for c in range(3):
                cols = slice(j * 384 + c * 128, j * 384 + (c + 1) * 128)
                wq[:, cols] = gflat[j, pl.ds(c, D, stride=3), :].astype(bf16)
            for c in range(2):
                cols = slice(c * 128, (c + 1) * 128)
                ow[j * 128 : (j + 1) * 128, cols] = gflat[
                    j, pl.ds(770 + c, HALF, stride=2), :
                ].astype(bf16)
            qbias[:, j * 384 : j * 384 + 128] = gflat[j, 768:769, :]
            qbias[:, j * 384 + 128 : j * 384 + 256] = jnp.zeros((1, 128), f32)
            qbias[:, j * 384 + 256 : j * 384 + 384] = gflat[j, 769:770, :]
            conv[j, 0:10] = gflat[j, 1026:1036, :]
        for ref in (a_wq, a_ow, a_uw, a_dwt, a_pb, a_ub, a_vec, a_conv):
            ref[...] = jnp.zeros_like(ref)

    scale_one = drop_ref[image, 0].astype(f32) / keep_prob
    scale_two = drop_ref[image, 1].astype(f32) / keep_prob
    down_bias, gain_one, shift_one = vecs[0:1], vecs[1:2], vecs[2:3]
    gain_two, shift_two, out_bias = vecs[3:4], vecs[4:5], vecs[5:6]
    masks = head_masks(bf16)
    ones = jnp.ones((8, TOK), bf16)
    key_row = lax.broadcasted_iota(jnp.int32, (1, SW, 16, STRIPE), 2)
    scale = HD ** (-0.5)

    values = x_ref[0].astype(f32)
    unit_one, inverse_one = norm_parts(values)
    normed = (unit_one * gain_one + shift_one).astype(bf16)
    triple = (nn(normed, wq[...]) + qbias[...]).astype(bf16)
    heads_out = []
    for j in range(2):
        qkv_ref[j] = nn(pp_ref[j], triple[:, j * 384 : (j + 1) * 384]).astype(bf16)
        parts = []
        for s in range(2):
            rows = slice(s * STRIPE, (s + 1) * STRIPE)
            query = qkv_ref[j, rows, 0:128]
            keys = spread_heads(qkv_ref[j, rows, 128:256], masks)
            value = qkv_ref[j, rows, 256:384]
            scores = nt(keys, query).reshape(HEADS, SW, 16, STRIPE) * scale
            scores = jnp.where(key_row < SIDE, scores, -1e30)
            scores = scores.reshape(HEADS, STRIPE, STRIPE)
            weights = jnp.exp(scores - jnp.max(scores, axis=1, keepdims=True))
            probs = weights * (1.0 / jnp.sum(weights, axis=1, keepdims=True))
            probs = probs.reshape(HEADS * STRIPE, STRIPE)
            p_ref[2 * j + s] = probs
            attended = tn(probs.astype(bf16), spread_heads(value, masks))
            near = neighbours(value.astype(f32))
            total = attended + conv[j, 9:10]
            for a in range(3):
                part = near[0] * conv[j, 3 * a : 3 * a + 1]
                for b in range(1, 3):
                    part = part + near[b] * conv[j, 3 * a + b : 3 * a + b + 1]
                total = total + row_shift(part, a - 1)
            parts.append(total.astype(bf16))
        padded = jnp.concatenate(parts, axis=0)
        heads_out.append(nn(ppt_ref[j], padded).astype(bf16))
    heads_out = jnp.concatenate(heads_out, axis=1)
    branch = nn(heads_out, ow[...])
    middle = values + scale_one * (branch + out_bias)
    unit_two, inverse_two = norm_parts(middle)
    normed_two = (unit_two * gain_two + shift_two).astype(bf16)
    grad_output = co_ref[0].astype(f32)
    grad_mlp_f = scale_two * grad_output
    a_vec[0:1] += column_sum(grad_mlp_f)
    grad_mlp = grad_mlp_f.astype(bf16)
    mlp = None
    grad_normed_two = None
    for c in range(4):
        cols = slice(c * 256, (c + 1) * 256)
        hidden = nn(normed_two, uw[:, cols]) + ubias[:, cols]
        density = jnp.exp(hidden * hidden * -0.5) * (1.0 / math.sqrt(2.0 * math.pi))
        phi = 0.5 + 0.5 * lax.erf(hidden * math.sqrt(0.5))
        active = (hidden * phi).astype(bf16)
        part = nn(active, dw[cols, :])
        mlp = part if mlp is None else mlp + part
        a_dwt[:, cols] += tn(grad_mlp, active)
        grad_active = nt(grad_mlp, dw[cols, :])
        grad_hidden = (grad_active * (phi + hidden * density)).astype(bf16)
        a_ub[:, cols] += nn(ones, grad_hidden)
        a_uw[:, cols] += tn(normed_two, grad_hidden)
        part = nt(grad_hidden, uw[:, cols])
        grad_normed_two = part if grad_normed_two is None else grad_normed_two + part
    out_ref[0] = middle + scale_two * (mlp + down_bias)

    a_vec[3:4] += column_sum(grad_normed_two * unit_two)
    a_vec[4:5] += column_sum(grad_normed_two)
    grad_middle = grad_output + norm_back(grad_normed_two, unit_two, inverse_two, gain_two)
    grad_branch_f = scale_one * grad_middle
    a_vec[5:6] += column_sum(grad_branch_f)
    grad_branch = grad_branch_f.astype(bf16)
    a_ow[...] += tn(heads_out, grad_branch)
    grad_heads = nt(grad_branch, ow[...]).astype(bf16)
    grad_triple = []
    for j in range(2):
        padded = nn(pp_ref[j], grad_heads[:, j * 128 : (j + 1) * 128])
        parts = []
        for s in range(2):
            rows = slice(s * STRIPE, (s + 1) * STRIPE)
            query = qkv_ref[j, rows, 0:128]
            keys = spread_heads(qkv_ref[j, rows, 128:256], masks)
            value = qkv_ref[j, rows, 256:384]
            grad_f = padded[rows]
            grad = grad_f.astype(bf16)
            probs = p_ref[2 * j + s]
            grad_probs = nt(spread_heads(value, masks), grad)
            product = (probs * grad_probs).reshape(HEADS, STRIPE, STRIPE)
            inner = jnp.sum(product, axis=1, keepdims=True)
            probs_three = probs.reshape(HEADS, STRIPE, STRIPE)
            grad_scores = product - probs_three * inner
            grad_scores = grad_scores.reshape(HEADS * STRIPE, STRIPE).astype(bf16)
            grad_query = tn(grad_scores, keys) * scale
            grad_key = pick_heads(nn(grad_scores, query)) * scale
            grad_value = pick_heads(nn(probs.astype(bf16), grad))
            near = neighbours(grad_f)
            for a in range(3):
                part = near[2] * conv[j, 3 * a : 3 * a + 1]
                for b in range(1, 3):
                    part = part + near[2 - b] * conv[j, 3 * a + b : 3 * a + b + 1]
                grad_value = grad_value + row_shift(part, 1 - a)
            near = neighbours(value.astype(f32))
            for b in range(3):
                a_conv[j, b] += tile_sum(grad_f[16:] * near[b][:-16])
                a_conv[j, 3 + b] += tile_sum(grad_f * near[b])
                a_conv[j, 6 + b] += tile_sum(grad_f[:-16] * near[b][16:])
            a_conv[j, 9] += tile_sum(grad_f)
            parts.append(
                jnp.concatenate([grad_query, grad_key, grad_value], axis=1).astype(bf16)
            )
        both = jnp.concatenate(parts, axis=0)
        grad_triple.append(nn(ppt_ref[j], both).astype(bf16))
    grad_triple = jnp.concatenate(grad_triple, axis=1)
    a_pb[...] += nn(ones, grad_triple)
    a_wq[...] += tn(normed, grad_triple)
    grad_normed = nt(grad_triple, wq[...])
    a_vec[1:2] += column_sum(grad_normed * unit_one)
    a_vec[2:3] += column_sum(grad_normed)
    gin_ref[0] = grad_middle + norm_back(grad_normed, unit_one, inverse_one, gain_one)

    @pl.when(image == pl.num_programs(0) - 1)
    def _():
        for c in range(8):
            cols = slice(c * 128, (c + 1) * 128)
            flat[pl.ds(c, D, stride=8), :] = a_uw[:, cols]
            flat[2048 + c : 2049 + c, :] = a_ub[0:1, cols]
        for q in range(4):
            turned = a_dwt[:, q * 256 : (q + 1) * 256].T
            for c in range(2):
                flat[pl.ds(2056 + 512 * q + c, 256, stride=2), :] = turned[
                    :, c * 128 : (c + 1) * 128
                ]
        for c in range(2):
            cols = slice(c * 128, (c + 1) * 128)
            for i in range(6):
                flat[4104 + 2 * i + c : 4105 + 2 * i + c, :] = a_vec[i : i + 1, cols]
        for j in range(2):
            for c in range(3):
                cols = slice(j * 384 + c * 128, j * 384 + (c + 1) * 128)
                gflat[j, pl.ds(c, D, stride=3), :] = a_wq[:, cols]
            for c in range(2):
                cols = slice(c * 128, (c + 1) * 128)
                gflat[j, pl.ds(770 + c, HALF, stride=2), :] = a_ow[
                    j * 128 : (j + 1) * 128, cols
                ]
            gflat[j, 768:769, :] = a_pb[0:1, j * 384 : j * 384 + 128]
            gflat[j, 769:770, :] = a_pb[0:1, j * 384 + 256 : j * 384 + 384]
            for i in range(10):
                gflat[j, 1026 + i : 1027 + i, :] = column_sum(a_conv[j, i])
        for k in range(n):
            at = first_row(SHARED_PARAMS, n, k)
            for h, low, high, begin, end in shared_parts:
                gradients[h][place_of(orders[h], k), low:high] = flat[at + begin : at + end]
            at = first_row(GROUP_PARAMS, n_dp, k // 2)
            for h, low, high, begin, end in group_parts:
                gradients[h][place_of(orders[h], k), low:high] = gflat[
                    k % 2, at + begin : at + end
                ]


def compute(n_dp, srows, grows, drops, images, cotangent, first, second):
    n = 2 * n_dp
    count = images.shape[0]
    halves = (first.shape[1], second.shape[1])
    flat_rows = max(4120, first_row(SHARED_PARAMS, n, n - 1) + srows)
    gflat_rows = max(1040, first_row(GROUP_PARAMS, n_dp, n_dp - 1) + grows)
    one_image = lambda i: (i, 0, 0)
    whole = lambda i: (0, 0, 0)
    return pl.pallas_call(
        partial(compute_kernel, n_dp, srows, grows, exchange_orders(n_dp), halves),
        grid=(count,),
        in_specs=[
            pl.BlockSpec(memory_space=pltpu.SMEM),
            pl.BlockSpec((1, TOK, D), one_image),
            pl.BlockSpec((1, TOK, D), one_image),
        ]
        + [
            pl.BlockSpec((n, half, 128), whole, pipeline_mode=pl.Buffered(1)) for half in halves
        ],
        out_specs=[
            pl.BlockSpec((1, TOK, D), one_image),
            pl.BlockSpec((1, TOK, D), one_image),
        ]
        + [
            pl.BlockSpec((n, half, 128), whole, pipeline_mode=pl.Buffered(1)) for half in halves
        ],
        out_shape=[
            jax.ShapeDtypeStruct((count, TOK, D), f32),
            jax.ShapeDtypeStruct((count, TOK, D), f32),
        ]
        + [jax.ShapeDtypeStruct((n, half, 128), f32) for half in halves],
        scratch_shapes=[
            pltpu.VMEM((flat_rows, 128), f32),
            pltpu.VMEM((2, gflat_rows, 128), f32),
            pltpu.VMEM((2, GRID, TOK), bf16),
            pltpu.VMEM((2, TOK, GRID), bf16),
            pltpu.VMEM((D, 768), bf16),
            pltpu.VMEM((D, D), bf16),
            pltpu.VMEM((D, FF), bf16),
            pltpu.VMEM((FF, D), bf16),
            pltpu.VMEM((1, 768), f32),
            pltpu.VMEM((1, FF), f32),
            pltpu.VMEM((8, D), f32),
            pltpu.VMEM((2, 16, 128), f32),
            pltpu.VMEM((D, 768), f32),
            pltpu.VMEM((D, D), f32),
            pltpu.VMEM((D, FF), f32),
            pltpu.VMEM((D, FF), f32),
            pltpu.VMEM((8, 768), f32),
            pltpu.VMEM((8, FF), f32),
            pltpu.VMEM((8, D), f32),
            pltpu.VMEM((2, 10, 8, 128), f32),
            pltpu.VMEM((4, HEADS * STRIPE, STRIPE), f32),
            pltpu.VMEM((2, GRID, 384), bf16),
        ],
        compiler_params=pltpu.CompilerParams(
            dimension_semantics=("arbitrary",), vmem_limit_bytes=56 * 1024 * 1024
        ),
        name="block",
    )(drops, images, cotangent, first, second)


def adam_step(master, gradient, first, second, step):
    first_new = beta_one * first + (1.0 - beta_one) * gradient
    second_new = beta_two * second + (1.0 - beta_two) * gradient * gradient
    first_hat = first_new / (1.0 - jnp.power(jnp.float32(beta_one), step))
    second_hat = second_new / (1.0 - jnp.power(jnp.float32(beta_two), step))
    master_new = master - learn_rate * (
        first_hat / (jnp.sqrt(second_hat) + adam_eps) + decay_rate * master
    )
    return (master_new, first_new, second_new)


def on_device(
    n_dp,
    images,
    cotangent,
    drop_masks,
    group_master,
    group_m1,
    group_m2,
    shared_master,
    shared_m1,
    shared_m2,
):
    n = 2 * n_dp
    srows = window_rows(SHARED_PARAMS, n)
    grows = window_rows(GROUP_PARAMS, n_dp)
    dp = lax.axis_index("dp")
    me = dp * 2 + lax.axis_index("heads")
    sshare, gshare = SHARED_PARAMS // n, GROUP_PARAMS // n_dp
    soff = lax.rem(me * sshare, UNIT)
    goff = lax.rem(dp * gshare, UNIT)
    sblock = lax.dynamic_update_slice(jnp.zeros((srows * 128,), f32), shared_master, (soff,))
    gblock = lax.dynamic_update_slice(jnp.zeros((grows * 128,), f32), group_master[0], (goff,))
    own = jnp.concatenate([sblock.reshape(srows, 128), gblock.reshape(grows, 128)], axis=0)
    first, second = gather(n_dp, srows + grows, own)
    output, input_grad, first, second = compute(
        n_dp, srows, grows, drop_masks, images, cotangent, first, second
    )
    mine, norm = reduce(n_dp, srows, first, second)
    shared_grad = lax.dynamic_slice(mine[:srows].reshape(-1), (soff,), (sshare,))
    group_grad = lax.dynamic_slice(mine[srows:].reshape(-1), (goff,), (gshare,))[None, :]
    step = jnp.float32(STEP)
    group_new, group_first, group_second = adam_step(
        group_master, group_grad, group_m1, group_m2, step
    )
    shared_new, shared_first, shared_second = adam_step(
        shared_master, shared_grad, shared_m1, shared_m2, step
    )
    return (
        output,
        input_grad,
        norm[0, 0:1],
        group_grad,
        group_new,
        group_first,
        group_second,
        group_new.astype(jnp.bfloat16),
        shared_grad,
        shared_new,
        shared_first,
        shared_second,
        shared_new.astype(jnp.bfloat16),
    )


def solution(mesh):
    both = P(("dp", "heads"))
    rows = P(("dp", "heads"), None, None)
    split = P("heads", "dp")
    in_specs = (rows, rows, P(("dp", "heads"), None), split, split, split, both, both, both)
    out_specs = (rows, rows, P(), split, split, split, split, split, both, both, both, both, both)
    return jax.shard_map(
        partial(on_device, mesh.shape["dp"]),
        mesh=mesh,
        in_specs=in_specs,
        out_specs=out_specs,
        check_vma=False,
    )
```

```python
from functools import partial
import math

import jax
import jax.numpy as jnp
from jax import lax
from jax.experimental import pallas as pl
from jax.experimental.pallas import tpu as pltpu
from jax.sharding import PartitionSpec as P

D = 256
FF = 1024
SIDE = 14
SW = 7
STEP = 10
HD = 32
HALF = 128
GROUP_PARAMS = 132608
SHARED_PARAMS = 526848
TOK = SIDE * SIDE
GRID = 16 * SIDE
STRIPE = 16 * SW
HEADS = HALF // HD
UNIT = 1024

eps_norm = 1e-05
keep_prob = 0.8
beta_one = 0.9
beta_two = 0.999
adam_eps = 1e-08
learn_rate = 0.04
decay_rate = 0.05

f32 = jnp.float32
bf16 = jnp.bfloat16


def window_rows(total, count):
    share = total // count
    most = max((share * k) % UNIT + share for k in range(count))
    return 16 * (-(-most // (2 * UNIT)))


def first_row(total, count, k):
    return (total // count * k) // UNIT * 8


HEADS_BIT = -1
FAST_BITS = 2


def exchange_orders(n_dp):
    bits = n_dp.bit_length() - 1
    far = list(range(bits - 1, 1, -1))
    near = [1] if bits > 1 else []
    core = [0] if bits > 0 else []
    return far + near + [HEADS_BIT] + core, far + [HEADS_BIT] + near + core


def place_of(order, k):
    dp, heads = k // 2, k % 2
    return sum(
        (heads if bit == HEADS_BIT else (dp >> bit) & 1) << t for t, bit in enumerate(order)
    )


def own_bits(order):
    dp, heads = lax.axis_index("dp"), lax.axis_index("heads")
    return [heads if bit == HEADS_BIT else (dp // (1 << bit)) % 2 for bit in order]


def partner(bit):
    if bit == HEADS_BIT:
        return {"heads": 1 - lax.axis_index("heads")}
    dp = lax.axis_index("dp")
    return {"dp": dp + (1 << bit) * (1 - 2 * ((dp // (1 << bit)) % 2))}


def half_rows(rows):
    first = 16 * (-(-rows // 32))
    return first, rows - first


def greet(devices):
    barrier = pltpu.get_barrier_semaphore()
    for device in devices:
        pl.semaphore_signal(barrier, inc=1, device_id=device)
    pl.semaphore_wait(barrier, len(devices))


def gather_kernel(orders, halves, own_ref, first_ref, second_ref, send_sem, recv_sem):
    greet([partner(bit) for bit in orders[0]])
    outs = (first_ref, second_ref)
    start = 0
    pending = []
    bits = [own_bits(order) for order in orders]
    for h in range(2):
        mine = sum(b * (1 << t) for t, b in enumerate(bits[h]))
        outs[h][mine] = own_ref[start : start + halves[h]].astype(bf16)
        start += halves[h]
        pending.append(None)
    for t in range(len(orders[0])):
        for h in range(2):
            if pending[h] is not None:
                pending[h].wait()
            base = sum(b * (1 << u) for u, b in enumerate(bits[h]) if u >= t)
            held = outs[h].at[pl.ds(base, 1 << t)]
            pending[h] = pltpu.make_async_remote_copy(
                src_ref=held,
                dst_ref=held,
                send_sem=send_sem.at[h, t],
                recv_sem=recv_sem.at[h, t],
                device_id=partner(orders[h][t]),
            )
            pending[h].start()
    for h in range(2):
        pending[h].wait()


def gather(n_dp, rows, own):
    n = 2 * n_dp
    orders = exchange_orders(n_dp)
    halves = half_rows(rows)
    stages = len(orders[0])
    return pl.pallas_call(
        partial(gather_kernel, orders, halves),
        in_specs=[pl.BlockSpec(memory_space=pltpu.VMEM)],
        out_specs=[pl.BlockSpec(memory_space=pltpu.VMEM)] * 2,
        out_shape=[jax.ShapeDtypeStruct((n, half, 128), bf16) for half in halves],
        scratch_shapes=[
            pltpu.SemaphoreType.DMA((2, stages)),
            pltpu.SemaphoreType.DMA((2, stages)),
        ],
        compiler_params=pltpu.CompilerParams(collective_id=0, has_side_effects=True),
        name="gather",
    )(own)


def group_peers(n_dp):
    dp, heads = lax.axis_index("dp"), lax.axis_index("heads")
    fast = min(1 << FAST_BITS, n_dp)
    low, high = dp % fast, dp // fast
    count = 2 * fast
    me = low * 2 + heads
    near = []
    for step in range(1, count):
        other = (me + step) % count
        near.append((other, {"dp": high * fast + other // 2, "heads": other % 2}))
    far = []
    for step in range(1, n_dp // fast):
        other = (high + step) % (n_dp // fast)
        far.append((other, {"dp": other * fast + low}))
    return (me, near), (high, far)


def all_share(me, peers, stat_ref, send_sem, recv_sem):
    copies = []
    for other, device in peers:
        copy = pltpu.make_async_remote_copy(
            src_ref=stat_ref.at[me],
            dst_ref=stat_ref.at[me],
            send_sem=send_sem.at[other],
            recv_sem=recv_sem.at[me],
            device_id=device,
        )
        copy.start()
        copies.append(copy)
    for other, device in peers:
        pltpu.make_async_remote_copy(
            src_ref=stat_ref.at[other],
            dst_ref=stat_ref.at[other],
            send_sem=send_sem.at[other],
            recv_sem=recv_sem.at[other],
            device_id=device,
        ).wait_recv()
    for copy in copies:
        copy.wait_send()
    return jnp.sum(stat_ref[...], axis=0)


def reduce_kernel(
    n_dp,
    srows,
    orders,
    halves,
    first_ref,
    second_ref,
    out_ref,
    norm_ref,
    acc_first,
    acc_second,
    out_first,
    out_second,
    in_first,
    in_second,
    near_stat,
    far_stat,
    send_sem,
    recv_sem,
    near_send,
    near_recv,
    far_send,
    far_recv,
):
    n = 2 * n_dp
    (near_me, near), (far_me, far) = group_peers(n_dp)
    greet([device for _, device in near] + [device for _, device in far])
    stages = len(orders[0])
    held = [first_ref, second_ref]
    accs = (acc_first, acc_second)
    outgoing = (out_first, out_second)
    incoming = (in_first, in_second)
    bits = [own_bits(order) for order in orders]
    pending = [None, None]
    start = [0, halves[0]]
    for t in range(stages - 1, -1, -1):
        count = 1 << t
        for h in range(2):
            source = held[h]
            if pending[h] is not None:
                pending[h].wait()
            arrived = 2 * count - 1
            keep, give = bits[h][t] * count, (1 - bits[h][t]) * count

            def value(i, at, h=h, source=source, arrived=arrived, last=pending[h] is None):
                got = source[at + i]
                if last:
                    return got
                return got + incoming[h][arrived + at + i].astype(f32)

            def fill(i, carry, h=h, give=give, count=count, value=value):
                outgoing[h][count - 1 + i] = value(i, give).astype(bf16)
                return carry

            lax.fori_loop(0, count, fill, 0)
            copy = pltpu.make_async_remote_copy(
                src_ref=outgoing[h].at[pl.ds(count - 1, count)],
                dst_ref=incoming[h].at[pl.ds(count - 1, count)],
                send_sem=send_sem.at[h, t],
                recv_sem=recv_sem.at[h, t],
                device_id=partner(orders[h][t]),
            )
            copy.start()
            pending[h] = copy

            def retain(i, carry, h=h, keep=keep, count=count, value=value):
                accs[h][count - 1 + i] = value(i, keep)
                return carry

            lax.fori_loop(0, count, retain, 0)
            held[h] = accs[h].at[pl.ds(count - 1, count)]
    dp = lax.axis_index("dp")
    me = dp * 2 + lax.axis_index("heads")
    sshare, gshare = SHARED_PARAMS // n, GROUP_PARAMS // n_dp
    soff = (me * sshare) % UNIT
    goff = (dp * gshare) % UNIT
    total = jnp.zeros((8, 128), f32)
    for h in range(2):
        pending[h].wait()
        value = held[h][0] + incoming[h][0].astype(f32)
        out_ref[start[h] : start[h] + halves[h]] = value
        row = lax.broadcasted_iota(jnp.int32, (halves[h], 128), 0) + start[h]
        place = row * 128 + lax.broadcasted_iota(jnp.int32, (halves[h], 128), 1)
        shared = (row < srows) & (place >= soff) & (place < soff + sshare)
        place = place - srows * 128
        grouped = (row >= srows) & (place >= goff) & (place < goff + gshare)
        own = jnp.where(shared | grouped, value, 0.0)
        total = total + jnp.sum((own * own).reshape(-1, 8, 128), axis=0)
    near_stat[near_me] = total
    far_stat[far_me] = all_share(near_me, near, near_stat, near_send, near_recv)
    total = all_share(far_me, far, far_stat, far_send, far_recv)
    total = jnp.sum(jnp.sum(total, axis=0, keepdims=True), axis=1, keepdims=True)
    norm = jnp.sqrt(total)
    norm_ref[...] = jnp.broadcast_to(norm, (8, 128))
    threshold = math.sqrt(2 * GROUP_PARAMS + SHARED_PARAMS)
    out_ref[...] = out_ref[...] * jnp.minimum(1.0, threshold / (norm + 1e-06))


def reduce(n_dp, srows, first, second):
    n = 2 * n_dp
    orders = exchange_orders(n_dp)
    halves = (first.shape[1], second.shape[1])
    stages = len(orders[0])
    fast = min(1 << FAST_BITS, n_dp)
    near, far = 2 * fast, n_dp // fast
    dma = pltpu.SemaphoreType.DMA
    return pl.pallas_call(
        partial(reduce_kernel, n_dp, srows, orders, halves),
        in_specs=[pl.BlockSpec(memory_space=pltpu.VMEM)] * 2,
        out_specs=[pl.BlockSpec(memory_space=pltpu.VMEM)] * 2,
        out_shape=[
            jax.ShapeDtypeStruct((sum(halves), 128), f32),
            jax.ShapeDtypeStruct((8, 128), f32),
        ],
        scratch_shapes=[pltpu.VMEM((n - 1, half, 128), f32) for half in halves]
        + [pltpu.VMEM((n - 1, half, 128), bf16) for half in halves] * 2
        + [
            pltpu.VMEM((near, 8, 128), f32),
            pltpu.VMEM((far, 8, 128), f32),
            dma((2, stages)),
            dma((2, stages)),
            dma((near,)),
            dma((near,)),
            dma((far,)),
            dma((far,)),
        ],
        compiler_params=pltpu.CompilerParams(
            collective_id=1, has_side_effects=True, vmem_limit_bytes=56 * 1024 * 1024
        ),
        name="reduce",
    )(first, second)


def window_parts(halves, rows):
    parts = []
    start = 0
    for h, size in enumerate(halves):
        low, high = max(rows[0], start), min(rows[1], start + size)
        if low < high:
            parts.append((h, low - start, high - start, low - rows[0], high - rows[0]))
        start += size
    return parts


def nn(a, b):
    return lax.dot_general(a, b, (((1,), (0,)), ((), ())), preferred_element_type=f32)


def nt(a, b):
    return lax.dot_general(a, b, (((1,), (1,)), ((), ())), preferred_element_type=f32)


def tn(a, b):
    return lax.dot_general(a, b, (((0,), (0,)), ((), ())), preferred_element_type=f32)


def norm_parts(values):
    center = values - jnp.mean(values, axis=-1, keepdims=True)
    inverse = lax.rsqrt(jnp.mean(center * center, axis=-1, keepdims=True) + eps_norm)
    return center * inverse, inverse


def norm_back(grad_after, unit, inverse, gain):
    scaled = grad_after * gain
    return inverse * (
        scaled
        - jnp.mean(scaled, axis=-1, keepdims=True)
        - unit * jnp.mean(scaled * unit, axis=-1, keepdims=True)
    )


def column_sum(values):
    return jnp.sum(values, axis=0, keepdims=True)


def head_masks(dtype):
    lane = lax.broadcasted_iota(jnp.int32, (1, HALF), 1) // HD
    return [(lane == h).astype(f32).astype(dtype) for h in range(HEADS)]


def spread_heads(values, masks):
    return jnp.concatenate([values * masks[h] for h in range(HEADS)], axis=0)


def pick_heads(stacked):
    lane = lax.broadcasted_iota(jnp.int32, (STRIPE, HALF), 1)
    picked = stacked[(HEADS - 1) * STRIPE :]
    for h in range(HEADS - 2, -1, -1):
        picked = jnp.where(lane < (h + 1) * HD, stacked[h * STRIPE : (h + 1) * STRIPE], picked)
    return picked


def row_shift(values, step):
    if step == 0:
        return values
    zero = jnp.zeros((16, HALF), f32)
    if step > 0:
        return jnp.concatenate([values[16:], zero], axis=0)
    return jnp.concatenate([zero, values[:-16]], axis=0)


def neighbours(values):
    return [pltpu.roll(values, 1, 0), values, pltpu.roll(values, STRIPE - 1, 0)]


def tile_sum(values):
    return jnp.sum(values.reshape(-1, 8, values.shape[1]), axis=0)


def turn_matrix():
    to = lax.broadcasted_iota(jnp.int32, (GRID, GRID), 0)
    src = lax.broadcasted_iota(jnp.int32, (GRID, GRID), 1)
    first, second = to // 16, to % 16
    return ((second < SIDE) & (src == second * 16 + first)).astype(f32).astype(bf16)


def row_mask():
    row = lax.broadcasted_iota(jnp.int32, (GRID, 1), 0)
    return (row % 16 < SIDE).astype(f32)


def to_grid(source, tokens, grid_ref):
    images = grid_ref.shape[0]
    grid_ref[...] = jnp.zeros_like(grid_ref)
    for half in range(2):
        cols = slice(half * 128, (half + 1) * 128)
        tokens[half] = source[:, cols].astype(f32)
        for image in range(images):
            for r in range(SIDE):
                grid_ref[image, 16 * r : 16 * r + SIDE, cols] = tokens[
                    half, pl.ds(r * SIDE * images + image, SIDE, stride=images), :
                ]


def from_grid(value, tokens, image, images):
    for half in range(2):
        for r in range(SIDE):
            tokens[half, pl.ds(r * SIDE * images + image, SIDE, stride=images), :] = value[
                16 * r : 16 * r + SIDE, half * 128 : (half + 1) * 128
            ]


def prepare_weights(n_dp, srows, grows, orders, halves, weights, sc):
    n = 2 * n_dp
    flat, gflat = sc["flat"], sc["gflat"]
    flat[...] = jnp.zeros_like(flat)
    gflat[...] = jnp.zeros_like(gflat)
    for k in range(n):
        at = first_row(SHARED_PARAMS, n, k)
        for h, low, high, begin, end in window_parts(halves, (0, srows)):
            window = weights[h][place_of(orders[h], k), low:high]
            flat[at + begin : at + end] += window.astype(f32)
        at = first_row(GROUP_PARAMS, n_dp, k // 2)
        for h, low, high, begin, end in window_parts(halves, (srows, srows + grows)):
            window = weights[h][place_of(orders[h], k), low:high]
            gflat[k % 2, at + begin : at + end] += window.astype(f32)
    for c in range(8):
        cols = slice(c * 128, (c + 1) * 128)
        sc["uw"][:, cols] = flat[pl.ds(c, D, stride=8), :].astype(bf16)
        sc["ubias"][:, cols] = flat[2048 + c : 2049 + c, :]
    for c in range(2):
        cols = slice(c * 128, (c + 1) * 128)
        sc["dw"][:, cols] = flat[pl.ds(2056 + c, FF, stride=2), :].astype(bf16)
        for i in range(6):
            sc["vecs"][i : i + 1, cols] = flat[4104 + 2 * i + c : 4105 + 2 * i + c, :]
    for j in range(2):
        for c in range(3):
            cols = slice(j * 384 + c * 128, j * 384 + (c + 1) * 128)
            sc["wq"][:, cols] = gflat[j, pl.ds(c, D, stride=3), :].astype(bf16)
        for c in range(2):
            cols = slice(c * 128, (c + 1) * 128)
            sc["ow"][j * 128 : (j + 1) * 128, cols] = gflat[
                j, pl.ds(770 + c, HALF, stride=2), :
            ].astype(bf16)
        sc["qbias"][:, j * 384 : j * 384 + 128] = gflat[j, 768:769, :]
        sc["qbias"][:, j * 384 + 128 : j * 384 + 256] = jnp.zeros((1, 128), f32)
        sc["qbias"][:, j * 384 + 256 : j * 384 + 384] = gflat[j, 769:770, :]
        sc["conv"][j, 0:10] = gflat[j, 1026:1036, :]


def place_gradients(n_dp, srows, grows, orders, halves, gradients, sc):
    n = 2 * n_dp
    flat, gflat = sc["flat"], sc["gflat"]
    for c in range(8):
        cols = slice(c * 128, (c + 1) * 128)
        flat[pl.ds(c, D, stride=8), :] = sc["a_uw"][:, cols]
        flat[2048 + c : 2049 + c, :] = sc["a_ub"][0:1, cols]
    for q in range(4):
        turned = sc["a_dwt"][:, q * 256 : (q + 1) * 256].T
        for c in range(2):
            flat[pl.ds(2056 + 512 * q + c, 256, stride=2), :] = turned[
                :, c * 128 : (c + 1) * 128
            ]
    for c in range(2):
        cols = slice(c * 128, (c + 1) * 128)
        for i in range(6):
            flat[4104 + 2 * i + c : 4105 + 2 * i + c, :] = column_sum(
                sc["a_vec"][i, :, cols]
            )
    for j in range(2):
        for c in range(3):
            cols = slice(j * 384 + c * 128, j * 384 + (c + 1) * 128)
            gflat[j, pl.ds(c, D, stride=3), :] = sc["a_wq"][:, cols]
        for c in range(2):
            cols = slice(c * 128, (c + 1) * 128)
            gflat[j, pl.ds(770 + c, HALF, stride=2), :] = sc["a_ow"][
                j * 128 : (j + 1) * 128, cols
            ]
        gflat[j, 768:769, :] = sc["a_pb"][0:1, j * 384 : j * 384 + 128]
        gflat[j, 769:770, :] = sc["a_pb"][0:1, j * 384 + 256 : j * 384 + 384]
        for i in range(10):
            gflat[j, 1026 + i : 1027 + i, :] = column_sum(sc["a_conv"][j, i])
    for k in range(n):
        at = first_row(SHARED_PARAMS, n, k)
        for h, low, high, begin, end in window_parts(halves, (0, srows)):
            gradients[h][place_of(orders[h], k), low:high] = flat[at + begin : at + end]
        at = first_row(GROUP_PARAMS, n_dp, k // 2)
        for h, low, high, begin, end in window_parts(halves, (srows, srows + grows)):
            gradients[h][place_of(orders[h], k), low:high] = gflat[
                k % 2, at + begin : at + end
            ]


def attention_forward(images, sc):
    scale = HD ** (-0.5)
    masks = head_masks(bf16)
    inside = row_mask()
    key_row = lax.broadcasted_iota(jnp.int32, (1, SW, 16, STRIPE), 2)
    gain_one, shift_one = sc["vecs"][1:2], sc["vecs"][2:3]
    qkv_ref, conv = sc["qkv"], sc["conv"]
    for image in images:
        unit, inverse = norm_parts(sc["x"][image])
        sc["unit"][image] = unit
        sc["inverse"][image] = inverse
        sc["normed"][image] = (unit * gain_one + shift_one).astype(bf16)
    for image in images:
        triple = (nn(sc["normed"][image], sc["wq"][...]) + sc["qbias"][...]) * inside
        triple = triple.astype(bf16)
        qkv_ref[image, 0] = triple[:, :384]
        qkv_ref[image, 1] = nn(sc["turn"][...], triple[:, 384:]).astype(bf16)
    for j in range(2):
        padded = [[] for _ in images]
        for s in range(2):
            for image, parts in zip(images, padded):
                rows = slice(s * STRIPE, (s + 1) * STRIPE)
                query = qkv_ref[image, j, rows, 0:128]
                keys = spread_heads(qkv_ref[image, j, rows, 128:256], masks)
                value = qkv_ref[image, j, rows, 256:384]
                scores = nt(keys, query).reshape(HEADS, SW, 16, STRIPE) * scale
                scores = jnp.where(key_row < SIDE, scores, -1e30)
                scores = scores.reshape(HEADS, STRIPE, STRIPE)
                weights = jnp.exp(scores - jnp.max(scores, axis=1, keepdims=True))
                probs = weights * (1.0 / jnp.sum(weights, axis=1, keepdims=True))
                probs = probs.reshape(HEADS * STRIPE, STRIPE)
                sc["probs"][image, 2 * j + s] = probs
                attended = tn(probs.astype(bf16), spread_heads(value, masks))
                near = neighbours(value.astype(f32))
                total = attended + conv[j, 9:10]
                for a in range(3):
                    part = near[0] * conv[j, 3 * a : 3 * a + 1]
                    for b in range(1, 3):
                        part = part + near[b] * conv[j, 3 * a + b : 3 * a + b + 1]
                    total = total + row_shift(part, a - 1)
                parts.append(total.astype(bf16))
        for image, parts in zip(images, padded):
            both = jnp.concatenate(parts, axis=0)
            if j == 1:
                both = nn(sc["turn"][...], both).astype(bf16)
            sc["heads"][image, :, j * 128 : (j + 1) * 128] = both


def mlp_both(images, count, drop_ref, sc):
    down_bias = sc["vecs"][0:1]
    gain_two, shift_two, out_bias = sc["vecs"][3:4], sc["vecs"][4:5], sc["vecs"][5:6]
    ones = jnp.ones((8, GRID), bf16)
    a_vec = sc["a_vec"]
    uw, dw, ubias = sc["uw"], sc["dw"], sc["ubias"]
    state = []
    for image in images:
        scale_one = drop_ref[0, image].astype(f32) / keep_prob
        scale_two = drop_ref[1, image].astype(f32) / keep_prob
        branch = nn(sc["heads"][image], sc["ow"][...])
        middle = sc["x"][image] + scale_one * (branch + out_bias)
        unit_two, inverse_two = norm_parts(middle)
        normed_two = (unit_two * gain_two + shift_two).astype(bf16)
        grad_output = sc["co"][image]
        grad_mlp_f = scale_two * grad_output
        a_vec[0] += tile_sum(grad_mlp_f)
        grad_mlp = grad_mlp_f.astype(bf16)
        state.append(
            (scale_one, scale_two, middle, unit_two, inverse_two, normed_two, grad_output, grad_mlp)
        )
    mlps = [None] * len(images)
    grads = [None] * len(images)
    for c in range(4):
        cols = slice(c * 256, (c + 1) * 256)
        for i in range(len(images)):
            normed_two, grad_mlp = state[i][5], state[i][7]
            hidden = nn(normed_two, uw[:, cols]) + ubias[:, cols]
            density = jnp.exp(hidden * hidden * -0.5) * (1.0 / math.sqrt(2.0 * math.pi))
            phi = 0.5 + 0.5 * lax.erf(hidden * math.sqrt(0.5))
            active = (hidden * phi).astype(bf16)
            part = nn(active, dw[cols, :])
            mlps[i] = part if mlps[i] is None else mlps[i] + part
            sc["a_dwt"][:, cols] += tn(grad_mlp, active)
            grad_active = nt(grad_mlp, dw[cols, :])
            grad_hidden = (grad_active * (phi + hidden * density)).astype(bf16)
            sc["a_ub"][:, cols] += nn(ones, grad_hidden)
            sc["a_uw"][:, cols] += tn(normed_two, grad_hidden)
            part = nt(grad_hidden, uw[:, cols])
            grads[i] = part if grads[i] is None else grads[i] + part
    for i, image in enumerate(images):
        scale_one, scale_two, middle, unit_two, inverse_two, _, grad_output, _ = state[i]
        from_grid(middle + scale_two * (mlps[i] + down_bias), sc["tokens"], image, count)
        a_vec[3] += tile_sum(grads[i] * unit_two)
        a_vec[4] += tile_sum(grads[i])
        grad_middle = grad_output + norm_back(grads[i], unit_two, inverse_two, gain_two)
        sc["gmid"][image] = grad_middle
        grad_branch_f = scale_one * grad_middle
        a_vec[5] += tile_sum(grad_branch_f)
        grad_branch = grad_branch_f.astype(bf16)
        sc["a_ow"][...] += tn(sc["heads"][image], grad_branch)
        sc["gheads"][image] = nt(grad_branch, sc["ow"][...]).astype(bf16)


def attention_back(images, count, sc):
    scale = HD ** (-0.5)
    masks = head_masks(bf16)
    inside = row_mask()[:STRIPE]
    gain_one = sc["vecs"][1:2]
    ones = jnp.ones((8, GRID), bf16)
    a_vec, a_conv = sc["a_vec"], sc["a_conv"]
    qkv_ref, conv = sc["qkv"], sc["conv"]
    for j in range(2):
        if j == 0:
            grads = [sc["gheads"][image, :, 0:128] for image in images]
        else:
            grads = [
                nn(sc["turn"][...], sc["gheads"][image, :, 128:256]).astype(bf16)
                for image in images
            ]
        padded = [[] for _ in images]
        for s in range(2):
            for image, parts, all_grad in zip(images, padded, grads):
                rows = slice(s * STRIPE, (s + 1) * STRIPE)
                query = qkv_ref[image, j, rows, 0:128]
                keys = spread_heads(qkv_ref[image, j, rows, 128:256], masks)
                value = qkv_ref[image, j, rows, 256:384]
                grad = all_grad[rows]
                grad_f = grad.astype(f32)
                probs = sc["probs"][image, 2 * j + s]
                grad_probs = nt(spread_heads(value, masks), grad)
                product = (probs * grad_probs).reshape(HEADS, STRIPE, STRIPE)
                inner = jnp.sum(product, axis=1, keepdims=True)
                grad_scores = product - probs.reshape(HEADS, STRIPE, STRIPE) * inner
                grad_scores = grad_scores.reshape(HEADS * STRIPE, STRIPE).astype(bf16)
                grad_query = tn(grad_scores, keys) * scale
                grad_key = pick_heads(nn(grad_scores, query)) * scale
                grad_value = pick_heads(nn(probs.astype(bf16), grad))
                near = neighbours(grad_f)
                for a in range(3):
                    part = near[2] * conv[j, 3 * a : 3 * a + 1]
                    for b in range(1, 3):
                        part = part + near[2 - b] * conv[j, 3 * a + b : 3 * a + b + 1]
                    grad_value = grad_value + row_shift(part, 1 - a)
                grad_value = grad_value * inside
                near = neighbours(value.astype(f32))
                for b in range(3):
                    a_conv[j, b] += tile_sum(grad_f[16:] * near[b][:-16])
                    a_conv[j, 3 + b] += tile_sum(grad_f * near[b])
                    a_conv[j, 6 + b] += tile_sum(grad_f[:-16] * near[b][16:])
                a_conv[j, 9] += tile_sum(grad_f)
                parts.append(
                    jnp.concatenate([grad_query, grad_key, grad_value], axis=1).astype(bf16)
                )
        for image, parts in zip(images, padded):
            both = jnp.concatenate(parts, axis=0)
            if j == 1:
                both = nn(sc["turn"][...], both).astype(bf16)
            sc["gtriple"][image, :, j * 384 : (j + 1) * 384] = both
    for image in images:
        grad_triple = sc["gtriple"][image]
        sc["a_pb"][...] += nn(ones, grad_triple)
        sc["a_wq"][...] += tn(sc["normed"][image], grad_triple)
        grad_normed = nt(grad_triple, sc["wq"][...])
        unit, inverse = sc["unit"][image], sc["inverse"][image]
        a_vec[1] += tile_sum(grad_normed * unit)
        a_vec[2] += tile_sum(grad_normed)
        grad = sc["gmid"][image] + norm_back(grad_normed, unit, inverse, gain_one)
        from_grid(grad, sc["tokens"], image, count)


def scratch_shapes(n_dp, srows, grows, count):
    n = 2 * n_dp
    flat_rows = max(4120, first_row(SHARED_PARAMS, n, n - 1) + srows)
    gflat_rows = max(1040, first_row(GROUP_PARAMS, n_dp, n_dp - 1) + grows)
    return dict(
        flat=((flat_rows, 128), f32),
        gflat=((2, gflat_rows, 128), f32),
        turn=((GRID, GRID), bf16),
        wq=((D, 768), bf16),
        ow=((D, D), bf16),
        uw=((D, FF), bf16),
        dw=((FF, D), bf16),
        qbias=((1, 768), f32),
        ubias=((1, FF), f32),
        vecs=((8, D), f32),
        conv=((2, 16, 128), f32),
        a_wq=((D, 768), f32),
        a_ow=((D, D), f32),
        a_uw=((D, FF), f32),
        a_dwt=((D, FF), f32),
        a_pb=((8, 768), f32),
        a_ub=((8, FF), f32),
        a_vec=((6, 8, D), f32),
        a_conv=((2, 10, 8, 128), f32),
        tokens=((2, TOK * count, 128), f32),
        x=((count, GRID, D), f32),
        co=((count, GRID, D), f32),
        unit=((count, GRID, D), f32),
        inverse=((count, GRID, 1), f32),
        normed=((count, GRID, D), bf16),
        qkv=((count, 2, GRID, 384), bf16),
        probs=((count, 4, HEADS * STRIPE, STRIPE), f32),
        heads=((count, GRID, D), bf16),
        gmid=((count, GRID, D), f32),
        gheads=((count, GRID, D), bf16),
        gtriple=((count, GRID, 768), bf16),
    )


ACCUMULATORS = ("a_wq", "a_ow", "a_uw", "a_dwt", "a_pb", "a_ub", "a_vec", "a_conv")
TOGETHER = 2


def compute_kernel(
    n_dp,
    srows,
    grows,
    orders,
    halves,
    count,
    names,
    drop_ref,
    x_ref,
    co_ref,
    first_ref,
    second_ref,
    out_ref,
    gin_ref,
    gfirst_ref,
    gsecond_ref,
    *scratch,
):
    sc = dict(zip(names, scratch))
    sc["turn"][...] = turn_matrix()
    to_grid(x_ref, sc["tokens"], sc["x"])
    to_grid(co_ref, sc["tokens"], sc["co"])
    for name in ACCUMULATORS:
        sc[name][...] = jnp.zeros_like(sc[name])
    prepare_weights(n_dp, srows, grows, orders, halves, (first_ref, second_ref), sc)

    def run(phase):
        def body(i, carry):
            phase([i * TOGETHER + k for k in range(TOGETHER)])
            return carry

        lax.fori_loop(0, count // TOGETHER, body, 0)

    run(lambda images: attention_forward(images, sc))
    run(lambda images: mlp_both(images, count, drop_ref, sc))
    for half in range(2):
        out_ref[:, half * 128 : (half + 1) * 128] = sc["tokens"][half]
    run(lambda images: attention_back(images, count, sc))
    for half in range(2):
        gin_ref[:, half * 128 : (half + 1) * 128] = sc["tokens"][half]
    place_gradients(n_dp, srows, grows, orders, halves, (gfirst_ref, gsecond_ref), sc)


def compute(n_dp, srows, grows, drops, images, cotangent, first, second):
    n = 2 * n_dp
    count = images.shape[0]
    halves = (first.shape[1], second.shape[1])
    shapes = scratch_shapes(n_dp, srows, grows, count)
    vmem = pl.BlockSpec(memory_space=pltpu.VMEM)

    def rows(array):
        return jnp.swapaxes(array, 0, 1).reshape(TOK * count, D)

    def unrows(array):
        return jnp.swapaxes(array.reshape(TOK, count, D), 0, 1)

    out, gin, first, second = pl.pallas_call(
        partial(
            compute_kernel,
            n_dp,
            srows,
            grows,
            exchange_orders(n_dp),
            halves,
            count,
            tuple(shapes),
        ),
        in_specs=[pl.BlockSpec(memory_space=pltpu.SMEM)] + [vmem] * 4,
        out_specs=[vmem] * 4,
        out_shape=[jax.ShapeDtypeStruct((TOK * count, D), f32)] * 2
        + [jax.ShapeDtypeStruct((n, half, 128), f32) for half in halves],
        scratch_shapes=[pltpu.VMEM(*shape) for shape in shapes.values()],
        compiler_params=pltpu.CompilerParams(vmem_limit_bytes=60 * 1024 * 1024),
        name="block",
    )(drops.T, rows(images), rows(cotangent), first, second)
    return unrows(out), unrows(gin), first, second


def adam_step(master, gradient, first, second, step):
    first_new = beta_one * first + (1.0 - beta_one) * gradient
    second_new = beta_two * second + (1.0 - beta_two) * gradient * gradient
    first_hat = first_new / (1.0 - jnp.power(jnp.float32(beta_one), step))
    second_hat = second_new / (1.0 - jnp.power(jnp.float32(beta_two), step))
    master_new = master - learn_rate * (
        first_hat / (jnp.sqrt(second_hat) + adam_eps) + decay_rate * master
    )
    return (master_new, first_new, second_new)


def on_device(
    n_dp,
    images,
    cotangent,
    drop_masks,
    group_master,
    group_m1,
    group_m2,
    shared_master,
    shared_m1,
    shared_m2,
):
    n = 2 * n_dp
    srows = window_rows(SHARED_PARAMS, n)
    grows = window_rows(GROUP_PARAMS, n_dp)
    dp = lax.axis_index("dp")
    me = dp * 2 + lax.axis_index("heads")
    sshare, gshare = SHARED_PARAMS // n, GROUP_PARAMS // n_dp
    soff = lax.rem(me * sshare, UNIT)
    goff = lax.rem(dp * gshare, UNIT)
    sblock = lax.dynamic_update_slice(jnp.zeros((srows * 128,), f32), shared_master, (soff,))
    gblock = lax.dynamic_update_slice(jnp.zeros((grows * 128,), f32), group_master[0], (goff,))
    own = jnp.concatenate([sblock.reshape(srows, 128), gblock.reshape(grows, 128)], axis=0)
    first, second = gather(n_dp, srows + grows, own)
    output, input_grad, first, second = compute(
        n_dp, srows, grows, drop_masks, images, cotangent, first, second
    )
    mine, norm = reduce(n_dp, srows, first, second)
    shared_grad = lax.dynamic_slice(mine[:srows].reshape(-1), (soff,), (sshare,))
    group_grad = lax.dynamic_slice(mine[srows:].reshape(-1), (goff,), (gshare,))[None, :]
    step = jnp.float32(STEP)
    group_new, group_first, group_second = adam_step(
        group_master, group_grad, group_m1, group_m2, step
    )
    shared_new, shared_first, shared_second = adam_step(
        shared_master, shared_grad, shared_m1, shared_m2, step
    )
    return (
        output,
        input_grad,
        norm[0, 0:1],
        group_grad,
        group_new,
        group_first,
        group_second,
        group_new.astype(jnp.bfloat16),
        shared_grad,
        shared_new,
        shared_first,
        shared_second,
        shared_new.astype(jnp.bfloat16),
    )


def solution(mesh):
    both = P(("dp", "heads"))
    rows = P(("dp", "heads"), None, None)
    split = P("heads", "dp")
    in_specs = (rows, rows, P(("dp", "heads"), None), split, split, split, both, both, both)
    out_specs = (rows, rows, P(), split, split, split, split, split, both, both, both, both, both)
    return jax.shard_map(
        partial(on_device, mesh.shape["dp"]),
        mesh=mesh,
        in_specs=in_specs,
        out_specs=out_specs,
        check_vma=False,
    )
```

```python
from functools import partial
import math

import jax
import jax.numpy as jnp
from jax import lax
from jax.experimental import pallas as pl
from jax.experimental.pallas import tpu as pltpu
from jax.sharding import PartitionSpec as P

D = 256
FF = 1024
SIDE = 14
SW = 7
STEP = 10
HD = 32
HALF = 128
GROUP_PARAMS = 132608
SHARED_PARAMS = 526848
TOK = SIDE * SIDE
GRID = 16 * SIDE
STRIPE = 16 * SW
HEADS = HALF // HD
UNIT = 1024

eps_norm = 1e-05
keep_prob = 0.8
beta_one = 0.9
beta_two = 0.999
adam_eps = 1e-08
learn_rate = 0.04
decay_rate = 0.05

f32 = jnp.float32
bf16 = jnp.bfloat16


def window_rows(total, count, extra=0):
    share = total // count
    most = max((share * k) % UNIT + share for k in range(count)) + extra * 128
    return 16 * (-(-most // (2 * UNIT)))


def first_row(total, count, k):
    return (total // count * k) // UNIT * 8


HEADS_BIT = -1
FAST_BITS = 2
CARRIED = 4
GAIN_ROW = 4106


def exchange_stages(n_dp):
    bits = n_dp.bit_length() - 1
    far = list(range(bits - 1, 1, -1))
    stages = [tuple(far[i : i + 2]) for i in range(0, len(far), 2)]
    stages.append((1, HEADS_BIT) if bits > 1 else (HEADS_BIT,))
    if bits > 0:
        stages.append((0,))
    return stages


def weight_of(bit):
    return 1 if bit == HEADS_BIT else 2 << bit


def flat_bits(stages):
    return [bit for stage in stages for bit in stage]


def place_of(stages, k):
    return sum(((k // weight_of(bit)) % 2) << t for t, bit in enumerate(flat_bits(stages)))


def device_at(stages, place, first=0):
    return sum(
        ((place // (1 << t)) % 2) * weight_of(bit)
        for t, bit in enumerate(flat_bits(stages))
        if t >= first
    )


def own_number():
    return lax.axis_index("dp") * 2 + lax.axis_index("heads")


def own_bits(stages):
    me = own_number()
    return [(me // weight_of(bit)) % 2 for bit in flat_bits(stages)]


def peer(bits, mask):
    dp, heads = lax.axis_index("dp"), lax.axis_index("heads")
    for i, bit in enumerate(bits):
        if mask >> i & 1:
            if bit == HEADS_BIT:
                heads = 1 - heads
            else:
                dp = dp + (1 << bit) * (1 - 2 * ((dp // (1 << bit)) % 2))
    return {"dp": dp, "heads": heads}


def group_peers(n_dp):
    dp, heads = lax.axis_index("dp"), lax.axis_index("heads")
    fast = min(1 << FAST_BITS, n_dp)
    low, high = dp % fast, dp // fast
    count = 2 * fast
    me = low * 2 + heads
    near = []
    for step in range(1, count):
        other = (me + step) % count
        near.append((other, {"dp": high * fast + other // 2, "heads": other % 2}))
    far = []
    for step in range(1, n_dp // fast):
        other = (high + step) % (n_dp // fast)
        far.append((other, {"dp": other * fast + low, "heads": heads}))
    return (me, near), (high, far)


class Gather:
    def __init__(self, stages, buffer, send_sem, recv_sem):
        self.stages, self.buffer = stages, buffer
        self.send_sem, self.recv_sem = send_sem, recv_sem
        self.bits = own_bits(stages)

    def copies(self, g, arriving):
        start = sum(len(stage) for stage in self.stages[:g])
        for mask in range(1, 1 << len(self.stages[g])):
            base = 0
            for u, bit in enumerate(self.bits):
                flipped = start <= u < start + len(self.stages[g]) and mask >> (u - start) & 1
                if u >= start:
                    base = base + (1 << u) * (1 - bit if flipped and arriving else bit)
            held = self.buffer.at[pl.ds(base, 1 << start)]
            yield pltpu.make_async_remote_copy(
                src_ref=held,
                dst_ref=held,
                send_sem=self.send_sem.at[g, mask - 1],
                recv_sem=self.recv_sem.at[g, mask - 1],
                device_id=peer(self.stages[g], mask),
            )

    def start(self, g):
        for copy in self.copies(g, False):
            copy.start()

    def wait(self, g):
        for copy in self.copies(g, True):
            copy.wait_recv()
        for copy in self.copies(g, False):
            copy.wait_send()


class Scatter:
    def __init__(self, stages, window, outgoing, incoming, sums, send_sem, recv_sem):
        self.stages, self.window = stages, window
        self.outgoing, self.incoming, self.sums = outgoing, incoming, sums
        self.send_sem, self.recv_sem = send_sem, recv_sem
        self.bits = own_bits(stages)

    def offset(self, g):
        return sum(len(stage) for stage in self.stages[:g])

    def held(self, g, place):
        if g == len(self.stages) - 1:
            return self.window(place)
        return self.sums[g + 1][place]

    def copy(self, g, mask):
        return pltpu.make_async_remote_copy(
            src_ref=self.outgoing[g].at[mask - 1],
            dst_ref=self.incoming[g].at[mask - 1],
            send_sem=self.send_sem.at[g, mask - 1],
            recv_sem=self.recv_sem.at[g, mask - 1],
            device_id=peer(self.stages[g], mask),
        )

    def part(self, g, mask):
        start = self.offset(g)
        return sum(
            (1 << (start + i)) * (1 - self.bits[start + i] if mask >> i & 1 else self.bits[start + i])
            for i in range(len(self.stages[g]))
        )

    def start(self, g):
        for mask in range(1, 1 << len(self.stages[g])):
            part = self.part(g, mask)

            def fill(i, carry, mask=mask, part=part):
                self.outgoing[g][mask - 1, i] = self.held(g, part + i).astype(bf16)
                return carry

            lax.fori_loop(0, 1 << self.offset(g), fill, 0)
            self.copy(g, mask).start()

    def wait(self, g):
        masks = range(1, 1 << len(self.stages[g]))
        for mask in masks:
            self.copy(g, mask).wait()
        part = self.part(g, 0)

        def add(i, carry):
            value = self.held(g, part + i)
            for mask in masks:
                value = value + self.incoming[g][mask - 1, i].astype(f32)
            self.sums[g][i] = value
            return carry

        lax.fori_loop(0, 1 << self.offset(g), add, 0)


def scatter_shapes(stages, rows):
    outgoing, sums = [], []
    start = 0
    for stage in stages:
        outgoing.append(((1 << len(stage)) - 1, 1 << start, rows, 128))
        sums.append((1 << start, rows, 128))
        start += len(stage)
    return outgoing, sums


def all_share(me, peers, stat_ref, send_sem, recv_sem):
    copies = []
    for other, device in peers:
        copy = pltpu.make_async_remote_copy(
            src_ref=stat_ref.at[me],
            dst_ref=stat_ref.at[me],
            send_sem=send_sem.at[other],
            recv_sem=recv_sem.at[me],
            device_id=device,
        )
        copy.start()
        copies.append(copy)
    for other, device in peers:
        pltpu.make_async_remote_copy(
            src_ref=stat_ref.at[other],
            dst_ref=stat_ref.at[other],
            send_sem=send_sem.at[other],
            recv_sem=recv_sem.at[other],
            device_id=device,
        ).wait_recv()
    for copy in copies:
        copy.wait_send()
    return jnp.sum(stat_ref[...], axis=0)


def shift_on(rows, amount):
    lanes = amount % 128
    turned = pltpu.roll(rows, lanes, 1)
    lane = lax.broadcasted_iota(jnp.int32, rows.shape, 1)
    turned = jnp.where(lane < lanes, pltpu.roll(turned, 1, 0), turned)
    return pltpu.roll(turned, amount // 128, 0)


def shift_back(rows, amount):
    count = rows.shape[0]
    lanes = amount % 128
    turned = pltpu.roll(rows, (128 - lanes) % 128, 1)
    lane = lax.broadcasted_iota(jnp.int32, rows.shape, 1)
    turned = jnp.where(lane >= 128 - lanes, pltpu.roll(turned, count - 1, 0), turned)
    return pltpu.roll(turned, (count - amount // 128) % count, 0)


def nn(a, b):
    return lax.dot_general(a, b, (((1,), (0,)), ((), ())), preferred_element_type=f32)


def nt(a, b):
    return lax.dot_general(a, b, (((1,), (1,)), ((), ())), preferred_element_type=f32)


def tn(a, b):
    return lax.dot_general(a, b, (((0,), (0,)), ((), ())), preferred_element_type=f32)


def norm_parts(values):
    center = values - jnp.mean(values, axis=-1, keepdims=True)
    inverse = lax.rsqrt(jnp.mean(center * center, axis=-1, keepdims=True) + eps_norm)
    return center * inverse, inverse


def norm_back(grad_after, unit, inverse, gain):
    scaled = grad_after * gain
    return inverse * (
        scaled
        - jnp.mean(scaled, axis=-1, keepdims=True)
        - unit * jnp.mean(scaled * unit, axis=-1, keepdims=True)
    )


def column_sum(values):
    return jnp.sum(values, axis=0, keepdims=True)


def head_masks(dtype):
    lane = lax.broadcasted_iota(jnp.int32, (1, HALF), 1) // HD
    return [(lane == h).astype(f32).astype(dtype) for h in range(HEADS)]


def spread_heads(values, masks):
    return jnp.concatenate([values * masks[h] for h in range(HEADS)], axis=0)


def pick_heads(stacked):
    lane = lax.broadcasted_iota(jnp.int32, (STRIPE, HALF), 1)
    picked = stacked[(HEADS - 1) * STRIPE :]
    for h in range(HEADS - 2, -1, -1):
        picked = jnp.where(lane < (h + 1) * HD, stacked[h * STRIPE : (h + 1) * STRIPE], picked)
    return picked


def row_shift(values, step):
    if step == 0:
        return values
    zero = jnp.zeros((16, HALF), f32)
    if step > 0:
        return jnp.concatenate([values[16:], zero], axis=0)
    return jnp.concatenate([zero, values[:-16]], axis=0)


def neighbours(values):
    return [pltpu.roll(values, 1, 0), values, pltpu.roll(values, STRIPE - 1, 0)]


def tile_sum(values):
    return jnp.sum(values.reshape(-1, 8, values.shape[1]), axis=0)


def turn_matrix():
    to = lax.broadcasted_iota(jnp.int32, (GRID, GRID), 0)
    src = lax.broadcasted_iota(jnp.int32, (GRID, GRID), 1)
    first, second = to // 16, to % 16
    return ((second < SIDE) & (src == second * 16 + first)).astype(f32).astype(bf16)


def row_mask():
    row = lax.broadcasted_iota(jnp.int32, (GRID, 1), 0)
    return (row % 16 < SIDE).astype(f32)


def to_grid(source, tokens, grid_ref):
    images = grid_ref.shape[0]
    grid_ref[...] = jnp.zeros_like(grid_ref)
    for half in range(2):
        cols = slice(half * 128, (half + 1) * 128)
        tokens[half] = source[:, cols].astype(f32)
        for image in range(images):
            for r in range(SIDE):
                grid_ref[image, 16 * r : 16 * r + SIDE, cols] = tokens[
                    half, pl.ds(r * SIDE * images + image, SIDE, stride=images), :
                ]


def from_grid(value, tokens, image, images):
    for half in range(2):
        for r in range(SIDE):
            tokens[half, pl.ds(r * SIDE * images + image, SIDE, stride=images), :] = value[
                16 * r : 16 * r + SIDE, half * 128 : (half + 1) * 128
            ]


def prepare_group(n_dp, stages, sc):
    n = 2 * n_dp
    gflat, buffer = sc["gflat"], sc["gweights"]
    grows = buffer.shape[1]
    gflat[...] = jnp.zeros_like(gflat)
    for k in range(n):
        at = first_row(GROUP_PARAMS, n_dp, k // 2)
        size = grows - CARRIED
        gflat[k % 2, at : at + size] += buffer[place_of(stages, k), 0:size].astype(f32)
    carried = buffer[place_of(stages, n - 1)].astype(f32)[grows - CARRIED :]
    for c in range(2):
        cols = slice(c * 128, (c + 1) * 128)
        sc["vecs"][1:2, cols] = carried[c : c + 1]
        sc["vecs"][2:3, cols] = carried[2 + c : 3 + c]
    for j in range(2):
        for c in range(3):
            cols = slice(j * 384 + c * 128, j * 384 + (c + 1) * 128)
            sc["wq"][:, cols] = gflat[j, pl.ds(c, D, stride=3), :].astype(bf16)
        for c in range(2):
            cols = slice(c * 128, (c + 1) * 128)
            sc["ow"][j * 128 : (j + 1) * 128, cols] = gflat[
                j, pl.ds(770 + c, HALF, stride=2), :
            ].astype(bf16)
        sc["qbias"][:, j * 384 : j * 384 + 128] = gflat[j, 768:769, :]
        sc["qbias"][:, j * 384 + 128 : j * 384 + 256] = jnp.zeros((1, 128), f32)
        sc["qbias"][:, j * 384 + 256 : j * 384 + 384] = gflat[j, 769:770, :]
        sc["conv"][j, 0:10] = gflat[j, 1026:1036, :]


def prepare_shared(n_dp, stages, sc):
    n = 2 * n_dp
    flat, buffer = sc["flat"], sc["sweights"]
    srows = buffer.shape[1]
    flat[...] = jnp.zeros_like(flat)
    for k in range(n):
        at = first_row(SHARED_PARAMS, n, k)
        flat[at : at + srows] += buffer[place_of(stages, k)].astype(f32)
    for c in range(8):
        cols = slice(c * 128, (c + 1) * 128)
        sc["uw"][:, cols] = flat[pl.ds(c, D, stride=8), :].astype(bf16)
        sc["ubias"][:, cols] = flat[2048 + c : 2049 + c, :]
    for c in range(2):
        cols = slice(c * 128, (c + 1) * 128)
        sc["dw"][:, cols] = flat[pl.ds(2056 + c, FF, stride=2), :].astype(bf16)
        for i in (0, 3, 4, 5):
            sc["vecs"][i : i + 1, cols] = flat[4104 + 2 * i + c : 4105 + 2 * i + c, :]


def place_shared(sc):
    flat = sc["flat"]
    for c in range(8):
        cols = slice(c * 128, (c + 1) * 128)
        flat[pl.ds(c, D, stride=8), :] = sc["a_uw"][:, cols]
        flat[2048 + c : 2049 + c, :] = sc["a_ub"][0:1, cols]
    for q in range(4):
        turned = sc["a_dwt"][:, q * 256 : (q + 1) * 256].T
        for c in range(2):
            flat[pl.ds(2056 + 512 * q + c, 256, stride=2), :] = turned[
                :, c * 128 : (c + 1) * 128
            ]
    for c in range(2):
        cols = slice(c * 128, (c + 1) * 128)
        for i in (0, 3, 4, 5):
            flat[4104 + 2 * i + c : 4105 + 2 * i + c, :] = column_sum(
                sc["a_vec"][i, :, cols]
            )
    flat[GAIN_ROW : GAIN_ROW + CARRIED, :] = jnp.zeros((CARRIED, 128), f32)


def place_group(sc):
    gflat = sc["gflat"]
    for j in range(2):
        for c in range(3):
            cols = slice(j * 384 + c * 128, j * 384 + (c + 1) * 128)
            gflat[j, pl.ds(c, D, stride=3), :] = sc["a_wq"][:, cols]
        for c in range(2):
            cols = slice(c * 128, (c + 1) * 128)
            gflat[j, pl.ds(770 + c, HALF, stride=2), :] = sc["a_ow"][
                j * 128 : (j + 1) * 128, cols
            ]
        gflat[j, 768:769, :] = sc["a_pb"][0:1, j * 384 : j * 384 + 128]
        gflat[j, 769:770, :] = sc["a_pb"][0:1, j * 384 + 256 : j * 384 + 384]
        for i in range(10):
            gflat[j, 1026 + i : 1027 + i, :] = column_sum(sc["a_conv"][j, i])
    for c in range(2):
        cols = slice(c * 128, (c + 1) * 128)
        sc["carried"][4 + c : 5 + c, :] = column_sum(sc["a_vec"][1, :, cols])
        sc["carried"][6 + c : 7 + c, :] = column_sum(sc["a_vec"][2, :, cols])
    sc["carried"][0:4, :] = jnp.zeros((4, 128), f32)


def first_norm(images, sc):
    for image in images:
        sc["unit"][image], sc["inverse"][image] = norm_parts(sc["x"][image])


def attention_forward(images, sc):
    scale = HD ** (-0.5)
    masks = head_masks(bf16)
    inside = row_mask()
    key_row = lax.broadcasted_iota(jnp.int32, (1, SW, 16, STRIPE), 2)
    gain_one, shift_one = sc["vecs"][1:2], sc["vecs"][2:3]
    qkv_ref, conv = sc["qkv"], sc["conv"]
    for image in images:
        sc["normed"][image] = (sc["unit"][image] * gain_one + shift_one).astype(bf16)
    for image in images:
        triple = (nn(sc["normed"][image], sc["wq"][...]) + sc["qbias"][...]) * inside
        triple = triple.astype(bf16)
        qkv_ref[image, 0] = triple[:, :384]
        qkv_ref[image, 1] = nn(sc["turn"][...], triple[:, 384:]).astype(bf16)
    for j in range(2):
        padded = [[] for _ in images]
        for s in range(2):
            for image, parts in zip(images, padded):
                rows = slice(s * STRIPE, (s + 1) * STRIPE)
                query = qkv_ref[image, j, rows, 0:128]
                keys = spread_heads(qkv_ref[image, j, rows, 128:256], masks)
                value = qkv_ref[image, j, rows, 256:384]
                scores = nt(keys, query).reshape(HEADS, SW, 16, STRIPE) * scale
                scores = jnp.where(key_row < SIDE, scores, -1e30)
                scores = scores.reshape(HEADS, STRIPE, STRIPE)
                weights = jnp.exp(scores - jnp.max(scores, axis=1, keepdims=True))
                probs = weights * (1.0 / jnp.sum(weights, axis=1, keepdims=True))
                probs = probs.reshape(HEADS * STRIPE, STRIPE)
                sc["probs"][image, 2 * j + s] = probs
                attended = tn(probs.astype(bf16), spread_heads(value, masks))
                near = neighbours(value.astype(f32))
                total = attended + conv[j, 9:10]
                for a in range(3):
                    part = near[0] * conv[j, 3 * a : 3 * a + 1]
                    for b in range(1, 3):
                        part = part + near[b] * conv[j, 3 * a + b : 3 * a + b + 1]
                    total = total + row_shift(part, a - 1)
                parts.append(total.astype(bf16))
        for image, parts in zip(images, padded):
            both = jnp.concatenate(parts, axis=0)
            if j == 1:
                both = nn(sc["turn"][...], both).astype(bf16)
            sc["heads"][image, :, j * 128 : (j + 1) * 128] = both


def mlp_both(images, count, drop_ref, sc):
    down_bias = sc["vecs"][0:1]
    gain_two, shift_two, out_bias = sc["vecs"][3:4], sc["vecs"][4:5], sc["vecs"][5:6]
    ones = jnp.ones((8, GRID), bf16)
    a_vec = sc["a_vec"]
    uw, dw, ubias = sc["uw"], sc["dw"], sc["ubias"]
    state = []
    for image in images:
        scale_one = drop_ref[0, image].astype(f32) / keep_prob
        scale_two = drop_ref[1, image].astype(f32) / keep_prob
        branch = nn(sc["heads"][image], sc["ow"][...])
        middle = sc["x"][image] + scale_one * (branch + out_bias)
        unit_two, inverse_two = norm_parts(middle)
        normed_two = (unit_two * gain_two + shift_two).astype(bf16)
        grad_output = sc["co"][image]
        grad_mlp_f = scale_two * grad_output
        a_vec[0] += tile_sum(grad_mlp_f)
        grad_mlp = grad_mlp_f.astype(bf16)
        state.append(
            (scale_one, scale_two, middle, unit_two, inverse_two, normed_two, grad_output, grad_mlp)
        )
    mlps = [None] * len(images)
    grads = [None] * len(images)
    for c in range(4):
        cols = slice(c * 256, (c + 1) * 256)
        for i in range(len(images)):
            normed_two, grad_mlp = state[i][5], state[i][7]
            hidden = nn(normed_two, uw[:, cols]) + ubias[:, cols]
            density = jnp.exp(hidden * hidden * -0.5) * (1.0 / math.sqrt(2.0 * math.pi))
            phi = 0.5 + 0.5 * lax.erf(hidden * math.sqrt(0.5))
            active = (hidden * phi).astype(bf16)
            part = nn(active, dw[cols, :])
            mlps[i] = part if mlps[i] is None else mlps[i] + part
            sc["a_dwt"][:, cols] += tn(grad_mlp, active)
            grad_active = nt(grad_mlp, dw[cols, :])
            grad_hidden = (grad_active * (phi + hidden * density)).astype(bf16)
            sc["a_ub"][:, cols] += nn(ones, grad_hidden)
            sc["a_uw"][:, cols] += tn(normed_two, grad_hidden)
            part = nt(grad_hidden, uw[:, cols])
            grads[i] = part if grads[i] is None else grads[i] + part
    for i, image in enumerate(images):
        scale_one, scale_two, middle, unit_two, inverse_two, _, grad_output, _ = state[i]
        from_grid(middle + scale_two * (mlps[i] + down_bias), sc["outs"], image, count)
        a_vec[3] += tile_sum(grads[i] * unit_two)
        a_vec[4] += tile_sum(grads[i])
        grad_middle = grad_output + norm_back(grads[i], unit_two, inverse_two, gain_two)
        sc["gmid"][image] = grad_middle
        grad_branch_f = scale_one * grad_middle
        a_vec[5] += tile_sum(grad_branch_f)
        grad_branch = grad_branch_f.astype(bf16)
        sc["a_ow"][...] += tn(sc["heads"][image], grad_branch)
        sc["gheads"][image] = nt(grad_branch, sc["ow"][...]).astype(bf16)


def attention_back(images, count, sc):
    scale = HD ** (-0.5)
    masks = head_masks(bf16)
    inside = row_mask()[:STRIPE]
    gain_one = sc["vecs"][1:2]
    ones = jnp.ones((8, GRID), bf16)
    a_vec, a_conv = sc["a_vec"], sc["a_conv"]
    qkv_ref, conv = sc["qkv"], sc["conv"]
    for j in range(2):
        if j == 0:
            grads = [sc["gheads"][image, :, 0:128] for image in images]
        else:
            grads = [
                nn(sc["turn"][...], sc["gheads"][image, :, 128:256]).astype(bf16)
                for image in images
            ]
        padded = [[] for _ in images]
        for s in range(2):
            for image, parts, all_grad in zip(images, padded, grads):
                rows = slice(s * STRIPE, (s + 1) * STRIPE)
                query = qkv_ref[image, j, rows, 0:128]
                keys = spread_heads(qkv_ref[image, j, rows, 128:256], masks)
                value = qkv_ref[image, j, rows, 256:384]
                grad = all_grad[rows]
                grad_f = grad.astype(f32)
                probs = sc["probs"][image, 2 * j + s]
                grad_probs = nt(spread_heads(value, masks), grad)
                product = (probs * grad_probs).reshape(HEADS, STRIPE, STRIPE)
                inner = jnp.sum(product, axis=1, keepdims=True)
                grad_scores = product - probs.reshape(HEADS, STRIPE, STRIPE) * inner
                grad_scores = grad_scores.reshape(HEADS * STRIPE, STRIPE).astype(bf16)
                grad_query = tn(grad_scores, keys) * scale
                grad_key = pick_heads(nn(grad_scores, query)) * scale
                grad_value = pick_heads(nn(probs.astype(bf16), grad))
                near = neighbours(grad_f)
                for a in range(3):
                    part = near[2] * conv[j, 3 * a : 3 * a + 1]
                    for b in range(1, 3):
                        part = part + near[2 - b] * conv[j, 3 * a + b : 3 * a + b + 1]
                    grad_value = grad_value + row_shift(part, 1 - a)
                grad_value = grad_value * inside
                near = neighbours(value.astype(f32))
                for b in range(3):
                    a_conv[j, b] += tile_sum(grad_f[16:] * near[b][:-16])
                    a_conv[j, 3 + b] += tile_sum(grad_f * near[b])
                    a_conv[j, 6 + b] += tile_sum(grad_f[:-16] * near[b][16:])
                a_conv[j, 9] += tile_sum(grad_f)
                parts.append(
                    jnp.concatenate([grad_query, grad_key, grad_value], axis=1).astype(bf16)
                )
        for image, parts in zip(images, padded):
            both = jnp.concatenate(parts, axis=0)
            if j == 1:
                both = nn(sc["turn"][...], both).astype(bf16)
            sc["gtriple"][image, :, j * 384 : (j + 1) * 384] = both
    for image in images:
        grad_triple = sc["gtriple"][image]
        sc["a_pb"][...] += nn(ones, grad_triple)
        sc["a_wq"][...] += tn(sc["normed"][image], grad_triple)
        grad_normed = nt(grad_triple, sc["wq"][...])
        unit, inverse = sc["unit"][image], sc["inverse"][image]
        a_vec[1] += tile_sum(grad_normed * unit)
        a_vec[2] += tile_sum(grad_normed)
        grad = sc["gmid"][image] + norm_back(grad_normed, unit, inverse, gain_one)
        from_grid(grad, sc["tokens"], image, count)


def scratch_shapes(n_dp, srows, grows, count):
    n = 2 * n_dp
    flat_rows = max(4120, first_row(SHARED_PARAMS, n, n - 1) + srows)
    gflat_rows = max(1040, first_row(GROUP_PARAMS, n_dp, n_dp - 1) + grows)
    shapes = dict(
        flat=((flat_rows, 128), f32),
        gflat=((2, gflat_rows, 128), f32),
        sweights=((n, srows, 128), bf16),
        gweights=((n, grows, 128), bf16),
        raw=((grows, 128), f32),
        carried=((8, 128), f32),
        turn=((GRID, GRID), bf16),
        wq=((D, 768), bf16),
        ow=((D, D), bf16),
        uw=((D, FF), bf16),
        dw=((FF, D), bf16),
        qbias=((1, 768), f32),
        ubias=((1, FF), f32),
        vecs=((8, D), f32),
        conv=((2, 16, 128), f32),
        a_wq=((D, 768), f32),
        a_ow=((D, D), f32),
        a_uw=((D, FF), f32),
        a_dwt=((D, FF), f32),
        a_pb=((8, 768), f32),
        a_ub=((8, FF), f32),
        a_vec=((6, 8, D), f32),
        a_conv=((2, 10, 8, 128), f32),
        x_in=((TOK * count, D), bf16),
        co_in=((TOK * count, D), bf16),
        tokens=((2, TOK * count, 128), f32),
        outs=((2, TOK * count, 128), f32),
        x=((count, GRID, D), f32),
        co=((count, GRID, D), f32),
        unit=((count, GRID, D), f32),
        inverse=((count, GRID, 1), f32),
        normed=((count, GRID, D), bf16),
        qkv=((count, 2, GRID, 384), bf16),
        probs=((count, 4, HEADS * STRIPE, STRIPE), f32),
        heads=((count, GRID, D), bf16),
        gmid=((count, GRID, D), f32),
        gheads=((count, GRID, D), bf16),
        gtriple=((count, GRID, 768), bf16),
    )
    stages = exchange_stages(n_dp)
    for name, rows in (("s", srows), ("g", grows)):
        outgoing, sums = scatter_shapes(stages, rows)
        for g, shape in enumerate(outgoing):
            shapes[f"{name}out{g}"] = (shape, bf16)
            shapes[f"{name}in{g}"] = (shape, bf16)
            shapes[f"{name}sum{g}"] = (sums[g], f32)
    fast = min(1 << FAST_BITS, n_dp)
    shapes["near_stat"] = ((2 * fast, 8, 128), f32)
    shapes["far_stat"] = ((n_dp // fast, 8, 128), f32)
    made = {name: pltpu.VMEM(*shape) for name, shape in shapes.items()}
    dma = pltpu.SemaphoreType.DMA
    for name in ("sgather", "ggather", "sscatter", "gscatter"):
        made[name + "_send"] = dma((len(stages), 3))
        made[name + "_recv"] = dma((len(stages), 3))
    for name, size in (("near", 2 * fast), ("far", n_dp // fast)):
        made[name + "_send"] = dma((size,))
        made[name + "_recv"] = dma((size,))
    made["local"] = dma((4,))
    return made


ACCUMULATORS = ("a_wq", "a_ow", "a_uw", "a_dwt", "a_pb", "a_ub", "a_vec", "a_conv")
TOGETHER = 2


def own_windows(n_dp, sown_ref, gown_ref, soff, goff, stages, sc):
    n = 2 * n_dp
    mine = sum((1 << t) * bit for t, bit in enumerate(own_bits(stages)))
    window = shift_on(sown_ref[...], soff)
    sc["sweights"][mine] = window.astype(bf16)
    raw = sc["raw"]
    grows = raw.shape[0]
    share = GROUP_PARAMS // n_dp
    raw[...] = jnp.zeros_like(raw)
    for r in range(-(-share // 128)):
        size = min(128, share - 128 * r)
        raw[r : r + 1, 0:size] = gown_ref[0:1, 128 * r : 128 * r + size]
    at = GAIN_ROW - first_row(SHARED_PARAMS, n, n - 1)
    raw[...] = shift_on(raw[...], goff)
    raw[grows - CARRIED :, :] = window[at : at + CARRIED]
    sc["gweights"][mine] = raw[...].astype(bf16)


def finish(n_dp, soff, goff, ssum, gsum, smine_ref, gmine_ref, norm_ref, near, far, sc):
    n = 2 * n_dp
    srows, grows = ssum.shape[0], gsum.shape[0]
    sshare, gshare = SHARED_PARAMS // n, GROUP_PARAMS // n_dp
    place = lax.broadcasted_iota(jnp.int32, (srows, 128), 0) * 128
    place = place + lax.broadcasted_iota(jnp.int32, (srows, 128), 1)
    shared = jnp.where((place >= soff) & (place < soff + sshare), ssum, 0.0)
    last = jnp.where(own_number() == n - 1, 1.0, 0.0)
    at = GAIN_ROW - first_row(SHARED_PARAMS, n, n - 1)
    smine_ref[...] = shared
    smine_ref[at : at + CARRIED, :] += gsum[grows - CARRIED :] * last
    shared = smine_ref[...]
    place = lax.broadcasted_iota(jnp.int32, (grows, 128), 0) * 128
    place = place + lax.broadcasted_iota(jnp.int32, (grows, 128), 1)
    grouped = jnp.where((place >= goff) & (place < goff + gshare), gsum, 0.0)
    near_me, near_peers = near
    far_me, far_peers = far
    sc["near_stat"][near_me] = tile_sum(shared * shared) + tile_sum(grouped * grouped)
    total = all_share(near_me, near_peers, sc["near_stat"], sc["near_send"], sc["near_recv"])
    sc["far_stat"][far_me] = total
    total = all_share(far_me, far_peers, sc["far_stat"], sc["far_send"], sc["far_recv"])
    total = jnp.sum(jnp.sum(total, axis=0, keepdims=True), axis=1, keepdims=True)
    norm = jnp.sqrt(total)
    norm_ref[...] = jnp.broadcast_to(norm, (8, 128))
    threshold = math.sqrt(2 * GROUP_PARAMS + SHARED_PARAMS)
    factor = jnp.minimum(1.0, threshold / (norm + 1e-06))
    smine_ref[...] = shift_back(shared * factor, soff)
    gmine_ref[...] = shift_back(grouped * factor, goff)


def step_kernel(
    n_dp,
    count,
    names,
    drop_ref,
    x_ref,
    co_ref,
    sown_ref,
    gown_ref,
    out_ref,
    gin_ref,
    smine_ref,
    gmine_ref,
    norm_ref,
    *scratch,
):
    sc = dict(zip(names, scratch))
    n = 2 * n_dp
    stages = exchange_stages(n_dp)
    near, far = group_peers(n_dp)
    devices = [device for _, device in near[1] + far[1]]
    barrier = pltpu.get_barrier_semaphore()
    for device in devices:
        pl.semaphore_signal(barrier, inc=1, device_id=device)
    load_x = pltpu.make_async_copy(x_ref, sc["x_in"], sc["local"].at[0])
    load_co = pltpu.make_async_copy(co_ref, sc["co_in"], sc["local"].at[1])
    load_x.start()
    load_co.start()
    soff = (own_number() * (SHARED_PARAMS // n)) % UNIT
    goff = (lax.axis_index("dp") * (GROUP_PARAMS // n_dp)) % UNIT
    own_windows(n_dp, sown_ref, gown_ref, soff, goff, stages, sc)
    pl.semaphore_wait(barrier, len(devices))
    ggather = Gather(stages, sc["gweights"], sc["ggather_send"], sc["ggather_recv"])
    sgather = Gather(stages, sc["sweights"], sc["sgather_send"], sc["sgather_recv"])

    def run(phase, extra=None, together=TOGETHER):
        def body(i, carry):
            if extra is not None:
                for at, action in extra.items():
                    pl.when(i == at)(action)
            phase([i * together + k for k in range(together)])
            return carry

        lax.fori_loop(0, count // together, body, 0)

    last = len(stages) - 1
    ggather.start(0)
    sgather.start(0)
    load_x.wait()
    to_grid(sc["x_in"], sc["tokens"], sc["x"])
    for g in range(last):
        ggather.wait(g)
        ggather.start(g + 1)
        if g == 0:
            sc["turn"][...] = turn_matrix()
            run(lambda images: first_norm(images, sc))
            for name in ACCUMULATORS:
                sc[name][...] = jnp.zeros_like(sc[name])
    load_co.wait()
    to_grid(sc["co_in"], sc["tokens"], sc["co"])
    ggather.wait(last)
    prepare_group(n_dp, stages, sc)

    steps = count // TOGETHER
    forward, backward = {}, {}
    for g in range(last):
        def advance(g=g):
            sgather.wait(g)
            sgather.start(g + 1)

        at = min(g, steps - 1)
        forward[at] = forward.get(at, []) + [advance]
    run(lambda images: attention_forward(images, sc), {at: chain(todo) for at, todo in forward.items()})
    sgather.wait(last)
    prepare_shared(n_dp, stages, sc)
    run(lambda images: mlp_both(images, count, drop_ref, sc))
    stores = []
    for half in range(2):
        cols = slice(half * 128, (half + 1) * 128)
        stores.append(
            pltpu.make_async_copy(sc["outs"].at[half], out_ref.at[:, cols], sc["local"].at[half])
        )
        stores[-1].start()
    place_shared(sc)

    half_bits = len(flat_bits(stages)) - 1
    top = own_bits(stages)[half_bits]
    srows, grows = sc["sweights"].shape[1], sc["gweights"].shape[1]

    def swindow(place):
        k = device_at(stages, place)
        row = (k * (SHARED_PARAMS // n)) // UNIT * 8
        return sc["flat"][pl.ds(pl.multiple_of(row, 8), srows), :]

    upper = (lax.broadcasted_iota(jnp.int32, (8, 128), 0) < 8 - CARRIED).astype(f32)

    def gwindow(place):
        k = device_at(stages, place)
        row = ((k // 2) * (GROUP_PARAMS // n_dp)) // UNIT * 8
        return jnp.concatenate(
            [
                sc["gflat"][k % 2, pl.ds(pl.multiple_of(row, 8), grows - 8), :],
                sc["gflat"][k % 2, pl.ds(pl.multiple_of(row + grows - 8, 8), 8), :] * upper
                + sc["carried"][...],
            ],
            axis=0,
        )

    def scatter(name, window):
        parts = [[sc[f"{name}{kind}{g}"] for g in range(last + 1)] for kind in ("out", "in", "sum")]
        return Scatter(
            stages, window, *parts, sc[name + "scatter_send"], sc[name + "scatter_recv"]
        )

    sscatter = scatter("s", swindow)
    gscatter = scatter("g", gwindow)
    sscatter.start(last)
    for g in range(last, -1, -1):
        def advance(g=g):
            sscatter.wait(g)
            if g > 0:
                sscatter.start(g - 1)

        at = min(last - g + 1, steps - 1)
        backward[at] = backward.get(at, []) + [advance]
    run(
        lambda images: attention_back(images, count, sc),
        {at: chain(todo) for at, todo in backward.items()},
    )
    for half in range(2):
        cols = slice(half * 128, (half + 1) * 128)
        stores.append(
            pltpu.make_async_copy(
                sc["tokens"].at[half], gin_ref.at[:, cols], sc["local"].at[2 + half]
            )
        )
        stores[-1].start()
    place_group(sc)
    gscatter.start(last)
    for g in range(last, -1, -1):
        gscatter.wait(g)
        if g > 0:
            gscatter.start(g - 1)
    finish(
        n_dp,
        soff,
        goff,
        sc["ssum0"][0],
        sc["gsum0"][0],
        smine_ref,
        gmine_ref,
        norm_ref,
        near,
        far,
        sc,
    )
    for store in stores:
        store.wait()


def chain(actions):
    def run_all():
        for action in actions:
            action()

    return run_all


def step(n_dp, drops, images, cotangent, sown, gown):
    count = images.shape[0]
    srows = sown.shape[0]
    grows = window_rows(GROUP_PARAMS, n_dp, CARRIED)
    shapes = scratch_shapes(n_dp, srows, grows, count)
    vmem = pl.BlockSpec(memory_space=pltpu.VMEM)
    anywhere = pl.BlockSpec(memory_space=pl.ANY)

    def rows(array):
        return jnp.swapaxes(array, 0, 1).reshape(TOK * count, D)

    def unrows(array):
        return jnp.swapaxes(array.reshape(TOK, count, D), 0, 1)

    out, gin, smine, gmine, norm = pl.pallas_call(
        partial(step_kernel, n_dp, count, tuple(shapes)),
        in_specs=[pl.BlockSpec(memory_space=pltpu.SMEM), anywhere, anywhere, vmem, vmem],
        out_specs=[anywhere, anywhere, vmem, vmem, vmem],
        out_shape=[jax.ShapeDtypeStruct((TOK * count, D), f32)] * 2
        + [
            jax.ShapeDtypeStruct((srows, 128), f32),
            jax.ShapeDtypeStruct((grows, 128), f32),
            jax.ShapeDtypeStruct((8, 128), f32),
        ],
        scratch_shapes=list(shapes.values()),
        compiler_params=pltpu.CompilerParams(
            collective_id=0, has_side_effects=True, vmem_limit_bytes=62 * 1024 * 1024
        ),
        name="step",
    )(drops.T, rows(images), rows(cotangent), sown, gown)
    return unrows(out), unrows(gin), smine, gmine, norm


def adam_step(master, gradient, first, second, step):
    first_new = beta_one * first + (1.0 - beta_one) * gradient
    second_new = beta_two * second + (1.0 - beta_two) * gradient * gradient
    first_hat = first_new / (1.0 - jnp.power(jnp.float32(beta_one), step))
    second_hat = second_new / (1.0 - jnp.power(jnp.float32(beta_two), step))
    master_new = master - learn_rate * (
        first_hat / (jnp.sqrt(second_hat) + adam_eps) + decay_rate * master
    )
    return (master_new, first_new, second_new)


def on_device(
    n_dp,
    images,
    cotangent,
    drop_masks,
    group_master,
    group_m1,
    group_m2,
    shared_master,
    shared_m1,
    shared_m2,
):
    n = 2 * n_dp
    srows = window_rows(SHARED_PARAMS, n)
    sshare, gshare = SHARED_PARAMS // n, GROUP_PARAMS // n_dp
    sown = jnp.pad(shared_master, (0, srows * 128 - sshare)).reshape(srows, 128)
    output, input_grad, smine, gmine, norm = step(
        n_dp, drop_masks, images, cotangent, sown, group_master
    )
    shared_grad = smine.reshape(-1)[:sshare]
    group_grad = gmine.reshape(-1)[:gshare][None, :]
    now = jnp.float32(STEP)
    group_new, group_first, group_second = adam_step(
        group_master, group_grad, group_m1, group_m2, now
    )
    shared_new, shared_first, shared_second = adam_step(
        shared_master, shared_grad, shared_m1, shared_m2, now
    )
    return (
        output,
        input_grad,
        norm[0, 0:1],
        group_grad,
        group_new,
        group_first,
        group_second,
        group_new.astype(jnp.bfloat16),
        shared_grad,
        shared_new,
        shared_first,
        shared_second,
        shared_new.astype(jnp.bfloat16),
    )


def solution(mesh):
    both = P(("dp", "heads"))
    rows = P(("dp", "heads"), None, None)
    split = P("heads", "dp")
    in_specs = (rows, rows, P(("dp", "heads"), None), split, split, split, both, both, both)
    out_specs = (rows, rows, P(), split, split, split, split, split, both, both, both, both, both)
    return jax.shard_map(
        partial(on_device, mesh.shape["dp"]),
        mesh=mesh,
        in_specs=in_specs,
        out_specs=out_specs,
        check_vma=False,
    )
```

```python
from functools import partial
import math

import jax
import jax.numpy as jnp
from jax import lax
from jax.experimental import pallas as pl
from jax.experimental.pallas import tpu as pltpu
from jax.sharding import PartitionSpec as P

D = 256
FF = 1024
SIDE = 14
SW = 7
STEP = 10
HD = 32
HALF = 128
GROUP_PARAMS = 132608
SHARED_PARAMS = 526848
TOK = SIDE * SIDE
GRID = 16 * SIDE
STRIPE = 16 * SW
HEADS = HALF // HD
UNIT = 1024

eps_norm = 1e-05
keep_prob = 0.8
beta_one = 0.9
beta_two = 0.999
adam_eps = 1e-08
learn_rate = 0.04
decay_rate = 0.05

f32 = jnp.float32
bf16 = jnp.bfloat16


def window_rows(total, count, extra=0):
    share = total // count
    most = max((share * k) % UNIT + share for k in range(count)) + extra * 128
    return 16 * (-(-most // (2 * UNIT)))


def first_row(total, count, k):
    return (total // count * k) // UNIT * 8


HEADS_BIT = -1
FAST_BITS = 4
CARRIED = 4
GAIN_ROW = 4106


def exchange_stages(n_dp):
    bits = n_dp.bit_length() - 1
    far = list(range(bits - 1, 1, -1))
    stages = [tuple(far[i : i + 2]) for i in range(0, len(far), 2)]
    stages.append((1, HEADS_BIT) if bits > 1 else (HEADS_BIT,))
    if bits > 0:
        stages.append((0,))
    return stages


def weight_of(bit):
    return 1 if bit == HEADS_BIT else 2 << bit


def flat_bits(stages):
    return [bit for stage in stages for bit in stage]


def place_of(stages, k):
    return sum(((k // weight_of(bit)) % 2) << t for t, bit in enumerate(flat_bits(stages)))


def device_at(stages, place, first=0):
    return sum(
        ((place // (1 << t)) % 2) * weight_of(bit)
        for t, bit in enumerate(flat_bits(stages))
        if t >= first
    )


def own_number():
    return lax.axis_index("dp") * 2 + lax.axis_index("heads")


def own_bits(stages):
    me = own_number()
    return [(me // weight_of(bit)) % 2 for bit in flat_bits(stages)]


def peer(bits, mask):
    dp, heads = lax.axis_index("dp"), lax.axis_index("heads")
    for i, bit in enumerate(bits):
        if mask >> i & 1:
            if bit == HEADS_BIT:
                heads = 1 - heads
            else:
                dp = dp + (1 << bit) * (1 - 2 * ((dp // (1 << bit)) % 2))
    return {"dp": dp, "heads": heads}


def group_peers(n_dp):
    dp, heads = lax.axis_index("dp"), lax.axis_index("heads")
    fast = min(1 << FAST_BITS, n_dp)
    low, high = dp % fast, dp // fast
    count = 2 * fast
    me = low * 2 + heads
    near = []
    for step in range(1, count):
        other = (me + step) % count
        near.append((other, {"dp": high * fast + other // 2, "heads": other % 2}))
    far = []
    for step in range(1, n_dp // fast):
        other = (high + step) % (n_dp // fast)
        far.append((other, {"dp": other * fast + low, "heads": heads}))
    return (me, near), (high, far)


class Gather:
    def __init__(self, stages, buffer, send_sem, recv_sem):
        self.stages, self.buffer = stages, buffer
        self.send_sem, self.recv_sem = send_sem, recv_sem
        self.bits = own_bits(stages)

    def copies(self, g, arriving):
        start = sum(len(stage) for stage in self.stages[:g])
        for mask in range(1, 1 << len(self.stages[g])):
            base = 0
            for u, bit in enumerate(self.bits):
                flipped = start <= u < start + len(self.stages[g]) and mask >> (u - start) & 1
                if u >= start:
                    base = base + (1 << u) * (1 - bit if flipped and arriving else bit)
            held = self.buffer.at[pl.ds(base, 1 << start)]
            yield pltpu.make_async_remote_copy(
                src_ref=held,
                dst_ref=held,
                send_sem=self.send_sem.at[g, mask - 1],
                recv_sem=self.recv_sem.at[g, mask - 1],
                device_id=peer(self.stages[g], mask),
            )

    def start(self, g):
        for copy in self.copies(g, False):
            copy.start()

    def wait(self, g):
        for copy in self.copies(g, True):
            copy.wait_recv()
        for copy in self.copies(g, False):
            copy.wait_send()


class Scatter:
    def __init__(self, stages, window, outgoing, incoming, sums, send_sem, recv_sem):
        self.stages, self.window = stages, window
        self.outgoing, self.incoming, self.sums = outgoing, incoming, sums
        self.send_sem, self.recv_sem = send_sem, recv_sem
        self.bits = own_bits(stages)

    def offset(self, g):
        return sum(len(stage) for stage in self.stages[:g])

    def held(self, g, place):
        if g == len(self.stages) - 1:
            return self.window(place)
        return self.sums[g + 1][place]

    def copy(self, g, mask):
        return pltpu.make_async_remote_copy(
            src_ref=self.outgoing[g].at[mask - 1],
            dst_ref=self.incoming[g].at[mask - 1],
            send_sem=self.send_sem.at[g, mask - 1],
            recv_sem=self.recv_sem.at[g, mask - 1],
            device_id=peer(self.stages[g], mask),
        )

    def part(self, g, mask):
        start = self.offset(g)
        return sum(
            (1 << (start + i)) * (1 - self.bits[start + i] if mask >> i & 1 else self.bits[start + i])
            for i in range(len(self.stages[g]))
        )

    def start(self, g):
        for mask in range(1, 1 << len(self.stages[g])):
            part = self.part(g, mask)

            def fill(i, carry, mask=mask, part=part):
                self.outgoing[g][mask - 1, i] = self.held(g, part + i).astype(bf16)
                return carry

            lax.fori_loop(0, 1 << self.offset(g), fill, 0)
            self.copy(g, mask).start()

    def wait(self, g):
        masks = range(1, 1 << len(self.stages[g]))
        for mask in masks:
            self.copy(g, mask).wait()
        part = self.part(g, 0)

        def add(i, carry):
            value = self.held(g, part + i)
            for mask in masks:
                value = value + self.incoming[g][mask - 1, i].astype(f32)
            self.sums[g][i] = value
            return carry

        lax.fori_loop(0, 1 << self.offset(g), add, 0)


def scatter_shapes(stages, rows):
    outgoing, sums = [], []
    start = 0
    for stage in stages:
        outgoing.append(((1 << len(stage)) - 1, 1 << start, rows, 128))
        sums.append((1 << start, rows, 128))
        start += len(stage)
    return outgoing, sums


def all_share(me, peers, stat_ref, send_sem, recv_sem):
    copies = []
    for other, device in peers:
        copy = pltpu.make_async_remote_copy(
            src_ref=stat_ref.at[me],
            dst_ref=stat_ref.at[me],
            send_sem=send_sem.at[other],
            recv_sem=recv_sem.at[me],
            device_id=device,
        )
        copy.start()
        copies.append(copy)
    for other, device in peers:
        pltpu.make_async_remote_copy(
            src_ref=stat_ref.at[other],
            dst_ref=stat_ref.at[other],
            send_sem=send_sem.at[other],
            recv_sem=recv_sem.at[other],
            device_id=device,
        ).wait_recv()
    for copy in copies:
        copy.wait_send()
    return jnp.sum(stat_ref[...], axis=0)


def shift_on(rows, amount):
    lanes = amount % 128
    turned = pltpu.roll(rows, lanes, 1)
    lane = lax.broadcasted_iota(jnp.int32, rows.shape, 1)
    turned = jnp.where(lane < lanes, pltpu.roll(turned, 1, 0), turned)
    return pltpu.roll(turned, amount // 128, 0)


def shift_back(rows, amount):
    count = rows.shape[0]
    lanes = amount % 128
    turned = pltpu.roll(rows, (128 - lanes) % 128, 1)
    lane = lax.broadcasted_iota(jnp.int32, rows.shape, 1)
    turned = jnp.where(lane >= 128 - lanes, pltpu.roll(turned, count - 1, 0), turned)
    return pltpu.roll(turned, (count - amount // 128) % count, 0)


def nn(a, b):
    return lax.dot_general(a, b, (((1,), (0,)), ((), ())), preferred_element_type=f32)


def nt(a, b):
    return lax.dot_general(a, b, (((1,), (1,)), ((), ())), preferred_element_type=f32)


def tn(a, b):
    return lax.dot_general(a, b, (((0,), (0,)), ((), ())), preferred_element_type=f32)


def norm_parts(values):
    center = values - jnp.mean(values, axis=-1, keepdims=True)
    inverse = lax.rsqrt(jnp.mean(center * center, axis=-1, keepdims=True) + eps_norm)
    return center * inverse, inverse


def norm_back(grad_after, unit, inverse, gain):
    scaled = grad_after * gain
    return inverse * (
        scaled
        - jnp.mean(scaled, axis=-1, keepdims=True)
        - unit * jnp.mean(scaled * unit, axis=-1, keepdims=True)
    )


def column_sum(values):
    return jnp.sum(values, axis=0, keepdims=True)


def head_masks(dtype):
    lane = lax.broadcasted_iota(jnp.int32, (1, HALF), 1) // HD
    return [(lane == h).astype(f32).astype(dtype) for h in range(HEADS)]


def spread_heads(values, masks):
    return jnp.concatenate([values * masks[h] for h in range(HEADS)], axis=0)


def pick_heads(stacked):
    lane = lax.broadcasted_iota(jnp.int32, (STRIPE, HALF), 1)
    picked = stacked[(HEADS - 1) * STRIPE :]
    for h in range(HEADS - 2, -1, -1):
        picked = jnp.where(lane < (h + 1) * HD, stacked[h * STRIPE : (h + 1) * STRIPE], picked)
    return picked


def row_shift(values, step):
    if step == 0:
        return values
    zero = jnp.zeros((16, HALF), f32)
    if step > 0:
        return jnp.concatenate([values[16:], zero], axis=0)
    return jnp.concatenate([zero, values[:-16]], axis=0)


def neighbours(values):
    return [pltpu.roll(values, 1, 0), values, pltpu.roll(values, STRIPE - 1, 0)]


def tile_sum(values):
    return jnp.sum(values.reshape(-1, 8, values.shape[1]), axis=0)


def turn_matrix():
    to = lax.broadcasted_iota(jnp.int32, (GRID, GRID), 0)
    src = lax.broadcasted_iota(jnp.int32, (GRID, GRID), 1)
    first, second = to // 16, to % 16
    return ((second < SIDE) & (src == second * 16 + first)).astype(f32).astype(bf16)


def row_mask():
    row = lax.broadcasted_iota(jnp.int32, (GRID, 1), 0)
    return (row % 16 < SIDE).astype(f32)


def to_grid(source, tokens, grid_ref):
    images = grid_ref.shape[0]
    grid_ref[...] = jnp.zeros_like(grid_ref)
    for half in range(2):
        cols = slice(half * 128, (half + 1) * 128)
        tokens[half] = source[:, cols].astype(f32)
        for image in range(images):
            for r in range(SIDE):
                grid_ref[image, 16 * r : 16 * r + SIDE, cols] = tokens[
                    half, pl.ds(r * SIDE * images + image, SIDE, stride=images), :
                ]


def from_grid(value, tokens, image, images):
    for half in range(2):
        for r in range(SIDE):
            tokens[half, pl.ds(r * SIDE * images + image, SIDE, stride=images), :] = value[
                16 * r : 16 * r + SIDE, half * 128 : (half + 1) * 128
            ]


def prepare_group(n_dp, stages, sc):
    n = 2 * n_dp
    gflat, buffer = sc["gflat"], sc["gweights"]
    grows = buffer.shape[1]
    gflat[...] = jnp.zeros_like(gflat)
    for k in range(n):
        at = first_row(GROUP_PARAMS, n_dp, k // 2)
        size = grows - CARRIED
        gflat[k % 2, at : at + size] += buffer[place_of(stages, k), 0:size].astype(f32)
    carried = buffer[place_of(stages, n - 1)].astype(f32)[grows - CARRIED :]
    for c in range(2):
        cols = slice(c * 128, (c + 1) * 128)
        sc["vecs"][1:2, cols] = carried[c : c + 1]
        sc["vecs"][2:3, cols] = carried[2 + c : 3 + c]
    for j in range(2):
        for c in range(3):
            cols = slice(j * 384 + c * 128, j * 384 + (c + 1) * 128)
            sc["wq"][:, cols] = gflat[j, pl.ds(c, D, stride=3), :].astype(bf16)
        for c in range(2):
            cols = slice(c * 128, (c + 1) * 128)
            sc["ow"][j * 128 : (j + 1) * 128, cols] = gflat[
                j, pl.ds(770 + c, HALF, stride=2), :
            ].astype(bf16)
        sc["qbias"][:, j * 384 : j * 384 + 128] = gflat[j, 768:769, :]
        sc["qbias"][:, j * 384 + 128 : j * 384 + 256] = jnp.zeros((1, 128), f32)
        sc["qbias"][:, j * 384 + 256 : j * 384 + 384] = gflat[j, 769:770, :]
        sc["conv"][j, 0:10] = gflat[j, 1026:1036, :]


def prepare_shared(n_dp, stages, sc):
    n = 2 * n_dp
    flat, buffer = sc["flat"], sc["sweights"]
    srows = buffer.shape[1]
    flat[...] = jnp.zeros_like(flat)
    for k in range(n):
        at = first_row(SHARED_PARAMS, n, k)
        flat[at : at + srows] += buffer[place_of(stages, k)].astype(f32)
    for c in range(8):
        cols = slice(c * 128, (c + 1) * 128)
        sc["uw"][:, cols] = flat[pl.ds(c, D, stride=8), :].astype(bf16)
        sc["ubias"][:, cols] = flat[2048 + c : 2049 + c, :]
    for c in range(2):
        cols = slice(c * 128, (c + 1) * 128)
        sc["dw"][:, cols] = flat[pl.ds(2056 + c, FF, stride=2), :].astype(bf16)
        for i in (0, 3, 4, 5):
            sc["vecs"][i : i + 1, cols] = flat[4104 + 2 * i + c : 4105 + 2 * i + c, :]


def place_shared(sc):
    flat = sc["flat"]
    for c in range(8):
        cols = slice(c * 128, (c + 1) * 128)
        flat[pl.ds(c, D, stride=8), :] = sc["a_uw"][:, cols]
        flat[2048 + c : 2049 + c, :] = sc["a_ub"][0:1, cols]
    for q in range(4):
        turned = sc["a_dwt"][:, q * 256 : (q + 1) * 256].T
        for c in range(2):
            flat[pl.ds(2056 + 512 * q + c, 256, stride=2), :] = turned[
                :, c * 128 : (c + 1) * 128
            ]
    for c in range(2):
        cols = slice(c * 128, (c + 1) * 128)
        for i in (0, 3, 4, 5):
            flat[4104 + 2 * i + c : 4105 + 2 * i + c, :] = column_sum(
                sc["a_vec"][i, :, cols]
            )
    flat[GAIN_ROW : GAIN_ROW + CARRIED, :] = jnp.zeros((CARRIED, 128), f32)


def place_group(sc):
    gflat = sc["gflat"]
    for j in range(2):
        for c in range(3):
            cols = slice(j * 384 + c * 128, j * 384 + (c + 1) * 128)
            gflat[j, pl.ds(c, D, stride=3), :] = sc["a_wq"][:, cols]
        for c in range(2):
            cols = slice(c * 128, (c + 1) * 128)
            gflat[j, pl.ds(770 + c, HALF, stride=2), :] = sc["a_ow"][
                j * 128 : (j + 1) * 128, cols
            ]
        gflat[j, 768:769, :] = sc["a_pb"][0:1, j * 384 : j * 384 + 128]
        gflat[j, 769:770, :] = sc["a_pb"][0:1, j * 384 + 256 : j * 384 + 384]
        for i in range(10):
            gflat[j, 1026 + i : 1027 + i, :] = column_sum(sc["a_conv"][j, i])
    for c in range(2):
        cols = slice(c * 128, (c + 1) * 128)
        sc["carried"][4 + c : 5 + c, :] = column_sum(sc["a_vec"][1, :, cols])
        sc["carried"][6 + c : 7 + c, :] = column_sum(sc["a_vec"][2, :, cols])
    sc["carried"][0:4, :] = jnp.zeros((4, 128), f32)


def first_norm(images, sc):
    for image in images:
        sc["unit"][image], sc["inverse"][image] = norm_parts(sc["x"][image])


def attention_forward(images, sc):
    scale = HD ** (-0.5)
    masks = head_masks(bf16)
    inside = row_mask()
    key_row = lax.broadcasted_iota(jnp.int32, (1, SW, 16, STRIPE), 2)
    gain_one, shift_one = sc["vecs"][1:2], sc["vecs"][2:3]
    qkv_ref, conv = sc["qkv"], sc["conv"]
    for image in images:
        sc["normed"][image] = (sc["unit"][image] * gain_one + shift_one).astype(bf16)
    for image in images:
        triple = (nn(sc["normed"][image], sc["wq"][...]) + sc["qbias"][...]) * inside
        triple = triple.astype(bf16)
        qkv_ref[image, 0] = triple[:, :384]
        qkv_ref[image, 1] = nn(sc["turn"][...], triple[:, 384:]).astype(bf16)
    for j in range(2):
        padded = [[] for _ in images]
        for s in range(2):
            for image, parts in zip(images, padded):
                rows = slice(s * STRIPE, (s + 1) * STRIPE)
                query = qkv_ref[image, j, rows, 0:128]
                keys = spread_heads(qkv_ref[image, j, rows, 128:256], masks)
                value = qkv_ref[image, j, rows, 256:384]
                scores = nt(keys, query).reshape(HEADS, SW, 16, STRIPE) * scale
                scores = jnp.where(key_row < SIDE, scores, -1e30)
                scores = scores.reshape(HEADS, STRIPE, STRIPE)
                weights = jnp.exp(scores - jnp.max(scores, axis=1, keepdims=True))
                probs = weights * (1.0 / jnp.sum(weights, axis=1, keepdims=True))
                probs = probs.reshape(HEADS * STRIPE, STRIPE)
                sc["probs"][image, 2 * j + s] = probs
                attended = tn(probs.astype(bf16), spread_heads(value, masks))
                near = neighbours(value.astype(f32))
                total = attended + conv[j, 9:10]
                for a in range(3):
                    part = near[0] * conv[j, 3 * a : 3 * a + 1]
                    for b in range(1, 3):
                        part = part + near[b] * conv[j, 3 * a + b : 3 * a + b + 1]
                    total = total + row_shift(part, a - 1)
                parts.append(total.astype(bf16))
        for image, parts in zip(images, padded):
            both = jnp.concatenate(parts, axis=0)
            if j == 1:
                both = nn(sc["turn"][...], both).astype(bf16)
            sc["heads"][image, :, j * 128 : (j + 1) * 128] = both


def mlp_both(images, count, drop_ref, sc):
    down_bias = sc["vecs"][0:1]
    gain_two, shift_two, out_bias = sc["vecs"][3:4], sc["vecs"][4:5], sc["vecs"][5:6]
    a_vec = sc["a_vec"]
    uw, dw, ubias = sc["uw"], sc["dw"], sc["ubias"]
    many = len(images)
    ones = jnp.ones((8, many * GRID), bf16)

    def join(parts):
        return jnp.concatenate(parts, axis=0)

    def part_of(joined, i):
        return joined[i * GRID : (i + 1) * GRID]

    heads = sc["heads"][pl.ds(images[0], many)].reshape(many * GRID, D)
    branch = nn(heads, sc["ow"][...])
    state = []
    for i, image in enumerate(images):
        scale_one = drop_ref[0, image].astype(f32) / keep_prob
        scale_two = drop_ref[1, image].astype(f32) / keep_prob
        middle = sc["x"][image] + scale_one * (part_of(branch, i) + out_bias)
        unit_two, inverse_two = norm_parts(middle)
        grad_output = sc["co"][image]
        grad_mlp_f = scale_two * grad_output
        a_vec[0] += tile_sum(grad_mlp_f)
        state.append((scale_one, scale_two, middle, unit_two, inverse_two, grad_output, grad_mlp_f))
    normed_two = join([(st[3] * gain_two + shift_two).astype(bf16) for st in state])
    grad_mlp = join([st[6].astype(bf16) for st in state])
    mlp = None
    grad_normed = None
    for c in range(4):
        cols = slice(c * 256, (c + 1) * 256)
        hidden = nn(normed_two, uw[:, cols]) + ubias[:, cols]
        density = jnp.exp(hidden * hidden * -0.5) * (1.0 / math.sqrt(2.0 * math.pi))
        phi = 0.5 + 0.5 * lax.erf(hidden * math.sqrt(0.5))
        active = (hidden * phi).astype(bf16)
        part = nn(active, dw[cols, :])
        mlp = part if mlp is None else mlp + part
        sc["a_dwt"][:, cols] += tn(grad_mlp, active)
        grad_active = nt(grad_mlp, dw[cols, :])
        grad_hidden = (grad_active * (phi + hidden * density)).astype(bf16)
        sc["a_ub"][:, cols] += nn(ones, grad_hidden)
        sc["a_uw"][:, cols] += tn(normed_two, grad_hidden)
        part = nt(grad_hidden, uw[:, cols])
        grad_normed = part if grad_normed is None else grad_normed + part
    grad_branch = []
    for i, image in enumerate(images):
        scale_one, scale_two, middle, unit_two, inverse_two, grad_output, _ = state[i]
        from_grid(
            middle + scale_two * (part_of(mlp, i) + down_bias), sc["outs"], image, count
        )
        grad = part_of(grad_normed, i)
        a_vec[3] += tile_sum(grad * unit_two)
        a_vec[4] += tile_sum(grad)
        grad_middle = grad_output + norm_back(grad, unit_two, inverse_two, gain_two)
        sc["gmid"][image] = grad_middle
        grad_branch_f = scale_one * grad_middle
        a_vec[5] += tile_sum(grad_branch_f)
        grad_branch.append(grad_branch_f.astype(bf16))
    grad_branch = join(grad_branch)
    sc["a_ow"][...] += tn(heads, grad_branch)
    grad_heads = nt(grad_branch, sc["ow"][...]).astype(bf16)
    sc["gheads"][pl.ds(images[0], many)] = grad_heads.reshape(many, GRID, D)


def attention_back(images, count, sc):
    scale = HD ** (-0.5)
    masks = head_masks(bf16)
    inside = row_mask()[:STRIPE]
    gain_one = sc["vecs"][1:2]
    ones = jnp.ones((8, GRID), bf16)
    a_vec, a_conv = sc["a_vec"], sc["a_conv"]
    qkv_ref, conv = sc["qkv"], sc["conv"]
    for j in range(2):
        if j == 0:
            grads = [sc["gheads"][image, :, 0:128] for image in images]
        else:
            grads = [
                nn(sc["turn"][...], sc["gheads"][image, :, 128:256]).astype(bf16)
                for image in images
            ]
        padded = [[] for _ in images]
        for s in range(2):
            for image, parts, all_grad in zip(images, padded, grads):
                rows = slice(s * STRIPE, (s + 1) * STRIPE)
                query = qkv_ref[image, j, rows, 0:128]
                keys = spread_heads(qkv_ref[image, j, rows, 128:256], masks)
                value = qkv_ref[image, j, rows, 256:384]
                grad = all_grad[rows]
                grad_f = grad.astype(f32)
                probs = sc["probs"][image, 2 * j + s]
                grad_probs = nt(spread_heads(value, masks), grad)
                product = (probs * grad_probs).reshape(HEADS, STRIPE, STRIPE)
                inner = jnp.sum(product, axis=1, keepdims=True)
                grad_scores = product - probs.reshape(HEADS, STRIPE, STRIPE) * inner
                grad_scores = grad_scores.reshape(HEADS * STRIPE, STRIPE).astype(bf16)
                grad_query = tn(grad_scores, keys) * scale
                grad_key = pick_heads(nn(grad_scores, query)) * scale
                grad_value = pick_heads(nn(probs.astype(bf16), grad))
                near = neighbours(grad_f)
                for a in range(3):
                    part = near[2] * conv[j, 3 * a : 3 * a + 1]
                    for b in range(1, 3):
                        part = part + near[2 - b] * conv[j, 3 * a + b : 3 * a + b + 1]
                    grad_value = grad_value + row_shift(part, 1 - a)
                grad_value = grad_value * inside
                near = neighbours(value.astype(f32))
                for b in range(3):
                    a_conv[j, b] += tile_sum(grad_f[16:] * near[b][:-16])
                    a_conv[j, 3 + b] += tile_sum(grad_f * near[b])
                    a_conv[j, 6 + b] += tile_sum(grad_f[:-16] * near[b][16:])
                a_conv[j, 9] += tile_sum(grad_f)
                parts.append(
                    jnp.concatenate([grad_query, grad_key, grad_value], axis=1).astype(bf16)
                )
        for image, parts in zip(images, padded):
            both = jnp.concatenate(parts, axis=0)
            if j == 1:
                both = nn(sc["turn"][...], both).astype(bf16)
            sc["gtriple"][image, :, j * 384 : (j + 1) * 384] = both
    for image in images:
        grad_triple = sc["gtriple"][image]
        sc["a_pb"][...] += nn(ones, grad_triple)
        sc["a_wq"][...] += tn(sc["normed"][image], grad_triple)
        grad_normed = nt(grad_triple, sc["wq"][...])
        unit, inverse = sc["unit"][image], sc["inverse"][image]
        a_vec[1] += tile_sum(grad_normed * unit)
        a_vec[2] += tile_sum(grad_normed)
        grad = sc["gmid"][image] + norm_back(grad_normed, unit, inverse, gain_one)
        from_grid(grad, sc["tokens"], image, count)


def scratch_shapes(n_dp, srows, grows, count):
    n = 2 * n_dp
    flat_rows = max(4120, first_row(SHARED_PARAMS, n, n - 1) + srows)
    gflat_rows = max(1040, first_row(GROUP_PARAMS, n_dp, n_dp - 1) + grows)
    shapes = dict(
        flat=((flat_rows, 128), f32),
        gflat=((2, gflat_rows, 128), f32),
        sweights=((n, srows, 128), bf16),
        gweights=((n, grows, 128), bf16),
        raw=((grows, 128), f32),
        carried=((8, 128), f32),
        turn=((GRID, GRID), bf16),
        wq=((D, 768), bf16),
        ow=((D, D), bf16),
        uw=((D, FF), bf16),
        dw=((FF, D), bf16),
        qbias=((1, 768), f32),
        ubias=((1, FF), f32),
        vecs=((8, D), f32),
        conv=((2, 16, 128), f32),
        a_wq=((D, 768), f32),
        a_ow=((D, D), f32),
        a_uw=((D, FF), f32),
        a_dwt=((D, FF), f32),
        a_pb=((8, 768), f32),
        a_ub=((8, FF), f32),
        a_vec=((6, 8, D), f32),
        a_conv=((2, 10, 8, 128), f32),
        x_in=((TOK * count, D), bf16),
        co_in=((TOK * count, D), bf16),
        tokens=((2, TOK * count, 128), f32),
        outs=((2, TOK * count, 128), f32),
        x=((count, GRID, D), f32),
        co=((count, GRID, D), f32),
        unit=((count, GRID, D), f32),
        inverse=((count, GRID, 1), f32),
        normed=((count, GRID, D), bf16),
        qkv=((count, 2, GRID, 384), bf16),
        probs=((count, 4, HEADS * STRIPE, STRIPE), f32),
        heads=((count, GRID, D), bf16),
        gmid=((count, GRID, D), f32),
        gheads=((count, GRID, D), bf16),
        gtriple=((count, GRID, 768), bf16),
    )
    stages = exchange_stages(n_dp)
    for name, rows in (("s", srows), ("g", grows)):
        outgoing, sums = scatter_shapes(stages, rows)
        for g, shape in enumerate(outgoing):
            shapes[f"{name}out{g}"] = (shape, bf16)
            shapes[f"{name}in{g}"] = (shape, bf16)
            shapes[f"{name}sum{g}"] = (sums[g], f32)
    fast = min(1 << FAST_BITS, n_dp)
    shapes["near_stat"] = ((2 * fast, 8, 128), f32)
    shapes["far_stat"] = ((n_dp // fast, 8, 128), f32)
    made = {name: pltpu.VMEM(*shape) for name, shape in shapes.items()}
    dma = pltpu.SemaphoreType.DMA
    for name in ("sgather", "ggather", "sscatter", "gscatter"):
        made[name + "_send"] = dma((len(stages), 3))
        made[name + "_recv"] = dma((len(stages), 3))
    for name, size in (("near", 2 * fast), ("far", n_dp // fast)):
        made[name + "_send"] = dma((size,))
        made[name + "_recv"] = dma((size,))
    made["local"] = dma((4,))
    return made


ACCUMULATORS = ("a_wq", "a_ow", "a_uw", "a_dwt", "a_pb", "a_ub", "a_vec", "a_conv")
TOGETHER = 2
MLP_TOGETHER = 4
GATHER_STEP = 2


def own_windows(n_dp, sown_ref, gown_ref, soff, goff, stages, sc):
    n = 2 * n_dp
    mine = sum((1 << t) * bit for t, bit in enumerate(own_bits(stages)))
    window = shift_on(sown_ref[...], soff)
    sc["sweights"][mine] = window.astype(bf16)
    raw = sc["raw"]
    grows = raw.shape[0]
    share = GROUP_PARAMS // n_dp
    raw[...] = jnp.zeros_like(raw)
    for r in range(-(-share // 128)):
        size = min(128, share - 128 * r)
        raw[r : r + 1, 0:size] = gown_ref[0:1, 128 * r : 128 * r + size]
    at = GAIN_ROW - first_row(SHARED_PARAMS, n, n - 1)
    raw[...] = shift_on(raw[...], goff)
    raw[grows - CARRIED :, :] = window[at : at + CARRIED]
    sc["gweights"][mine] = raw[...].astype(bf16)


def finish(n_dp, soff, goff, ssum, gsum, smine_ref, gmine_ref, norm_ref, near, far, sc):
    n = 2 * n_dp
    srows, grows = ssum.shape[0], gsum.shape[0]
    sshare, gshare = SHARED_PARAMS // n, GROUP_PARAMS // n_dp
    place = lax.broadcasted_iota(jnp.int32, (srows, 128), 0) * 128
    place = place + lax.broadcasted_iota(jnp.int32, (srows, 128), 1)
    shared = jnp.where((place >= soff) & (place < soff + sshare), ssum, 0.0)
    last = jnp.where(own_number() == n - 1, 1.0, 0.0)
    at = GAIN_ROW - first_row(SHARED_PARAMS, n, n - 1)
    smine_ref[...] = shared
    smine_ref[at : at + CARRIED, :] += gsum[grows - CARRIED :] * last
    shared = smine_ref[...]
    place = lax.broadcasted_iota(jnp.int32, (grows, 128), 0) * 128
    place = place + lax.broadcasted_iota(jnp.int32, (grows, 128), 1)
    grouped = jnp.where((place >= goff) & (place < goff + gshare), gsum, 0.0)
    near_me, near_peers = near
    far_me, far_peers = far
    sc["near_stat"][near_me] = tile_sum(shared * shared) + tile_sum(grouped * grouped)
    total = all_share(near_me, near_peers, sc["near_stat"], sc["near_send"], sc["near_recv"])
    sc["far_stat"][far_me] = total
    total = all_share(far_me, far_peers, sc["far_stat"], sc["far_send"], sc["far_recv"])
    total = jnp.sum(jnp.sum(total, axis=0, keepdims=True), axis=1, keepdims=True)
    norm = jnp.sqrt(total)
    norm_ref[...] = jnp.broadcast_to(norm, (8, 128))
    threshold = math.sqrt(2 * GROUP_PARAMS + SHARED_PARAMS)
    factor = jnp.minimum(1.0, threshold / (norm + 1e-06))
    smine_ref[...] = shift_back(shared * factor, soff)
    gmine_ref[...] = shift_back(grouped * factor, goff)


def step_kernel(
    n_dp,
    count,
    names,
    drop_ref,
    x_ref,
    co_ref,
    sown_ref,
    gown_ref,
    out_ref,
    gin_ref,
    smine_ref,
    gmine_ref,
    norm_ref,
    *scratch,
):
    sc = dict(zip(names, scratch))
    n = 2 * n_dp
    stages = exchange_stages(n_dp)
    near, far = group_peers(n_dp)
    devices = [device for _, device in near[1] + far[1]]
    barrier = pltpu.get_barrier_semaphore()
    for device in devices:
        pl.semaphore_signal(barrier, inc=1, device_id=device)
    load_x = pltpu.make_async_copy(x_ref, sc["x_in"], sc["local"].at[0])
    load_co = pltpu.make_async_copy(co_ref, sc["co_in"], sc["local"].at[1])
    load_x.start()
    load_co.start()
    soff = (own_number() * (SHARED_PARAMS // n)) % UNIT
    goff = (lax.axis_index("dp") * (GROUP_PARAMS // n_dp)) % UNIT
    own_windows(n_dp, sown_ref, gown_ref, soff, goff, stages, sc)
    sc["turn"][...] = turn_matrix()
    load_x.wait()
    to_grid(sc["x_in"], sc["tokens"], sc["x"])
    pl.semaphore_wait(barrier, len(devices))
    ggather = Gather(stages, sc["gweights"], sc["ggather_send"], sc["ggather_recv"])
    sgather = Gather(stages, sc["sweights"], sc["sgather_send"], sc["sgather_recv"])

    def run(phase, extra=None, together=TOGETHER):
        def body(i, carry):
            if extra is not None:
                for at, action in extra.items():
                    pl.when(i == at)(action)
            phase([i * together + k for k in range(together)])
            return carry

        lax.fori_loop(0, count // together, body, 0)

    last = len(stages) - 1
    ggather.start(0)
    sgather.start(0)
    for g in range(last):
        if g == last - 1:
            run(lambda images: first_norm(images, sc))
        ggather.wait(g)
        ggather.start(g + 1)
        if g < last - 1:
            sgather.wait(g)
            sgather.start(g + 1)
    for name in ACCUMULATORS:
        sc[name][...] = jnp.zeros_like(sc[name])
    load_co.wait()
    to_grid(sc["co_in"], sc["tokens"], sc["co"])
    ggather.wait(last)
    prepare_group(n_dp, stages, sc)

    steps = count // TOGETHER
    backward = {}
    def spread_cores():
        sgather.wait(last - 1)
        sgather.start(last)

    run(lambda images: attention_forward(images, sc), {min(GATHER_STEP, steps - 1): spread_cores})
    sgather.wait(last)
    prepare_shared(n_dp, stages, sc)
    run(lambda images: mlp_both(images, count, drop_ref, sc), None, MLP_TOGETHER)
    stores = []
    for half in range(2):
        cols = slice(half * 128, (half + 1) * 128)
        stores.append(
            pltpu.make_async_copy(sc["outs"].at[half], out_ref.at[:, cols], sc["local"].at[half])
        )
        stores[-1].start()
    place_shared(sc)

    half_bits = len(flat_bits(stages)) - 1
    top = own_bits(stages)[half_bits]
    srows, grows = sc["sweights"].shape[1], sc["gweights"].shape[1]

    def swindow(place):
        k = device_at(stages, place)
        row = (k * (SHARED_PARAMS // n)) // UNIT * 8
        return sc["flat"][pl.ds(pl.multiple_of(row, 8), srows), :]

    upper = (lax.broadcasted_iota(jnp.int32, (8, 128), 0) < 8 - CARRIED).astype(f32)

    def gwindow(place):
        k = device_at(stages, place)
        row = ((k // 2) * (GROUP_PARAMS // n_dp)) // UNIT * 8
        return jnp.concatenate(
            [
                sc["gflat"][k % 2, pl.ds(pl.multiple_of(row, 8), grows - 8), :],
                sc["gflat"][k % 2, pl.ds(pl.multiple_of(row + grows - 8, 8), 8), :] * upper
                + sc["carried"][...],
            ],
            axis=0,
        )

    def scatter(name, window):
        parts = [[sc[f"{name}{kind}{g}"] for g in range(last + 1)] for kind in ("out", "in", "sum")]
        return Scatter(
            stages, window, *parts, sc[name + "scatter_send"], sc[name + "scatter_recv"]
        )

    sscatter = scatter("s", swindow)
    gscatter = scatter("g", gwindow)
    sscatter.start(last)
    for g in range(last, 0, -1):
        def advance(g=g):
            sscatter.wait(g)
            sscatter.start(g - 1)

        at = min(1 + 2 * (last - g), steps - 1)
        backward[at] = backward.get(at, []) + [advance]
    run(
        lambda images: attention_back(images, count, sc),
        {at: chain(todo) for at, todo in backward.items()},
    )
    for half in range(2):
        cols = slice(half * 128, (half + 1) * 128)
        stores.append(
            pltpu.make_async_copy(
                sc["tokens"].at[half], gin_ref.at[:, cols], sc["local"].at[2 + half]
            )
        )
        stores[-1].start()
    place_group(sc)
    gscatter.start(last)
    sscatter.wait(0)
    for g in range(last, -1, -1):
        gscatter.wait(g)
        if g > 0:
            gscatter.start(g - 1)
    finish(
        n_dp,
        soff,
        goff,
        sc["ssum0"][0],
        sc["gsum0"][0],
        smine_ref,
        gmine_ref,
        norm_ref,
        near,
        far,
        sc,
    )
    for store in stores:
        store.wait()


def chain(actions):
    def run_all():
        for action in actions:
            action()

    return run_all


def step(n_dp, drops, images, cotangent, sown, gown):
    count = images.shape[0]
    srows = sown.shape[0]
    grows = window_rows(GROUP_PARAMS, n_dp, CARRIED)
    shapes = scratch_shapes(n_dp, srows, grows, count)
    vmem = pl.BlockSpec(memory_space=pltpu.VMEM)
    anywhere = pl.BlockSpec(memory_space=pl.ANY)

    def rows(array):
        return jnp.swapaxes(array, 0, 1).reshape(TOK * count, D)

    def unrows(array):
        return jnp.swapaxes(array.reshape(TOK, count, D), 0, 1)

    out, gin, smine, gmine, norm = pl.pallas_call(
        partial(step_kernel, n_dp, count, tuple(shapes)),
        in_specs=[pl.BlockSpec(memory_space=pltpu.SMEM), anywhere, anywhere, vmem, vmem],
        out_specs=[anywhere, anywhere, vmem, vmem, vmem],
        out_shape=[jax.ShapeDtypeStruct((TOK * count, D), f32)] * 2
        + [
            jax.ShapeDtypeStruct((srows, 128), f32),
            jax.ShapeDtypeStruct((grows, 128), f32),
            jax.ShapeDtypeStruct((8, 128), f32),
        ],
        scratch_shapes=list(shapes.values()),
        compiler_params=pltpu.CompilerParams(
            collective_id=0, has_side_effects=True, vmem_limit_bytes=62 * 1024 * 1024
        ),
        name="step",
    )(drops.T, rows(images), rows(cotangent), sown, gown)
    return unrows(out), unrows(gin), smine, gmine, norm


def adam_step(master, gradient, first, second, step):
    first_new = beta_one * first + (1.0 - beta_one) * gradient
    second_new = beta_two * second + (1.0 - beta_two) * gradient * gradient
    first_hat = first_new / (1.0 - jnp.power(jnp.float32(beta_one), step))
    second_hat = second_new / (1.0 - jnp.power(jnp.float32(beta_two), step))
    master_new = master - learn_rate * (
        first_hat / (jnp.sqrt(second_hat) + adam_eps) + decay_rate * master
    )
    return (master_new, first_new, second_new)


def on_device(
    n_dp,
    images,
    cotangent,
    drop_masks,
    group_master,
    group_m1,
    group_m2,
    shared_master,
    shared_m1,
    shared_m2,
):
    n = 2 * n_dp
    srows = window_rows(SHARED_PARAMS, n)
    sshare, gshare = SHARED_PARAMS // n, GROUP_PARAMS // n_dp
    sown = jnp.pad(shared_master, (0, srows * 128 - sshare)).reshape(srows, 128)
    output, input_grad, smine, gmine, norm = step(
        n_dp, drop_masks, images, cotangent, sown, group_master
    )
    shared_grad = smine.reshape(-1)[:sshare]
    group_grad = gmine.reshape(-1)[:gshare][None, :]
    now = jnp.float32(STEP)
    group_new, group_first, group_second = adam_step(
        group_master, group_grad, group_m1, group_m2, now
    )
    shared_new, shared_first, shared_second = adam_step(
        shared_master, shared_grad, shared_m1, shared_m2, now
    )
    return (
        output,
        input_grad,
        norm[0, 0:1],
        group_grad,
        group_new,
        group_first,
        group_second,
        group_new.astype(jnp.bfloat16),
        shared_grad,
        shared_new,
        shared_first,
        shared_second,
        shared_new.astype(jnp.bfloat16),
    )


def solution(mesh):
    both = P(("dp", "heads"))
    rows = P(("dp", "heads"), None, None)
    split = P("heads", "dp")
    in_specs = (rows, rows, P(("dp", "heads"), None), split, split, split, both, both, both)
    out_specs = (rows, rows, P(), split, split, split, split, split, both, both, both, both, both)
    return jax.shard_map(
        partial(on_device, mesh.shape["dp"]),
        mesh=mesh,
        in_specs=in_specs,
        out_specs=out_specs,
        check_vma=False,
    )
```

```python
from functools import partial
import math

import jax
import jax.numpy as jnp
from jax import lax
from jax.experimental import pallas as pl
from jax.experimental.pallas import tpu as pltpu
from jax.sharding import PartitionSpec as P

D = 256
FF = 1024
SIDE = 14
SW = 7
STEP = 10
HD = 32
HALF = 128
GROUP_PARAMS = 132608
SHARED_PARAMS = 526848
TOK = SIDE * SIDE
GRID = 16 * SIDE
STRIPE = 16 * SW
HEADS = HALF // HD
UNIT = 1024

eps_norm = 1e-05
keep_prob = 0.8
beta_one = 0.9
beta_two = 0.999
adam_eps = 1e-08
learn_rate = 0.04
decay_rate = 0.05

f32 = jnp.float32
bf16 = jnp.bfloat16


def window_rows(total, count, extra=0):
    share = total // count
    most = max((share * k) % UNIT + share for k in range(count)) + extra * 128
    return 16 * (-(-most // (2 * UNIT)))


def first_row(total, count, k):
    return (total // count * k) // UNIT * 8


HEADS_BIT = -1
FAST_BITS = 4
CARRIED = 4
GAIN_ROW = 4106


def exchange_stages(n_dp):
    bits = n_dp.bit_length() - 1
    far = list(range(bits - 1, 1, -1))
    stages = [tuple(far[i : i + 2]) for i in range(0, len(far), 2)]
    stages.append((1, HEADS_BIT) if bits > 1 else (HEADS_BIT,))
    if bits > 0:
        stages.append((0,))
    return stages


def weight_of(bit):
    return 1 if bit == HEADS_BIT else 2 << bit


def flat_bits(stages):
    return [bit for stage in stages for bit in stage]


def place_of(stages, k):
    return sum(((k // weight_of(bit)) % 2) << t for t, bit in enumerate(flat_bits(stages)))


def device_at(stages, place, first=0):
    return sum(
        ((place // (1 << t)) % 2) * weight_of(bit)
        for t, bit in enumerate(flat_bits(stages))
        if t >= first
    )


def own_number():
    return lax.axis_index("dp") * 2 + lax.axis_index("heads")


def own_bits(stages):
    me = own_number()
    return [(me // weight_of(bit)) % 2 for bit in flat_bits(stages)]


def peer(bits, mask):
    dp, heads = lax.axis_index("dp"), lax.axis_index("heads")
    for i, bit in enumerate(bits):
        if mask >> i & 1:
            if bit == HEADS_BIT:
                heads = 1 - heads
            else:
                dp = dp + (1 << bit) * (1 - 2 * ((dp // (1 << bit)) % 2))
    return {"dp": dp, "heads": heads}


def group_peers(n_dp):
    dp, heads = lax.axis_index("dp"), lax.axis_index("heads")
    fast = min(1 << FAST_BITS, n_dp)
    low, high = dp % fast, dp // fast
    count = 2 * fast
    me = low * 2 + heads
    near = []
    for step in range(1, count):
        other = (me + step) % count
        near.append((other, {"dp": high * fast + other // 2, "heads": other % 2}))
    far = []
    for step in range(1, n_dp // fast):
        other = (high + step) % (n_dp // fast)
        far.append((other, {"dp": other * fast + low, "heads": heads}))
    return (me, near), (high, far)


class Gather:
    def __init__(self, stages, buffer, send_sem, recv_sem):
        self.stages, self.buffer = stages, buffer
        self.send_sem, self.recv_sem = send_sem, recv_sem
        self.bits = own_bits(stages)

    def copies(self, g, arriving):
        start = sum(len(stage) for stage in self.stages[:g])
        for mask in range(1, 1 << len(self.stages[g])):
            base = 0
            for u, bit in enumerate(self.bits):
                flipped = start <= u < start + len(self.stages[g]) and mask >> (u - start) & 1
                if u >= start:
                    base = base + (1 << u) * (1 - bit if flipped and arriving else bit)
            held = self.buffer.at[pl.ds(base, 1 << start)]
            yield pltpu.make_async_remote_copy(
                src_ref=held,
                dst_ref=held,
                send_sem=self.send_sem.at[g, mask - 1],
                recv_sem=self.recv_sem.at[g, mask - 1],
                device_id=peer(self.stages[g], mask),
            )

    def start(self, g):
        for copy in self.copies(g, False):
            copy.start()

    def wait(self, g):
        for copy in self.copies(g, True):
            copy.wait_recv()
        for copy in self.copies(g, False):
            copy.wait_send()


class Scatter:
    def __init__(self, stages, window, outgoing, incoming, sums, send_sem, recv_sem):
        self.stages, self.window = stages, window
        self.outgoing, self.incoming, self.sums = outgoing, incoming, sums
        self.send_sem, self.recv_sem = send_sem, recv_sem
        self.bits = own_bits(stages)

    def offset(self, g):
        return sum(len(stage) for stage in self.stages[:g])

    def held(self, g, place):
        if g == len(self.stages) - 1:
            return self.window(place)
        return self.sums[g + 1][place]

    def copy(self, g, mask):
        return pltpu.make_async_remote_copy(
            src_ref=self.outgoing[g].at[mask - 1],
            dst_ref=self.incoming[g].at[mask - 1],
            send_sem=self.send_sem.at[g, mask - 1],
            recv_sem=self.recv_sem.at[g, mask - 1],
            device_id=peer(self.stages[g], mask),
        )

    def part(self, g, mask):
        start = self.offset(g)
        return sum(
            (1 << (start + i)) * (1 - self.bits[start + i] if mask >> i & 1 else self.bits[start + i])
            for i in range(len(self.stages[g]))
        )

    def start(self, g):
        for mask in range(1, 1 << len(self.stages[g])):
            part = self.part(g, mask)

            def fill(i, carry, mask=mask, part=part):
                self.outgoing[g][mask - 1, i] = self.held(g, part + i).astype(bf16)
                return carry

            lax.fori_loop(0, 1 << self.offset(g), fill, 0)
            self.copy(g, mask).start()

    def wait(self, g):
        masks = range(1, 1 << len(self.stages[g]))
        for mask in masks:
            self.copy(g, mask).wait()
        part = self.part(g, 0)

        def add(i, carry):
            value = self.held(g, part + i)
            for mask in masks:
                value = value + self.incoming[g][mask - 1, i].astype(f32)
            self.sums[g][i] = value
            return carry

        lax.fori_loop(0, 1 << self.offset(g), add, 0)


def scatter_shapes(stages, rows):
    outgoing, sums = [], []
    start = 0
    for stage in stages:
        outgoing.append(((1 << len(stage)) - 1, 1 << start, rows, 128))
        sums.append((1 << start, rows, 128))
        start += len(stage)
    return outgoing, sums


def all_share(me, peers, stat_ref, send_sem, recv_sem):
    copies = []
    for other, device in peers:
        copy = pltpu.make_async_remote_copy(
            src_ref=stat_ref.at[me],
            dst_ref=stat_ref.at[me],
            send_sem=send_sem.at[other],
            recv_sem=recv_sem.at[me],
            device_id=device,
        )
        copy.start()
        copies.append(copy)
    for other, device in peers:
        pltpu.make_async_remote_copy(
            src_ref=stat_ref.at[other],
            dst_ref=stat_ref.at[other],
            send_sem=send_sem.at[other],
            recv_sem=recv_sem.at[other],
            device_id=device,
        ).wait_recv()
    for copy in copies:
        copy.wait_send()
    return jnp.sum(stat_ref[...], axis=0)


def shift_on(rows, amount):
    lanes = amount % 128
    turned = pltpu.roll(rows, lanes, 1)
    lane = lax.broadcasted_iota(jnp.int32, rows.shape, 1)
    turned = jnp.where(lane < lanes, pltpu.roll(turned, 1, 0), turned)
    return pltpu.roll(turned, amount // 128, 0)


def shift_back(rows, amount):
    count = rows.shape[0]
    lanes = amount % 128
    turned = pltpu.roll(rows, (128 - lanes) % 128, 1)
    lane = lax.broadcasted_iota(jnp.int32, rows.shape, 1)
    turned = jnp.where(lane >= 128 - lanes, pltpu.roll(turned, count - 1, 0), turned)
    return pltpu.roll(turned, (count - amount // 128) % count, 0)


def nn(a, b):
    return lax.dot_general(a, b, (((1,), (0,)), ((), ())), preferred_element_type=f32)


def nt(a, b):
    return lax.dot_general(a, b, (((1,), (1,)), ((), ())), preferred_element_type=f32)


def tn(a, b):
    return lax.dot_general(a, b, (((0,), (0,)), ((), ())), preferred_element_type=f32)


def norm_parts(values):
    center = values - jnp.mean(values, axis=-1, keepdims=True)
    inverse = lax.rsqrt(jnp.mean(center * center, axis=-1, keepdims=True) + eps_norm)
    return center * inverse, inverse


def norm_back(grad_after, unit, inverse, gain):
    scaled = grad_after * gain
    return inverse * (
        scaled
        - jnp.mean(scaled, axis=-1, keepdims=True)
        - unit * jnp.mean(scaled * unit, axis=-1, keepdims=True)
    )


def column_sum(values):
    return jnp.sum(values, axis=0, keepdims=True)


def head_masks(dtype):
    lane = lax.broadcasted_iota(jnp.int32, (1, D), 1) % HALF // HD
    return [(lane == h).astype(f32).astype(dtype) for h in range(HEADS)]


def spread_heads(values, masks):
    return jnp.concatenate([values * masks[h] for h in range(HEADS)], axis=0)


def pick_heads(stacked):
    lane = lax.broadcasted_iota(jnp.int32, (STRIPE, D), 1) % HALF
    picked = stacked[(HEADS - 1) * STRIPE :]
    for h in range(HEADS - 2, -1, -1):
        picked = jnp.where(lane < (h + 1) * HD, stacked[h * STRIPE : (h + 1) * STRIPE], picked)
    return picked


def beside(rows):
    return jnp.concatenate([rows[:STRIPE], rows[STRIPE:]], axis=1)


def above(columns):
    return jnp.concatenate([columns[:, :HALF], columns[:, HALF:]], axis=0)


def diagonal(rows):
    gap = jnp.zeros((HALF - STRIPE, HALF), rows.dtype)
    other = jnp.zeros((HALF, HALF), rows.dtype)
    first = jnp.concatenate([rows[:STRIPE], gap], axis=0)
    second = jnp.concatenate([rows[STRIPE:], gap], axis=0)
    return jnp.concatenate(
        [jnp.concatenate([first, other], axis=1), jnp.concatenate([other, second], axis=1)], axis=0
    )


def from_diagonal(square):
    return jnp.concatenate(
        [square[:STRIPE, :HALF], square[HALF : HALF + STRIPE, HALF:]], axis=1
    )


def row_shift(values, rows):
    if rows == 0:
        return values
    zero = jnp.zeros((abs(rows), values.shape[1]), f32)
    if rows > 0:
        return jnp.concatenate([values[rows:], zero], axis=0)
    return jnp.concatenate([zero, values[:rows]], axis=0)


def neighbours(values, j):
    before, after = pltpu.roll(values, 1, 0), pltpu.roll(values, STRIPE - 1, 0)
    if j == 0:
        row = lax.broadcasted_iota(jnp.int32, values.shape, 0) % 16
        before = jnp.where(row == 8, pltpu.roll(values, 2, 0), before)
        after = jnp.where(row == 6, pltpu.roll(values, STRIPE - 2, 0), after)
    return [before, values, after]


SHIFT = (16, 8)


def tap(j, outer, inner):
    return 3 * outer + inner if j == 0 else 3 * inner + outer


def to_stripes(rows):
    tiles = rows.reshape(SIDE, 2, 8, rows.shape[1])
    return jnp.concatenate(
        [tiles[:, s].reshape(STRIPE, rows.shape[1]) for s in range(2)], axis=0
    )


def from_stripes(columns):
    halves = [columns[:, s * HALF : (s + 1) * HALF].reshape(SIDE, 1, 8, HALF) for s in range(2)]
    return jnp.concatenate(halves, axis=1).reshape(GRID, HALF)


def tile_sum(values):
    return jnp.sum(values.reshape(-1, 8, values.shape[1]), axis=0)


def row_mask():
    row = lax.broadcasted_iota(jnp.int32, (GRID, 1), 0)
    return (row % 8 < SW).astype(f32)


def to_grid(source, tokens, grid_ref):
    images = grid_ref.shape[0]
    grid_ref[...] = jnp.zeros_like(grid_ref)
    for half in range(2):
        cols = slice(half * 128, (half + 1) * 128)
        tokens[half] = source[:, cols].astype(f32)
        for image in range(images):
            for r in range(2 * SIDE):
                grid_ref[image, 8 * r : 8 * r + SW, cols] = tokens[
                    half, pl.ds(r * SW * images + image, SW, stride=images), :
                ]


def from_grid(value, tokens, image, images):
    for half in range(2):
        for r in range(2 * SIDE):
            tokens[half, pl.ds(r * SW * images + image, SW, stride=images), :] = value[
                8 * r : 8 * r + SW, half * 128 : (half + 1) * 128
            ]


def prepare_group(n_dp, stages, sc):
    n = 2 * n_dp
    gflat, buffer = sc["gflat"], sc["gweights"]
    grows = buffer.shape[1]
    gflat[...] = jnp.zeros_like(gflat)
    for k in range(n):
        at = first_row(GROUP_PARAMS, n_dp, k // 2)
        size = grows - CARRIED
        gflat[k % 2, at : at + size] += buffer[place_of(stages, k), 0:size].astype(f32)
    carried = buffer[place_of(stages, n - 1)].astype(f32)[grows - CARRIED :]
    for c in range(2):
        cols = slice(c * 128, (c + 1) * 128)
        sc["vecs"][1:2, cols] = carried[c : c + 1]
        sc["vecs"][2:3, cols] = carried[2 + c : 3 + c]
    for j in range(2):
        for c in range(3):
            cols = slice(j * 384 + c * 128, j * 384 + (c + 1) * 128)
            sc["wq"][:, cols] = gflat[j, pl.ds(c, D, stride=3), :].astype(bf16)
        for c in range(2):
            cols = slice(c * 128, (c + 1) * 128)
            sc["ow"][j * 128 : (j + 1) * 128, cols] = gflat[
                j, pl.ds(770 + c, HALF, stride=2), :
            ].astype(bf16)
        sc["qbias"][:, j * 384 : j * 384 + 128] = gflat[j, 768:769, :]
        sc["qbias"][:, j * 384 + 128 : j * 384 + 256] = jnp.zeros((1, 128), f32)
        sc["qbias"][:, j * 384 + 256 : j * 384 + 384] = gflat[j, 769:770, :]
        for half in range(2):
            cols = slice(half * 128, (half + 1) * 128)
            sc["conv"][j, 0:10, cols] = gflat[j, 1026:1036, :]


def prepare_shared(n_dp, stages, sc):
    n = 2 * n_dp
    flat, buffer = sc["flat"], sc["sweights"]
    srows = buffer.shape[1]
    flat[...] = jnp.zeros_like(flat)
    for k in range(n):
        at = first_row(SHARED_PARAMS, n, k)
        flat[at : at + srows] += buffer[place_of(stages, k)].astype(f32)
    for c in range(8):
        cols = slice(c * 128, (c + 1) * 128)
        sc["uw"][:, cols] = flat[pl.ds(c, D, stride=8), :].astype(bf16)
        sc["ubias"][:, cols] = flat[2048 + c : 2049 + c, :]
    for c in range(2):
        cols = slice(c * 128, (c + 1) * 128)
        sc["dw"][:, cols] = flat[pl.ds(2056 + c, FF, stride=2), :].astype(bf16)
        for i in (0, 3, 4, 5):
            sc["vecs"][i : i + 1, cols] = flat[4104 + 2 * i + c : 4105 + 2 * i + c, :]


def place_shared(sc):
    flat = sc["flat"]
    for c in range(8):
        cols = slice(c * 128, (c + 1) * 128)
        flat[pl.ds(c, D, stride=8), :] = sc["a_uw"][:, cols]
        flat[2048 + c : 2049 + c, :] = sc["a_ub"][0:1, cols]
    for q in range(4):
        turned = sc["a_dwt"][:, q * 256 : (q + 1) * 256].T
        for c in range(2):
            flat[pl.ds(2056 + 512 * q + c, 256, stride=2), :] = turned[
                :, c * 128 : (c + 1) * 128
            ]
    for c in range(2):
        cols = slice(c * 128, (c + 1) * 128)
        for i in (0, 3, 4, 5):
            flat[4104 + 2 * i + c : 4105 + 2 * i + c, :] = column_sum(
                sc["a_vec"][i, :, cols]
            )
    flat[GAIN_ROW : GAIN_ROW + CARRIED, :] = jnp.zeros((CARRIED, 128), f32)


def place_group(sc):
    gflat = sc["gflat"]
    for j in range(2):
        for c in range(3):
            cols = slice(j * 384 + c * 128, j * 384 + (c + 1) * 128)
            gflat[j, pl.ds(c, D, stride=3), :] = sc["a_wq"][:, cols]
        for c in range(2):
            cols = slice(c * 128, (c + 1) * 128)
            gflat[j, pl.ds(770 + c, HALF, stride=2), :] = sc["a_ow"][
                j * 128 : (j + 1) * 128, cols
            ]
        gflat[j, 768:769, :] = sc["a_pb"][0:1, j * 384 : j * 384 + 128]
        gflat[j, 769:770, :] = sc["a_pb"][0:1, j * 384 + 256 : j * 384 + 384]
        for i in range(10):
            both = column_sum(sc["a_conv"][j, i])
            gflat[j, 1026 + i : 1027 + i, :] = both[:, :HALF] + both[:, HALF:]
    for c in range(2):
        cols = slice(c * 128, (c + 1) * 128)
        sc["carried"][4 + c : 5 + c, :] = column_sum(sc["a_vec"][1, :, cols])
        sc["carried"][6 + c : 7 + c, :] = column_sum(sc["a_vec"][2, :, cols])
    sc["carried"][0:4, :] = jnp.zeros((4, 128), f32)


def first_norm(images, sc):
    for image in images:
        sc["unit"][image], sc["inverse"][image] = norm_parts(sc["x"][image])


def attention_forward(images, sc):
    scale = HD ** (-0.5)
    masks = head_masks(bf16)
    inside = row_mask()
    key_row = lax.broadcasted_iota(jnp.int32, (1, SIDE, 8, D), 2)
    gain_one, shift_one = sc["vecs"][1:2], sc["vecs"][2:3]
    qkv_ref, conv = sc["qkv"], sc["conv"]
    many = len(images)
    for image in images:
        sc["normed"][image] = (sc["unit"][image] * gain_one + shift_one).astype(bf16)
    normed = sc["normed"][pl.ds(images[0], many)].reshape(many * GRID, D)
    triples = nn(normed, sc["wq"][...]) + sc["qbias"][...]
    for i, image in enumerate(images):
        triple = triples[i * GRID : (i + 1) * GRID] * inside
        qkv_ref[image, 0] = triple[:, :384].astype(bf16)
        qkv_ref[image, 1] = to_stripes(triple[:, 384:]).astype(bf16)
    for j in range(2):
        for image in images:
            query = diagonal(qkv_ref[image, j, :, 0:128])
            keys = spread_heads(beside(qkv_ref[image, j, :, 128:256]), masks)
            value = beside(qkv_ref[image, j, :, 256:384])
            scores = nt(keys, query).reshape(HEADS, SIDE, 8, D) * scale
            scores = jnp.where(key_row < SW, scores, -1e30)
            scores = scores.reshape(HEADS, STRIPE, D)
            weights = jnp.exp(scores - jnp.max(scores, axis=1, keepdims=True))
            probs = weights * (1.0 / jnp.sum(weights, axis=1, keepdims=True))
            probs = probs.reshape(HEADS * STRIPE, D)
            sc["probs"][image, j] = probs
            total = from_diagonal(tn(probs.astype(bf16), spread_heads(value, masks)))
            total = total + conv[j, 9:10]
            near = neighbours(value.astype(f32), j)
            for outer in range(3):
                part = None
                for inner in range(3):
                    k = tap(j, outer, inner)
                    term = near[inner] * conv[j, k : k + 1]
                    part = term if part is None else part + term
                total = total + row_shift(part, SHIFT[j] * (outer - 1))
            both = above(total) if j == 0 else from_stripes(total)
            sc["heads"][image, :, j * 128 : (j + 1) * 128] = both.astype(bf16)


def mlp_both(images, count, drop_ref, sc):
    down_bias = sc["vecs"][0:1]
    gain_two, shift_two, out_bias = sc["vecs"][3:4], sc["vecs"][4:5], sc["vecs"][5:6]
    a_vec = sc["a_vec"]
    uw, dw, ubias = sc["uw"], sc["dw"], sc["ubias"]
    many = len(images)
    ones = jnp.ones((8, many * GRID), bf16)

    def join(parts):
        return jnp.concatenate(parts, axis=0)

    def part_of(joined, i):
        return joined[i * GRID : (i + 1) * GRID]

    heads = sc["heads"][pl.ds(images[0], many)].reshape(many * GRID, D)
    branch = nn(heads, sc["ow"][...])
    state = []
    for i, image in enumerate(images):
        scale_one = drop_ref[0, image].astype(f32) / keep_prob
        scale_two = drop_ref[1, image].astype(f32) / keep_prob
        middle = sc["x"][image] + scale_one * (part_of(branch, i) + out_bias)
        unit_two, inverse_two = norm_parts(middle)
        grad_output = sc["co"][image]
        grad_mlp_f = scale_two * grad_output
        a_vec[0] += tile_sum(grad_mlp_f)
        state.append((scale_one, scale_two, middle, unit_two, inverse_two, grad_output, grad_mlp_f))
    normed_two = join([(st[3] * gain_two + shift_two).astype(bf16) for st in state])
    grad_mlp = join([st[6].astype(bf16) for st in state])
    mlp = None
    grad_normed = None
    for c in range(4):
        cols = slice(c * 256, (c + 1) * 256)
        hidden = nn(normed_two, uw[:, cols]) + ubias[:, cols]
        density = jnp.exp(hidden * hidden * -0.5) * (1.0 / math.sqrt(2.0 * math.pi))
        phi = 0.5 + 0.5 * lax.erf(hidden * math.sqrt(0.5))
        active = (hidden * phi).astype(bf16)
        part = nn(active, dw[cols, :])
        mlp = part if mlp is None else mlp + part
        sc["a_dwt"][:, cols] += tn(grad_mlp, active)
        grad_active = nt(grad_mlp, dw[cols, :])
        grad_hidden = (grad_active * (phi + hidden * density)).astype(bf16)
        sc["a_ub"][:, cols] += nn(ones, grad_hidden)
        sc["a_uw"][:, cols] += tn(normed_two, grad_hidden)
        part = nt(grad_hidden, uw[:, cols])
        grad_normed = part if grad_normed is None else grad_normed + part
    grad_branch = []
    for i, image in enumerate(images):
        scale_one, scale_two, middle, unit_two, inverse_two, grad_output, _ = state[i]
        from_grid(
            middle + scale_two * (part_of(mlp, i) + down_bias), sc["outs"], image, count
        )
        grad = part_of(grad_normed, i)
        a_vec[3] += tile_sum(grad * unit_two)
        a_vec[4] += tile_sum(grad)
        grad_middle = grad_output + norm_back(grad, unit_two, inverse_two, gain_two)
        sc["gmid"][image] = grad_middle
        grad_branch_f = scale_one * grad_middle
        a_vec[5] += tile_sum(grad_branch_f)
        grad_branch.append(grad_branch_f.astype(bf16))
    grad_branch = join(grad_branch)
    sc["a_ow"][...] += tn(heads, grad_branch)
    grad_heads = nt(grad_branch, sc["ow"][...])
    for i, image in enumerate(images):
        grad = part_of(grad_heads, i)
        sc["gheads"][image, :, :128] = grad[:, :128].astype(bf16)
        sc["gheads"][image, :, 128:] = to_stripes(grad[:, 128:]).astype(bf16)


def attention_back(images, count, sc):
    scale = HD ** (-0.5)
    masks = head_masks(bf16)
    inside = row_mask()[:STRIPE]
    gain_one = sc["vecs"][1:2]
    many = len(images)
    ones = jnp.ones((8, many * GRID), bf16)
    a_vec, a_conv = sc["a_vec"], sc["a_conv"]
    qkv_ref, conv = sc["qkv"], sc["conv"]
    for j in range(2):
        for image in images:
            grad = sc["gheads"][image, :, j * 128 : (j + 1) * 128]
            grad_square = diagonal(grad)
            grad_f = beside(grad).astype(f32)
            query = diagonal(qkv_ref[image, j, :, 0:128])
            keys = spread_heads(beside(qkv_ref[image, j, :, 128:256]), masks)
            value = beside(qkv_ref[image, j, :, 256:384])
            probs = sc["probs"][image, j]
            grad_probs = nt(spread_heads(value, masks), grad_square)
            product = (probs * grad_probs).reshape(HEADS, STRIPE, D)
            inner = jnp.sum(product, axis=1, keepdims=True)
            grad_scores = product - probs.reshape(HEADS, STRIPE, D) * inner
            grad_scores = grad_scores.reshape(HEADS * STRIPE, D).astype(bf16)
            grad_query = from_diagonal(tn(grad_scores, keys)) * scale
            grad_key = pick_heads(nn(grad_scores, query)) * scale
            grad_value = pick_heads(nn(probs.astype(bf16), grad_square))
            near = neighbours(grad_f, j)
            for outer in range(3):
                part = None
                for inner in range(3):
                    k = tap(j, outer, inner)
                    term = near[2 - inner] * conv[j, k : k + 1]
                    part = term if part is None else part + term
                grad_value = grad_value + row_shift(part, SHIFT[j] * (1 - outer))
            grad_value = grad_value * inside
            near = neighbours(value.astype(f32), j)
            step = SHIFT[j]
            for inner in range(3):
                a_conv[j, tap(j, 0, inner)] += tile_sum(grad_f[step:] * near[inner][:-step])
                a_conv[j, tap(j, 1, inner)] += tile_sum(grad_f * near[inner])
                a_conv[j, tap(j, 2, inner)] += tile_sum(grad_f[:-step] * near[inner][step:])
            a_conv[j, 9] += tile_sum(grad_f)
            order = above if j == 0 else from_stripes
            both = jnp.concatenate(
                [order(part) for part in (grad_query, grad_key, grad_value)], axis=1
            ).astype(bf16)
            sc["gtriple"][image, :, j * 384 : (j + 1) * 384] = both
    grad_triple = sc["gtriple"][pl.ds(images[0], many)].reshape(many * GRID, 768)
    normed = sc["normed"][pl.ds(images[0], many)].reshape(many * GRID, D)
    sc["a_pb"][...] += nn(ones, grad_triple)
    sc["a_wq"][...] += tn(normed, grad_triple)
    grads = nt(grad_triple, sc["wq"][...])
    for i, image in enumerate(images):
        grad_normed = grads[i * GRID : (i + 1) * GRID]
        unit, inverse = sc["unit"][image], sc["inverse"][image]
        a_vec[1] += tile_sum(grad_normed * unit)
        a_vec[2] += tile_sum(grad_normed)
        grad = sc["gmid"][image] + norm_back(grad_normed, unit, inverse, gain_one)
        from_grid(grad, sc["tokens"], image, count)


def scratch_shapes(n_dp, srows, grows, count):
    n = 2 * n_dp
    flat_rows = max(4120, first_row(SHARED_PARAMS, n, n - 1) + srows)
    gflat_rows = max(1040, first_row(GROUP_PARAMS, n_dp, n_dp - 1) + grows)
    shapes = dict(
        flat=((flat_rows, 128), f32),
        gflat=((2, gflat_rows, 128), f32),
        sweights=((n, srows, 128), bf16),
        gweights=((n, grows, 128), bf16),
        raw=((grows, 128), f32),
        sraw=((srows, 128), f32),
        carried=((8, 128), f32),
        wq=((D, 768), bf16),
        ow=((D, D), bf16),
        uw=((D, FF), bf16),
        dw=((FF, D), bf16),
        qbias=((1, 768), f32),
        ubias=((1, FF), f32),
        vecs=((8, D), f32),
        conv=((2, 16, D), f32),
        a_wq=((D, 768), f32),
        a_ow=((D, D), f32),
        a_uw=((D, FF), f32),
        a_dwt=((D, FF), f32),
        a_pb=((8, 768), f32),
        a_ub=((8, FF), f32),
        a_vec=((6, 8, D), f32),
        a_conv=((2, 10, 8, D), f32),
        x_in=((TOK * count, D), bf16),
        co_in=((TOK * count, D), bf16),
        tokens=((2, TOK * count, 128), f32),
        outs=((2, TOK * count, 128), f32),
        x=((count, GRID, D), f32),
        co=((count, GRID, D), f32),
        unit=((count, GRID, D), f32),
        inverse=((count, GRID, 1), f32),
        normed=((count, GRID, D), bf16),
        qkv=((count, 2, GRID, 384), bf16),
        probs=((count, 2, HEADS * STRIPE, D), f32),
        heads=((count, GRID, D), bf16),
        gmid=((count, GRID, D), f32),
        gheads=((count, GRID, D), bf16),
        gtriple=((count, GRID, 768), bf16),
    )
    stages = exchange_stages(n_dp)
    for name, rows in (("s", srows), ("g", grows)):
        outgoing, sums = scatter_shapes(stages, rows)
        for g, shape in enumerate(outgoing):
            shapes[f"{name}out{g}"] = (shape, bf16)
            shapes[f"{name}in{g}"] = (shape, bf16)
            shapes[f"{name}sum{g}"] = (sums[g], f32)
    fast = min(1 << FAST_BITS, n_dp)
    shapes["near_stat"] = ((2 * fast, 8, 128), f32)
    shapes["far_stat"] = ((n_dp // fast, 8, 128), f32)
    made = {name: pltpu.VMEM(*shape) for name, shape in shapes.items()}
    dma = pltpu.SemaphoreType.DMA
    for name in ("sgather", "ggather", "sscatter", "gscatter"):
        made[name + "_send"] = dma((len(stages), 3))
        made[name + "_recv"] = dma((len(stages), 3))
    for name, size in (("near", 2 * fast), ("far", n_dp // fast)):
        made[name + "_send"] = dma((size,))
        made[name + "_recv"] = dma((size,))
    made["local"] = dma((4,))
    return made


ACCUMULATORS = ("a_wq", "a_ow", "a_uw", "a_dwt", "a_pb", "a_ub", "a_vec", "a_conv")
TOGETHER = 2
MLP_TOGETHER = 4
GATHER_STEP = 2


def own_windows(n_dp, sown_ref, gown_ref, soff, goff, stages, sc):
    n = 2 * n_dp
    mine = sum((1 << t) * bit for t, bit in enumerate(own_bits(stages)))
    raw = sc["sraw"]
    share = sown_ref.shape[0]
    whole = share // UNIT * UNIT
    raw[...] = jnp.zeros_like(raw)
    raw[0 : whole // 128, :] = sown_ref[0:whole].reshape(whole // 128, 128)
    for r in range(whole // 128, -(-share // 128)):
        size = min(128, share - 128 * r)
        raw[r : r + 1, 0:size] = sown_ref[128 * r : 128 * r + size].reshape(1, size)
    window = shift_on(raw[...], soff)
    sc["sweights"][mine] = window.astype(bf16)
    raw = sc["raw"]
    grows = raw.shape[0]
    share = gown_ref.shape[1]
    raw[...] = jnp.zeros_like(raw)
    for r in range(-(-share // 128)):
        size = min(128, share - 128 * r)
        raw[r : r + 1, 0:size] = gown_ref[0:1, 128 * r : 128 * r + size]
    at = GAIN_ROW - first_row(SHARED_PARAMS, n, n - 1)
    raw[...] = shift_on(raw[...], goff)
    raw[grows - CARRIED :, :] = window[at : at + CARRIED]
    sc["gweights"][mine] = raw[...].astype(bf16)


def finish(n_dp, soff, goff, ssum, gsum, smine_ref, gmine_ref, norm_ref, near, far, sc):
    n = 2 * n_dp
    srows, grows = ssum.shape[0], gsum.shape[0]
    sshare, gshare = SHARED_PARAMS // n, GROUP_PARAMS // n_dp
    place = lax.broadcasted_iota(jnp.int32, (srows, 128), 0) * 128
    place = place + lax.broadcasted_iota(jnp.int32, (srows, 128), 1)
    shared = jnp.where((place >= soff) & (place < soff + sshare), ssum, 0.0)
    last = jnp.where(own_number() == n - 1, 1.0, 0.0)
    at = GAIN_ROW - first_row(SHARED_PARAMS, n, n - 1)
    smine_ref[...] = shared
    smine_ref[at : at + CARRIED, :] += gsum[grows - CARRIED :] * last
    shared = smine_ref[...]
    place = lax.broadcasted_iota(jnp.int32, (grows, 128), 0) * 128
    place = place + lax.broadcasted_iota(jnp.int32, (grows, 128), 1)
    grouped = jnp.where((place >= goff) & (place < goff + gshare), gsum, 0.0)
    near_me, near_peers = near
    far_me, far_peers = far
    sc["near_stat"][near_me] = tile_sum(shared * shared) + tile_sum(grouped * grouped)
    total = all_share(near_me, near_peers, sc["near_stat"], sc["near_send"], sc["near_recv"])
    sc["far_stat"][far_me] = total
    total = all_share(far_me, far_peers, sc["far_stat"], sc["far_send"], sc["far_recv"])
    total = jnp.sum(jnp.sum(total, axis=0, keepdims=True), axis=1, keepdims=True)
    norm = jnp.sqrt(total)
    norm_ref[...] = jnp.broadcast_to(norm, (8, 128))
    threshold = math.sqrt(2 * GROUP_PARAMS + SHARED_PARAMS)
    factor = jnp.minimum(1.0, threshold / (norm + 1e-06))
    smine_ref[...] = shift_back(shared * factor, soff)
    grouped = shift_back(grouped * factor, goff)
    for r in range(-(-gshare // 128)):
        size = min(128, gshare - 128 * r)
        gmine_ref[0:1, 128 * r : 128 * r + size] = grouped[r : r + 1, 0:size]


def step_kernel(
    n_dp,
    count,
    names,
    drop_ref,
    x_ref,
    co_ref,
    sown_ref,
    gown_ref,
    out_ref,
    gin_ref,
    smine_ref,
    gmine_ref,
    norm_ref,
    *scratch,
):
    sc = dict(zip(names, scratch))
    n = 2 * n_dp
    stages = exchange_stages(n_dp)
    near, far = group_peers(n_dp)
    devices = [device for _, device in near[1] + far[1]]
    barrier = pltpu.get_barrier_semaphore()
    for device in devices:
        pl.semaphore_signal(barrier, inc=1, device_id=device)
    load_x = pltpu.make_async_copy(x_ref, sc["x_in"], sc["local"].at[0])
    load_co = pltpu.make_async_copy(co_ref, sc["co_in"], sc["local"].at[1])
    load_x.start()
    load_co.start()
    soff = (own_number() * (SHARED_PARAMS // n)) % UNIT
    goff = (lax.axis_index("dp") * (GROUP_PARAMS // n_dp)) % UNIT
    own_windows(n_dp, sown_ref, gown_ref, soff, goff, stages, sc)
    load_x.wait()
    to_grid(sc["x_in"], sc["tokens"], sc["x"])
    pl.semaphore_wait(barrier, len(devices))
    ggather = Gather(stages, sc["gweights"], sc["ggather_send"], sc["ggather_recv"])
    sgather = Gather(stages, sc["sweights"], sc["sgather_send"], sc["sgather_recv"])

    def run(phase, extra=None, together=TOGETHER):
        def body(i, carry):
            if extra is not None:
                for at, action in extra.items():
                    pl.when(i == at)(action)
            phase([i * together + k for k in range(together)])
            return carry

        lax.fori_loop(0, count // together, body, 0)

    last = len(stages) - 1
    ggather.start(0)
    sgather.start(0)
    for g in range(last):
        if g == last - 1:
            run(lambda images: first_norm(images, sc))
        ggather.wait(g)
        ggather.start(g + 1)
        if g < last - 1:
            sgather.wait(g)
            sgather.start(g + 1)
    for name in ACCUMULATORS:
        sc[name][...] = jnp.zeros_like(sc[name])
    load_co.wait()
    to_grid(sc["co_in"], sc["tokens"], sc["co"])
    ggather.wait(last)
    prepare_group(n_dp, stages, sc)

    steps = count // TOGETHER
    backward = {}
    def spread_cores():
        sgather.wait(last - 1)
        sgather.start(last)

    run(lambda images: attention_forward(images, sc), {min(GATHER_STEP, steps - 1): spread_cores})
    sgather.wait(last)
    prepare_shared(n_dp, stages, sc)
    run(lambda images: mlp_both(images, count, drop_ref, sc), None, MLP_TOGETHER)
    stores = []
    for half in range(2):
        cols = slice(half * 128, (half + 1) * 128)
        stores.append(
            pltpu.make_async_copy(sc["outs"].at[half], out_ref.at[:, cols], sc["local"].at[half])
        )
        stores[-1].start()
    place_shared(sc)

    half_bits = len(flat_bits(stages)) - 1
    top = own_bits(stages)[half_bits]
    srows, grows = sc["sweights"].shape[1], sc["gweights"].shape[1]

    def swindow(place):
        k = device_at(stages, place)
        row = (k * (SHARED_PARAMS // n)) // UNIT * 8
        return sc["flat"][pl.ds(pl.multiple_of(row, 8), srows), :]

    upper = (lax.broadcasted_iota(jnp.int32, (8, 128), 0) < 8 - CARRIED).astype(f32)

    def gwindow(place):
        k = device_at(stages, place)
        row = ((k // 2) * (GROUP_PARAMS // n_dp)) // UNIT * 8
        return jnp.concatenate(
            [
                sc["gflat"][k % 2, pl.ds(pl.multiple_of(row, 8), grows - 8), :],
                sc["gflat"][k % 2, pl.ds(pl.multiple_of(row + grows - 8, 8), 8), :] * upper
                + sc["carried"][...],
            ],
            axis=0,
        )

    def scatter(name, window):
        parts = [[sc[f"{name}{kind}{g}"] for g in range(last + 1)] for kind in ("out", "in", "sum")]
        return Scatter(
            stages, window, *parts, sc[name + "scatter_send"], sc[name + "scatter_recv"]
        )

    sscatter = scatter("s", swindow)
    gscatter = scatter("g", gwindow)
    sscatter.start(last)
    for g in range(last, 0, -1):
        def advance(g=g):
            sscatter.wait(g)
            sscatter.start(g - 1)

        at = min(1 + 2 * (last - g), steps - 1)
        backward[at] = backward.get(at, []) + [advance]
    run(
        lambda images: attention_back(images, count, sc),
        {at: chain(todo) for at, todo in backward.items()},
    )
    for half in range(2):
        cols = slice(half * 128, (half + 1) * 128)
        stores.append(
            pltpu.make_async_copy(
                sc["tokens"].at[half], gin_ref.at[:, cols], sc["local"].at[2 + half]
            )
        )
        stores[-1].start()
    place_group(sc)
    gscatter.start(last)
    sscatter.wait(0)
    for g in range(last, -1, -1):
        gscatter.wait(g)
        if g > 0:
            gscatter.start(g - 1)
    finish(
        n_dp,
        soff,
        goff,
        sc["ssum0"][0],
        sc["gsum0"][0],
        smine_ref,
        gmine_ref,
        norm_ref,
        near,
        far,
        sc,
    )
    for store in stores:
        store.wait()


def chain(actions):
    def run_all():
        for action in actions:
            action()

    return run_all


def step(n_dp, drops, images, cotangent, state):
    count = images.shape[0]
    gown, _, _, sown, _, _ = state
    srows = window_rows(SHARED_PARAMS, 2 * n_dp)
    grows = window_rows(GROUP_PARAMS, n_dp, CARRIED)
    shapes = scratch_shapes(n_dp, srows, grows, count)
    vmem = pl.BlockSpec(memory_space=pltpu.VMEM)
    anywhere = pl.BlockSpec(memory_space=pl.ANY)

    def rows(array):
        return jnp.swapaxes(array, 0, 1).reshape(TOK * count, D)

    def unrows(array):
        return jnp.swapaxes(array.reshape(TOK, count, D), 0, 1)

    out, gin, smine, gmine, norm = pl.pallas_call(
        partial(step_kernel, n_dp, count, tuple(shapes)),
        in_specs=[pl.BlockSpec(memory_space=pltpu.SMEM), anywhere, anywhere, vmem, vmem],
        out_specs=[anywhere, anywhere, vmem, vmem, vmem],
        out_shape=[jax.ShapeDtypeStruct((TOK * count, D), f32)] * 2
        + [
            jax.ShapeDtypeStruct((srows, 128), f32),
            jax.ShapeDtypeStruct(gown.shape, f32),
            jax.ShapeDtypeStruct((8, 128), f32),
        ],
        scratch_shapes=list(shapes.values()),
        compiler_params=pltpu.CompilerParams(
            collective_id=0, has_side_effects=True, vmem_limit_bytes=62 * 1024 * 1024
        ),
        name="step",
    )(drops.T, rows(images), rows(cotangent), sown, gown)
    first, second, *updated = update(out, gin, smine.reshape(-1), gmine, norm, *state)
    return (unrows(first), unrows(second), *updated)


def adam_step(master, gradient, first, second):
    first_new = beta_one * first + (1.0 - beta_one) * gradient
    second_new = beta_two * second + (1.0 - beta_two) * gradient * gradient
    first_hat = first_new / (1.0 - beta_one**STEP)
    second_hat = second_new / (1.0 - beta_two**STEP)
    master_new = master - learn_rate * (
        first_hat / (jnp.sqrt(second_hat) + adam_eps) + decay_rate * master
    )
    return (master_new, first_new, second_new)


CHUNKS = 4


def update_kernel(out_in, gin_in, smine, gmine, norm_in, *refs):
    gstate, sstate, refs = refs[:3], refs[3:6], refs[6:]
    out_ref, gin_ref, norm_ref = refs[:3]
    gnew, snew, (out_buf, gin_buf, in_sem, out_sem) = refs[3:8], refs[8:13], refs[13:]
    size = out_in.shape[0] // CHUNKS
    arrays = ((out_in, out_buf, out_ref), (gin_in, gin_buf, gin_ref))
    loads, stores = [], []
    for i in range(CHUNKS):
        rows = pl.ds(i * size, size)
        for k, (source, held, target) in enumerate(arrays):
            loads.append(
                pltpu.make_async_copy(source.at[rows], held.at[rows], in_sem.at[k, i])
            )
            stores.append(
                pltpu.make_async_copy(held.at[rows], target.at[rows], out_sem.at[k, i])
            )
            loads[-1].start()
    for load, store in zip(loads, stores):
        load.wait()
        store.start()
    norm_ref[...] = norm_in[0:1, 0:1]
    for gradient, (master, first, second), new in (
        (gmine[...], gstate, gnew),
        (smine[0 : sstate[0].shape[0]], sstate, snew),
    ):
        new[0][...] = gradient
        new[1][...], new[2][...], new[3][...] = adam_step(
            master[...], gradient, first[...], second[...]
        )
        new[4][...] = new[1][...].astype(bf16)
    for store in stores:
        store.wait()


def update(out, gin, smine, gmine, norm, *state):
    vmem = pl.BlockSpec(memory_space=pltpu.VMEM)
    anywhere = pl.BlockSpec(memory_space=pl.ANY)
    like = jax.ShapeDtypeStruct
    big = like(out.shape, f32)
    news = []
    for master in (state[0], state[3]):
        news += [like(master.shape, f32)] * 4 + [like(master.shape, bf16)]
    return pl.pallas_call(
        update_kernel,
        in_specs=[anywhere] * 2 + [vmem] * 9,
        out_specs=[anywhere] * 2 + [vmem] * 11,
        out_shape=[big, big, like((1, 1), f32)] + news,
        scratch_shapes=[pltpu.VMEM(out.shape, f32)] * 2
        + [pltpu.SemaphoreType.DMA((2, CHUNKS))] * 2,
        compiler_params=pltpu.CompilerParams(vmem_limit_bytes=62 * 1024 * 1024),
        name="update",
    )(out, gin, smine, gmine, norm, *state)


def on_device(
    n_dp,
    images,
    cotangent,
    drop_masks,
    group_master,
    group_m1,
    group_m2,
    shared_master,
    shared_m1,
    shared_m2,
):
    state = (group_master, group_m1, group_m2, shared_master, shared_m1, shared_m2)
    output, input_grad, norm, *updated = step(n_dp, drop_masks, images, cotangent, state)
    return (output, input_grad, norm.reshape(1), *updated)


def solution(mesh):
    both = P(("dp", "heads"))
    rows = P(("dp", "heads"), None, None)
    split = P("heads", "dp")
    in_specs = (rows, rows, P(("dp", "heads"), None), split, split, split, both, both, both)
    out_specs = (rows, rows, P(), split, split, split, split, split, both, both, both, both, both)
    return jax.shard_map(
        partial(on_device, mesh.shape["dp"]),
        mesh=mesh,
        in_specs=in_specs,
        out_specs=out_specs,
        check_vma=False,
    )
```

```python
from functools import partial
import math

import jax
import jax.numpy as jnp
from jax import lax
from jax.experimental import pallas as pl
from jax.experimental.pallas import tpu as pltpu
from jax.sharding import PartitionSpec as P

D = 256
FF = 1024
SIDE = 14
SW = 7
STEP = 10
HD = 32
HALF = 128
GROUP_PARAMS = 132608
SHARED_PARAMS = 526848
TOK = SIDE * SIDE
GRID = 16 * SIDE
STRIPE = 16 * SW
HEADS = HALF // HD
UNIT = 1024

eps_norm = 1e-05
keep_prob = 0.8
beta_one = 0.9
beta_two = 0.999
adam_eps = 1e-08
learn_rate = 0.04
decay_rate = 0.05

f32 = jnp.float32
bf16 = jnp.bfloat16


def window_rows(total, count, extra=0):
    share = total // count
    most = max((share * k) % UNIT + share for k in range(count)) + extra * 128
    return 16 * (-(-most // (2 * UNIT)))


def first_row(total, count, k):
    return (total // count * k) // UNIT * 8


HEADS_BIT = -1
FAST_BITS = 4
CARRIED = 4
GAIN_ROW = 4106


def exchange_stages(n_dp):
    bits = n_dp.bit_length() - 1
    far = list(range(bits - 1, 1, -1))
    stages = [tuple(far[i : i + 2]) for i in range(0, len(far), 2)]
    stages.append((1, HEADS_BIT) if bits > 1 else (HEADS_BIT,))
    if bits > 0:
        stages.append((0,))
    return stages


def weight_of(bit):
    return 1 if bit == HEADS_BIT else 2 << bit


def flat_bits(stages):
    return [bit for stage in stages for bit in stage]


def place_of(stages, k):
    return sum(((k // weight_of(bit)) % 2) << t for t, bit in enumerate(flat_bits(stages)))


def device_at(stages, place, first=0):
    return sum(
        ((place // (1 << t)) % 2) * weight_of(bit)
        for t, bit in enumerate(flat_bits(stages))
        if t >= first
    )


def own_number():
    return lax.axis_index("dp") * 2 + lax.axis_index("heads")


def own_bits(stages):
    me = own_number()
    return [(me // weight_of(bit)) % 2 for bit in flat_bits(stages)]


def peer(bits, mask):
    dp, heads = lax.axis_index("dp"), lax.axis_index("heads")
    for i, bit in enumerate(bits):
        if mask >> i & 1:
            if bit == HEADS_BIT:
                heads = 1 - heads
            else:
                dp = dp + (1 << bit) * (1 - 2 * ((dp // (1 << bit)) % 2))
    return {"dp": dp, "heads": heads}


def group_peers(n_dp):
    dp, heads = lax.axis_index("dp"), lax.axis_index("heads")
    fast = min(1 << FAST_BITS, n_dp)
    low, high = dp % fast, dp // fast
    count = 2 * fast
    me = low * 2 + heads
    near = []
    for step in range(1, count):
        other = (me + step) % count
        near.append((other, {"dp": high * fast + other // 2, "heads": other % 2}))
    far = []
    for step in range(1, n_dp // fast):
        other = (high + step) % (n_dp // fast)
        far.append((other, {"dp": other * fast + low, "heads": heads}))
    return (me, near), (high, far)


UNROLL = 4


class Gather:
    def __init__(self, stages, buffer, send_sem, recv_sem):
        self.stages, self.buffer = stages, buffer
        self.send_sem, self.recv_sem = send_sem, recv_sem
        self.bits = own_bits(stages)

    def copy(self, g, held, mask):
        return pltpu.make_async_remote_copy(
            src_ref=held,
            dst_ref=held,
            send_sem=self.send_sem.at[g],
            recv_sem=self.recv_sem.at[g],
            device_id=peer(self.stages[g], mask),
        )

    def start(self, g):
        start = sum(len(stage) for stage in self.stages[:g])
        base = sum((1 << u) * bit for u, bit in enumerate(self.bits) if u >= start)
        held = self.buffer.at[pl.ds(base, 1 << start)]
        for mask in range(1, 1 << len(self.stages[g])):
            self.copy(g, held, mask).start()

    def wait(self, g):
        start = sum(len(stage) for stage in self.stages[:g])
        peers = (1 << len(self.stages[g])) - 1
        every = self.copy(g, self.buffer.at[pl.ds(0, peers << start)], 1)
        every.wait_recv()
        every.wait_send()


class Scatter:
    def __init__(self, stages, window, outgoing, incoming, sums, send_sem, recv_sem):
        self.stages, self.window = stages, window
        self.outgoing, self.incoming, self.sums = outgoing, incoming, sums
        self.send_sem, self.recv_sem = send_sem, recv_sem
        self.bits = own_bits(stages)

    def offset(self, g):
        return sum(len(stage) for stage in self.stages[:g])

    def held(self, g, place):
        if g == len(self.stages) - 1:
            return self.window(place)
        return self.sums[g + 1][place]

    def copy(self, g, mask, at):
        return pltpu.make_async_remote_copy(
            src_ref=self.outgoing[g].at[at],
            dst_ref=self.incoming[g].at[at],
            send_sem=self.send_sem.at[g],
            recv_sem=self.recv_sem.at[g],
            device_id=peer(self.stages[g], mask),
        )

    def part(self, g, mask):
        start = self.offset(g)
        return sum(
            (1 << (start + i)) * (1 - self.bits[start + i] if mask >> i & 1 else self.bits[start + i])
            for i in range(len(self.stages[g]))
        )

    def start(self, g):
        for mask in range(1, 1 << len(self.stages[g])):
            part = self.part(g, mask)

            def fill(i, carry, mask=mask, part=part):
                self.outgoing[g][mask - 1, i] = self.held(g, part + i).astype(bf16)
                return carry

            blocks = 1 << self.offset(g)
            lax.fori_loop(0, blocks, fill, 0, unroll=min(blocks, UNROLL))
            self.copy(g, mask, mask - 1).start()

    def wait(self, g):
        masks = range(1, 1 << len(self.stages[g]))
        self.copy(g, 1, pl.ds(0, len(masks))).wait()
        part = self.part(g, 0)

        def add(i, carry):
            value = self.held(g, part + i)
            for mask in masks:
                value = value + self.incoming[g][mask - 1, i].astype(f32)
            self.sums[g][i] = value
            return carry

        blocks = 1 << self.offset(g)
        lax.fori_loop(0, blocks, add, 0, unroll=min(blocks, UNROLL))


def scatter_shapes(stages, rows):
    outgoing, sums = [], []
    start = 0
    for stage in stages:
        outgoing.append(((1 << len(stage)) - 1, 1 << start, rows, 128))
        sums.append((1 << start, rows, 128))
        start += len(stage)
    return outgoing, sums


def all_share(me, peers, stat_ref, send_sem, recv_sem):
    def copy(held, device):
        return pltpu.make_async_remote_copy(
            src_ref=held,
            dst_ref=held,
            send_sem=send_sem.at[0],
            recv_sem=recv_sem.at[0],
            device_id=device,
        )

    for _, device in peers:
        copy(stat_ref.at[me], device).start()
    if peers:
        every = copy(stat_ref.at[pl.ds(0, len(peers))], peers[0][1])
        every.wait_recv()
        every.wait_send()
    return jnp.sum(stat_ref[...], axis=0)


def shift_on(rows, amount):
    lanes = amount % 128
    turned = pltpu.roll(rows, lanes, 1)
    lane = lax.broadcasted_iota(jnp.int32, rows.shape, 1)
    turned = jnp.where(lane < lanes, pltpu.roll(turned, 1, 0), turned)
    return pltpu.roll(turned, amount // 128, 0)


def shift_back(rows, amount):
    count = rows.shape[0]
    lanes = amount % 128
    turned = pltpu.roll(rows, (128 - lanes) % 128, 1)
    lane = lax.broadcasted_iota(jnp.int32, rows.shape, 1)
    turned = jnp.where(lane >= 128 - lanes, pltpu.roll(turned, count - 1, 0), turned)
    return pltpu.roll(turned, (count - amount // 128) % count, 0)


def nn(a, b):
    return lax.dot_general(a, b, (((1,), (0,)), ((), ())), preferred_element_type=f32)


def nt(a, b):
    return lax.dot_general(a, b, (((1,), (1,)), ((), ())), preferred_element_type=f32)


def tn(a, b):
    return lax.dot_general(a, b, (((0,), (0,)), ((), ())), preferred_element_type=f32)


def norm_parts(values):
    center = values - jnp.mean(values, axis=-1, keepdims=True)
    inverse = lax.rsqrt(jnp.mean(center * center, axis=-1, keepdims=True) + eps_norm)
    return center * inverse, inverse


def norm_back(grad_after, unit, inverse, gain):
    scaled = grad_after * gain
    return inverse * (
        scaled
        - jnp.mean(scaled, axis=-1, keepdims=True)
        - unit * jnp.mean(scaled * unit, axis=-1, keepdims=True)
    )


def column_sum(values):
    return jnp.sum(values, axis=0, keepdims=True)


def head_masks(dtype):
    lane = lax.broadcasted_iota(jnp.int32, (1, D), 1) % HALF // HD
    return [(lane == h).astype(f32).astype(dtype) for h in range(HEADS)]


def spread_heads(values, masks):
    return jnp.concatenate([values * masks[h] for h in range(HEADS)], axis=0)


def pick_heads(stacked):
    lane = lax.broadcasted_iota(jnp.int32, (STRIPE, D), 1) % HALF
    picked = stacked[(HEADS - 1) * STRIPE :]
    for h in range(HEADS - 2, -1, -1):
        picked = jnp.where(lane < (h + 1) * HD, stacked[h * STRIPE : (h + 1) * STRIPE], picked)
    return picked


def beside(rows):
    return jnp.concatenate([rows[:STRIPE], rows[STRIPE:]], axis=1)


def above(columns):
    return jnp.concatenate([columns[:, :HALF], columns[:, HALF:]], axis=0)


def diagonal(rows):
    gap = jnp.zeros((HALF - STRIPE, HALF), rows.dtype)
    other = jnp.zeros((HALF, HALF), rows.dtype)
    first = jnp.concatenate([rows[:STRIPE], gap], axis=0)
    second = jnp.concatenate([rows[STRIPE:], gap], axis=0)
    return jnp.concatenate(
        [jnp.concatenate([first, other], axis=1), jnp.concatenate([other, second], axis=1)], axis=0
    )


def from_diagonal(square):
    return jnp.concatenate(
        [square[:STRIPE, :HALF], square[HALF : HALF + STRIPE, HALF:]], axis=1
    )


def row_shift(values, rows):
    if rows == 0:
        return values
    zero = jnp.zeros((abs(rows), values.shape[1]), f32)
    if rows > 0:
        return jnp.concatenate([values[rows:], zero], axis=0)
    return jnp.concatenate([zero, values[:rows]], axis=0)


def neighbours(values, j):
    before, after = pltpu.roll(values, 1, 0), pltpu.roll(values, STRIPE - 1, 0)
    if j == 0:
        row = lax.broadcasted_iota(jnp.int32, values.shape, 0) % 16
        before = jnp.where(row == 8, pltpu.roll(values, 2, 0), before)
        after = jnp.where(row == 6, pltpu.roll(values, STRIPE - 2, 0), after)
    return [before, values, after]


SHIFT = (16, 8)


def tap(j, outer, inner):
    return 3 * outer + inner if j == 0 else 3 * inner + outer


def to_stripes(rows):
    tiles = rows.reshape(SIDE, 2, 8, rows.shape[1])
    return jnp.concatenate(
        [tiles[:, s].reshape(STRIPE, rows.shape[1]) for s in range(2)], axis=0
    )


def from_stripes(columns):
    halves = [columns[:, s * HALF : (s + 1) * HALF].reshape(SIDE, 1, 8, HALF) for s in range(2)]
    return jnp.concatenate(halves, axis=1).reshape(GRID, HALF)


def tile_sum(values):
    return jnp.sum(values.reshape(-1, 8, values.shape[1]), axis=0)


def row_mask():
    row = lax.broadcasted_iota(jnp.int32, (GRID, 1), 0)
    return (row % 8 < SW).astype(f32)


def to_grid(source, tokens, grid_ref):
    images = grid_ref.shape[0]
    grid_ref[...] = jnp.zeros_like(grid_ref)
    for half in range(2):
        cols = slice(half * 128, (half + 1) * 128)
        tokens[half] = source[:, cols].astype(f32)
        for image in range(images):
            for r in range(2 * SIDE):
                grid_ref[image, 8 * r : 8 * r + SW, cols] = tokens[
                    half, pl.ds(r * SW * images + image, SW, stride=images), :
                ]


def from_grid(value, tokens, image, images):
    for half in range(2):
        for r in range(2 * SIDE):
            tokens[half, pl.ds(r * SW * images + image, SW, stride=images), :] = value[
                8 * r : 8 * r + SW, half * 128 : (half + 1) * 128
            ]


def prepare_group(n_dp, stages, sc):
    n = 2 * n_dp
    gflat, buffer = sc["gflat"], sc["gweights"]
    grows = buffer.shape[1]
    gflat[...] = jnp.zeros_like(gflat)
    for k in range(n):
        at = first_row(GROUP_PARAMS, n_dp, k // 2)
        size = grows - CARRIED
        gflat[k % 2, at : at + size] += buffer[place_of(stages, k), 0:size].astype(f32)
    carried = buffer[place_of(stages, n - 1)].astype(f32)[grows - CARRIED :]
    for c in range(2):
        cols = slice(c * 128, (c + 1) * 128)
        sc["vecs"][1:2, cols] = carried[c : c + 1]
        sc["vecs"][2:3, cols] = carried[2 + c : 3 + c]
    for j in range(2):
        for c in range(3):
            cols = slice(j * 384 + c * 128, j * 384 + (c + 1) * 128)
            sc["wq"][:, cols] = gflat[j, pl.ds(c, D, stride=3), :].astype(bf16)
        for c in range(2):
            cols = slice(c * 128, (c + 1) * 128)
            sc["ow"][j * 128 : (j + 1) * 128, cols] = gflat[
                j, pl.ds(770 + c, HALF, stride=2), :
            ].astype(bf16)
        sc["qbias"][:, j * 384 : j * 384 + 128] = gflat[j, 768:769, :]
        sc["qbias"][:, j * 384 + 128 : j * 384 + 256] = jnp.zeros((1, 128), f32)
        sc["qbias"][:, j * 384 + 256 : j * 384 + 384] = gflat[j, 769:770, :]
        for half in range(2):
            cols = slice(half * 128, (half + 1) * 128)
            sc["conv"][j, 0:10, cols] = gflat[j, 1026:1036, :]


def prepare_shared(n_dp, stages, sc):
    n = 2 * n_dp
    flat, buffer = sc["flat"], sc["sweights"]
    srows = buffer.shape[1]
    flat[...] = jnp.zeros_like(flat)
    for k in range(n):
        at = first_row(SHARED_PARAMS, n, k)
        flat[at : at + srows] += buffer[place_of(stages, k)].astype(f32)
    for c in range(8):
        cols = slice(c * 128, (c + 1) * 128)
        sc["uw"][:, cols] = flat[pl.ds(c, D, stride=8), :].astype(bf16)
        sc["ubias"][:, cols] = flat[2048 + c : 2049 + c, :]
    for c in range(2):
        cols = slice(c * 128, (c + 1) * 128)
        sc["dw"][:, cols] = flat[pl.ds(2056 + c, FF, stride=2), :].astype(bf16)
        for i in (0, 3, 4, 5):
            sc["vecs"][i : i + 1, cols] = flat[4104 + 2 * i + c : 4105 + 2 * i + c, :]


def place_shared(sc):
    flat = sc["flat"]
    for c in range(8):
        cols = slice(c * 128, (c + 1) * 128)
        flat[pl.ds(c, D, stride=8), :] = sc["a_uw"][:, cols]
        flat[2048 + c : 2049 + c, :] = sc["a_ub"][0:1, cols]
    for q in range(4):
        turned = sc["a_dwt"][:, q * 256 : (q + 1) * 256].T
        for c in range(2):
            flat[pl.ds(2056 + 512 * q + c, 256, stride=2), :] = turned[
                :, c * 128 : (c + 1) * 128
            ]
    for c in range(2):
        cols = slice(c * 128, (c + 1) * 128)
        for i in (0, 3, 4, 5):
            flat[4104 + 2 * i + c : 4105 + 2 * i + c, :] = column_sum(
                sc["a_vec"][i, :, cols]
            )
    flat[GAIN_ROW : GAIN_ROW + CARRIED, :] = jnp.zeros((CARRIED, 128), f32)


def place_group(sc):
    gflat = sc["gflat"]
    for j in range(2):
        for c in range(3):
            cols = slice(j * 384 + c * 128, j * 384 + (c + 1) * 128)
            gflat[j, pl.ds(c, D, stride=3), :] = sc["a_wq"][:, cols]
        for c in range(2):
            cols = slice(c * 128, (c + 1) * 128)
            gflat[j, pl.ds(770 + c, HALF, stride=2), :] = sc["a_ow"][
                j * 128 : (j + 1) * 128, cols
            ]
        gflat[j, 768:769, :] = sc["a_pb"][0:1, j * 384 : j * 384 + 128]
        gflat[j, 769:770, :] = sc["a_pb"][0:1, j * 384 + 256 : j * 384 + 384]
        for i in range(10):
            both = column_sum(sc["a_conv"][j, i])
            gflat[j, 1026 + i : 1027 + i, :] = both[:, :HALF] + both[:, HALF:]


def first_norm(images, sc):
    for image in images:
        sc["unit"][image], sc["inverse"][image] = norm_parts(sc["x"][image])


def attention_forward(images, sc):
    scale = HD ** (-0.5)
    masks = head_masks(bf16)
    inside = row_mask()
    key_row = lax.broadcasted_iota(jnp.int32, (1, SIDE, 8, D), 2)
    gain_one, shift_one = sc["vecs"][1:2], sc["vecs"][2:3]
    qkv_ref, conv = sc["qkv"], sc["conv"]
    many = len(images)
    for image in images:
        sc["normed"][image] = (sc["unit"][image] * gain_one + shift_one).astype(bf16)
    normed = sc["normed"][pl.ds(images[0], many)].reshape(many * GRID, D)
    triples = nn(normed, sc["wq"][...]) + sc["qbias"][...]
    for i, image in enumerate(images):
        triple = triples[i * GRID : (i + 1) * GRID] * inside
        qkv_ref[image, 0] = triple[:, :384].astype(bf16)
        qkv_ref[image, 1] = to_stripes(triple[:, 384:]).astype(bf16)
    for j in range(2):
        for image in images:
            query = diagonal(qkv_ref[image, j, :, 0:128])
            keys = spread_heads(beside(qkv_ref[image, j, :, 128:256]), masks)
            value = beside(qkv_ref[image, j, :, 256:384])
            scores = nt(keys, query).reshape(HEADS, SIDE, 8, D) * scale
            scores = jnp.where(key_row < SW, scores, -1e30)
            scores = scores.reshape(HEADS, STRIPE, D)
            weights = jnp.exp(scores - jnp.max(scores, axis=1, keepdims=True))
            probs = weights * (1.0 / jnp.sum(weights, axis=1, keepdims=True))
            probs = probs.reshape(HEADS * STRIPE, D)
            sc["probs"][image, j] = probs
            total = from_diagonal(tn(probs.astype(bf16), spread_heads(value, masks)))
            total = total + conv[j, 9:10]
            near = neighbours(value.astype(f32), j)
            for outer in range(3):
                part = None
                for inner in range(3):
                    k = tap(j, outer, inner)
                    term = near[inner] * conv[j, k : k + 1]
                    part = term if part is None else part + term
                total = total + row_shift(part, SHIFT[j] * (outer - 1))
            both = above(total) if j == 0 else from_stripes(total)
            sc["heads"][image, :, j * 128 : (j + 1) * 128] = both.astype(bf16)


def mlp_output(images, count, drop_ref, sc):
    many = len(images)
    active = sc["active"][pl.ds(images[0], many)].reshape(many * GRID, FF)
    mlp = nn(active, sc["dw"][...]) + sc["vecs"][0:1]
    for i, image in enumerate(images):
        scale_two = drop_ref[1, image].astype(f32) / keep_prob
        value = sc["x"][image] + scale_two * mlp[i * GRID : (i + 1) * GRID]
        from_grid(value, sc["outs"], image, count)


def mlp_both(images, drop_ref, sc):
    gain_two, shift_two, out_bias = sc["vecs"][3:4], sc["vecs"][4:5], sc["vecs"][5:6]
    a_vec = sc["a_vec"]
    uw, dw, ubias = sc["uw"], sc["dw"], sc["ubias"]
    many = len(images)
    ones = jnp.ones((8, many * GRID), bf16)

    def join(parts):
        return jnp.concatenate(parts, axis=0)

    def part_of(joined, i):
        return joined[i * GRID : (i + 1) * GRID]

    heads = sc["heads"][pl.ds(images[0], many)].reshape(many * GRID, D)
    branch = nn(heads, sc["ow"][...])
    state = []
    for i, image in enumerate(images):
        scale_one = drop_ref[0, image].astype(f32) / keep_prob
        scale_two = drop_ref[1, image].astype(f32) / keep_prob
        middle = sc["x"][image] + scale_one * (part_of(branch, i) + out_bias)
        unit_two, inverse_two = norm_parts(middle)
        grad_output = sc["co"][image]
        grad_mlp_f = scale_two * grad_output
        a_vec[0] += tile_sum(grad_mlp_f)
        state.append((scale_one, scale_two, middle, unit_two, inverse_two, grad_output, grad_mlp_f))
    normed_two = join([(st[3] * gain_two + shift_two).astype(bf16) for st in state])
    grad_mlp = join([st[6].astype(bf16) for st in state])
    grad_normed = None
    for c in range(4):
        cols = slice(c * 256, (c + 1) * 256)
        hidden = nn(normed_two, uw[:, cols]) + ubias[:, cols]
        density = jnp.exp(hidden * hidden * -0.5) * (1.0 / math.sqrt(2.0 * math.pi))
        phi = 0.5 + 0.5 * lax.erf(hidden * math.sqrt(0.5))
        active = (hidden * phi).astype(bf16)
        sc["active"][pl.ds(images[0], many), :, cols] = active.reshape(many, GRID, 256)
        sc["a_dwt"][:, cols] += tn(grad_mlp, active)
        grad_active = nt(grad_mlp, dw[cols, :])
        grad_hidden = (grad_active * (phi + hidden * density)).astype(bf16)
        sc["a_ub"][:, cols] += nn(ones, grad_hidden)
        sc["a_uw"][:, cols] += tn(normed_two, grad_hidden)
        part = nt(grad_hidden, uw[:, cols])
        grad_normed = part if grad_normed is None else grad_normed + part
    grad_branch = []
    for i, image in enumerate(images):
        scale_one, _, middle, unit_two, inverse_two, grad_output, _ = state[i]
        sc["x"][image] = middle
        grad = part_of(grad_normed, i)
        a_vec[3] += tile_sum(grad * unit_two)
        a_vec[4] += tile_sum(grad)
        grad_middle = grad_output + norm_back(grad, unit_two, inverse_two, gain_two)
        sc["gmid"][image] = grad_middle
        grad_branch_f = scale_one * grad_middle
        a_vec[5] += tile_sum(grad_branch_f)
        grad_branch.append(grad_branch_f.astype(bf16))
    grad_branch = join(grad_branch)
    sc["a_ow"][...] += tn(heads, grad_branch)
    grad_heads = nt(grad_branch, sc["ow"][...])
    for i, image in enumerate(images):
        grad = part_of(grad_heads, i)
        sc["gheads"][image, :, :128] = grad[:, :128].astype(bf16)
        sc["gheads"][image, :, 128:] = to_stripes(grad[:, 128:]).astype(bf16)


def attention_back(images, sc):
    scale = HD ** (-0.5)
    masks = head_masks(bf16)
    inside = row_mask()[:STRIPE]
    many = len(images)
    ones = jnp.ones((8, many * GRID), bf16)
    a_conv = sc["a_conv"]
    qkv_ref, conv = sc["qkv"], sc["conv"]
    for j in range(2):
        for image in images:
            grad = sc["gheads"][image, :, j * 128 : (j + 1) * 128]
            grad_square = diagonal(grad)
            grad_f = beside(grad).astype(f32)
            query = diagonal(qkv_ref[image, j, :, 0:128])
            keys = spread_heads(beside(qkv_ref[image, j, :, 128:256]), masks)
            value = beside(qkv_ref[image, j, :, 256:384])
            probs = sc["probs"][image, j]
            grad_probs = nt(spread_heads(value, masks), grad_square)
            product = (probs * grad_probs).reshape(HEADS, STRIPE, D)
            inner = jnp.sum(product, axis=1, keepdims=True)
            grad_scores = product - probs.reshape(HEADS, STRIPE, D) * inner
            grad_scores = grad_scores.reshape(HEADS * STRIPE, D).astype(bf16)
            grad_query = from_diagonal(tn(grad_scores, keys)) * scale
            grad_key = pick_heads(nn(grad_scores, query)) * scale
            grad_value = pick_heads(nn(probs.astype(bf16), grad_square))
            near = neighbours(grad_f, j)
            for outer in range(3):
                part = None
                for inner in range(3):
                    k = tap(j, outer, inner)
                    term = near[2 - inner] * conv[j, k : k + 1]
                    part = term if part is None else part + term
                grad_value = grad_value + row_shift(part, SHIFT[j] * (1 - outer))
            grad_value = grad_value * inside
            near = neighbours(value.astype(f32), j)
            step = SHIFT[j]
            for inner in range(3):
                a_conv[j, tap(j, 0, inner)] += tile_sum(grad_f[step:] * near[inner][:-step])
                a_conv[j, tap(j, 1, inner)] += tile_sum(grad_f * near[inner])
                a_conv[j, tap(j, 2, inner)] += tile_sum(grad_f[:-step] * near[inner][step:])
            a_conv[j, 9] += tile_sum(grad_f)
            order = above if j == 0 else from_stripes
            both = jnp.concatenate(
                [order(part) for part in (grad_query, grad_key, grad_value)], axis=1
            ).astype(bf16)
            sc["gtriple"][image, :, j * 384 : (j + 1) * 384] = both
    grad_triple = sc["gtriple"][pl.ds(images[0], many)].reshape(many * GRID, 768)
    normed = sc["normed"][pl.ds(images[0], many)].reshape(many * GRID, D)
    sc["a_pb"][...] += nn(ones, grad_triple)
    sc["a_wq"][...] += tn(normed, grad_triple)


def input_gradient(images, count, sc):
    many = len(images)
    gain_one = sc["vecs"][1:2]
    a_vec = sc["a_vec"]
    grad_triple = sc["gtriple"][pl.ds(images[0], many)].reshape(many * GRID, 768)
    grads = nt(grad_triple, sc["wq"][...])
    for i, image in enumerate(images):
        grad_normed = grads[i * GRID : (i + 1) * GRID]
        unit, inverse = sc["unit"][image], sc["inverse"][image]
        a_vec[1] += tile_sum(grad_normed * unit)
        a_vec[2] += tile_sum(grad_normed)
        grad = sc["gmid"][image] + norm_back(grad_normed, unit, inverse, gain_one)
        from_grid(grad, sc["tokens"], image, count)


def scratch_shapes(n_dp, srows, grows, count):
    n = 2 * n_dp
    flat_rows = max(4120, first_row(SHARED_PARAMS, n, n - 1) + srows)
    gflat_rows = max(1040, first_row(GROUP_PARAMS, n_dp, n_dp - 1) + grows)
    shapes = dict(
        flat=((flat_rows, 128), f32),
        gflat=((2, gflat_rows, 128), f32),
        sweights=((n, srows, 128), bf16),
        gweights=((n, grows, 128), bf16),
        raw=((grows, 128), f32),
        sraw=((srows, 128), f32),
        sown=((SHARED_PARAMS // n,), f32),
        gown=((1, GROUP_PARAMS // n_dp), f32),
        wq=((D, 768), bf16),
        ow=((D, D), bf16),
        uw=((D, FF), bf16),
        dw=((FF, D), bf16),
        qbias=((1, 768), f32),
        ubias=((1, FF), f32),
        vecs=((8, D), f32),
        conv=((2, 16, D), f32),
        a_wq=((D, 768), f32),
        a_ow=((D, D), f32),
        a_uw=((D, FF), f32),
        a_dwt=((D, FF), f32),
        a_pb=((8, 768), f32),
        a_ub=((8, FF), f32),
        a_vec=((6, 8, D), f32),
        a_conv=((2, 10, 8, D), f32),
        x_in=((TOK * count, D), bf16),
        tokens=((2, TOK * count, 128), f32),
        outs=((2, TOK * count, 128), f32),
        x=((count, GRID, D), f32),
        co=((count, GRID, D), f32),
        unit=((count, GRID, D), f32),
        inverse=((count, GRID, 1), f32),
        normed=((count, GRID, D), bf16),
        qkv=((count, 2, GRID, 384), bf16),
        probs=((count, 2, HEADS * STRIPE, D), f32),
        heads=((count, GRID, D), bf16),
        gmid=((count, GRID, D), f32),
        active=((count, GRID, FF), bf16),
        gheads=((count, GRID, D), bf16),
        gtriple=((count, GRID, 768), bf16),
    )
    stages = exchange_stages(n_dp)
    for name, rows in (("s", srows), ("g", grows)):
        outgoing, sums = scatter_shapes(stages, rows)
        for g, shape in enumerate(outgoing):
            shapes[f"{name}out{g}"] = (shape, bf16)
            shapes[f"{name}in{g}"] = (shape, bf16)
            shapes[f"{name}sum{g}"] = (sums[g], f32)
    fast = min(1 << FAST_BITS, n_dp)
    shapes["near_stat"] = ((2 * fast, 8, 128), f32)
    shapes["far_stat"] = ((n_dp // fast, 8, 128), f32)
    made = {name: pltpu.VMEM(*shape) for name, shape in shapes.items()}
    dma = pltpu.SemaphoreType.DMA
    for name in ("sgather", "ggather", "sscatter", "gscatter"):
        made[name + "_send"] = dma((len(stages),))
        made[name + "_recv"] = dma((len(stages),))
    for name in ("near", "far"):
        made[name + "_send"] = dma((1,))
        made[name + "_recv"] = dma((1,))
    made["local"] = dma((5,))
    made["drops"] = pltpu.SMEM((2, count), jnp.int32)
    return made


ACCUMULATORS = ("a_wq", "a_ow", "a_uw", "a_dwt", "a_pb", "a_ub", "a_vec", "a_conv")
TOGETHER = 2
MLP_TOGETHER = 4
GATHER_STEP = 2
CORE_STEP = 1
OUT_STEP = 3
OUT_TOGETHER = 2


def own_windows(n_dp, sown_ref, gown_ref, soff, goff, stages, sc):
    n = 2 * n_dp
    mine = sum((1 << t) * bit for t, bit in enumerate(own_bits(stages)))
    raw = sc["sraw"]
    share = sown_ref.shape[0]
    whole = share // UNIT * UNIT
    raw[...] = jnp.zeros_like(raw)
    raw[0 : whole // 128, :] = sown_ref[0:whole].reshape(whole // 128, 128)
    for r in range(whole // 128, -(-share // 128)):
        size = min(128, share - 128 * r)
        raw[r : r + 1, 0:size] = sown_ref[128 * r : 128 * r + size].reshape(1, size)
    window = shift_on(raw[...], soff)
    sc["sweights"][mine] = window.astype(bf16)
    raw = sc["raw"]
    grows = raw.shape[0]
    share = gown_ref.shape[1]
    raw[...] = jnp.zeros_like(raw)
    for r in range(-(-share // 128)):
        size = min(128, share - 128 * r)
        raw[r : r + 1, 0:size] = gown_ref[0:1, 128 * r : 128 * r + size]
    at = GAIN_ROW - first_row(SHARED_PARAMS, n, n - 1)
    raw[...] = shift_on(raw[...], goff)
    raw[grows - CARRIED :, :] = window[at : at + CARRIED]
    sc["gweights"][mine] = raw[...].astype(bf16)


def finish(n_dp, soff, goff, ssum, gsum, smine_ref, gmine_ref, norm_ref, near, far, sc):
    n = 2 * n_dp
    srows, grows = ssum.shape[0], gsum.shape[0]
    sshare, gshare = SHARED_PARAMS // n, GROUP_PARAMS // n_dp
    place = lax.broadcasted_iota(jnp.int32, (srows, 128), 0) * 128
    place = place + lax.broadcasted_iota(jnp.int32, (srows, 128), 1)
    shared = jnp.where((place >= soff) & (place < soff + sshare), ssum, 0.0)
    place = lax.broadcasted_iota(jnp.int32, (grows, 128), 0) * 128
    place = place + lax.broadcasted_iota(jnp.int32, (grows, 128), 1)
    grouped = jnp.where((place >= goff) & (place < goff + gshare), gsum, 0.0)
    near_me, near_peers = near
    far_me, far_peers = far
    squares = column_sum(tile_sum(shared * shared) + tile_sum(grouped * grouped))
    sums = [
        column_sum(sc["a_vec"][i, :, c * 128 : (c + 1) * 128]) for i in (1, 2) for c in range(2)
    ]
    tile = jnp.concatenate([*sums, squares, jnp.zeros((3, 128), f32)], axis=0)
    sc["near_stat"][near_me] = tile
    tile = all_share(near_me, near_peers, sc["near_stat"], sc["near_send"], sc["near_recv"])
    sc["far_stat"][far_me] = tile
    tile = all_share(far_me, far_peers, sc["far_stat"], sc["far_send"], sc["far_recv"])
    carried = tile[:CARRIED]
    total = column_sum(carried * carried) + tile[CARRIED : CARRIED + 1]
    total = jnp.sum(total, axis=1, keepdims=True)
    last = jnp.where(own_number() == n - 1, 1.0, 0.0)
    at = GAIN_ROW - first_row(SHARED_PARAMS, n, n - 1)
    smine_ref[...] = shared
    smine_ref[at : at + CARRIED, :] += carried * last
    shared = smine_ref[...]
    norm = jnp.sqrt(total)
    norm_ref[...] = jnp.broadcast_to(norm, (8, 128))
    threshold = math.sqrt(2 * GROUP_PARAMS + SHARED_PARAMS)
    factor = jnp.minimum(1.0, threshold / (norm + 1e-06))
    smine_ref[...] = shift_back(shared * factor, soff)
    grouped = shift_back(grouped * factor, goff)
    for r in range(-(-gshare // 128)):
        size = min(128, gshare - 128 * r)
        gmine_ref[0:1, 128 * r : 128 * r + size] = grouped[r : r + 1, 0:size]


def step_kernel(
    n_dp,
    count,
    names,
    drop_in,
    x_ref,
    co_ref,
    sown_ref,
    gown_ref,
    out_ref,
    gin_ref,
    smine_ref,
    gmine_ref,
    norm_ref,
    *scratch,
):
    sc = dict(zip(names, scratch))
    n = 2 * n_dp
    stages = exchange_stages(n_dp)
    near, far = group_peers(n_dp)
    devices = [device for _, device in near[1] + far[1]]
    barrier = pltpu.get_barrier_semaphore()
    for device in devices:
        pl.semaphore_signal(barrier, inc=1, device_id=device)
    load_x = pltpu.make_async_copy(x_ref, sc["x_in"], sc["local"].at[0])
    load_co = pltpu.make_async_copy(co_ref, sc["x_in"], sc["local"].at[1])
    loads = [
        pltpu.make_async_copy(source, sc[name], sc["local"].at[2 + i])
        for i, (source, name) in enumerate(
            ((sown_ref, "sown"), (gown_ref, "gown"), (drop_in, "drops"))
        )
    ]
    for load in (*loads, load_x):
        load.start()
    drop_ref = sc["drops"]
    soff = (own_number() * (SHARED_PARAMS // n)) % UNIT
    goff = (lax.axis_index("dp") * (GROUP_PARAMS // n_dp)) % UNIT
    for load in loads:
        load.wait()
    own_windows(n_dp, sc["sown"], sc["gown"], soff, goff, stages, sc)
    load_x.wait()
    to_grid(sc["x_in"], sc["tokens"], sc["x"])
    load_co.start()
    pl.semaphore_wait(barrier, len(devices))
    ggather = Gather(stages, sc["gweights"], sc["ggather_send"], sc["ggather_recv"])
    sgather = Gather(stages, sc["sweights"], sc["sgather_send"], sc["sgather_recv"])

    def run(phase, extra=None, together=TOGETHER):
        def body(i, carry):
            if extra is not None:
                for at, action in extra.items():
                    pl.when(i == at)(action)
            phase([i * together + k for k in range(together)])
            return carry

        lax.fori_loop(0, count // together, body, 0)

    last = len(stages) - 1
    ggather.start(0)
    sgather.start(0)
    for g in range(last):
        if g == last - 1:
            run(lambda images: first_norm(images, sc))
        ggather.wait(g)
        ggather.start(g + 1)
        if g < last - 1:
            sgather.wait(g)
            sgather.start(g + 1)
    for name in ACCUMULATORS:
        sc[name][...] = jnp.zeros_like(sc[name])
    load_co.wait()
    to_grid(sc["x_in"], sc["tokens"], sc["co"])
    ggather.wait(last)
    prepare_group(n_dp, stages, sc)

    steps = count // TOGETHER
    backward = {}
    def spread_cores():
        sgather.wait(last - 1)
        sgather.start(last)

    run(lambda images: attention_forward(images, sc), {min(GATHER_STEP, steps - 1): spread_cores})
    sgather.wait(last)
    prepare_shared(n_dp, stages, sc)
    run(lambda images: mlp_both(images, drop_ref, sc), None, MLP_TOGETHER)
    place_shared(sc)

    srows, grows = sc["sweights"].shape[1], sc["gweights"].shape[1]

    def swindow(place):
        k = device_at(stages, place)
        row = (k * (SHARED_PARAMS // n)) // UNIT * 8
        return sc["flat"][pl.ds(pl.multiple_of(row, 8), srows), :]

    def gwindow(place):
        k = device_at(stages, place)
        row = ((k // 2) * (GROUP_PARAMS // n_dp)) // UNIT * 8
        return sc["gflat"][k % 2, pl.ds(pl.multiple_of(row, 8), grows), :]

    def scatter(name, window):
        parts = [[sc[f"{name}{kind}{g}"] for g in range(last + 1)] for kind in ("out", "in", "sum")]
        return Scatter(
            stages, window, *parts, sc[name + "scatter_send"], sc[name + "scatter_recv"]
        )

    sscatter = scatter("s", swindow)
    gscatter = scatter("g", gwindow)
    sscatter.start(last)
    def advance(scatter, g):
        def action():
            scatter.wait(g)
            scatter.start(g - 1)

        return action

    backward[min(1, steps - 1)] = [advance(sscatter, last)]
    run(
        lambda images: attention_back(images, sc),
        {at: chain(todo) for at, todo in backward.items()},
    )
    place_group(sc)
    gscatter.start(last)
    stores = []

    def store(held, target):
        for half in range(2):
            cols = slice(half * 128, (half + 1) * 128)
            copy = pltpu.make_async_copy(
                sc[held].at[half], target.at[:, cols], sc["local"].at[len(stores)]
            )
            copy.start()
            stores.append(copy)

    for g in range(last - 1, 0, -1):
        advance(sscatter, g)()
    run(lambda images: input_gradient(images, count, sc), {CORE_STEP: advance(gscatter, last)})
    store("tokens", gin_ref)
    for g in range(last - 1, 1, -1):
        advance(gscatter, g)()
    run(
        lambda images: mlp_output(images, count, drop_ref, sc),
        {OUT_STEP: advance(gscatter, 1)} if last > 1 else None,
        OUT_TOGETHER,
    )
    store("outs", out_ref)
    sscatter.wait(0)
    gscatter.wait(0)
    finish(
        n_dp,
        soff,
        goff,
        sc["ssum0"][0],
        sc["gsum0"][0],
        smine_ref,
        gmine_ref,
        norm_ref,
        near,
        far,
        sc,
    )
    for copy in stores:
        copy.wait()


def chain(actions):
    def run_all():
        for action in actions:
            action()

    return run_all


def step(n_dp, drops, images, cotangent, state):
    count = images.shape[0]
    gown, _, _, sown, _, _ = state
    srows = window_rows(SHARED_PARAMS, 2 * n_dp)
    grows = window_rows(GROUP_PARAMS, n_dp, CARRIED)
    shapes = scratch_shapes(n_dp, srows, grows, count)
    vmem = pl.BlockSpec(memory_space=pltpu.VMEM)
    anywhere = pl.BlockSpec(memory_space=pl.ANY)

    def rows(array):
        return jnp.swapaxes(array, 0, 1).reshape(TOK * count, D)

    def unrows(array):
        return jnp.swapaxes(array.reshape(TOK, count, D), 0, 1)

    out, gin, smine, gmine, norm = pl.pallas_call(
        partial(step_kernel, n_dp, count, tuple(shapes)),
        in_specs=[anywhere] * 5,
        out_specs=[anywhere, anywhere, vmem, vmem, vmem],
        out_shape=[jax.ShapeDtypeStruct((TOK * count, D), f32)] * 2
        + [
            jax.ShapeDtypeStruct((srows, 128), f32),
            jax.ShapeDtypeStruct(gown.shape, f32),
            jax.ShapeDtypeStruct((8, 128), f32),
        ],
        scratch_shapes=list(shapes.values()),
        compiler_params=pltpu.CompilerParams(
            collective_id=0, has_side_effects=True, vmem_limit_bytes=62 * 1024 * 1024
        ),
        name="step",
    )(drops.T, rows(images), rows(cotangent), sown, gown)
    first, second, *updated = update(out, gin, smine.reshape(-1), gmine, norm, *state)
    return (unrows(first), unrows(second), *updated)


def adam_step(master, gradient, first, second):
    first_new = beta_one * first + (1.0 - beta_one) * gradient
    second_new = beta_two * second + (1.0 - beta_two) * gradient * gradient
    first_hat = first_new / (1.0 - beta_one**STEP)
    second_hat = second_new / (1.0 - beta_two**STEP)
    master_new = master - learn_rate * (
        first_hat / (jnp.sqrt(second_hat) + adam_eps) + decay_rate * master
    )
    return (master_new, first_new, second_new)


CHUNKS = 4


def update_kernel(out_in, gin_in, smine, gmine, norm_in, *refs):
    gstate, sstate, refs = refs[:3], refs[3:6], refs[6:]
    out_ref, gin_ref, norm_ref = refs[:3]
    gnew, snew, (out_buf, gin_buf, in_sem, out_sem) = refs[3:8], refs[8:13], refs[13:]
    size = out_in.shape[0] // CHUNKS
    arrays = ((out_in, out_buf, out_ref), (gin_in, gin_buf, gin_ref))
    loads, stores = [], []
    for i in range(CHUNKS):
        rows = pl.ds(i * size, size)
        for k, (source, held, target) in enumerate(arrays):
            loads.append(
                pltpu.make_async_copy(source.at[rows], held.at[rows], in_sem.at[k, i])
            )
            stores.append(
                pltpu.make_async_copy(held.at[rows], target.at[rows], out_sem.at[k, i])
            )
            loads[-1].start()
    for load, store in zip(loads, stores):
        load.wait()
        store.start()
    norm_ref[...] = norm_in[0:1, 0:1]
    for gradient, (master, first, second), new in (
        (gmine[...], gstate, gnew),
        (smine[0 : sstate[0].shape[0]], sstate, snew),
    ):
        new[0][...] = gradient
        new[1][...], new[2][...], new[3][...] = adam_step(
            master[...], gradient, first[...], second[...]
        )
        new[4][...] = new[1][...].astype(bf16)
    for store in stores:
        store.wait()


def update(out, gin, smine, gmine, norm, *state):
    vmem = pl.BlockSpec(memory_space=pltpu.VMEM)
    anywhere = pl.BlockSpec(memory_space=pl.ANY)
    like = jax.ShapeDtypeStruct
    big = like(out.shape, f32)
    news = []
    for master in (state[0], state[3]):
        news += [like(master.shape, f32)] * 4 + [like(master.shape, bf16)]
    return pl.pallas_call(
        update_kernel,
        in_specs=[anywhere] * 2 + [vmem] * 9,
        out_specs=[anywhere] * 2 + [vmem] * 11,
        out_shape=[big, big, like((1, 1), f32)] + news,
        scratch_shapes=[pltpu.VMEM(out.shape, f32)] * 2
        + [pltpu.SemaphoreType.DMA((2, CHUNKS))] * 2,
        compiler_params=pltpu.CompilerParams(vmem_limit_bytes=62 * 1024 * 1024),
        name="update",
    )(out, gin, smine, gmine, norm, *state)


def on_device(
    n_dp,
    images,
    cotangent,
    drop_masks,
    group_master,
    group_m1,
    group_m2,
    shared_master,
    shared_m1,
    shared_m2,
):
    state = (group_master, group_m1, group_m2, shared_master, shared_m1, shared_m2)
    output, input_grad, norm, *updated = step(n_dp, drop_masks, images, cotangent, state)
    return (output, input_grad, norm.reshape(1), *updated)


def solution(mesh):
    both = P(("dp", "heads"))
    rows = P(("dp", "heads"), None, None)
    split = P("heads", "dp")
    in_specs = (rows, rows, P(("dp", "heads"), None), split, split, split, both, both, both)
    out_specs = (rows, rows, P(), split, split, split, split, split, both, both, both, both, both)
    return jax.shard_map(
        partial(on_device, mesh.shape["dp"]),
        mesh=mesh,
        in_specs=in_specs,
        out_specs=out_specs,
        check_vma=False,
    )
```

```python
from functools import partial
import math

import jax
import jax.numpy as jnp
from jax import lax
from jax.experimental import pallas as pl
from jax.experimental.pallas import tpu as pltpu
from jax.sharding import PartitionSpec as P

D = 256
FF = 1024
SIDE = 14
SW = 7
STEP = 10
HD = 32
HALF = 128
GROUP_PARAMS = 132608
SHARED_PARAMS = 526848
TOK = SIDE * SIDE
GRID = 16 * SIDE
STRIPE = 16 * SW
HEADS = HALF // HD
UNIT = 1024

eps_norm = 1e-05
keep_prob = 0.8
beta_one = 0.9
beta_two = 0.999
adam_eps = 1e-08
learn_rate = 0.04
decay_rate = 0.05

f32 = jnp.float32
bf16 = jnp.bfloat16


def window_rows(total, count, extra=0):
    share = total // count
    most = max((share * k) % UNIT + share for k in range(count)) + extra * 128
    return 16 * (-(-most // (2 * UNIT)))


def first_row(total, count, k):
    return (total // count * k) // UNIT * 8


HEADS_BIT = -1
FAST_BITS = 4
CARRIED = 4
GAIN_ROW = 4106


def exchange_stages(n_dp):
    bits = n_dp.bit_length() - 1
    far = list(range(bits - 1, 1, -1))
    stages = [tuple(far[i : i + 2]) for i in range(0, len(far), 2)]
    stages.append((1, HEADS_BIT) if bits > 1 else (HEADS_BIT,))
    if bits > 0:
        stages.append((0,))
    return stages


def weight_of(bit):
    return 1 if bit == HEADS_BIT else 2 << bit


def flat_bits(stages):
    return [bit for stage in stages for bit in stage]


def place_of(stages, k):
    return sum(((k // weight_of(bit)) % 2) << t for t, bit in enumerate(flat_bits(stages)))


def device_at(stages, place, first=0):
    return sum(
        ((place // (1 << t)) % 2) * weight_of(bit)
        for t, bit in enumerate(flat_bits(stages))
        if t >= first
    )


def own_number():
    return lax.axis_index("dp") * 2 + lax.axis_index("heads")


def own_bits(stages):
    me = own_number()
    return [(me // weight_of(bit)) % 2 for bit in flat_bits(stages)]


def peer(bits, mask):
    dp, heads = lax.axis_index("dp"), lax.axis_index("heads")
    for i, bit in enumerate(bits):
        if mask >> i & 1:
            if bit == HEADS_BIT:
                heads = 1 - heads
            else:
                dp = dp + (1 << bit) * (1 - 2 * ((dp // (1 << bit)) % 2))
    return {"dp": dp, "heads": heads}


def group_peers(n_dp):
    dp, heads = lax.axis_index("dp"), lax.axis_index("heads")
    fast = min(1 << FAST_BITS, n_dp)
    low, high = dp % fast, dp // fast
    count = 2 * fast
    me = low * 2 + heads
    near = []
    for step in range(1, count):
        other = (me + step) % count
        near.append((other, {"dp": high * fast + other // 2, "heads": other % 2}))
    far = []
    for step in range(1, n_dp // fast):
        other = (high + step) % (n_dp // fast)
        far.append((other, {"dp": other * fast + low, "heads": heads}))
    return (me, near), (high, far)


UNROLL = 16


class Gather:
    def __init__(self, stages, buffer, send_sem, recv_sem):
        self.stages, self.buffer = stages, buffer
        self.send_sem, self.recv_sem = send_sem, recv_sem
        self.bits = own_bits(stages)

    def copy(self, g, held, mask):
        return pltpu.make_async_remote_copy(
            src_ref=held,
            dst_ref=held,
            send_sem=self.send_sem.at[g],
            recv_sem=self.recv_sem.at[g],
            device_id=peer(self.stages[g], mask),
        )

    def start(self, g):
        start = sum(len(stage) for stage in self.stages[:g])
        base = sum((1 << u) * bit for u, bit in enumerate(self.bits) if u >= start)
        held = self.buffer.at[pl.ds(base, 1 << start)]
        for mask in range(1, 1 << len(self.stages[g])):
            self.copy(g, held, mask).start()

    def wait(self, g):
        start = sum(len(stage) for stage in self.stages[:g])
        peers = (1 << len(self.stages[g])) - 1
        every = self.copy(g, self.buffer.at[pl.ds(0, peers << start)], 1)
        every.wait_recv()
        every.wait_send()


class Scatter:
    def __init__(self, stages, window, outgoing, incoming, sums, send_sem, recv_sem):
        self.stages, self.window = stages, window
        self.outgoing, self.incoming, self.sums = outgoing, incoming, sums
        self.send_sem, self.recv_sem = send_sem, recv_sem
        self.bits = own_bits(stages)

    def offset(self, g):
        return sum(len(stage) for stage in self.stages[:g])

    def held(self, g, place):
        if g == len(self.stages) - 1:
            return self.window(place)
        return self.sums[g + 1][place]

    def copy(self, g, mask, at):
        return pltpu.make_async_remote_copy(
            src_ref=self.outgoing[g].at[at],
            dst_ref=self.incoming[g].at[at],
            send_sem=self.send_sem.at[g],
            recv_sem=self.recv_sem.at[g],
            device_id=peer(self.stages[g], mask),
        )

    def part(self, g, mask):
        start = self.offset(g)
        return sum(
            (1 << (start + i)) * (1 - self.bits[start + i] if mask >> i & 1 else self.bits[start + i])
            for i in range(len(self.stages[g]))
        )

    def start(self, g):
        for mask in range(1, 1 << len(self.stages[g])):
            part = self.part(g, mask)

            def fill(i, carry, mask=mask, part=part):
                self.outgoing[g][mask - 1, i] = self.held(g, part + i).astype(bf16)
                return carry

            blocks = 1 << self.offset(g)
            lax.fori_loop(0, blocks, fill, 0, unroll=min(blocks, UNROLL))
            self.copy(g, mask, mask - 1).start()

    def wait(self, g):
        masks = range(1, 1 << len(self.stages[g]))
        self.copy(g, 1, pl.ds(0, len(masks))).wait()
        part = self.part(g, 0)

        def add(i, carry):
            value = self.held(g, part + i)
            for mask in masks:
                value = value + self.incoming[g][mask - 1, i].astype(f32)
            self.sums[g][i] = value
            return carry

        blocks = 1 << self.offset(g)
        lax.fori_loop(0, blocks, add, 0, unroll=min(blocks, UNROLL))


def scatter_shapes(stages, rows):
    outgoing, sums = [], []
    start = 0
    for stage in stages:
        outgoing.append(((1 << len(stage)) - 1, 1 << start, rows, 128))
        sums.append((1 << start, rows, 128))
        start += len(stage)
    return outgoing, sums


def all_share(me, peers, stat_ref, send_sem, recv_sem):
    def copy(held, device):
        return pltpu.make_async_remote_copy(
            src_ref=held,
            dst_ref=held,
            send_sem=send_sem.at[0],
            recv_sem=recv_sem.at[0],
            device_id=device,
        )

    for _, device in peers:
        copy(stat_ref.at[me], device).start()
    if peers:
        every = copy(stat_ref.at[pl.ds(0, len(peers))], peers[0][1])
        every.wait_recv()
        every.wait_send()
    return jnp.sum(stat_ref[...], axis=0)


def shift_on(rows, amount):
    lanes = amount % 128
    turned = pltpu.roll(rows, lanes, 1)
    lane = lax.broadcasted_iota(jnp.int32, rows.shape, 1)
    turned = jnp.where(lane < lanes, pltpu.roll(turned, 1, 0), turned)
    return pltpu.roll(turned, amount // 128, 0)


def shift_back(rows, amount):
    count = rows.shape[0]
    lanes = amount % 128
    turned = pltpu.roll(rows, (128 - lanes) % 128, 1)
    lane = lax.broadcasted_iota(jnp.int32, rows.shape, 1)
    turned = jnp.where(lane >= 128 - lanes, pltpu.roll(turned, count - 1, 0), turned)
    return pltpu.roll(turned, (count - amount // 128) % count, 0)


def nn(a, b):
    return lax.dot_general(a, b, (((1,), (0,)), ((), ())), preferred_element_type=f32)


def nt(a, b):
    return lax.dot_general(a, b, (((1,), (1,)), ((), ())), preferred_element_type=f32)


def tn(a, b):
    return lax.dot_general(a, b, (((0,), (0,)), ((), ())), preferred_element_type=f32)


def norm_parts(values):
    center = values - jnp.mean(values, axis=-1, keepdims=True)
    inverse = lax.rsqrt(jnp.mean(center * center, axis=-1, keepdims=True) + eps_norm)
    return center * inverse, inverse


def norm_back(grad_after, unit, inverse, gain):
    scaled = grad_after * gain
    return inverse * (
        scaled
        - jnp.mean(scaled, axis=-1, keepdims=True)
        - unit * jnp.mean(scaled * unit, axis=-1, keepdims=True)
    )


def column_sum(values):
    return jnp.sum(values, axis=0, keepdims=True)


def head_masks(dtype):
    lane = lax.broadcasted_iota(jnp.int32, (1, D), 1) % HALF // HD
    return [(lane == h).astype(f32).astype(dtype) for h in range(HEADS)]


def spread_heads(values, masks):
    return jnp.concatenate([values * masks[h] for h in range(HEADS)], axis=0)


def pick_heads(stacked):
    lane = lax.broadcasted_iota(jnp.int32, (STRIPE, D), 1) % HALF
    picked = stacked[(HEADS - 1) * STRIPE :]
    for h in range(HEADS - 2, -1, -1):
        picked = jnp.where(lane < (h + 1) * HD, stacked[h * STRIPE : (h + 1) * STRIPE], picked)
    return picked


def beside(rows):
    return jnp.concatenate([rows[:STRIPE], rows[STRIPE:]], axis=1)


def above(columns):
    return jnp.concatenate([columns[:, :HALF], columns[:, HALF:]], axis=0)


def diagonal(rows):
    gap = jnp.zeros((HALF - STRIPE, HALF), rows.dtype)
    other = jnp.zeros((HALF, HALF), rows.dtype)
    first = jnp.concatenate([rows[:STRIPE], gap], axis=0)
    second = jnp.concatenate([rows[STRIPE:], gap], axis=0)
    return jnp.concatenate(
        [jnp.concatenate([first, other], axis=1), jnp.concatenate([other, second], axis=1)], axis=0
    )


def turn_heads(stacked):
    gap = jnp.zeros((HALF - STRIPE, HALF), stacked.dtype)
    parts = []
    for h in range(HEADS):
        rows = stacked[h * STRIPE : (h + 1) * STRIPE]
        blocks = [
            jnp.concatenate([rows[:, s * HALF : (s + 1) * HALF], gap], axis=0).T for s in range(2)
        ]
        parts.append(jnp.concatenate(blocks, axis=1)[:STRIPE])
    return jnp.concatenate(parts, axis=0)


def row_shift(values, rows):
    if rows == 0:
        return values
    zero = jnp.zeros((abs(rows), values.shape[1]), f32)
    if rows > 0:
        return jnp.concatenate([values[rows:], zero], axis=0)
    return jnp.concatenate([zero, values[:rows]], axis=0)


def neighbours(values, j):
    before, after = pltpu.roll(values, 1, 0), pltpu.roll(values, STRIPE - 1, 0)
    if j == 0:
        row = lax.broadcasted_iota(jnp.int32, values.shape, 0) % 16
        before = jnp.where(row == 8, pltpu.roll(values, 2, 0), before)
        after = jnp.where(row == 6, pltpu.roll(values, STRIPE - 2, 0), after)
    return [before, values, after]


SHIFT = (16, 8)


def tap(j, outer, inner):
    return 3 * outer + inner if j == 0 else 3 * inner + outer


def to_stripes(rows):
    tiles = rows.reshape(SIDE, 2, 8, rows.shape[1])
    return jnp.concatenate(
        [tiles[:, s].reshape(STRIPE, rows.shape[1]) for s in range(2)], axis=0
    )


def from_stripes(columns):
    halves = [columns[:, s * HALF : (s + 1) * HALF].reshape(SIDE, 1, 8, HALF) for s in range(2)]
    return jnp.concatenate(halves, axis=1).reshape(GRID, HALF)


def tile_sum(values):
    return jnp.sum(values.reshape(-1, 8, values.shape[1]), axis=0)


def row_mask():
    row = lax.broadcasted_iota(jnp.int32, (GRID, 1), 0)
    return (row % 8 < SW).astype(f32)


def to_grid(source, tokens, grid_ref):
    images = grid_ref.shape[0]
    grid_ref[...] = jnp.zeros_like(grid_ref)
    for half in range(2):
        cols = slice(half * 128, (half + 1) * 128)
        tokens[half] = source[:, cols].astype(f32)
        for image in range(images):
            for r in range(2 * SIDE):
                grid_ref[image, 8 * r : 8 * r + SW, cols] = tokens[
                    half, pl.ds(r * SW * images + image, SW, stride=images), :
                ]


def from_grid(value, tokens, image, images):
    for half in range(2):
        for r in range(2 * SIDE):
            tokens[half, pl.ds(r * SW * images + image, SW, stride=images), :] = value[
                8 * r : 8 * r + SW, half * 128 : (half + 1) * 128
            ]


def prepare_group(n_dp, stages, sc):
    n = 2 * n_dp
    gflat, buffer = sc["gflat"], sc["gweights"]
    grows = buffer.shape[1]
    gflat[...] = jnp.zeros_like(gflat)
    for k in range(n):
        at = first_row(GROUP_PARAMS, n_dp, k // 2)
        size = grows - CARRIED
        gflat[k % 2, at : at + size] += buffer[place_of(stages, k), 0:size].astype(f32)
    carried = buffer[place_of(stages, n - 1)].astype(f32)[grows - CARRIED :]
    for c in range(2):
        cols = slice(c * 128, (c + 1) * 128)
        sc["vecs"][1:2, cols] = carried[c : c + 1]
        sc["vecs"][2:3, cols] = carried[2 + c : 3 + c]
    for j in range(2):
        for c in range(3):
            cols = slice(j * 384 + c * 128, j * 384 + (c + 1) * 128)
            sc["wq"][:, cols] = gflat[j, pl.ds(c, D, stride=3), :].astype(bf16)
        for c in range(2):
            cols = slice(c * 128, (c + 1) * 128)
            sc["ow"][j * 128 : (j + 1) * 128, cols] = gflat[
                j, pl.ds(770 + c, HALF, stride=2), :
            ].astype(bf16)
        sc["qbias"][:, j * 384 : j * 384 + 128] = gflat[j, 768:769, :]
        sc["qbias"][:, j * 384 + 128 : j * 384 + 256] = jnp.zeros((1, 128), f32)
        sc["qbias"][:, j * 384 + 256 : j * 384 + 384] = gflat[j, 769:770, :]
        for half in range(2):
            cols = slice(half * 128, (half + 1) * 128)
            sc["conv"][j, 0:10, cols] = gflat[j, 1026:1036, :]


def prepare_shared(n_dp, stages, sc):
    n = 2 * n_dp
    flat, buffer = sc["flat"], sc["sweights"]
    srows = buffer.shape[1]
    flat[...] = jnp.zeros_like(flat)
    for k in range(n):
        at = first_row(SHARED_PARAMS, n, k)
        flat[at : at + srows] += buffer[place_of(stages, k)].astype(f32)
    for c in range(8):
        cols = slice(c * 128, (c + 1) * 128)
        sc["uw"][:, cols] = flat[pl.ds(c, D, stride=8), :].astype(bf16)
        sc["ubias"][:, cols] = flat[2048 + c : 2049 + c, :]
    for c in range(2):
        cols = slice(c * 128, (c + 1) * 128)
        sc["dw"][:, cols] = flat[pl.ds(2056 + c, FF, stride=2), :].astype(bf16)
        for i in (0, 3, 4, 5):
            sc["vecs"][i : i + 1, cols] = flat[4104 + 2 * i + c : 4105 + 2 * i + c, :]


def place_shared(sc):
    flat = sc["flat"]
    for c in range(8):
        cols = slice(c * 128, (c + 1) * 128)
        flat[pl.ds(c, D, stride=8), :] = sc["a_uw"][:, cols]
        flat[2048 + c : 2049 + c, :] = sc["a_ub"][0:1, cols]
    for q in range(4):
        turned = sc["a_dwt"][:, q * 256 : (q + 1) * 256].T
        for c in range(2):
            flat[pl.ds(2056 + 512 * q + c, 256, stride=2), :] = turned[
                :, c * 128 : (c + 1) * 128
            ]
    for c in range(2):
        cols = slice(c * 128, (c + 1) * 128)
        for i in (0, 3, 4, 5):
            flat[4104 + 2 * i + c : 4105 + 2 * i + c, :] = column_sum(
                sc["a_vec"][i, :, cols]
            )
    flat[GAIN_ROW : GAIN_ROW + CARRIED, :] = jnp.zeros((CARRIED, 128), f32)


def place_group(sc):
    gflat = sc["gflat"]
    for j in range(2):
        for c in range(3):
            cols = slice(j * 384 + c * 128, j * 384 + (c + 1) * 128)
            gflat[j, pl.ds(c, D, stride=3), :] = sc["a_wq"][:, cols]
        for c in range(2):
            cols = slice(c * 128, (c + 1) * 128)
            gflat[j, pl.ds(770 + c, HALF, stride=2), :] = sc["a_ow"][
                j * 128 : (j + 1) * 128, cols
            ]
        gflat[j, 768:769, :] = sc["a_pb"][0:1, j * 384 : j * 384 + 128]
        gflat[j, 769:770, :] = sc["a_pb"][0:1, j * 384 + 256 : j * 384 + 384]
        for i in range(10):
            both = column_sum(sc["a_conv"][j, i])
            gflat[j, 1026 + i : 1027 + i, :] = both[:, :HALF] + both[:, HALF:]


def first_norm(images, sc):
    for image in images:
        sc["unit"][image], sc["inverse"][image] = norm_parts(sc["x"][image])


def attention_forward(images, sc):
    scale = HD ** (-0.5)
    masks = head_masks(bf16)
    inside = row_mask()
    key_row = lax.broadcasted_iota(jnp.int32, (1, SIDE, 8, D), 2)
    gain_one, shift_one = sc["vecs"][1:2], sc["vecs"][2:3]
    qkv_ref, conv = sc["qkv"], sc["conv"]
    many = len(images)
    for image in images:
        sc["normed"][image] = (sc["unit"][image] * gain_one + shift_one).astype(bf16)
    normed = sc["normed"][pl.ds(images[0], many)].reshape(many * GRID, D)
    triples = nn(normed, sc["wq"][...]) + sc["qbias"][...]
    for i, image in enumerate(images):
        triple = triples[i * GRID : (i + 1) * GRID] * inside
        qkv_ref[image, 0] = triple[:, :384].astype(bf16)
        qkv_ref[image, 1] = to_stripes(triple[:, 384:]).astype(bf16)
    for j in range(2):
        for image in images:
            query = diagonal(qkv_ref[image, j, :, 0:128])
            keys = spread_heads(beside(qkv_ref[image, j, :, 128:256]), masks)
            value = beside(qkv_ref[image, j, :, 256:384])
            scores = nt(keys, query).reshape(HEADS, SIDE, 8, D) * scale
            scores = jnp.where(key_row < SW, scores, -1e30)
            scores = scores.reshape(HEADS, STRIPE, D)
            weights = jnp.exp(scores - jnp.max(scores, axis=1, keepdims=True))
            probs = weights * (1.0 / jnp.sum(weights, axis=1, keepdims=True))
            probs = probs.reshape(HEADS * STRIPE, D)
            sc["probs"][image, j] = probs
            values = diagonal(qkv_ref[image, j, :, 256:384])
            total = pick_heads(nn(turn_heads(probs.astype(bf16)), values)) + conv[j, 9:10]
            near = neighbours(value.astype(f32), j)
            for outer in range(3):
                part = None
                for inner in range(3):
                    k = tap(j, outer, inner)
                    term = near[inner] * conv[j, k : k + 1]
                    part = term if part is None else part + term
                total = total + row_shift(part, SHIFT[j] * (outer - 1))
            both = above(total) if j == 0 else from_stripes(total)
            sc["heads"][image, :, j * 128 : (j + 1) * 128] = both.astype(bf16)


def mlp_output(images, count, drop_ref, sc):
    many = len(images)
    active = sc["active"][pl.ds(images[0], many)].reshape(many * GRID, FF)
    mlp = nn(active, sc["dw"][...]) + sc["vecs"][0:1]
    for i, image in enumerate(images):
        scale_two = drop_ref[1, image].astype(f32) / keep_prob
        value = sc["x"][image] + scale_two * mlp[i * GRID : (i + 1) * GRID]
        from_grid(value, sc["outs"], image, count)


def mlp_both(images, drop_ref, sc):
    gain_two, shift_two, out_bias = sc["vecs"][3:4], sc["vecs"][4:5], sc["vecs"][5:6]
    a_vec = sc["a_vec"]
    uw, dw, ubias = sc["uw"], sc["dw"], sc["ubias"]
    many = len(images)
    ones = jnp.ones((8, many * GRID), bf16)

    def join(parts):
        return jnp.concatenate(parts, axis=0)

    def part_of(joined, i):
        return joined[i * GRID : (i + 1) * GRID]

    heads = sc["heads"][pl.ds(images[0], many)].reshape(many * GRID, D)
    branch = nn(heads, sc["ow"][...])
    state = []
    for i, image in enumerate(images):
        scale_one = drop_ref[0, image].astype(f32) / keep_prob
        scale_two = drop_ref[1, image].astype(f32) / keep_prob
        middle = sc["x"][image] + scale_one * (part_of(branch, i) + out_bias)
        unit_two, inverse_two = norm_parts(middle)
        grad_output = sc["co"][image]
        grad_mlp_f = scale_two * grad_output
        a_vec[0] += tile_sum(grad_mlp_f)
        state.append((scale_one, scale_two, middle, unit_two, inverse_two, grad_output, grad_mlp_f))
    normed_two = join([(st[3] * gain_two + shift_two).astype(bf16) for st in state])
    grad_mlp = join([st[6].astype(bf16) for st in state])
    grad_normed = None
    for c in range(4):
        cols = slice(c * 256, (c + 1) * 256)
        hidden = nn(normed_two, uw[:, cols]) + ubias[:, cols]
        density = jnp.exp(hidden * hidden * -0.5) * (1.0 / math.sqrt(2.0 * math.pi))
        phi = 0.5 + 0.5 * lax.erf(hidden * math.sqrt(0.5))
        active = (hidden * phi).astype(bf16)
        sc["active"][pl.ds(images[0], many), :, cols] = active.reshape(many, GRID, 256)
        sc["a_dwt"][:, cols] += tn(grad_mlp, active)
        grad_active = nt(grad_mlp, dw[cols, :])
        grad_hidden = (grad_active * (phi + hidden * density)).astype(bf16)
        sc["a_ub"][:, cols] += nn(ones, grad_hidden)
        sc["a_uw"][:, cols] += tn(normed_two, grad_hidden)
        part = nt(grad_hidden, uw[:, cols])
        grad_normed = part if grad_normed is None else grad_normed + part
    grad_branch = []
    for i, image in enumerate(images):
        scale_one, _, middle, unit_two, inverse_two, grad_output, _ = state[i]
        sc["x"][image] = middle
        grad = part_of(grad_normed, i)
        a_vec[3] += tile_sum(grad * unit_two)
        a_vec[4] += tile_sum(grad)
        grad_middle = grad_output + norm_back(grad, unit_two, inverse_two, gain_two)
        sc["gmid"][image] = grad_middle
        grad_branch_f = scale_one * grad_middle
        a_vec[5] += tile_sum(grad_branch_f)
        grad_branch.append(grad_branch_f.astype(bf16))
    grad_branch = join(grad_branch)
    sc["a_ow"][...] += tn(heads, grad_branch)
    grad_heads = nt(grad_branch, sc["ow"][...])
    for i, image in enumerate(images):
        grad = part_of(grad_heads, i)
        sc["gheads"][image, :, :128] = grad[:, :128].astype(bf16)
        sc["gheads"][image, :, 128:] = to_stripes(grad[:, 128:]).astype(bf16)


def attention_back(images, sc, now, between):
    scale = HD ** (-0.5)
    masks = head_masks(bf16)
    inside = row_mask()[:STRIPE]
    many = len(images)
    ones = jnp.ones((8, many * GRID), bf16)
    a_conv = sc["a_conv"]
    qkv_ref, conv = sc["qkv"], sc["conv"]
    for j in range(2):
        if j == 1:
            pl.when(now)(between)
        for image in images:
            grad = sc["gheads"][image, :, j * 128 : (j + 1) * 128]
            grad_square = diagonal(grad)
            grad_f = beside(grad).astype(f32)
            query = diagonal(qkv_ref[image, j, :, 0:128])
            value = beside(qkv_ref[image, j, :, 256:384])
            probs = sc["probs"][image, j]
            grad_probs = nt(spread_heads(value, masks), grad_square)
            product = (probs * grad_probs).reshape(HEADS, STRIPE, D)
            inner = jnp.sum(product, axis=1, keepdims=True)
            grad_scores = product - probs.reshape(HEADS, STRIPE, D) * inner
            grad_scores = grad_scores.reshape(HEADS * STRIPE, D).astype(bf16)
            keys = diagonal(qkv_ref[image, j, :, 128:256])
            grad_query = pick_heads(nn(turn_heads(grad_scores), keys)) * scale
            grad_key = pick_heads(nn(grad_scores, query)) * scale
            grad_value = pick_heads(nn(probs.astype(bf16), grad_square))
            near = neighbours(grad_f, j)
            for outer in range(3):
                part = None
                for inner in range(3):
                    k = tap(j, outer, inner)
                    term = near[2 - inner] * conv[j, k : k + 1]
                    part = term if part is None else part + term
                grad_value = grad_value + row_shift(part, SHIFT[j] * (1 - outer))
            grad_value = grad_value * inside
            near = neighbours(value.astype(f32), j)
            step = SHIFT[j]
            for inner in range(3):
                a_conv[j, tap(j, 0, inner)] += tile_sum(grad_f[step:] * near[inner][:-step])
                a_conv[j, tap(j, 1, inner)] += tile_sum(grad_f * near[inner])
                a_conv[j, tap(j, 2, inner)] += tile_sum(grad_f[:-step] * near[inner][step:])
            a_conv[j, 9] += tile_sum(grad_f)
            order = above if j == 0 else from_stripes
            both = jnp.concatenate(
                [order(part) for part in (grad_query, grad_key, grad_value)], axis=1
            ).astype(bf16)
            sc["gtriple"][image, :, j * 384 : (j + 1) * 384] = both
    grad_triple = sc["gtriple"][pl.ds(images[0], many)].reshape(many * GRID, 768)
    normed = sc["normed"][pl.ds(images[0], many)].reshape(many * GRID, D)
    sc["a_pb"][...] += nn(ones, grad_triple)
    sc["a_wq"][...] += tn(normed, grad_triple)


def input_gradient(images, count, sc):
    many = len(images)
    gain_one = sc["vecs"][1:2]
    a_vec = sc["a_vec"]
    grad_triple = sc["gtriple"][pl.ds(images[0], many)].reshape(many * GRID, 768)
    grads = nt(grad_triple, sc["wq"][...])
    for i, image in enumerate(images):
        grad_normed = grads[i * GRID : (i + 1) * GRID]
        unit, inverse = sc["unit"][image], sc["inverse"][image]
        a_vec[1] += tile_sum(grad_normed * unit)
        a_vec[2] += tile_sum(grad_normed)
        grad = sc["gmid"][image] + norm_back(grad_normed, unit, inverse, gain_one)
        from_grid(grad, sc["tokens"], image, count)


def scratch_shapes(n_dp, srows, grows, count):
    n = 2 * n_dp
    flat_rows = max(4120, first_row(SHARED_PARAMS, n, n - 1) + srows)
    gflat_rows = max(1040, first_row(GROUP_PARAMS, n_dp, n_dp - 1) + grows)
    shapes = dict(
        flat=((flat_rows, 128), f32),
        gflat=((2, gflat_rows, 128), f32),
        sweights=((n, srows, 128), bf16),
        gweights=((n, grows, 128), bf16),
        raw=((grows, 128), f32),
        sraw=((srows, 128), f32),
        sown=((SHARED_PARAMS // n,), f32),
        gown=((1, GROUP_PARAMS // n_dp), f32),
        wq=((D, 768), bf16),
        ow=((D, D), bf16),
        uw=((D, FF), bf16),
        dw=((FF, D), bf16),
        qbias=((1, 768), f32),
        ubias=((1, FF), f32),
        vecs=((8, D), f32),
        conv=((2, 16, D), f32),
        a_wq=((D, 768), f32),
        a_ow=((D, D), f32),
        a_uw=((D, FF), f32),
        a_dwt=((D, FF), f32),
        a_pb=((8, 768), f32),
        a_ub=((8, FF), f32),
        a_vec=((6, 8, D), f32),
        a_conv=((2, 10, 8, D), f32),
        x_in=((TOK * count, D), bf16),
        tokens=((2, TOK * count, 128), f32),
        outs=((2, TOK * count, 128), f32),
        x=((count, GRID, D), f32),
        co=((count, GRID, D), f32),
        unit=((count, GRID, D), f32),
        inverse=((count, GRID, 1), f32),
        normed=((count, GRID, D), bf16),
        qkv=((count, 2, GRID, 384), bf16),
        probs=((count, 2, HEADS * STRIPE, D), f32),
        heads=((count, GRID, D), bf16),
        gmid=((count, GRID, D), f32),
        active=((count, GRID, FF), bf16),
        gheads=((count, GRID, D), bf16),
        gtriple=((count, GRID, 768), bf16),
    )
    stages = exchange_stages(n_dp)
    for name, rows in (("s", srows), ("g", grows)):
        outgoing, sums = scatter_shapes(stages, rows)
        for g, shape in enumerate(outgoing):
            shapes[f"{name}out{g}"] = (shape, bf16)
            shapes[f"{name}in{g}"] = (shape, bf16)
            shapes[f"{name}sum{g}"] = (sums[g], f32)
    fast = min(1 << FAST_BITS, n_dp)
    shapes["near_stat"] = ((2 * fast, 8, 128), f32)
    shapes["far_stat"] = ((n_dp // fast, 8, 128), f32)
    made = {name: pltpu.VMEM(*shape) for name, shape in shapes.items()}
    dma = pltpu.SemaphoreType.DMA
    for name in ("sgather", "ggather", "sscatter", "gscatter"):
        made[name + "_send"] = dma((len(stages),))
        made[name + "_recv"] = dma((len(stages),))
    for name in ("near", "far"):
        made[name + "_send"] = dma((1,))
        made[name + "_recv"] = dma((1,))
    made["local"] = dma((5,))
    made["drops"] = pltpu.SMEM((2, count), jnp.int32)
    return made


ACCUMULATORS = ("a_wq", "a_ow", "a_uw", "a_dwt", "a_pb", "a_ub", "a_vec", "a_conv")
TOGETHER = 2
FORWARD_TOGETHER = 4
BACK_TOGETHER = 4
MLP_TOGETHER = 4
GATHER_STEP = 1
CORE_STEP = 1
OUT_STEP = 3
BACK_IMAGE = 0
OUT_TOGETHER = 2


def own_windows(n_dp, sown_ref, gown_ref, soff, goff, stages, sc):
    n = 2 * n_dp
    mine = sum((1 << t) * bit for t, bit in enumerate(own_bits(stages)))
    raw = sc["sraw"]
    share = sown_ref.shape[0]
    whole = share // UNIT * UNIT
    raw[...] = jnp.zeros_like(raw)
    raw[0 : whole // 128, :] = sown_ref[0:whole].reshape(whole // 128, 128)
    for r in range(whole // 128, -(-share // 128)):
        size = min(128, share - 128 * r)
        raw[r : r + 1, 0:size] = sown_ref[128 * r : 128 * r + size].reshape(1, size)
    window = shift_on(raw[...], soff)
    sc["sweights"][mine] = window.astype(bf16)
    raw = sc["raw"]
    grows = raw.shape[0]
    share = gown_ref.shape[1]
    raw[...] = jnp.zeros_like(raw)
    for r in range(-(-share // 128)):
        size = min(128, share - 128 * r)
        raw[r : r + 1, 0:size] = gown_ref[0:1, 128 * r : 128 * r + size]
    at = GAIN_ROW - first_row(SHARED_PARAMS, n, n - 1)
    raw[...] = shift_on(raw[...], goff)
    raw[grows - CARRIED :, :] = window[at : at + CARRIED]
    sc["gweights"][mine] = raw[...].astype(bf16)


def finish(n_dp, soff, goff, ssum, gsum, smine_ref, gmine_ref, norm_ref, near, far, sc):
    n = 2 * n_dp
    srows, grows = ssum.shape[0], gsum.shape[0]
    sshare, gshare = SHARED_PARAMS // n, GROUP_PARAMS // n_dp
    place = lax.broadcasted_iota(jnp.int32, (srows, 128), 0) * 128
    place = place + lax.broadcasted_iota(jnp.int32, (srows, 128), 1)
    shared = jnp.where((place >= soff) & (place < soff + sshare), ssum, 0.0)
    place = lax.broadcasted_iota(jnp.int32, (grows, 128), 0) * 128
    place = place + lax.broadcasted_iota(jnp.int32, (grows, 128), 1)
    grouped = jnp.where((place >= goff) & (place < goff + gshare), gsum, 0.0)
    near_me, near_peers = near
    far_me, far_peers = far
    squares = column_sum(tile_sum(shared * shared) + tile_sum(grouped * grouped))
    sums = [
        column_sum(sc["a_vec"][i, :, c * 128 : (c + 1) * 128]) for i in (1, 2) for c in range(2)
    ]
    tile = jnp.concatenate([*sums, squares, jnp.zeros((3, 128), f32)], axis=0)
    sc["near_stat"][near_me] = tile
    tile = all_share(near_me, near_peers, sc["near_stat"], sc["near_send"], sc["near_recv"])
    sc["far_stat"][far_me] = tile
    tile = all_share(far_me, far_peers, sc["far_stat"], sc["far_send"], sc["far_recv"])
    carried = tile[:CARRIED]
    total = column_sum(carried * carried) + tile[CARRIED : CARRIED + 1]
    total = jnp.sum(total, axis=1, keepdims=True)
    last = jnp.where(own_number() == n - 1, 1.0, 0.0)
    at = GAIN_ROW - first_row(SHARED_PARAMS, n, n - 1)
    smine_ref[...] = shared
    smine_ref[at : at + CARRIED, :] += carried * last
    shared = smine_ref[...]
    norm = jnp.sqrt(total)
    norm_ref[...] = jnp.broadcast_to(norm, (8, 128))
    threshold = math.sqrt(2 * GROUP_PARAMS + SHARED_PARAMS)
    factor = jnp.minimum(1.0, threshold / (norm + 1e-06))
    smine_ref[...] = shift_back(shared * factor, soff)
    grouped = shift_back(grouped * factor, goff)
    for r in range(-(-gshare // 128)):
        size = min(128, gshare - 128 * r)
        gmine_ref[0:1, 128 * r : 128 * r + size] = grouped[r : r + 1, 0:size]


def step_kernel(
    n_dp,
    count,
    names,
    drop_in,
    x_ref,
    co_ref,
    sown_ref,
    gown_ref,
    out_ref,
    gin_ref,
    smine_ref,
    gmine_ref,
    norm_ref,
    *scratch,
):
    sc = dict(zip(names, scratch))
    n = 2 * n_dp
    stages = exchange_stages(n_dp)
    near, far = group_peers(n_dp)
    devices = [device for _, device in near[1] + far[1]]
    barrier = pltpu.get_barrier_semaphore()
    for device in devices:
        pl.semaphore_signal(barrier, inc=1, device_id=device)
    load_x = pltpu.make_async_copy(x_ref, sc["x_in"], sc["local"].at[0])
    load_co = pltpu.make_async_copy(co_ref, sc["x_in"], sc["local"].at[1])
    loads = [
        pltpu.make_async_copy(source, sc[name], sc["local"].at[2 + i])
        for i, (source, name) in enumerate(
            ((sown_ref, "sown"), (gown_ref, "gown"), (drop_in, "drops"))
        )
    ]
    for load in (*loads, load_x):
        load.start()
    drop_ref = sc["drops"]
    soff = (own_number() * (SHARED_PARAMS // n)) % UNIT
    goff = (lax.axis_index("dp") * (GROUP_PARAMS // n_dp)) % UNIT
    for load in loads:
        load.wait()
    own_windows(n_dp, sc["sown"], sc["gown"], soff, goff, stages, sc)
    load_x.wait()
    to_grid(sc["x_in"], sc["tokens"], sc["x"])
    load_co.start()
    pl.semaphore_wait(barrier, len(devices))
    ggather = Gather(stages, sc["gweights"], sc["ggather_send"], sc["ggather_recv"])
    sgather = Gather(stages, sc["sweights"], sc["sgather_send"], sc["sgather_recv"])

    def run(phase, extra=None, together=TOGETHER):
        def body(i, carry):
            if extra is not None:
                for at, action in extra.items():
                    pl.when(i == at)(action)
            phase([i * together + k for k in range(together)])
            return carry

        lax.fori_loop(0, count // together, body, 0)

    last = len(stages) - 1
    ggather.start(0)
    sgather.start(0)
    for g in range(last):
        if g == last - 1:
            run(lambda images: first_norm(images, sc))
        ggather.wait(g)
        ggather.start(g + 1)
        if g < last - 1:
            sgather.wait(g)
            sgather.start(g + 1)
    for name in ACCUMULATORS:
        sc[name][...] = jnp.zeros_like(sc[name])
    load_co.wait()
    to_grid(sc["x_in"], sc["tokens"], sc["co"])
    ggather.wait(last)
    prepare_group(n_dp, stages, sc)

    def spread_cores():
        sgather.wait(last - 1)
        sgather.start(last)

    steps = count // FORWARD_TOGETHER
    run(
        lambda images: attention_forward(images, sc),
        {min(GATHER_STEP, steps - 1): spread_cores},
        FORWARD_TOGETHER,
    )
    sgather.wait(last)
    prepare_shared(n_dp, stages, sc)
    run(lambda images: mlp_both(images, drop_ref, sc), None, MLP_TOGETHER)
    place_shared(sc)

    srows, grows = sc["sweights"].shape[1], sc["gweights"].shape[1]

    def swindow(place):
        k = device_at(stages, place)
        row = (k * (SHARED_PARAMS // n)) // UNIT * 8
        return sc["flat"][pl.ds(pl.multiple_of(row, 8), srows), :]

    def gwindow(place):
        k = device_at(stages, place)
        row = ((k // 2) * (GROUP_PARAMS // n_dp)) // UNIT * 8
        return sc["gflat"][k % 2, pl.ds(pl.multiple_of(row, 8), grows), :]

    def scatter(name, window):
        parts = [[sc[f"{name}{kind}{g}"] for g in range(last + 1)] for kind in ("out", "in", "sum")]
        return Scatter(
            stages, window, *parts, sc[name + "scatter_send"], sc[name + "scatter_recv"]
        )

    sscatter = scatter("s", swindow)
    gscatter = scatter("g", gwindow)
    sscatter.start(last)
    def advance(scatter, g):
        def action():
            scatter.wait(g)
            scatter.start(g - 1)

        return action

    run(
        lambda images: attention_back(
            images, sc, images[0] == BACK_IMAGE, advance(sscatter, last)
        ),
        None,
        BACK_TOGETHER,
    )
    place_group(sc)
    gscatter.start(last)
    stores = []

    def store(held, target):
        for half in range(2):
            cols = slice(half * 128, (half + 1) * 128)
            copy = pltpu.make_async_copy(
                sc[held].at[half], target.at[:, cols], sc["local"].at[len(stores)]
            )
            copy.start()
            stores.append(copy)

    for g in range(last - 1, 0, -1):
        advance(sscatter, g)()
    run(lambda images: input_gradient(images, count, sc), {CORE_STEP: advance(gscatter, last)})
    store("tokens", gin_ref)
    for g in range(last - 1, 1, -1):
        advance(gscatter, g)()
    run(
        lambda images: mlp_output(images, count, drop_ref, sc),
        {OUT_STEP: advance(gscatter, 1)} if last > 1 else None,
        OUT_TOGETHER,
    )
    store("outs", out_ref)
    sscatter.wait(0)
    gscatter.wait(0)
    finish(
        n_dp,
        soff,
        goff,
        sc["ssum0"][0],
        sc["gsum0"][0],
        smine_ref,
        gmine_ref,
        norm_ref,
        near,
        far,
        sc,
    )
    for copy in stores:
        copy.wait()


def step(n_dp, drops, images, cotangent, state):
    count = images.shape[0]
    gown, _, _, sown, _, _ = state
    srows = window_rows(SHARED_PARAMS, 2 * n_dp)
    grows = window_rows(GROUP_PARAMS, n_dp, CARRIED)
    shapes = scratch_shapes(n_dp, srows, grows, count)
    vmem = pl.BlockSpec(memory_space=pltpu.VMEM)
    anywhere = pl.BlockSpec(memory_space=pl.ANY)

    def rows(array):
        return jnp.swapaxes(array, 0, 1).reshape(TOK * count, D)

    def unrows(array):
        return jnp.swapaxes(array.reshape(TOK, count, D), 0, 1)

    out, gin, smine, gmine, norm = pl.pallas_call(
        partial(step_kernel, n_dp, count, tuple(shapes)),
        in_specs=[anywhere] * 5,
        out_specs=[anywhere, anywhere, vmem, vmem, vmem],
        out_shape=[jax.ShapeDtypeStruct((TOK * count, D), f32)] * 2
        + [
            jax.ShapeDtypeStruct((srows, 128), f32),
            jax.ShapeDtypeStruct(gown.shape, f32),
            jax.ShapeDtypeStruct((8, 128), f32),
        ],
        scratch_shapes=list(shapes.values()),
        compiler_params=pltpu.CompilerParams(
            collective_id=0, has_side_effects=True, vmem_limit_bytes=62 * 1024 * 1024
        ),
        name="step",
    )(drops.T, rows(images), rows(cotangent), sown, gown)
    first, second, *updated = update(out, gin, smine.reshape(-1), gmine, norm, *state)
    return (unrows(first), unrows(second), *updated)


def adam_step(master, gradient, first, second):
    first_new = beta_one * first + (1.0 - beta_one) * gradient
    second_new = beta_two * second + (1.0 - beta_two) * gradient * gradient
    first_hat = first_new / (1.0 - beta_one**STEP)
    second_hat = second_new / (1.0 - beta_two**STEP)
    master_new = master - learn_rate * (
        first_hat / (jnp.sqrt(second_hat) + adam_eps) + decay_rate * master
    )
    return (master_new, first_new, second_new)


CHUNKS = 1


def update_kernel(*refs):
    big_in, small_in, refs = refs[:2], refs[2:11], refs[11:]
    big_out, small_out, refs = refs[:2], refs[2:13], refs[13:]
    big_buf, refs = refs[:2], refs[2:]
    held_in, held_out, sems = refs[:9], refs[9:20], refs[20:]
    big_load, big_store, small_load, small_store = sems
    size = big_in[0].shape[0] // CHUNKS

    def small_loads():
        for i in range(9):
            yield pltpu.make_async_copy(small_in[i], held_in[i], small_load.at[i])

    loads, stores = [], []
    for i in range(CHUNKS):
        rows = pl.ds(i * size, size)
        for k in range(2):
            held = big_buf[k].at[rows]
            loads.append(pltpu.make_async_copy(big_in[k].at[rows], held, big_load.at[k, i]))
            stores.append(pltpu.make_async_copy(held, big_out[k].at[rows], big_store.at[k, i]))
    small = list(small_loads())
    for load in (*small, *loads):
        load.start()
    for load in small:
        load.wait()
    smine, gmine, norm = held_in[:3]
    states = (held_in[3:6], held_in[6:9])
    held_out[0][...] = norm[0:1, 0:1]
    for gradient, (master, first, second), new in (
        (gmine[...], states[0], held_out[1:6]),
        (smine[0 : states[1][0].shape[0]], states[1], held_out[6:11]),
    ):
        new[0][...] = gradient
        new[1][...], new[2][...], new[3][...] = adam_step(
            master[...], gradient, first[...], second[...]
        )
        new[4][...] = new[1][...].astype(bf16)
    small = [
        pltpu.make_async_copy(held_out[i], small_out[i], small_store.at[i]) for i in range(11)
    ]
    for load, store in zip(loads, stores):
        load.wait()
        store.start()
    for store in small:
        store.start()
    for store in (*stores, *small):
        store.wait()


def update(out, gin, smine, gmine, norm, *state):
    anywhere = pl.BlockSpec(memory_space=pl.ANY)
    like = jax.ShapeDtypeStruct
    news = [like((1, 1), f32)]
    for master in (state[0], state[3]):
        news += [like(master.shape, f32)] * 4 + [like(master.shape, bf16)]
    small = (smine, gmine, norm, *state)
    dma = pltpu.SemaphoreType.DMA
    return pl.pallas_call(
        update_kernel,
        in_specs=[anywhere] * (2 + len(small)),
        out_specs=[anywhere] * (2 + len(news)),
        out_shape=[like(out.shape, f32)] * 2 + news,
        scratch_shapes=[pltpu.VMEM(out.shape, f32)] * 2
        + [pltpu.VMEM(array.shape, array.dtype) for array in (*small, *news)]
        + [dma((2, CHUNKS))] * 2
        + [dma((len(small),)), dma((len(news),))],
        compiler_params=pltpu.CompilerParams(vmem_limit_bytes=62 * 1024 * 1024),
        name="update",
    )(out, gin, *small)


def on_device(
    n_dp,
    images,
    cotangent,
    drop_masks,
    group_master,
    group_m1,
    group_m2,
    shared_master,
    shared_m1,
    shared_m2,
):
    state = (group_master, group_m1, group_m2, shared_master, shared_m1, shared_m2)
    output, input_grad, norm, *updated = step(n_dp, drop_masks, images, cotangent, state)
    return (output, input_grad, norm.reshape(1), *updated)


def solution(mesh):
    both = P(("dp", "heads"))
    rows = P(("dp", "heads"), None, None)
    split = P("heads", "dp")
    in_specs = (rows, rows, P(("dp", "heads"), None), split, split, split, both, both, both)
    out_specs = (rows, rows, P(), split, split, split, split, split, both, both, both, both, both)
    return jax.shard_map(
        partial(on_device, mesh.shape["dp"]),
        mesh=mesh,
        in_specs=in_specs,
        out_specs=out_specs,
        check_vma=False,
    )
```

```python
from functools import partial
import math

import jax
import jax.numpy as jnp
from jax import lax
from jax.experimental import pallas as pl
from jax.experimental.pallas import tpu as pltpu
from jax.sharding import PartitionSpec as P

D = 256
FF = 1024
SIDE = 14
SW = 7
STEP = 10
HD = 32
HALF = 128
GROUP_PARAMS = 132608
SHARED_PARAMS = 526848
TOK = SIDE * SIDE
GRID = 16 * SIDE
STRIPE = 16 * SW
HEADS = HALF // HD
UNIT = 1024

eps_norm = 1e-05
keep_prob = 0.8
beta_one = 0.9
beta_two = 0.999
adam_eps = 1e-08
learn_rate = 0.04
decay_rate = 0.05

f32 = jnp.float32
bf16 = jnp.bfloat16


def window_rows(total, count, extra=0):
    share = total // count
    most = max((share * k) % UNIT + share for k in range(count)) + extra * 128
    return 16 * (-(-most // (2 * UNIT)))


def first_row(total, count, k):
    return (total // count * k) // UNIT * 8


HEADS_BIT = -1
FAST_BITS = 4
CARRIED = 4
GAIN_ROW = 4106


def exchange_stages(n_dp):
    bits = n_dp.bit_length() - 1
    far = list(range(bits - 1, 1, -1))
    stages = [tuple(far[i : i + 2]) for i in range(0, len(far), 2)]
    stages.append((1, HEADS_BIT) if bits > 1 else (HEADS_BIT,))
    if bits > 0:
        stages.append((0,))
    return stages


def weight_of(bit):
    return 1 if bit == HEADS_BIT else 2 << bit


def flat_bits(stages):
    return [bit for stage in stages for bit in stage]


def place_of(stages, k):
    return sum(((k // weight_of(bit)) % 2) << t for t, bit in enumerate(flat_bits(stages)))


def device_at(stages, place, first=0):
    return sum(
        ((place // (1 << t)) % 2) * weight_of(bit)
        for t, bit in enumerate(flat_bits(stages))
        if t >= first
    )


def own_number():
    return lax.axis_index("dp") * 2 + lax.axis_index("heads")


def own_bits(stages):
    me = own_number()
    return [(me // weight_of(bit)) % 2 for bit in flat_bits(stages)]


def peer(bits, mask):
    dp, heads = lax.axis_index("dp"), lax.axis_index("heads")
    for i, bit in enumerate(bits):
        if mask >> i & 1:
            if bit == HEADS_BIT:
                heads = 1 - heads
            else:
                dp = dp + (1 << bit) * (1 - 2 * ((dp // (1 << bit)) % 2))
    return {"dp": dp, "heads": heads}


def group_peers(n_dp):
    dp, heads = lax.axis_index("dp"), lax.axis_index("heads")
    fast = min(1 << FAST_BITS, n_dp)
    low, high = dp % fast, dp // fast
    count = 2 * fast
    me = low * 2 + heads
    near = []
    for step in range(1, count):
        other = (me + step) % count
        near.append((other, {"dp": high * fast + other // 2, "heads": other % 2}))
    far = []
    for step in range(1, n_dp // fast):
        other = (high + step) % (n_dp // fast)
        far.append((other, {"dp": other * fast + low, "heads": heads}))
    return (me, near), (high, far)


UNROLL = 16


class Gather:
    def __init__(self, stages, buffer, send_sem, recv_sem):
        self.stages, self.buffer = stages, buffer
        self.send_sem, self.recv_sem = send_sem, recv_sem
        self.bits = own_bits(stages)

    def copy(self, g, held, mask):
        return pltpu.make_async_remote_copy(
            src_ref=held,
            dst_ref=held,
            send_sem=self.send_sem.at[g],
            recv_sem=self.recv_sem.at[g],
            device_id=peer(self.stages[g], mask),
        )

    def start(self, g):
        start = sum(len(stage) for stage in self.stages[:g])
        base = sum((1 << u) * bit for u, bit in enumerate(self.bits) if u >= start)
        held = self.buffer.at[pl.ds(base, 1 << start)]
        for mask in range(1, 1 << len(self.stages[g])):
            self.copy(g, held, mask).start()

    def wait(self, g):
        start = sum(len(stage) for stage in self.stages[:g])
        peers = (1 << len(self.stages[g])) - 1
        every = self.copy(g, self.buffer.at[pl.ds(0, peers << start)], 1)
        every.wait_recv()
        every.wait_send()


class Scatter:
    def __init__(self, stages, window, outgoing, incoming, sums, send_sem, recv_sem):
        self.stages, self.window = stages, window
        self.outgoing, self.incoming, self.sums = outgoing, incoming, sums
        self.send_sem, self.recv_sem = send_sem, recv_sem
        self.bits = own_bits(stages)

    def offset(self, g):
        return sum(len(stage) for stage in self.stages[:g])

    def held(self, g, place):
        if g == len(self.stages) - 1:
            return self.window(place)
        return self.sums[g + 1][place]

    def copy(self, g, mask, at):
        return pltpu.make_async_remote_copy(
            src_ref=self.outgoing[g].at[at],
            dst_ref=self.incoming[g].at[at],
            send_sem=self.send_sem.at[g],
            recv_sem=self.recv_sem.at[g],
            device_id=peer(self.stages[g], mask),
        )

    def part(self, g, mask):
        start = self.offset(g)
        return sum(
            (1 << (start + i)) * (1 - self.bits[start + i] if mask >> i & 1 else self.bits[start + i])
            for i in range(len(self.stages[g]))
        )

    def start(self, g):
        for mask in range(1, 1 << len(self.stages[g])):
            part = self.part(g, mask)

            def fill(i, carry, mask=mask, part=part):
                self.outgoing[g][mask - 1, i] = self.held(g, part + i).astype(bf16)
                return carry

            blocks = 1 << self.offset(g)
            lax.fori_loop(0, blocks, fill, 0, unroll=min(blocks, UNROLL))
            self.copy(g, mask, mask - 1).start()

    def wait(self, g):
        masks = range(1, 1 << len(self.stages[g]))
        self.copy(g, 1, pl.ds(0, len(masks))).wait()
        part = self.part(g, 0)

        def add(i, carry):
            value = self.held(g, part + i)
            for mask in masks:
                value = value + self.incoming[g][mask - 1, i].astype(f32)
            self.sums[g][i] = value
            return carry

        blocks = 1 << self.offset(g)
        lax.fori_loop(0, blocks, add, 0, unroll=min(blocks, UNROLL))


def group_halves(grows):
    first = 16 * (-(-grows // 32))
    return first, grows - first


def scatter_shapes(stages, rows):
    outgoing, sums = [], []
    start = 0
    for stage in stages:
        outgoing.append(((1 << len(stage)) - 1, 1 << start, rows, 128))
        sums.append((1 << start, rows, 128))
        start += len(stage)
    return outgoing, sums


def all_share(me, peers, stat_ref, send_sem, recv_sem):
    def copy(held, device):
        return pltpu.make_async_remote_copy(
            src_ref=held,
            dst_ref=held,
            send_sem=send_sem.at[0],
            recv_sem=recv_sem.at[0],
            device_id=device,
        )

    for _, device in peers:
        copy(stat_ref.at[me], device).start()
    if peers:
        every = copy(stat_ref.at[pl.ds(0, len(peers))], peers[0][1])
        every.wait_recv()
        every.wait_send()
    return jnp.sum(stat_ref[...], axis=0)


def shift_on(rows, amount):
    lanes = amount % 128
    turned = pltpu.roll(rows, lanes, 1)
    lane = lax.broadcasted_iota(jnp.int32, rows.shape, 1)
    turned = jnp.where(lane < lanes, pltpu.roll(turned, 1, 0), turned)
    return pltpu.roll(turned, amount // 128, 0)


def shift_back(rows, amount):
    count = rows.shape[0]
    lanes = amount % 128
    turned = pltpu.roll(rows, (128 - lanes) % 128, 1)
    lane = lax.broadcasted_iota(jnp.int32, rows.shape, 1)
    turned = jnp.where(lane >= 128 - lanes, pltpu.roll(turned, count - 1, 0), turned)
    return pltpu.roll(turned, (count - amount // 128) % count, 0)


def nn(a, b):
    return lax.dot_general(a, b, (((1,), (0,)), ((), ())), preferred_element_type=f32)


def nt(a, b):
    return lax.dot_general(a, b, (((1,), (1,)), ((), ())), preferred_element_type=f32)


def tn(a, b):
    return lax.dot_general(a, b, (((0,), (0,)), ((), ())), preferred_element_type=f32)


def norm_parts(values):
    center = values - jnp.mean(values, axis=-1, keepdims=True)
    inverse = lax.rsqrt(jnp.mean(center * center, axis=-1, keepdims=True) + eps_norm)
    return center * inverse, inverse


def norm_back(grad_after, unit, inverse, gain):
    scaled = grad_after * gain
    return inverse * (
        scaled
        - jnp.mean(scaled, axis=-1, keepdims=True)
        - unit * jnp.mean(scaled * unit, axis=-1, keepdims=True)
    )


def column_sum(values):
    return jnp.sum(values, axis=0, keepdims=True)


def head_masks(dtype):
    lane = lax.broadcasted_iota(jnp.int32, (1, D), 1) % HALF // HD
    return [(lane == h).astype(f32).astype(dtype) for h in range(HEADS)]


def spread_heads(values, masks):
    return jnp.concatenate([values * masks[h] for h in range(HEADS)], axis=0)


def pick_heads(stacked):
    lane = lax.broadcasted_iota(jnp.int32, (STRIPE, D), 1) % HALF
    picked = stacked[(HEADS - 1) * STRIPE :]
    for h in range(HEADS - 2, -1, -1):
        picked = jnp.where(lane < (h + 1) * HD, stacked[h * STRIPE : (h + 1) * STRIPE], picked)
    return picked


def beside(rows):
    return jnp.concatenate([rows[:STRIPE], rows[STRIPE:]], axis=1)


def above(columns):
    return jnp.concatenate([columns[:, :HALF], columns[:, HALF:]], axis=0)


def diagonal(rows):
    gap = jnp.zeros((HALF - STRIPE, HALF), rows.dtype)
    other = jnp.zeros((HALF, HALF), rows.dtype)
    first = jnp.concatenate([rows[:STRIPE], gap], axis=0)
    second = jnp.concatenate([rows[STRIPE:], gap], axis=0)
    return jnp.concatenate(
        [jnp.concatenate([first, other], axis=1), jnp.concatenate([other, second], axis=1)], axis=0
    )


def turn_heads(stacked):
    gap = jnp.zeros((HALF - STRIPE, HALF), stacked.dtype)
    parts = []
    for h in range(HEADS):
        rows = stacked[h * STRIPE : (h + 1) * STRIPE]
        blocks = [
            jnp.concatenate([rows[:, s * HALF : (s + 1) * HALF], gap], axis=0).T for s in range(2)
        ]
        parts.append(jnp.concatenate(blocks, axis=1)[:STRIPE])
    return jnp.concatenate(parts, axis=0)


def row_shift(values, rows):
    if rows == 0:
        return values
    zero = jnp.zeros((abs(rows), values.shape[1]), f32)
    if rows > 0:
        return jnp.concatenate([values[rows:], zero], axis=0)
    return jnp.concatenate([zero, values[:rows]], axis=0)


def neighbours(values, j):
    before, after = pltpu.roll(values, 1, 0), pltpu.roll(values, STRIPE - 1, 0)
    if j == 0:
        row = lax.broadcasted_iota(jnp.int32, values.shape, 0) % 16
        before = jnp.where(row == 8, pltpu.roll(values, 2, 0), before)
        after = jnp.where(row == 6, pltpu.roll(values, STRIPE - 2, 0), after)
    return [before, values, after]


SHIFT = (16, 8)


def tap(j, outer, inner):
    return 3 * outer + inner if j == 0 else 3 * inner + outer


def to_stripes(rows):
    tiles = rows.reshape(SIDE, 2, 8, rows.shape[1])
    return jnp.concatenate(
        [tiles[:, s].reshape(STRIPE, rows.shape[1]) for s in range(2)], axis=0
    )


def from_stripes(columns):
    halves = [columns[:, s * HALF : (s + 1) * HALF].reshape(SIDE, 1, 8, HALF) for s in range(2)]
    return jnp.concatenate(halves, axis=1).reshape(GRID, HALF)


def tile_sum(values):
    return jnp.sum(values.reshape(-1, 8, values.shape[1]), axis=0)


def row_mask():
    row = lax.broadcasted_iota(jnp.int32, (GRID, 1), 0)
    return (row % 8 < SW).astype(f32)


def to_grid(source, tokens, grid_ref):
    images = grid_ref.shape[0]
    grid_ref[...] = jnp.zeros_like(grid_ref)
    for half in range(2):
        cols = slice(half * 128, (half + 1) * 128)
        tokens[half] = source[:, cols].astype(f32)
        for image in range(images):
            for r in range(2 * SIDE):
                grid_ref[image, 8 * r : 8 * r + SW, cols] = tokens[
                    half, pl.ds(r * SW * images + image, SW, stride=images), :
                ]


def from_grid(value, tokens, image, images):
    for half in range(2):
        for r in range(2 * SIDE):
            tokens[half, pl.ds(r * SW * images + image, SW, stride=images), :] = value[
                8 * r : 8 * r + SW, half * 128 : (half + 1) * 128
            ]


def prepare_group(n_dp, stages, sc):
    n = 2 * n_dp
    gflat, buffer = sc["gflat"], sc["gweights"]
    grows = buffer.shape[1]
    gflat[...] = jnp.zeros_like(gflat)
    for k in range(n):
        at = first_row(GROUP_PARAMS, n_dp, k // 2)
        size = grows - CARRIED
        gflat[k % 2, at : at + size] += buffer[place_of(stages, k), 0:size].astype(f32)
    carried = buffer[place_of(stages, n - 1)].astype(f32)[grows - CARRIED :]
    for c in range(2):
        cols = slice(c * 128, (c + 1) * 128)
        sc["vecs"][1:2, cols] = carried[c : c + 1]
        sc["vecs"][2:3, cols] = carried[2 + c : 3 + c]
    for j in range(2):
        for c in range(3):
            cols = slice(j * 384 + c * 128, j * 384 + (c + 1) * 128)
            sc["wq"][:, cols] = gflat[j, pl.ds(c, D, stride=3), :].astype(bf16)
        for c in range(2):
            cols = slice(c * 128, (c + 1) * 128)
            sc["ow"][j * 128 : (j + 1) * 128, cols] = gflat[
                j, pl.ds(770 + c, HALF, stride=2), :
            ].astype(bf16)
        sc["qbias"][:, j * 384 : j * 384 + 128] = gflat[j, 768:769, :]
        sc["qbias"][:, j * 384 + 128 : j * 384 + 256] = jnp.zeros((1, 128), f32)
        sc["qbias"][:, j * 384 + 256 : j * 384 + 384] = gflat[j, 769:770, :]
        for half in range(2):
            cols = slice(half * 128, (half + 1) * 128)
            sc["conv"][j, 0:10, cols] = gflat[j, 1026:1036, :]


def prepare_shared(n_dp, stages, sc):
    n = 2 * n_dp
    flat, buffer = sc["flat"], sc["sweights"]
    srows = buffer.shape[1]
    flat[...] = jnp.zeros_like(flat)
    for k in range(n):
        at = first_row(SHARED_PARAMS, n, k)
        flat[at : at + srows] += buffer[place_of(stages, k)].astype(f32)
    for c in range(8):
        cols = slice(c * 128, (c + 1) * 128)
        sc["uw"][:, cols] = flat[pl.ds(c, D, stride=8), :].astype(bf16)
        sc["ubias"][:, cols] = flat[2048 + c : 2049 + c, :]
    for c in range(2):
        cols = slice(c * 128, (c + 1) * 128)
        sc["dw"][:, cols] = flat[pl.ds(2056 + c, FF, stride=2), :].astype(bf16)
        for i in (0, 3, 4, 5):
            sc["vecs"][i : i + 1, cols] = flat[4104 + 2 * i + c : 4105 + 2 * i + c, :]


def place_shared(sc):
    flat = sc["flat"]
    for c in range(8):
        cols = slice(c * 128, (c + 1) * 128)
        flat[pl.ds(c, D, stride=8), :] = sc["a_uw"][:, cols]
        flat[2048 + c : 2049 + c, :] = column_sum(sc["a_ub"][:, cols])
    for q in range(4):
        turned = sc["a_dwt"][:, q * 256 : (q + 1) * 256].T
        for c in range(2):
            flat[pl.ds(2056 + 512 * q + c, 256, stride=2), :] = turned[
                :, c * 128 : (c + 1) * 128
            ]
    for c in range(2):
        cols = slice(c * 128, (c + 1) * 128)
        for i in (0, 3, 4, 5):
            flat[4104 + 2 * i + c : 4105 + 2 * i + c, :] = column_sum(
                sc["a_vec"][i, :, cols]
            )
    flat[GAIN_ROW : GAIN_ROW + CARRIED, :] = jnp.zeros((CARRIED, 128), f32)


def place_group(sc):
    gflat = sc["gflat"]
    for j in range(2):
        for c in range(3):
            cols = slice(j * 384 + c * 128, j * 384 + (c + 1) * 128)
            gflat[j, pl.ds(c, D, stride=3), :] = sc["a_wq"][:, cols]
        for c in range(2):
            cols = slice(c * 128, (c + 1) * 128)
            gflat[j, pl.ds(770 + c, HALF, stride=2), :] = sc["a_ow"][
                j * 128 : (j + 1) * 128, cols
            ]
        gflat[j, 768:769, :] = column_sum(sc["a_pb"][:, j * 384 : j * 384 + 128])
        gflat[j, 769:770, :] = column_sum(sc["a_pb"][:, j * 384 + 256 : j * 384 + 384])
        for i in range(10):
            both = column_sum(sc["a_conv"][j, i])
            gflat[j, 1026 + i : 1027 + i, :] = both[:, :HALF] + both[:, HALF:]


def first_norm(images, sc):
    for image in images:
        sc["unit"][image], sc["inverse"][image] = norm_parts(sc["x"][image])


def attention_forward(images, sc):
    scale = HD ** (-0.5)
    masks = head_masks(bf16)
    inside = row_mask()
    key_row = lax.broadcasted_iota(jnp.int32, (1, SIDE, 8, D), 2)
    gain_one, shift_one = sc["vecs"][1:2], sc["vecs"][2:3]
    qkv_ref, conv = sc["qkv"], sc["conv"]
    many = len(images)
    for image in images:
        sc["normed"][image] = (sc["unit"][image] * gain_one + shift_one).astype(bf16)
    normed = sc["normed"][pl.ds(images[0], many)].reshape(many * GRID, D)
    triples = nn(normed, sc["wq"][...]) + sc["qbias"][...]
    for i, image in enumerate(images):
        triple = triples[i * GRID : (i + 1) * GRID] * inside
        qkv_ref[image, 0] = triple[:, :384].astype(bf16)
        qkv_ref[image, 1] = to_stripes(triple[:, 384:]).astype(bf16)
    for j in range(2):
        for image in images:
            query = diagonal(qkv_ref[image, j, :, 0:128])
            keys = spread_heads(beside(qkv_ref[image, j, :, 128:256]), masks)
            value = beside(qkv_ref[image, j, :, 256:384])
            scores = nt(keys, query).reshape(HEADS, SIDE, 8, D) * scale
            scores = jnp.where(key_row < SW, scores, -1e30)
            scores = scores.reshape(HEADS, STRIPE, D)
            weights = jnp.exp(scores - jnp.max(scores, axis=1, keepdims=True))
            probs = weights * (1.0 / jnp.sum(weights, axis=1, keepdims=True))
            probs = probs.reshape(HEADS * STRIPE, D)
            sc["probs"][image, j] = probs
            values = diagonal(qkv_ref[image, j, :, 256:384])
            total = pick_heads(nn(turn_heads(probs.astype(bf16)), values)) + conv[j, 9:10]
            near = neighbours(value.astype(f32), j)
            for outer in range(3):
                part = None
                for inner in range(3):
                    k = tap(j, outer, inner)
                    term = near[inner] * conv[j, k : k + 1]
                    part = term if part is None else part + term
                total = total + row_shift(part, SHIFT[j] * (outer - 1))
            both = above(total) if j == 0 else from_stripes(total)
            sc["heads"][image, :, j * 128 : (j + 1) * 128] = both.astype(bf16)


def mlp_output(images, count, drop_ref, sc):
    many = len(images)
    active = sc["active"][pl.ds(images[0], many)].reshape(many * GRID, FF)
    mlp = nn(active, sc["dw"][...]) + sc["vecs"][0:1]
    for i, image in enumerate(images):
        scale_two = drop_ref[1, image].astype(f32) / keep_prob
        value = sc["x"][image] + scale_two * mlp[i * GRID : (i + 1) * GRID]
        from_grid(value, sc["outs"], image, count)


def mlp_both(images, drop_ref, sc):
    gain_two, shift_two, out_bias = sc["vecs"][3:4], sc["vecs"][4:5], sc["vecs"][5:6]
    a_vec = sc["a_vec"]
    uw, dw, ubias = sc["uw"], sc["dw"], sc["ubias"]
    many = len(images)

    def join(parts):
        return jnp.concatenate(parts, axis=0)

    def part_of(joined, i):
        return joined[i * GRID : (i + 1) * GRID]

    heads = sc["heads"][pl.ds(images[0], many)].reshape(many * GRID, D)
    branch = nn(heads, sc["ow"][...])
    state = []
    for i, image in enumerate(images):
        scale_one = drop_ref[0, image].astype(f32) / keep_prob
        scale_two = drop_ref[1, image].astype(f32) / keep_prob
        middle = sc["x"][image] + scale_one * (part_of(branch, i) + out_bias)
        unit_two, inverse_two = norm_parts(middle)
        grad_output = sc["co"][image]
        grad_mlp_f = scale_two * grad_output
        a_vec[0] += tile_sum(grad_mlp_f)
        state.append((scale_one, scale_two, middle, unit_two, inverse_two, grad_output, grad_mlp_f))
    normed_two = join([(st[3] * gain_two + shift_two).astype(bf16) for st in state])
    grad_mlp = join([st[6].astype(bf16) for st in state])
    grad_normed = None
    for c in range(4):
        cols = slice(c * 256, (c + 1) * 256)
        hidden = nn(normed_two, uw[:, cols]) + ubias[:, cols]
        density = jnp.exp(hidden * hidden * -0.5) * (1.0 / math.sqrt(2.0 * math.pi))
        phi = 0.5 + 0.5 * lax.erf(hidden * math.sqrt(0.5))
        active = (hidden * phi).astype(bf16)
        sc["active"][pl.ds(images[0], many), :, cols] = active.reshape(many, GRID, 256)
        sc["a_dwt"][:, cols] += tn(grad_mlp, active)
        grad_active = nt(grad_mlp, dw[cols, :])
        grad_hidden = (grad_active * (phi + hidden * density)).astype(bf16)
        sc["a_ub"][:, cols] += tile_sum(grad_hidden.astype(f32))
        sc["a_uw"][:, cols] += tn(normed_two, grad_hidden)
        part = nt(grad_hidden, uw[:, cols])
        grad_normed = part if grad_normed is None else grad_normed + part
    grad_branch = []
    for i, image in enumerate(images):
        scale_one, _, middle, unit_two, inverse_two, grad_output, _ = state[i]
        sc["x"][image] = middle
        grad = part_of(grad_normed, i)
        a_vec[3] += tile_sum(grad * unit_two)
        a_vec[4] += tile_sum(grad)
        grad_middle = grad_output + norm_back(grad, unit_two, inverse_two, gain_two)
        sc["gmid"][image] = grad_middle
        grad_branch_f = scale_one * grad_middle
        a_vec[5] += tile_sum(grad_branch_f)
        grad_branch.append(grad_branch_f.astype(bf16))
    grad_branch = join(grad_branch)
    sc["a_ow"][...] += tn(heads, grad_branch)
    grad_heads = nt(grad_branch, sc["ow"][...])
    for i, image in enumerate(images):
        grad = part_of(grad_heads, i)
        sc["gheads"][image, :, :128] = grad[:, :128].astype(bf16)
        sc["gheads"][image, :, 128:] = to_stripes(grad[:, 128:]).astype(bf16)


def attention_back(images, sc, now, between):
    scale = HD ** (-0.5)
    masks = head_masks(bf16)
    inside = row_mask()[:STRIPE]
    many = len(images)
    a_conv = sc["a_conv"]
    qkv_ref, conv = sc["qkv"], sc["conv"]
    for j in range(2):
        if j == 1:
            pl.when(now)(between)
        for image in images:
            grad = sc["gheads"][image, :, j * 128 : (j + 1) * 128]
            grad_square = diagonal(grad)
            grad_f = beside(grad).astype(f32)
            query = diagonal(qkv_ref[image, j, :, 0:128])
            value = beside(qkv_ref[image, j, :, 256:384])
            probs = sc["probs"][image, j]
            grad_probs = nt(spread_heads(value, masks), grad_square)
            product = (probs * grad_probs).reshape(HEADS, STRIPE, D)
            inner = jnp.sum(product, axis=1, keepdims=True)
            grad_scores = product - probs.reshape(HEADS, STRIPE, D) * inner
            grad_scores = grad_scores.reshape(HEADS * STRIPE, D).astype(bf16)
            keys = diagonal(qkv_ref[image, j, :, 128:256])
            grad_query = pick_heads(nn(turn_heads(grad_scores), keys)) * scale
            grad_key = pick_heads(nn(grad_scores, query)) * scale
            grad_value = pick_heads(nn(probs.astype(bf16), grad_square))
            near = neighbours(grad_f, j)
            for outer in range(3):
                part = None
                for inner in range(3):
                    k = tap(j, outer, inner)
                    term = near[2 - inner] * conv[j, k : k + 1]
                    part = term if part is None else part + term
                grad_value = grad_value + row_shift(part, SHIFT[j] * (1 - outer))
            grad_value = grad_value * inside
            near = neighbours(value.astype(f32), j)
            step = SHIFT[j]
            for inner in range(3):
                a_conv[j, tap(j, 0, inner)] += tile_sum(grad_f[step:] * near[inner][:-step])
                a_conv[j, tap(j, 1, inner)] += tile_sum(grad_f * near[inner])
                a_conv[j, tap(j, 2, inner)] += tile_sum(grad_f[:-step] * near[inner][step:])
            a_conv[j, 9] += tile_sum(grad_f)
            order = above if j == 0 else from_stripes
            both = jnp.concatenate(
                [order(part) for part in (grad_query, grad_key, grad_value)], axis=1
            ).astype(bf16)
            sc["gtriple"][image, :, j * 384 : (j + 1) * 384] = both
    grad_triple = sc["gtriple"][pl.ds(images[0], many)].reshape(many * GRID, 768)
    normed = sc["normed"][pl.ds(images[0], many)].reshape(many * GRID, D)
    sc["a_pb"][...] += tile_sum(grad_triple.astype(f32))
    sc["a_wq"][...] += tn(normed, grad_triple)


def input_gradient(images, count, sc):
    many = len(images)
    gain_one = sc["vecs"][1:2]
    a_vec = sc["a_vec"]
    grad_triple = sc["gtriple"][pl.ds(images[0], many)].reshape(many * GRID, 768)
    grads = nt(grad_triple, sc["wq"][...])
    for i, image in enumerate(images):
        grad_normed = grads[i * GRID : (i + 1) * GRID]
        unit, inverse = sc["unit"][image], sc["inverse"][image]
        a_vec[1] += tile_sum(grad_normed * unit)
        a_vec[2] += tile_sum(grad_normed)
        grad = sc["gmid"][image] + norm_back(grad_normed, unit, inverse, gain_one)
        from_grid(grad, sc["tokens"], image, count)


def scratch_shapes(n_dp, srows, grows, count):
    n = 2 * n_dp
    flat_rows = max(4120, first_row(SHARED_PARAMS, n, n - 1) + srows)
    gflat_rows = max(1040, first_row(GROUP_PARAMS, n_dp, n_dp - 1) + grows)
    shapes = dict(
        flat=((flat_rows, 128), f32),
        gflat=((2, gflat_rows, 128), f32),
        sweights=((n, srows, 128), bf16),
        gweights=((n, grows, 128), bf16),
        raw=((grows, 128), f32),
        sraw=((srows, 128), f32),
        sown=((SHARED_PARAMS // n,), f32),
        gown=((1, GROUP_PARAMS // n_dp), f32),
        wq=((D, 768), bf16),
        ow=((D, D), bf16),
        uw=((D, FF), bf16),
        dw=((FF, D), bf16),
        qbias=((1, 768), f32),
        ubias=((1, FF), f32),
        vecs=((8, D), f32),
        conv=((2, 16, D), f32),
        a_wq=((D, 768), f32),
        a_ow=((D, D), f32),
        a_uw=((D, FF), f32),
        a_dwt=((D, FF), f32),
        a_pb=((8, 768), f32),
        a_ub=((8, FF), f32),
        a_vec=((6, 8, D), f32),
        a_conv=((2, 10, 8, D), f32),
        x_in=((TOK * count, D), bf16),
        tokens=((2, TOK * count, 128), f32),
        outs=((2, TOK * count, 128), f32),
        x=((count, GRID, D), f32),
        co=((count, GRID, D), f32),
        unit=((count, GRID, D), f32),
        inverse=((count, GRID, 1), f32),
        normed=((count, GRID, D), bf16),
        qkv=((count, 2, GRID, 384), bf16),
        probs=((count, 2, HEADS * STRIPE, D), f32),
        heads=((count, GRID, D), bf16),
        gmid=((count, GRID, D), f32),
        active=((count, GRID, FF), bf16),
        gheads=((count, GRID, D), bf16),
        gtriple=((count, GRID, 768), bf16),
    )
    stages = exchange_stages(n_dp)
    first, second = group_halves(grows)
    for name, rows in (("s", srows), ("g", first), ("h", second)):
        outgoing, sums = scatter_shapes(stages, rows)
        for g, shape in enumerate(outgoing):
            shapes[f"{name}out{g}"] = (shape, bf16)
            shapes[f"{name}in{g}"] = (shape, bf16)
            shapes[f"{name}sum{g}"] = (sums[g], f32)
    fast = min(1 << FAST_BITS, n_dp)
    shapes["near_stat"] = ((2 * fast, 8, 128), f32)
    shapes["far_stat"] = ((n_dp // fast, 8, 128), f32)
    made = {name: pltpu.VMEM(*shape) for name, shape in shapes.items()}
    dma = pltpu.SemaphoreType.DMA
    for name in ("sgather", "ggather", "sscatter", "gscatter", "hscatter"):
        made[name + "_send"] = dma((len(stages),))
        made[name + "_recv"] = dma((len(stages),))
    for name in ("near", "far"):
        made[name + "_send"] = dma((1,))
        made[name + "_recv"] = dma((1,))
    made["local"] = dma((5,))
    made["drops"] = pltpu.SMEM((2, count), jnp.int32)
    return made


ACCUMULATORS = ("a_wq", "a_ow", "a_uw", "a_dwt", "a_pb", "a_ub", "a_vec", "a_conv")
TOGETHER = 2
FORWARD_TOGETHER = 4
BACK_TOGETHER = 4
MLP_TOGETHER = 4
GATHER_STEP = 1
CORE_STEP = 1
OUT_STEP = 3
BACK_IMAGE = 0
OUT_TOGETHER = 2


def own_windows(n_dp, sown_ref, gown_ref, soff, goff, stages, sc):
    n = 2 * n_dp
    mine = sum((1 << t) * bit for t, bit in enumerate(own_bits(stages)))
    raw = sc["sraw"]
    share = sown_ref.shape[0]
    whole = share // UNIT * UNIT
    raw[...] = jnp.zeros_like(raw)
    raw[0 : whole // 128, :] = sown_ref[0:whole].reshape(whole // 128, 128)
    for r in range(whole // 128, -(-share // 128)):
        size = min(128, share - 128 * r)
        raw[r : r + 1, 0:size] = sown_ref[128 * r : 128 * r + size].reshape(1, size)
    window = shift_on(raw[...], soff)
    sc["sweights"][mine] = window.astype(bf16)
    raw = sc["raw"]
    grows = raw.shape[0]
    share = gown_ref.shape[1]
    raw[...] = jnp.zeros_like(raw)
    for r in range(-(-share // 128)):
        size = min(128, share - 128 * r)
        raw[r : r + 1, 0:size] = gown_ref[0:1, 128 * r : 128 * r + size]
    at = GAIN_ROW - first_row(SHARED_PARAMS, n, n - 1)
    raw[...] = shift_on(raw[...], goff)
    raw[grows - CARRIED :, :] = window[at : at + CARRIED]
    sc["gweights"][mine] = raw[...].astype(bf16)


def finish(n_dp, soff, goff, ssum, gsum, smine_ref, gmine_ref, norm_ref, near, far, sc):
    n = 2 * n_dp
    srows, grows = ssum.shape[0], gsum.shape[0]
    sshare, gshare = SHARED_PARAMS // n, GROUP_PARAMS // n_dp
    place = lax.broadcasted_iota(jnp.int32, (srows, 128), 0) * 128
    place = place + lax.broadcasted_iota(jnp.int32, (srows, 128), 1)
    shared = jnp.where((place >= soff) & (place < soff + sshare), ssum, 0.0)
    place = lax.broadcasted_iota(jnp.int32, (grows, 128), 0) * 128
    place = place + lax.broadcasted_iota(jnp.int32, (grows, 128), 1)
    grouped = jnp.where((place >= goff) & (place < goff + gshare), gsum, 0.0)
    near_me, near_peers = near
    far_me, far_peers = far
    squares = column_sum(tile_sum(shared * shared) + tile_sum(grouped * grouped))
    sums = [
        column_sum(sc["a_vec"][i, :, c * 128 : (c + 1) * 128]) for i in (1, 2) for c in range(2)
    ]
    tile = jnp.concatenate([*sums, squares, jnp.zeros((3, 128), f32)], axis=0)
    sc["near_stat"][near_me] = tile
    tile = all_share(near_me, near_peers, sc["near_stat"], sc["near_send"], sc["near_recv"])
    sc["far_stat"][far_me] = tile
    tile = all_share(far_me, far_peers, sc["far_stat"], sc["far_send"], sc["far_recv"])
    carried = tile[:CARRIED]
    total = column_sum(carried * carried) + tile[CARRIED : CARRIED + 1]
    total = jnp.sum(total, axis=1, keepdims=True)
    last = jnp.where(own_number() == n - 1, 1.0, 0.0)
    at = GAIN_ROW - first_row(SHARED_PARAMS, n, n - 1)
    smine_ref[...] = shared
    smine_ref[at : at + CARRIED, :] += carried * last
    shared = smine_ref[...]
    norm = jnp.sqrt(total)
    norm_ref[...] = jnp.broadcast_to(norm, (8, 128))
    threshold = math.sqrt(2 * GROUP_PARAMS + SHARED_PARAMS)
    factor = jnp.minimum(1.0, threshold / (norm + 1e-06))
    smine_ref[...] = shift_back(shared * factor, soff)
    grouped = shift_back(grouped * factor, goff)
    for r in range(-(-gshare // 128)):
        size = min(128, gshare - 128 * r)
        gmine_ref[0:1, 128 * r : 128 * r + size] = grouped[r : r + 1, 0:size]


def step_kernel(
    n_dp,
    count,
    names,
    drop_in,
    x_ref,
    co_ref,
    sown_ref,
    gown_ref,
    out_ref,
    gin_ref,
    smine_ref,
    gmine_ref,
    norm_ref,
    *scratch,
):
    sc = dict(zip(names, scratch))
    n = 2 * n_dp
    stages = exchange_stages(n_dp)
    near, far = group_peers(n_dp)
    devices = [device for _, device in near[1] + far[1]]
    barrier = pltpu.get_barrier_semaphore()
    for device in devices:
        pl.semaphore_signal(barrier, inc=1, device_id=device)
    load_x = pltpu.make_async_copy(x_ref, sc["x_in"], sc["local"].at[0])
    load_co = pltpu.make_async_copy(co_ref, sc["x_in"], sc["local"].at[1])
    loads = [
        pltpu.make_async_copy(source, sc[name], sc["local"].at[2 + i])
        for i, (source, name) in enumerate(
            ((sown_ref, "sown"), (gown_ref, "gown"), (drop_in, "drops"))
        )
    ]
    for load in (*loads, load_x):
        load.start()
    drop_ref = sc["drops"]
    soff = (own_number() * (SHARED_PARAMS // n)) % UNIT
    goff = (lax.axis_index("dp") * (GROUP_PARAMS // n_dp)) % UNIT
    for load in loads:
        load.wait()
    own_windows(n_dp, sc["sown"], sc["gown"], soff, goff, stages, sc)
    load_x.wait()
    to_grid(sc["x_in"], sc["tokens"], sc["x"])
    load_co.start()
    pl.semaphore_wait(barrier, len(devices))
    ggather = Gather(stages, sc["gweights"], sc["ggather_send"], sc["ggather_recv"])
    sgather = Gather(stages, sc["sweights"], sc["sgather_send"], sc["sgather_recv"])

    def run(phase, extra=None, together=TOGETHER):
        def body(i, carry):
            if extra is not None:
                for at, action in extra.items():
                    pl.when(i == at)(action)
            phase([i * together + k for k in range(together)])
            return carry

        lax.fori_loop(0, count // together, body, 0)

    last = len(stages) - 1
    ggather.start(0)
    sgather.start(0)
    for g in range(last):
        if g == last - 1:
            run(lambda images: first_norm(images, sc))
        ggather.wait(g)
        ggather.start(g + 1)
        if g < last - 1:
            sgather.wait(g)
            sgather.start(g + 1)
    for name in ACCUMULATORS:
        sc[name][...] = jnp.zeros_like(sc[name])
    load_co.wait()
    to_grid(sc["x_in"], sc["tokens"], sc["co"])
    ggather.wait(last)
    prepare_group(n_dp, stages, sc)

    def spread_cores():
        sgather.wait(last - 1)
        sgather.start(last)

    steps = count // FORWARD_TOGETHER
    run(
        lambda images: attention_forward(images, sc),
        {min(GATHER_STEP, steps - 1): spread_cores},
        FORWARD_TOGETHER,
    )
    sgather.wait(last)
    prepare_shared(n_dp, stages, sc)
    run(lambda images: mlp_both(images, drop_ref, sc), None, MLP_TOGETHER)
    place_shared(sc)

    srows, grows = sc["sweights"].shape[1], sc["gweights"].shape[1]

    def swindow(place):
        k = device_at(stages, place)
        row = (k * (SHARED_PARAMS // n)) // UNIT * 8
        return sc["flat"][pl.ds(pl.multiple_of(row, 8), srows), :]

    first, second = group_halves(grows)

    def gwindow(begin, size):
        def window(place):
            k = device_at(stages, place)
            row = ((k // 2) * (GROUP_PARAMS // n_dp)) // UNIT * 8 + begin
            return sc["gflat"][k % 2, pl.ds(pl.multiple_of(row, 8), size), :]

        return window

    def scatter(name, window):
        parts = [[sc[f"{name}{kind}{g}"] for g in range(last + 1)] for kind in ("out", "in", "sum")]
        return Scatter(
            stages, window, *parts, sc[name + "scatter_send"], sc[name + "scatter_recv"]
        )

    sscatter = scatter("s", swindow)
    gscatters = (scatter("g", gwindow(0, first)), scatter("h", gwindow(first, second)))
    sscatter.start(last)
    def advance(scatters, g):
        def action():
            for scatter in scatters:
                scatter.wait(g)
                scatter.start(g - 1)

        return action

    run(
        lambda images: attention_back(
            images, sc, images[0] == BACK_IMAGE, advance((sscatter,), last)
        ),
        None,
        BACK_TOGETHER,
    )
    place_group(sc)
    for half in gscatters:
        half.start(last)
    stores = []

    def store(held, target):
        for half in range(2):
            cols = slice(half * 128, (half + 1) * 128)
            copy = pltpu.make_async_copy(
                sc[held].at[half], target.at[:, cols], sc["local"].at[len(stores)]
            )
            copy.start()
            stores.append(copy)

    for g in range(last - 1, 0, -1):
        advance((sscatter,), g)()
    run(lambda images: input_gradient(images, count, sc), {CORE_STEP: advance(gscatters, last)})
    store("tokens", gin_ref)
    for g in range(last - 1, 1, -1):
        advance(gscatters, g)()
    run(
        lambda images: mlp_output(images, count, drop_ref, sc),
        {OUT_STEP: advance(gscatters, 1)} if last > 1 else None,
        OUT_TOGETHER,
    )
    store("outs", out_ref)
    sscatter.wait(0)
    for half in gscatters:
        half.wait(0)
    finish(
        n_dp,
        soff,
        goff,
        sc["ssum0"][0],
        jnp.concatenate([sc["gsum0"][0], sc["hsum0"][0]], axis=0),
        smine_ref,
        gmine_ref,
        norm_ref,
        near,
        far,
        sc,
    )
    for copy in stores:
        copy.wait()


def step(n_dp, drops, images, cotangent, state):
    count = images.shape[0]
    gown, _, _, sown, _, _ = state
    srows = window_rows(SHARED_PARAMS, 2 * n_dp)
    grows = window_rows(GROUP_PARAMS, n_dp, CARRIED)
    shapes = scratch_shapes(n_dp, srows, grows, count)
    vmem = pl.BlockSpec(memory_space=pltpu.VMEM)
    anywhere = pl.BlockSpec(memory_space=pl.ANY)

    def rows(array):
        return jnp.swapaxes(array, 0, 1).reshape(TOK * count, D)

    def unrows(array):
        return jnp.swapaxes(array.reshape(TOK, count, D), 0, 1)

    out, gin, smine, gmine, norm = pl.pallas_call(
        partial(step_kernel, n_dp, count, tuple(shapes)),
        in_specs=[anywhere] * 5,
        out_specs=[anywhere, anywhere, vmem, vmem, vmem],
        out_shape=[jax.ShapeDtypeStruct((TOK * count, D), f32)] * 2
        + [
            jax.ShapeDtypeStruct((srows, 128), f32),
            jax.ShapeDtypeStruct(gown.shape, f32),
            jax.ShapeDtypeStruct((8, 128), f32),
        ],
        scratch_shapes=list(shapes.values()),
        compiler_params=pltpu.CompilerParams(
            collective_id=0, has_side_effects=True, vmem_limit_bytes=62 * 1024 * 1024
        ),
        name="step",
    )(drops.T, rows(images), rows(cotangent), sown, gown)
    first, second, *updated = update(out, gin, smine.reshape(-1), gmine, norm, *state)
    return (unrows(first), unrows(second), *updated)


def adam_step(master, gradient, first, second):
    first_new = beta_one * first + (1.0 - beta_one) * gradient
    second_new = beta_two * second + (1.0 - beta_two) * gradient * gradient
    first_hat = first_new / (1.0 - beta_one**STEP)
    second_hat = second_new / (1.0 - beta_two**STEP)
    master_new = master - learn_rate * (
        first_hat / (jnp.sqrt(second_hat) + adam_eps) + decay_rate * master
    )
    return (master_new, first_new, second_new)


CHUNKS = 1


def update_kernel(*refs):
    big_in, small_in, refs = refs[:2], refs[2:11], refs[11:]
    big_out, small_out, refs = refs[:2], refs[2:13], refs[13:]
    big_buf, refs = refs[:2], refs[2:]
    held_in, held_out, sems = refs[:9], refs[9:20], refs[20:]
    big_load, big_store, small_load, small_store = sems
    size = big_in[0].shape[0] // CHUNKS

    def small_loads():
        for i in range(9):
            yield pltpu.make_async_copy(small_in[i], held_in[i], small_load.at[i])

    loads, stores = [], []
    for i in range(CHUNKS):
        rows = pl.ds(i * size, size)
        for k in range(2):
            held = big_buf[k].at[rows]
            loads.append(pltpu.make_async_copy(big_in[k].at[rows], held, big_load.at[k, i]))
            stores.append(pltpu.make_async_copy(held, big_out[k].at[rows], big_store.at[k, i]))
    small = list(small_loads())
    for load in (*small, *loads):
        load.start()
    for load in small:
        load.wait()
    smine, gmine, norm = held_in[:3]
    states = (held_in[3:6], held_in[6:9])
    held_out[0][...] = norm[0:1, 0:1]
    for gradient, (master, first, second), new in (
        (gmine[...], states[0], held_out[1:6]),
        (smine[0 : states[1][0].shape[0]], states[1], held_out[6:11]),
    ):
        new[0][...] = gradient
        new[1][...], new[2][...], new[3][...] = adam_step(
            master[...], gradient, first[...], second[...]
        )
        new[4][...] = new[1][...].astype(bf16)
    small = [
        pltpu.make_async_copy(held_out[i], small_out[i], small_store.at[i]) for i in range(11)
    ]
    for load, store in zip(loads, stores):
        load.wait()
        store.start()
    for store in small:
        store.start()
    for store in (*stores, *small):
        store.wait()


def update(out, gin, smine, gmine, norm, *state):
    anywhere = pl.BlockSpec(memory_space=pl.ANY)
    like = jax.ShapeDtypeStruct
    news = [like((1, 1), f32)]
    for master in (state[0], state[3]):
        news += [like(master.shape, f32)] * 4 + [like(master.shape, bf16)]
    small = (smine, gmine, norm, *state)
    dma = pltpu.SemaphoreType.DMA
    return pl.pallas_call(
        update_kernel,
        in_specs=[anywhere] * (2 + len(small)),
        out_specs=[anywhere] * (2 + len(news)),
        out_shape=[like(out.shape, f32)] * 2 + news,
        scratch_shapes=[pltpu.VMEM(out.shape, f32)] * 2
        + [pltpu.VMEM(array.shape, array.dtype) for array in (*small, *news)]
        + [dma((2, CHUNKS))] * 2
        + [dma((len(small),)), dma((len(news),))],
        compiler_params=pltpu.CompilerParams(vmem_limit_bytes=62 * 1024 * 1024),
        name="update",
    )(out, gin, *small)


def on_device(
    n_dp,
    images,
    cotangent,
    drop_masks,
    group_master,
    group_m1,
    group_m2,
    shared_master,
    shared_m1,
    shared_m2,
):
    state = (group_master, group_m1, group_m2, shared_master, shared_m1, shared_m2)
    output, input_grad, norm, *updated = step(n_dp, drop_masks, images, cotangent, state)
    return (output, input_grad, norm.reshape(1), *updated)


def solution(mesh):
    both = P(("dp", "heads"))
    rows = P(("dp", "heads"), None, None)
    split = P("heads", "dp")
    in_specs = (rows, rows, P(("dp", "heads"), None), split, split, split, both, both, both)
    out_specs = (rows, rows, P(), split, split, split, split, split, both, both, both, both, both)
    return jax.shard_map(
        partial(on_device, mesh.shape["dp"]),
        mesh=mesh,
        in_specs=in_specs,
        out_specs=out_specs,
        check_vma=False,
    )
```

```python
from functools import partial
import math

import jax
import jax.numpy as jnp
from jax import lax
from jax.experimental import pallas as pl
from jax.experimental.pallas import tpu as pltpu
from jax.sharding import PartitionSpec as P

D = 256
FF = 1024
SIDE = 14
SW = 7
STEP = 10
HD = 32
HALF = 128
GROUP_PARAMS = 132608
SHARED_PARAMS = 526848
TOK = SIDE * SIDE
GRID = 16 * SIDE
STRIPE = 16 * SW
HEADS = HALF // HD
UNIT = 1024

eps_norm = 1e-05
keep_prob = 0.8
beta_one = 0.9
beta_two = 0.999
adam_eps = 1e-08
learn_rate = 0.04
decay_rate = 0.05

f32 = jnp.float32
bf16 = jnp.bfloat16


def window_rows(total, count, extra=0):
    share = total // count
    most = max((share * k) % UNIT + share for k in range(count)) + extra * 128
    return 16 * (-(-most // (2 * UNIT)))


def first_row(total, count, k):
    return (total // count * k) // UNIT * 8


HEADS_BIT = -1
FAST_BITS = 4
CARRIED = 4
GAIN_ROW = 4106


def exchange_stages(n_dp):
    bits = n_dp.bit_length() - 1
    far = list(range(bits - 1, 1, -1))
    stages = [tuple(far[i : i + 2]) for i in range(0, len(far), 2)]
    stages.append((1, HEADS_BIT) if bits > 1 else (HEADS_BIT,))
    if bits > 0:
        stages.append((0,))
    return stages


def weight_of(bit):
    return 1 if bit == HEADS_BIT else 2 << bit


def flat_bits(stages):
    return [bit for stage in stages for bit in stage]


def place_of(stages, k):
    return sum(((k // weight_of(bit)) % 2) << t for t, bit in enumerate(flat_bits(stages)))


def device_at(stages, place, first=0):
    return sum(
        ((place // (1 << t)) % 2) * weight_of(bit)
        for t, bit in enumerate(flat_bits(stages))
        if t >= first
    )


def own_number():
    return lax.axis_index("dp") * 2 + lax.axis_index("heads")


def own_bits(stages):
    me = own_number()
    return [(me // weight_of(bit)) % 2 for bit in flat_bits(stages)]


def peer(bits, mask):
    dp, heads = lax.axis_index("dp"), lax.axis_index("heads")
    for i, bit in enumerate(bits):
        if mask >> i & 1:
            if bit == HEADS_BIT:
                heads = 1 - heads
            else:
                dp = dp + (1 << bit) * (1 - 2 * ((dp // (1 << bit)) % 2))
    return {"dp": dp, "heads": heads}


def group_peers(n_dp):
    dp, heads = lax.axis_index("dp"), lax.axis_index("heads")
    fast = min(1 << FAST_BITS, n_dp)
    low, high = dp % fast, dp // fast
    count = 2 * fast
    me = low * 2 + heads
    near = []
    for step in range(1, count):
        other = (me + step) % count
        near.append((other, {"dp": high * fast + other // 2, "heads": other % 2}))
    far = []
    for step in range(1, n_dp // fast):
        other = (high + step) % (n_dp // fast)
        far.append((other, {"dp": other * fast + low, "heads": heads}))
    return (me, near), (high, far)


UNROLL = 16


class Gather:
    def __init__(self, stages, buffer, send_sem, recv_sem):
        self.stages, self.buffer = stages, buffer
        self.send_sem, self.recv_sem = send_sem, recv_sem
        self.bits = own_bits(stages)

    def copy(self, g, held, mask):
        return pltpu.make_async_remote_copy(
            src_ref=held,
            dst_ref=held,
            send_sem=self.send_sem.at[g],
            recv_sem=self.recv_sem.at[g],
            device_id=peer(self.stages[g], mask),
        )

    def start(self, g):
        start = sum(len(stage) for stage in self.stages[:g])
        base = sum((1 << u) * bit for u, bit in enumerate(self.bits) if u >= start)
        held = self.buffer.at[pl.ds(base, 1 << start)]
        for mask in range(1, 1 << len(self.stages[g])):
            self.copy(g, held, mask).start()

    def wait(self, g):
        start = sum(len(stage) for stage in self.stages[:g])
        peers = (1 << len(self.stages[g])) - 1
        every = self.copy(g, self.buffer.at[pl.ds(0, peers << start)], 1)
        every.wait_recv()
        every.wait_send()


class Scatter:
    def __init__(self, stages, window, outgoing, incoming, sums, send_sem, recv_sem):
        self.stages, self.window = stages, window
        self.outgoing, self.incoming, self.sums = outgoing, incoming, sums
        self.send_sem, self.recv_sem = send_sem, recv_sem
        self.bits = own_bits(stages)

    def offset(self, g):
        return sum(len(stage) for stage in self.stages[:g])

    def held(self, g, place):
        if g == len(self.stages) - 1:
            return self.window(place)
        return self.sums[g + 1][place]

    def copy(self, g, mask, at):
        return pltpu.make_async_remote_copy(
            src_ref=self.outgoing[g].at[at],
            dst_ref=self.incoming[g].at[at],
            send_sem=self.send_sem.at[g],
            recv_sem=self.recv_sem.at[g],
            device_id=peer(self.stages[g], mask),
        )

    def part(self, g, mask):
        start = self.offset(g)
        return sum(
            (1 << (start + i)) * (1 - self.bits[start + i] if mask >> i & 1 else self.bits[start + i])
            for i in range(len(self.stages[g]))
        )

    def start(self, g):
        for mask in range(1, 1 << len(self.stages[g])):
            part = self.part(g, mask)

            def fill(i, carry, mask=mask, part=part):
                self.outgoing[g][mask - 1, i] = self.held(g, part + i).astype(bf16)
                return carry

            blocks = 1 << self.offset(g)
            lax.fori_loop(0, blocks, fill, 0, unroll=min(blocks, UNROLL))
            self.copy(g, mask, mask - 1).start()

    def wait(self, g):
        masks = range(1, 1 << len(self.stages[g]))
        self.copy(g, 1, pl.ds(0, len(masks))).wait()
        part = self.part(g, 0)

        def add(i, carry):
            value = self.held(g, part + i)
            for mask in masks:
                value = value + self.incoming[g][mask - 1, i].astype(f32)
            self.sums[g][i] = value
            return carry

        blocks = 1 << self.offset(g)
        lax.fori_loop(0, blocks, add, 0, unroll=min(blocks, UNROLL))


def group_halves(grows):
    first = 16 * (-(-grows // 32))
    return first, grows - first


def scatter_shapes(stages, rows):
    outgoing, sums = [], []
    start = 0
    for stage in stages:
        outgoing.append(((1 << len(stage)) - 1, 1 << start, rows, 128))
        sums.append((1 << start, rows, 128))
        start += len(stage)
    return outgoing, sums


def all_share(me, peers, stat_ref, send_sem, recv_sem):
    def copy(held, device):
        return pltpu.make_async_remote_copy(
            src_ref=held,
            dst_ref=held,
            send_sem=send_sem.at[0],
            recv_sem=recv_sem.at[0],
            device_id=device,
        )

    for _, device in peers:
        copy(stat_ref.at[me], device).start()
    if peers:
        every = copy(stat_ref.at[pl.ds(0, len(peers))], peers[0][1])
        every.wait_recv()
        every.wait_send()
    return jnp.sum(stat_ref[...], axis=0)


def shift_on(rows, amount):
    lanes = amount % 128
    turned = pltpu.roll(rows, lanes, 1)
    lane = lax.broadcasted_iota(jnp.int32, rows.shape, 1)
    turned = jnp.where(lane < lanes, pltpu.roll(turned, 1, 0), turned)
    return pltpu.roll(turned, amount // 128, 0)


def shift_back(rows, amount):
    count = rows.shape[0]
    lanes = amount % 128
    turned = pltpu.roll(rows, (128 - lanes) % 128, 1)
    lane = lax.broadcasted_iota(jnp.int32, rows.shape, 1)
    turned = jnp.where(lane >= 128 - lanes, pltpu.roll(turned, count - 1, 0), turned)
    return pltpu.roll(turned, (count - amount // 128) % count, 0)


def nn(a, b):
    return lax.dot_general(a, b, (((1,), (0,)), ((), ())), preferred_element_type=f32)


def nt(a, b):
    return lax.dot_general(a, b, (((1,), (1,)), ((), ())), preferred_element_type=f32)


def tn(a, b):
    return lax.dot_general(a, b, (((0,), (0,)), ((), ())), preferred_element_type=f32)


def norm_parts(values):
    center = values - jnp.mean(values, axis=-1, keepdims=True)
    inverse = lax.rsqrt(jnp.mean(center * center, axis=-1, keepdims=True) + eps_norm)
    return center * inverse, inverse


def norm_back(grad_after, unit, inverse, gain):
    scaled = grad_after * gain
    return inverse * (
        scaled
        - jnp.mean(scaled, axis=-1, keepdims=True)
        - unit * jnp.mean(scaled * unit, axis=-1, keepdims=True)
    )


def column_sum(values):
    return jnp.sum(values, axis=0, keepdims=True)


def head_masks(dtype):
    lane = lax.broadcasted_iota(jnp.int32, (1, D), 1) % HALF // HD
    return [(lane == h).astype(f32).astype(dtype) for h in range(HEADS)]


def spread_heads(values, masks):
    return jnp.concatenate([values * masks[h] for h in range(HEADS)], axis=0)


def pick_heads(stacked):
    lane = lax.broadcasted_iota(jnp.int32, (STRIPE, D), 1) % HALF
    picked = stacked[(HEADS - 1) * STRIPE :]
    for h in range(HEADS - 2, -1, -1):
        picked = jnp.where(lane < (h + 1) * HD, stacked[h * STRIPE : (h + 1) * STRIPE], picked)
    return picked


def beside(rows):
    return jnp.concatenate([rows[:STRIPE], rows[STRIPE:]], axis=1)


def above(columns):
    return jnp.concatenate([columns[:, :HALF], columns[:, HALF:]], axis=0)


def diagonal(rows):
    gap = jnp.zeros((HALF - STRIPE, HALF), rows.dtype)
    other = jnp.zeros((HALF, HALF), rows.dtype)
    first = jnp.concatenate([rows[:STRIPE], gap], axis=0)
    second = jnp.concatenate([rows[STRIPE:], gap], axis=0)
    return jnp.concatenate(
        [jnp.concatenate([first, other], axis=1), jnp.concatenate([other, second], axis=1)], axis=0
    )


def turn_heads(stacked):
    gap = jnp.zeros((HALF - STRIPE, HALF), stacked.dtype)
    parts = []
    for h in range(HEADS):
        rows = stacked[h * STRIPE : (h + 1) * STRIPE]
        blocks = [
            jnp.concatenate([rows[:, s * HALF : (s + 1) * HALF], gap], axis=0).T for s in range(2)
        ]
        parts.append(jnp.concatenate(blocks, axis=1)[:STRIPE])
    return jnp.concatenate(parts, axis=0)


def row_shift(values, rows):
    if rows == 0:
        return values
    zero = jnp.zeros((abs(rows), values.shape[1]), f32)
    if rows > 0:
        return jnp.concatenate([values[rows:], zero], axis=0)
    return jnp.concatenate([zero, values[:rows]], axis=0)


def neighbours(values, j):
    before, after = pltpu.roll(values, 1, 0), pltpu.roll(values, STRIPE - 1, 0)
    if j == 0:
        row = lax.broadcasted_iota(jnp.int32, values.shape, 0) % 16
        before = jnp.where(row == 8, pltpu.roll(values, 2, 0), before)
        after = jnp.where(row == 6, pltpu.roll(values, STRIPE - 2, 0), after)
    return [before, values, after]


SHIFT = (16, 8)


def tap(j, outer, inner):
    return 3 * outer + inner if j == 0 else 3 * inner + outer


def to_stripes(rows):
    tiles = rows.reshape(SIDE, 2, 8, rows.shape[1])
    return jnp.concatenate(
        [tiles[:, s].reshape(STRIPE, rows.shape[1]) for s in range(2)], axis=0
    )


def from_stripes(columns):
    halves = [columns[:, s * HALF : (s + 1) * HALF].reshape(SIDE, 1, 8, HALF) for s in range(2)]
    return jnp.concatenate(halves, axis=1).reshape(GRID, HALF)


def tile_sum(values):
    return jnp.sum(values.reshape(-1, 8, values.shape[1]), axis=0)


def row_mask():
    row = lax.broadcasted_iota(jnp.int32, (GRID, 1), 0)
    return (row % 8 < SW).astype(f32)


def to_grid(source, tokens, grid_ref):
    images = grid_ref.shape[0]
    grid_ref[...] = jnp.zeros_like(grid_ref)
    for half in range(2):
        cols = slice(half * 128, (half + 1) * 128)
        tokens[half] = source[:, cols].astype(f32)
        for image in range(images):
            for r in range(2 * SIDE):
                grid_ref[image, 8 * r : 8 * r + SW, cols] = tokens[
                    half, pl.ds(r * SW * images + image, SW, stride=images), :
                ]


def from_grid(value, tokens, image, images):
    for half in range(2):
        for r in range(2 * SIDE):
            tokens[half, pl.ds(r * SW * images + image, SW, stride=images), :] = value[
                8 * r : 8 * r + SW, half * 128 : (half + 1) * 128
            ]


def prepare_group(n_dp, stages, sc):
    n = 2 * n_dp
    gflat, buffer = sc["gflat"], sc["gweights"]
    grows = buffer.shape[1]
    gflat[...] = jnp.zeros_like(gflat)
    for k in range(n):
        at = first_row(GROUP_PARAMS, n_dp, k // 2)
        size = grows - CARRIED
        gflat[k % 2, at : at + size] += buffer[place_of(stages, k), 0:size].astype(f32)
    carried = buffer[place_of(stages, n - 1)].astype(f32)[grows - CARRIED :]
    for c in range(2):
        cols = slice(c * 128, (c + 1) * 128)
        sc["vecs"][1:2, cols] = carried[c : c + 1]
        sc["vecs"][2:3, cols] = carried[2 + c : 3 + c]
    for j in range(2):
        for c in range(3):
            cols = slice(j * 384 + c * 128, j * 384 + (c + 1) * 128)
            sc["wq"][:, cols] = gflat[j, pl.ds(c, D, stride=3), :].astype(bf16)
        for c in range(2):
            cols = slice(c * 128, (c + 1) * 128)
            sc["ow"][j * 128 : (j + 1) * 128, cols] = gflat[
                j, pl.ds(770 + c, HALF, stride=2), :
            ].astype(bf16)
        sc["qbias"][:, j * 384 : j * 384 + 128] = gflat[j, 768:769, :]
        sc["qbias"][:, j * 384 + 128 : j * 384 + 256] = jnp.zeros((1, 128), f32)
        sc["qbias"][:, j * 384 + 256 : j * 384 + 384] = gflat[j, 769:770, :]
        for half in range(2):
            cols = slice(half * 128, (half + 1) * 128)
            sc["conv"][j, 0:10, cols] = gflat[j, 1026:1036, :]


def prepare_shared(n_dp, stages, sc):
    n = 2 * n_dp
    flat, buffer = sc["flat"], sc["sweights"]
    srows = buffer.shape[1]
    done = 0
    for k in range(n):
        at = first_row(SHARED_PARAMS, n, k)
        window = buffer[place_of(stages, k)].astype(f32)
        both = max(done - at, 0)
        if both:
            flat[at:done] += window[:both]
        done = at + srows
        flat[at + both : done] = window[both:]
    for c in range(8):
        cols = slice(c * 128, (c + 1) * 128)
        sc["uw"][:, cols] = flat[pl.ds(c, D, stride=8), :].astype(bf16)
        sc["ubias"][:, cols] = flat[2048 + c : 2049 + c, :]
    for c in range(2):
        cols = slice(c * 128, (c + 1) * 128)
        sc["dw"][:, cols] = flat[pl.ds(2056 + c, FF, stride=2), :].astype(bf16)
        for i in (0, 3, 4, 5):
            sc["vecs"][i : i + 1, cols] = flat[4104 + 2 * i + c : 4105 + 2 * i + c, :]


def place_shared(sc):
    flat = sc["flat"]
    for c in range(8):
        cols = slice(c * 128, (c + 1) * 128)
        flat[pl.ds(c, D, stride=8), :] = sc["a_uw"][:, cols]
        flat[2048 + c : 2049 + c, :] = column_sum(sc["a_ub"][:, cols])
    for q in range(4):
        turned = sc["a_dwt"][:, q * 256 : (q + 1) * 256].T
        for c in range(2):
            flat[pl.ds(2056 + 512 * q + c, 256, stride=2), :] = turned[
                :, c * 128 : (c + 1) * 128
            ]
    for c in range(2):
        cols = slice(c * 128, (c + 1) * 128)
        for i in (0, 3, 4, 5):
            flat[4104 + 2 * i + c : 4105 + 2 * i + c, :] = column_sum(
                sc["a_vec"][i, :, cols]
            )
    flat[GAIN_ROW : GAIN_ROW + CARRIED, :] = jnp.zeros((CARRIED, 128), f32)


def place_group(sc):
    gflat = sc["gflat"]
    for j in range(2):
        for c in range(3):
            cols = slice(j * 384 + c * 128, j * 384 + (c + 1) * 128)
            gflat[j, pl.ds(c, D, stride=3), :] = sc["a_wq"][:, cols]
        for c in range(2):
            cols = slice(c * 128, (c + 1) * 128)
            gflat[j, pl.ds(770 + c, HALF, stride=2), :] = sc["a_ow"][
                j * 128 : (j + 1) * 128, cols
            ]
        gflat[j, 768:769, :] = column_sum(sc["a_pb"][:, j * 384 : j * 384 + 128])
        gflat[j, 769:770, :] = column_sum(sc["a_pb"][:, j * 384 + 256 : j * 384 + 384])
        for i in range(10):
            both = column_sum(sc["a_conv"][j, i])
            gflat[j, 1026 + i : 1027 + i, :] = both[:, :HALF] + both[:, HALF:]


def first_norm(images, sc):
    for image in images:
        sc["unit"][image], sc["inverse"][image] = norm_parts(sc["x"][image])


def attention_forward(images, sc):
    scale = HD ** (-0.5)
    masks = head_masks(bf16)
    inside = row_mask()
    key_row = lax.broadcasted_iota(jnp.int32, (1, SIDE, 8, D), 2)
    gain_one, shift_one = sc["vecs"][1:2], sc["vecs"][2:3]
    qkv_ref, conv = sc["qkv"], sc["conv"]
    many = len(images)
    for image in images:
        sc["normed"][image] = (sc["unit"][image] * gain_one + shift_one).astype(bf16)
    normed = sc["normed"][pl.ds(images[0], many)].reshape(many * GRID, D)
    triples = nn(normed, sc["wq"][...]) + sc["qbias"][...]
    for i, image in enumerate(images):
        triple = triples[i * GRID : (i + 1) * GRID] * inside
        qkv_ref[image, 0] = triple[:, :384].astype(bf16)
        qkv_ref[image, 1] = to_stripes(triple[:, 384:]).astype(bf16)
    for j in range(2):
        for image in images:
            query = diagonal(qkv_ref[image, j, :, 0:128])
            keys = spread_heads(beside(qkv_ref[image, j, :, 128:256]), masks)
            value = beside(qkv_ref[image, j, :, 256:384])
            scores = nt(keys, query).reshape(HEADS, SIDE, 8, D) * scale
            scores = jnp.where(key_row < SW, scores, -jnp.inf)
            scores = scores.reshape(HEADS, STRIPE, D)
            weights = jnp.exp(scores - jnp.max(scores, axis=1, keepdims=True))
            probs = weights * (1.0 / jnp.sum(weights, axis=1, keepdims=True))
            probs = probs.reshape(HEADS * STRIPE, D)
            sc["probs"][image, j] = probs
            values = diagonal(qkv_ref[image, j, :, 256:384])
            total = pick_heads(nn(turn_heads(probs.astype(bf16)), values)) + conv[j, 9:10]
            near = neighbours(value.astype(f32), j)
            for outer in range(3):
                part = None
                for inner in range(3):
                    k = tap(j, outer, inner)
                    term = near[inner] * conv[j, k : k + 1]
                    part = term if part is None else part + term
                total = total + row_shift(part, SHIFT[j] * (outer - 1))
            both = above(total) if j == 0 else from_stripes(total)
            sc["heads"][image, :, j * 128 : (j + 1) * 128] = both.astype(bf16)


def mlp_output(images, count, drop_ref, sc):
    many = len(images)
    active = sc["active"][pl.ds(images[0], many)].reshape(many * GRID, FF)
    mlp = nn(active, sc["dw"][...]) + sc["vecs"][0:1]
    for i, image in enumerate(images):
        scale_two = drop_ref[1, image].astype(f32) / keep_prob
        value = sc["x"][image] + scale_two * mlp[i * GRID : (i + 1) * GRID]
        from_grid(value, sc["outs"], image, count)


def mlp_both(images, drop_ref, sc):
    gain_two, shift_two, out_bias = sc["vecs"][3:4], sc["vecs"][4:5], sc["vecs"][5:6]
    a_vec = sc["a_vec"]
    uw, dw, ubias = sc["uw"], sc["dw"], sc["ubias"]
    many = len(images)

    def join(parts):
        return jnp.concatenate(parts, axis=0)

    def part_of(joined, i):
        return joined[i * GRID : (i + 1) * GRID]

    heads = sc["heads"][pl.ds(images[0], many)].reshape(many * GRID, D)
    branch = nn(heads, sc["ow"][...])
    state = []
    for i, image in enumerate(images):
        scale_one = drop_ref[0, image].astype(f32) / keep_prob
        scale_two = drop_ref[1, image].astype(f32) / keep_prob
        middle = sc["x"][image] + scale_one * (part_of(branch, i) + out_bias)
        unit_two, inverse_two = norm_parts(middle)
        grad_output = sc["co"][image]
        grad_mlp_f = scale_two * grad_output
        a_vec[0] += tile_sum(grad_mlp_f)
        state.append((scale_one, scale_two, middle, unit_two, inverse_two, grad_output, grad_mlp_f))
    normed_two = join([(st[3] * gain_two + shift_two).astype(bf16) for st in state])
    grad_mlp = join([st[6].astype(bf16) for st in state])
    grad_normed = None
    for c in range(4):
        cols = slice(c * 256, (c + 1) * 256)
        hidden = nn(normed_two, uw[:, cols]) + ubias[:, cols]
        density = jnp.exp(hidden * hidden * -0.5) * (1.0 / math.sqrt(2.0 * math.pi))
        phi = 0.5 + 0.5 * lax.erf(hidden * math.sqrt(0.5))
        active = (hidden * phi).astype(bf16)
        sc["active"][pl.ds(images[0], many), :, cols] = active.reshape(many, GRID, 256)
        sc["a_dwt"][:, cols] += tn(grad_mlp, active)
        grad_active = nt(grad_mlp, dw[cols, :])
        grad_hidden = (grad_active * (phi + hidden * density)).astype(bf16)
        sc["a_ub"][:, cols] += tile_sum(grad_hidden.astype(f32))
        sc["a_uw"][:, cols] += tn(normed_two, grad_hidden)
        part = nt(grad_hidden, uw[:, cols])
        grad_normed = part if grad_normed is None else grad_normed + part
    grad_branch = []
    for i, image in enumerate(images):
        scale_one, _, middle, unit_two, inverse_two, grad_output, _ = state[i]
        sc["x"][image] = middle
        grad = part_of(grad_normed, i)
        a_vec[3] += tile_sum(grad * unit_two)
        a_vec[4] += tile_sum(grad)
        grad_middle = grad_output + norm_back(grad, unit_two, inverse_two, gain_two)
        sc["gmid"][image] = grad_middle
        grad_branch_f = scale_one * grad_middle
        a_vec[5] += tile_sum(grad_branch_f)
        grad_branch.append(grad_branch_f.astype(bf16))
    grad_branch = join(grad_branch)
    sc["a_ow"][...] += tn(heads, grad_branch)
    grad_heads = nt(grad_branch, sc["ow"][...])
    for i, image in enumerate(images):
        grad = part_of(grad_heads, i)
        sc["gheads"][image, :, :128] = grad[:, :128].astype(bf16)
        sc["gheads"][image, :, 128:] = to_stripes(grad[:, 128:]).astype(bf16)


def attention_back(images, sc, now, between):
    scale = HD ** (-0.5)
    masks = head_masks(bf16)
    inside = row_mask()[:STRIPE]
    many = len(images)
    a_conv = sc["a_conv"]
    qkv_ref, conv = sc["qkv"], sc["conv"]
    for j in range(2):
        if j == 1:
            pl.when(now)(between)
        for image in images:
            grad = sc["gheads"][image, :, j * 128 : (j + 1) * 128]
            grad_square = diagonal(grad)
            grad_f = beside(grad).astype(f32)
            query = diagonal(qkv_ref[image, j, :, 0:128])
            value = beside(qkv_ref[image, j, :, 256:384])
            probs = sc["probs"][image, j]
            grad_probs = nt(spread_heads(value, masks), grad_square)
            product = (probs * grad_probs).reshape(HEADS, STRIPE, D)
            inner = jnp.sum(product, axis=1, keepdims=True)
            grad_scores = product - probs.reshape(HEADS, STRIPE, D) * inner
            grad_scores = grad_scores.reshape(HEADS * STRIPE, D).astype(bf16)
            keys = diagonal(qkv_ref[image, j, :, 128:256])
            grad_query = pick_heads(nn(turn_heads(grad_scores), keys)) * scale
            grad_key = pick_heads(nn(grad_scores, query)) * scale
            grad_value = pick_heads(nn(probs.astype(bf16), grad_square))
            near = neighbours(grad_f, j)
            for outer in range(3):
                part = None
                for inner in range(3):
                    k = tap(j, outer, inner)
                    term = near[2 - inner] * conv[j, k : k + 1]
                    part = term if part is None else part + term
                grad_value = grad_value + row_shift(part, SHIFT[j] * (1 - outer))
            grad_value = grad_value * inside
            near = neighbours(value.astype(f32), j)
            step = SHIFT[j]
            for inner in range(3):
                a_conv[j, tap(j, 0, inner)] += tile_sum(grad_f[step:] * near[inner][:-step])
                a_conv[j, tap(j, 1, inner)] += tile_sum(grad_f * near[inner])
                a_conv[j, tap(j, 2, inner)] += tile_sum(grad_f[:-step] * near[inner][step:])
            a_conv[j, 9] += tile_sum(grad_f)
            order = above if j == 0 else from_stripes
            both = jnp.concatenate(
                [order(part) for part in (grad_query, grad_key, grad_value)], axis=1
            ).astype(bf16)
            sc["gtriple"][image, :, j * 384 : (j + 1) * 384] = both
    grad_triple = sc["gtriple"][pl.ds(images[0], many)].reshape(many * GRID, 768)
    normed = sc["normed"][pl.ds(images[0], many)].reshape(many * GRID, D)
    sc["a_pb"][...] += tile_sum(grad_triple.astype(f32))
    sc["a_wq"][...] += tn(normed, grad_triple)


def input_gradient(images, count, sc):
    many = len(images)
    gain_one = sc["vecs"][1:2]
    a_vec = sc["a_vec"]
    grad_triple = sc["gtriple"][pl.ds(images[0], many)].reshape(many * GRID, 768)
    grads = nt(grad_triple, sc["wq"][...])
    for i, image in enumerate(images):
        grad_normed = grads[i * GRID : (i + 1) * GRID]
        unit, inverse = sc["unit"][image], sc["inverse"][image]
        a_vec[1] += tile_sum(grad_normed * unit)
        a_vec[2] += tile_sum(grad_normed)
        grad = sc["gmid"][image] + norm_back(grad_normed, unit, inverse, gain_one)
        from_grid(grad, sc["tokens"], image, count)


def scratch_shapes(n_dp, srows, grows, count):
    n = 2 * n_dp
    flat_rows = max(4120, first_row(SHARED_PARAMS, n, n - 1) + srows)
    gflat_rows = max(1040, first_row(GROUP_PARAMS, n_dp, n_dp - 1) + grows)
    shapes = dict(
        flat=((flat_rows, 128), f32),
        gflat=((2, gflat_rows, 128), f32),
        sweights=((n, srows, 128), bf16),
        gweights=((n, grows, 128), bf16),
        raw=((grows, 128), f32),
        sraw=((srows, 128), f32),
        sown=((SHARED_PARAMS // n,), f32),
        gown=((1, GROUP_PARAMS // n_dp), f32),
        wq=((D, 768), bf16),
        ow=((D, D), bf16),
        uw=((D, FF), bf16),
        dw=((FF, D), bf16),
        qbias=((1, 768), f32),
        ubias=((1, FF), f32),
        vecs=((8, D), f32),
        conv=((2, 16, D), f32),
        a_wq=((D, 768), f32),
        a_ow=((D, D), f32),
        a_uw=((D, FF), f32),
        a_dwt=((D, FF), f32),
        a_pb=((8, 768), f32),
        a_ub=((8, FF), f32),
        a_vec=((6, 8, D), f32),
        a_conv=((2, 10, 8, D), f32),
        x_in=((TOK * count, D), bf16),
        tokens=((2, TOK * count, 128), f32),
        outs=((2, TOK * count, 128), f32),
        x=((count, GRID, D), f32),
        co=((count, GRID, D), f32),
        unit=((count, GRID, D), f32),
        inverse=((count, GRID, 1), f32),
        normed=((count, GRID, D), bf16),
        qkv=((count, 2, GRID, 384), bf16),
        probs=((count, 2, HEADS * STRIPE, D), f32),
        heads=((count, GRID, D), bf16),
        gmid=((count, GRID, D), f32),
        active=((count, GRID, FF), bf16),
        gheads=((count, GRID, D), bf16),
        gtriple=((count, GRID, 768), bf16),
    )
    stages = exchange_stages(n_dp)
    first, second = group_halves(grows)
    for name, rows in (("s", srows), ("g", first), ("h", second)):
        outgoing, sums = scatter_shapes(stages, rows)
        for g, shape in enumerate(outgoing):
            shapes[f"{name}out{g}"] = (shape, bf16)
            shapes[f"{name}in{g}"] = (shape, bf16)
            shapes[f"{name}sum{g}"] = (sums[g], f32)
    fast = min(1 << FAST_BITS, n_dp)
    shapes["near_stat"] = ((2 * fast, 8, 128), f32)
    shapes["far_stat"] = ((n_dp // fast, 8, 128), f32)
    made = {name: pltpu.VMEM(*shape) for name, shape in shapes.items()}
    dma = pltpu.SemaphoreType.DMA
    for name in ("sgather", "ggather", "sscatter", "gscatter", "hscatter"):
        made[name + "_send"] = dma((len(stages),))
        made[name + "_recv"] = dma((len(stages),))
    for name in ("near", "far"):
        made[name + "_send"] = dma((1,))
        made[name + "_recv"] = dma((1,))
    made["local"] = dma((5,))
    made["drops"] = pltpu.SMEM((2, count), jnp.int32)
    return made


ACCUMULATORS = ("a_wq", "a_ow", "a_uw", "a_dwt", "a_pb", "a_ub", "a_vec", "a_conv")
TOGETHER = 2
FORWARD_TOGETHER = 4
BACK_TOGETHER = 4
MLP_TOGETHER = 4
GATHER_STEP = 1
CORE_STEP = 1
OUT_STEP = 3
BACK_IMAGE = 0
OUT_TOGETHER = 2


def own_windows(n_dp, sown_ref, gown_ref, soff, goff, stages, sc):
    n = 2 * n_dp
    mine = sum((1 << t) * bit for t, bit in enumerate(own_bits(stages)))
    raw = sc["sraw"]
    share = sown_ref.shape[0]
    whole = share // UNIT * UNIT
    raw[...] = jnp.zeros_like(raw)
    raw[0 : whole // 128, :] = sown_ref[0:whole].reshape(whole // 128, 128)
    for r in range(whole // 128, -(-share // 128)):
        size = min(128, share - 128 * r)
        raw[r : r + 1, 0:size] = sown_ref[128 * r : 128 * r + size].reshape(1, size)
    window = shift_on(raw[...], soff)
    sc["sweights"][mine] = window.astype(bf16)
    raw = sc["raw"]
    grows = raw.shape[0]
    share = gown_ref.shape[1]
    raw[...] = jnp.zeros_like(raw)
    for r in range(-(-share // 128)):
        size = min(128, share - 128 * r)
        raw[r : r + 1, 0:size] = gown_ref[0:1, 128 * r : 128 * r + size]
    at = GAIN_ROW - first_row(SHARED_PARAMS, n, n - 1)
    raw[...] = shift_on(raw[...], goff)
    raw[grows - CARRIED :, :] = window[at : at + CARRIED]
    sc["gweights"][mine] = raw[...].astype(bf16)


def finish(n_dp, soff, goff, ssum, gsum, smine_ref, gmine_ref, norm_ref, near, far, sc):
    n = 2 * n_dp
    srows, grows = ssum.shape[0], gsum.shape[0]
    sshare, gshare = SHARED_PARAMS // n, GROUP_PARAMS // n_dp
    place = lax.broadcasted_iota(jnp.int32, (srows, 128), 0) * 128
    place = place + lax.broadcasted_iota(jnp.int32, (srows, 128), 1)
    shared = jnp.where((place >= soff) & (place < soff + sshare), ssum, 0.0)
    place = lax.broadcasted_iota(jnp.int32, (grows, 128), 0) * 128
    place = place + lax.broadcasted_iota(jnp.int32, (grows, 128), 1)
    grouped = jnp.where((place >= goff) & (place < goff + gshare), gsum, 0.0)
    near_me, near_peers = near
    far_me, far_peers = far
    squares = column_sum(tile_sum(shared * shared) + tile_sum(grouped * grouped))
    sums = [
        column_sum(sc["a_vec"][i, :, c * 128 : (c + 1) * 128]) for i in (1, 2) for c in range(2)
    ]
    tile = jnp.concatenate([*sums, squares, jnp.zeros((3, 128), f32)], axis=0)
    sc["near_stat"][near_me] = tile
    tile = all_share(near_me, near_peers, sc["near_stat"], sc["near_send"], sc["near_recv"])
    sc["far_stat"][far_me] = tile
    tile = all_share(far_me, far_peers, sc["far_stat"], sc["far_send"], sc["far_recv"])
    carried = tile[:CARRIED]
    total = column_sum(carried * carried) + tile[CARRIED : CARRIED + 1]
    total = jnp.sum(total, axis=1, keepdims=True)
    last = jnp.where(own_number() == n - 1, 1.0, 0.0)
    at = GAIN_ROW - first_row(SHARED_PARAMS, n, n - 1)
    smine_ref[...] = shared
    smine_ref[at : at + CARRIED, :] += carried * last
    shared = smine_ref[...]
    norm = jnp.sqrt(total)
    norm_ref[...] = jnp.broadcast_to(norm, (8, 128))
    threshold = math.sqrt(2 * GROUP_PARAMS + SHARED_PARAMS)
    factor = jnp.minimum(1.0, threshold / (norm + 1e-06))
    smine_ref[...] = shift_back(shared * factor, soff)
    grouped = shift_back(grouped * factor, goff)
    for r in range(-(-gshare // 128)):
        size = min(128, gshare - 128 * r)
        gmine_ref[0:1, 128 * r : 128 * r + size] = grouped[r : r + 1, 0:size]


def step_kernel(
    n_dp,
    count,
    names,
    drop_in,
    x_ref,
    co_ref,
    sown_ref,
    gown_ref,
    out_ref,
    gin_ref,
    smine_ref,
    gmine_ref,
    norm_ref,
    *scratch,
):
    sc = dict(zip(names, scratch))
    n = 2 * n_dp
    stages = exchange_stages(n_dp)
    near, far = group_peers(n_dp)
    devices = [device for _, device in near[1] + far[1]]
    barrier = pltpu.get_barrier_semaphore()
    for device in devices:
        pl.semaphore_signal(barrier, inc=1, device_id=device)
    load_x = pltpu.make_async_copy(x_ref, sc["x_in"], sc["local"].at[0])
    load_co = pltpu.make_async_copy(co_ref, sc["x_in"], sc["local"].at[1])
    loads = [
        pltpu.make_async_copy(source, sc[name], sc["local"].at[2 + i])
        for i, (source, name) in enumerate(
            ((sown_ref, "sown"), (gown_ref, "gown"), (drop_in, "drops"))
        )
    ]
    for load in (*loads, load_x):
        load.start()
    drop_ref = sc["drops"]
    soff = (own_number() * (SHARED_PARAMS // n)) % UNIT
    goff = (lax.axis_index("dp") * (GROUP_PARAMS // n_dp)) % UNIT
    for load in loads:
        load.wait()
    own_windows(n_dp, sc["sown"], sc["gown"], soff, goff, stages, sc)
    load_x.wait()
    to_grid(sc["x_in"], sc["tokens"], sc["x"])
    load_co.start()
    pl.semaphore_wait(barrier, len(devices))
    ggather = Gather(stages, sc["gweights"], sc["ggather_send"], sc["ggather_recv"])
    sgather = Gather(stages, sc["sweights"], sc["sgather_send"], sc["sgather_recv"])

    def run(phase, extra=None, together=TOGETHER):
        def body(i, carry):
            if extra is not None:
                for at, action in extra.items():
                    pl.when(i == at)(action)
            phase([i * together + k for k in range(together)])
            return carry

        lax.fori_loop(0, count // together, body, 0)

    last = len(stages) - 1
    ggather.start(0)
    sgather.start(0)
    for g in range(last):
        if g == last - 1:
            run(lambda images: first_norm(images, sc))
        ggather.wait(g)
        ggather.start(g + 1)
        if g < last - 1:
            sgather.wait(g)
            sgather.start(g + 1)
    for name in ACCUMULATORS:
        sc[name][...] = jnp.zeros_like(sc[name])
    load_co.wait()
    to_grid(sc["x_in"], sc["tokens"], sc["co"])
    ggather.wait(last)
    prepare_group(n_dp, stages, sc)

    def spread_cores():
        sgather.wait(last - 1)
        sgather.start(last)

    steps = count // FORWARD_TOGETHER
    run(
        lambda images: attention_forward(images, sc),
        {min(GATHER_STEP, steps - 1): spread_cores},
        FORWARD_TOGETHER,
    )
    sgather.wait(last)
    prepare_shared(n_dp, stages, sc)
    run(lambda images: mlp_both(images, drop_ref, sc), None, MLP_TOGETHER)
    place_shared(sc)

    srows, grows = sc["sweights"].shape[1], sc["gweights"].shape[1]

    def swindow(place):
        k = device_at(stages, place)
        row = (k * (SHARED_PARAMS // n)) // UNIT * 8
        return sc["flat"][pl.ds(pl.multiple_of(row, 8), srows), :]

    first, second = group_halves(grows)

    def gwindow(begin, size):
        def window(place):
            k = device_at(stages, place)
            row = ((k // 2) * (GROUP_PARAMS // n_dp)) // UNIT * 8 + begin
            return sc["gflat"][k % 2, pl.ds(pl.multiple_of(row, 8), size), :]

        return window

    def scatter(name, window):
        parts = [[sc[f"{name}{kind}{g}"] for g in range(last + 1)] for kind in ("out", "in", "sum")]
        return Scatter(
            stages, window, *parts, sc[name + "scatter_send"], sc[name + "scatter_recv"]
        )

    sscatter = scatter("s", swindow)
    gscatters = (scatter("g", gwindow(0, first)), scatter("h", gwindow(first, second)))
    sscatter.start(last)
    def advance(scatters, g):
        def action():
            for scatter in scatters:
                scatter.wait(g)
                scatter.start(g - 1)

        return action

    run(
        lambda images: attention_back(
            images, sc, images[0] == BACK_IMAGE, advance((sscatter,), last)
        ),
        None,
        BACK_TOGETHER,
    )
    place_group(sc)
    for half in gscatters:
        half.start(last)
    stores = []

    def store(held, target):
        for half in range(2):
            cols = slice(half * 128, (half + 1) * 128)
            copy = pltpu.make_async_copy(
                sc[held].at[half], target.at[:, cols], sc["local"].at[len(stores)]
            )
            copy.start()
            stores.append(copy)

    for g in range(last - 1, 0, -1):
        advance((sscatter,), g)()
    run(lambda images: input_gradient(images, count, sc), {CORE_STEP: advance(gscatters, last)})
    store("tokens", gin_ref)
    for g in range(last - 1, 1, -1):
        advance(gscatters, g)()
    run(
        lambda images: mlp_output(images, count, drop_ref, sc),
        {OUT_STEP: advance(gscatters, 1)} if last > 1 else None,
        OUT_TOGETHER,
    )
    store("outs", out_ref)
    sscatter.wait(0)
    for half in gscatters:
        half.wait(0)
    finish(
        n_dp,
        soff,
        goff,
        sc["ssum0"][0],
        jnp.concatenate([sc["gsum0"][0], sc["hsum0"][0]], axis=0),
        smine_ref,
        gmine_ref,
        norm_ref,
        near,
        far,
        sc,
    )
    for copy in stores:
        copy.wait()


def step(n_dp, drops, images, cotangent, state):
    count = images.shape[0]
    gown, _, _, sown, _, _ = state
    srows = window_rows(SHARED_PARAMS, 2 * n_dp)
    grows = window_rows(GROUP_PARAMS, n_dp, CARRIED)
    shapes = scratch_shapes(n_dp, srows, grows, count)
    vmem = pl.BlockSpec(memory_space=pltpu.VMEM)
    anywhere = pl.BlockSpec(memory_space=pl.ANY)

    def rows(array):
        return jnp.swapaxes(array, 0, 1).reshape(TOK * count, D)

    def unrows(array):
        return jnp.swapaxes(array.reshape(TOK, count, D), 0, 1)

    out, gin, smine, gmine, norm = pl.pallas_call(
        partial(step_kernel, n_dp, count, tuple(shapes)),
        in_specs=[anywhere] * 5,
        out_specs=[anywhere, anywhere, vmem, vmem, vmem],
        out_shape=[jax.ShapeDtypeStruct((TOK * count, D), f32)] * 2
        + [
            jax.ShapeDtypeStruct((srows, 128), f32),
            jax.ShapeDtypeStruct(gown.shape, f32),
            jax.ShapeDtypeStruct((8, 128), f32),
        ],
        scratch_shapes=list(shapes.values()),
        compiler_params=pltpu.CompilerParams(
            collective_id=0, has_side_effects=True, vmem_limit_bytes=62 * 1024 * 1024
        ),
        name="step",
    )(drops.T, rows(images), rows(cotangent), sown, gown)
    first, second, *updated = update(out, gin, smine.reshape(-1), gmine, norm, *state)
    return (unrows(first), unrows(second), *updated)


def adam_step(master, gradient, first, second):
    first_new = beta_one * first + (1.0 - beta_one) * gradient
    second_new = beta_two * second + (1.0 - beta_two) * gradient * gradient
    first_hat = first_new / (1.0 - beta_one**STEP)
    second_hat = second_new / (1.0 - beta_two**STEP)
    master_new = master - learn_rate * (
        first_hat / (jnp.sqrt(second_hat) + adam_eps) + decay_rate * master
    )
    return (master_new, first_new, second_new)


CHUNKS = 1


def update_kernel(*refs):
    big_in, small_in, refs = refs[:2], refs[2:11], refs[11:]
    big_out, small_out, refs = refs[:2], refs[2:13], refs[13:]
    big_buf, refs = refs[:2], refs[2:]
    held_in, held_out, sems = refs[:9], refs[9:20], refs[20:]
    big_load, big_store, small_load, small_store = sems
    size = big_in[0].shape[0] // CHUNKS

    def small_loads():
        for i in range(9):
            yield pltpu.make_async_copy(small_in[i], held_in[i], small_load.at[i])

    loads, stores = [], []
    for i in range(CHUNKS):
        rows = pl.ds(i * size, size)
        for k in range(2):
            held = big_buf[k].at[rows]
            loads.append(pltpu.make_async_copy(big_in[k].at[rows], held, big_load.at[k, i]))
            stores.append(pltpu.make_async_copy(held, big_out[k].at[rows], big_store.at[k, i]))
    small = list(small_loads())
    for load in (*small, *loads):
        load.start()
    for load in small:
        load.wait()
    smine, gmine, norm = held_in[:3]
    states = (held_in[3:6], held_in[6:9])
    held_out[0][...] = norm[0:1, 0:1]
    for gradient, (master, first, second), new in (
        (gmine[...], states[0], held_out[1:6]),
        (smine[0 : states[1][0].shape[0]], states[1], held_out[6:11]),
    ):
        new[0][...] = gradient
        new[1][...], new[2][...], new[3][...] = adam_step(
            master[...], gradient, first[...], second[...]
        )
        new[4][...] = new[1][...].astype(bf16)
    small = [
        pltpu.make_async_copy(held_out[i], small_out[i], small_store.at[i]) for i in range(11)
    ]
    for load, store in zip(loads, stores):
        load.wait()
        store.start()
    for store in small:
        store.start()
    for store in (*stores, *small):
        store.wait()


def update(out, gin, smine, gmine, norm, *state):
    anywhere = pl.BlockSpec(memory_space=pl.ANY)
    like = jax.ShapeDtypeStruct
    news = [like((1, 1), f32)]
    for master in (state[0], state[3]):
        news += [like(master.shape, f32)] * 4 + [like(master.shape, bf16)]
    small = (smine, gmine, norm, *state)
    dma = pltpu.SemaphoreType.DMA
    return pl.pallas_call(
        update_kernel,
        in_specs=[anywhere] * (2 + len(small)),
        out_specs=[anywhere] * (2 + len(news)),
        out_shape=[like(out.shape, f32)] * 2 + news,
        scratch_shapes=[pltpu.VMEM(out.shape, f32)] * 2
        + [pltpu.VMEM(array.shape, array.dtype) for array in (*small, *news)]
        + [dma((2, CHUNKS))] * 2
        + [dma((len(small),)), dma((len(news),))],
        compiler_params=pltpu.CompilerParams(vmem_limit_bytes=62 * 1024 * 1024),
        name="update",
    )(out, gin, *small)


def on_device(
    n_dp,
    images,
    cotangent,
    drop_masks,
    group_master,
    group_m1,
    group_m2,
    shared_master,
    shared_m1,
    shared_m2,
):
    state = (group_master, group_m1, group_m2, shared_master, shared_m1, shared_m2)
    output, input_grad, norm, *updated = step(n_dp, drop_masks, images, cotangent, state)
    return (output, input_grad, norm.reshape(1), *updated)


def solution(mesh):
    both = P(("dp", "heads"))
    rows = P(("dp", "heads"), None, None)
    split = P("heads", "dp")
    in_specs = (rows, rows, P(("dp", "heads"), None), split, split, split, both, both, both)
    out_specs = (rows, rows, P(), split, split, split, split, split, both, both, both, both, both)
    return jax.shard_map(
        partial(on_device, mesh.shape["dp"]),
        mesh=mesh,
        in_specs=in_specs,
        out_specs=out_specs,
        check_vma=False,
    )
```

```python
from functools import partial
import math

import jax
import jax.numpy as jnp
from jax import lax
from jax.experimental import pallas as pl
from jax.experimental.pallas import tpu as pltpu
from jax.sharding import PartitionSpec as P

D = 256
FF = 1024
SIDE = 14
SW = 7
STEP = 10
HD = 32
HALF = 128
GROUP_PARAMS = 132608
SHARED_PARAMS = 526848
TOK = SIDE * SIDE
GRID = 16 * SIDE
STRIPE = 16 * SW
HEADS = HALF // HD
UNIT = 1024

eps_norm = 1e-05
keep_prob = 0.8
beta_one = 0.9
beta_two = 0.999
adam_eps = 1e-08
learn_rate = 0.04
decay_rate = 0.05

f32 = jnp.float32
bf16 = jnp.bfloat16


def window_rows(total, count, extra=0):
    share = total // count
    most = max((share * k) % UNIT + share for k in range(count)) + extra * 128
    return 16 * (-(-most // (2 * UNIT)))


def first_row(total, count, k):
    return (total // count * k) // UNIT * 8


HEADS_BIT = -1
FAST_BITS = 4
CARRIED = 4
GAIN_ROW = 4106


def exchange_stages(n_dp):
    bits = n_dp.bit_length() - 1
    far = list(range(bits - 1, 1, -1))
    stages = [tuple(far[i : i + 2]) for i in range(0, len(far), 2)]
    stages.append((1, HEADS_BIT) if bits > 1 else (HEADS_BIT,))
    if bits > 0:
        stages.append((0,))
    return stages


def weight_of(bit):
    return 1 if bit == HEADS_BIT else 2 << bit


def flat_bits(stages):
    return [bit for stage in stages for bit in stage]


def place_of(stages, k):
    return sum(((k // weight_of(bit)) % 2) << t for t, bit in enumerate(flat_bits(stages)))


def device_at(stages, place, first=0):
    return sum(
        ((place // (1 << t)) % 2) * weight_of(bit)
        for t, bit in enumerate(flat_bits(stages))
        if t >= first
    )


def own_number():
    return lax.axis_index("dp") * 2 + lax.axis_index("heads")


def own_bits(stages):
    me = own_number()
    return [(me // weight_of(bit)) % 2 for bit in flat_bits(stages)]


def peer(bits, mask):
    dp, heads = lax.axis_index("dp"), lax.axis_index("heads")
    for i, bit in enumerate(bits):
        if mask >> i & 1:
            if bit == HEADS_BIT:
                heads = 1 - heads
            else:
                dp = dp + (1 << bit) * (1 - 2 * ((dp // (1 << bit)) % 2))
    return {"dp": dp, "heads": heads}


def group_peers(n_dp):
    dp, heads = lax.axis_index("dp"), lax.axis_index("heads")
    fast = min(1 << FAST_BITS, n_dp)
    low, high = dp % fast, dp // fast
    count = 2 * fast
    me = low * 2 + heads
    near = []
    for step in range(1, count):
        other = (me + step) % count
        near.append((other, {"dp": high * fast + other // 2, "heads": other % 2}))
    far = []
    for step in range(1, n_dp // fast):
        other = (high + step) % (n_dp // fast)
        far.append((other, {"dp": other * fast + low, "heads": heads}))
    return (me, near), (high, far)


UNROLL = 16


class Gather:
    def __init__(self, stages, buffer, send_sem, recv_sem):
        self.stages, self.buffer = stages, buffer
        self.send_sem, self.recv_sem = send_sem, recv_sem
        self.bits = own_bits(stages)

    def copy(self, g, held, mask):
        return pltpu.make_async_remote_copy(
            src_ref=held,
            dst_ref=held,
            send_sem=self.send_sem.at[g],
            recv_sem=self.recv_sem.at[g],
            device_id=peer(self.stages[g], mask),
        )

    def start(self, g):
        start = sum(len(stage) for stage in self.stages[:g])
        base = sum((1 << u) * bit for u, bit in enumerate(self.bits) if u >= start)
        held = self.buffer.at[pl.ds(base, 1 << start)]
        for mask in range(1, 1 << len(self.stages[g])):
            self.copy(g, held, mask).start()

    def wait(self, g):
        start = sum(len(stage) for stage in self.stages[:g])
        peers = (1 << len(self.stages[g])) - 1
        every = self.copy(g, self.buffer.at[pl.ds(0, peers << start)], 1)
        every.wait_recv()
        every.wait_send()


class Scatter:
    def __init__(self, stages, window, outgoing, incoming, sums, send_sem, recv_sem):
        self.stages, self.window = stages, window
        self.outgoing, self.incoming, self.sums = outgoing, incoming, sums
        self.send_sem, self.recv_sem = send_sem, recv_sem
        self.bits = own_bits(stages)

    def offset(self, g):
        return sum(len(stage) for stage in self.stages[:g])

    def held(self, g, place):
        if g == len(self.stages) - 1:
            return self.window(place)
        return self.sums[g + 1][place]

    def copy(self, g, mask, at):
        return pltpu.make_async_remote_copy(
            src_ref=self.outgoing[g].at[at],
            dst_ref=self.incoming[g].at[at],
            send_sem=self.send_sem.at[g],
            recv_sem=self.recv_sem.at[g],
            device_id=peer(self.stages[g], mask),
        )

    def part(self, g, mask):
        start = self.offset(g)
        return sum(
            (1 << (start + i)) * (1 - self.bits[start + i] if mask >> i & 1 else self.bits[start + i])
            for i in range(len(self.stages[g]))
        )

    def start(self, g):
        for mask in range(1, 1 << len(self.stages[g])):
            part = self.part(g, mask)

            def fill(i, carry, mask=mask, part=part):
                self.outgoing[g][mask - 1, i] = self.held(g, part + i).astype(bf16)
                return carry

            blocks = 1 << self.offset(g)
            lax.fori_loop(0, blocks, fill, 0, unroll=min(blocks, UNROLL))
            self.copy(g, mask, mask - 1).start()

    def wait(self, g):
        masks = range(1, 1 << len(self.stages[g]))
        self.copy(g, 1, pl.ds(0, len(masks))).wait()
        part = self.part(g, 0)

        def add(i, carry):
            value = self.held(g, part + i)
            for mask in masks:
                value = value + self.incoming[g][mask - 1, i].astype(f32)
            self.sums[g][i] = value
            return carry

        blocks = 1 << self.offset(g)
        lax.fori_loop(0, blocks, add, 0, unroll=min(blocks, UNROLL))


def group_halves(grows):
    first = 16 * (-(-grows // 32))
    return first, grows - first


def scatter_shapes(stages, rows):
    outgoing, sums = [], []
    start = 0
    for stage in stages:
        outgoing.append(((1 << len(stage)) - 1, 1 << start, rows, 128))
        sums.append((1 << start, rows, 128))
        start += len(stage)
    return outgoing, sums


def all_share(me, peers, stat_ref, send_sem, recv_sem):
    def copy(held, device):
        return pltpu.make_async_remote_copy(
            src_ref=held,
            dst_ref=held,
            send_sem=send_sem.at[0],
            recv_sem=recv_sem.at[0],
            device_id=device,
        )

    for _, device in peers:
        copy(stat_ref.at[me], device).start()
    if peers:
        every = copy(stat_ref.at[pl.ds(0, len(peers))], peers[0][1])
        every.wait_recv()
        every.wait_send()
    return jnp.sum(stat_ref[...], axis=0)


def shift_on(rows, amount):
    lanes = amount % 128
    turned = pltpu.roll(rows, lanes, 1)
    lane = lax.broadcasted_iota(jnp.int32, rows.shape, 1)
    turned = jnp.where(lane < lanes, pltpu.roll(turned, 1, 0), turned)
    return pltpu.roll(turned, amount // 128, 0)


def shift_back(rows, amount):
    count = rows.shape[0]
    lanes = amount % 128
    turned = pltpu.roll(rows, (128 - lanes) % 128, 1)
    lane = lax.broadcasted_iota(jnp.int32, rows.shape, 1)
    turned = jnp.where(lane >= 128 - lanes, pltpu.roll(turned, count - 1, 0), turned)
    return pltpu.roll(turned, (count - amount // 128) % count, 0)


def nn(a, b):
    return lax.dot_general(a, b, (((1,), (0,)), ((), ())), preferred_element_type=f32)


def nt(a, b):
    return lax.dot_general(a, b, (((1,), (1,)), ((), ())), preferred_element_type=f32)


def tn(a, b):
    return lax.dot_general(a, b, (((0,), (0,)), ((), ())), preferred_element_type=f32)


def norm_parts(values):
    center = values - jnp.mean(values, axis=-1, keepdims=True)
    inverse = lax.rsqrt(jnp.mean(center * center, axis=-1, keepdims=True) + eps_norm)
    return center * inverse, inverse


def norm_back(grad_after, unit, inverse, gain):
    scaled = grad_after * gain
    return inverse * (
        scaled
        - jnp.mean(scaled, axis=-1, keepdims=True)
        - unit * jnp.mean(scaled * unit, axis=-1, keepdims=True)
    )


def column_sum(values):
    return jnp.sum(values, axis=0, keepdims=True)


def head_masks(dtype):
    lane = lax.broadcasted_iota(jnp.int32, (1, D), 1) % HALF // HD
    return [(lane == h).astype(f32).astype(dtype) for h in range(HEADS)]


def spread_heads(values, masks):
    return jnp.concatenate([values * masks[h] for h in range(HEADS)], axis=0)


def pick_heads(stacked):
    lane = lax.broadcasted_iota(jnp.int32, (STRIPE, D), 1) % HALF
    picked = stacked[(HEADS - 1) * STRIPE :]
    for h in range(HEADS - 2, -1, -1):
        picked = jnp.where(lane < (h + 1) * HD, stacked[h * STRIPE : (h + 1) * STRIPE], picked)
    return picked


def beside(rows):
    return jnp.concatenate([rows[:STRIPE], rows[STRIPE:]], axis=1)


def above(columns):
    return jnp.concatenate([columns[:, :HALF], columns[:, HALF:]], axis=0)


def diagonal(rows):
    gap = jnp.zeros((HALF - STRIPE, HALF), rows.dtype)
    other = jnp.zeros((HALF, HALF), rows.dtype)
    first = jnp.concatenate([rows[:STRIPE], gap], axis=0)
    second = jnp.concatenate([rows[STRIPE:], gap], axis=0)
    return jnp.concatenate(
        [jnp.concatenate([first, other], axis=1), jnp.concatenate([other, second], axis=1)], axis=0
    )


def turn_heads(stacked):
    gap = jnp.zeros((HALF - STRIPE, HALF), stacked.dtype)
    parts = []
    for h in range(HEADS):
        rows = stacked[h * STRIPE : (h + 1) * STRIPE]
        blocks = [
            jnp.concatenate([rows[:, s * HALF : (s + 1) * HALF], gap], axis=0).T for s in range(2)
        ]
        parts.append(jnp.concatenate(blocks, axis=1)[:STRIPE])
    return jnp.concatenate(parts, axis=0)


def row_shift(values, rows):
    if rows == 0:
        return values
    zero = jnp.zeros((abs(rows), values.shape[1]), f32)
    if rows > 0:
        return jnp.concatenate([values[rows:], zero], axis=0)
    return jnp.concatenate([zero, values[:rows]], axis=0)


def neighbours(values, j):
    before, after = pltpu.roll(values, 1, 0), pltpu.roll(values, STRIPE - 1, 0)
    if j == 0:
        row = lax.broadcasted_iota(jnp.int32, values.shape, 0) % 16
        before = jnp.where(row == 8, pltpu.roll(values, 2, 0), before)
        after = jnp.where(row == 6, pltpu.roll(values, STRIPE - 2, 0), after)
    return [before, values, after]


SHIFT = (16, 8)


def tap(j, outer, inner):
    return 3 * outer + inner if j == 0 else 3 * inner + outer


def to_stripes(rows):
    tiles = rows.reshape(SIDE, 2, 8, rows.shape[1])
    return jnp.concatenate(
        [tiles[:, s].reshape(STRIPE, rows.shape[1]) for s in range(2)], axis=0
    )


def from_stripes(columns):
    halves = [columns[:, s * HALF : (s + 1) * HALF].reshape(SIDE, 1, 8, HALF) for s in range(2)]
    return jnp.concatenate(halves, axis=1).reshape(GRID, HALF)


def tile_sum(values):
    return jnp.sum(values.reshape(-1, 8, values.shape[1]), axis=0)


def row_mask():
    row = lax.broadcasted_iota(jnp.int32, (GRID, 1), 0)
    return (row % 8 < SW).astype(f32)


def to_grid(source, tokens, grid_ref):
    images = grid_ref.shape[0]
    grid_ref[...] = jnp.zeros_like(grid_ref)
    for half in range(2):
        cols = slice(half * 128, (half + 1) * 128)
        tokens[half] = source[:, cols].astype(f32)
        for image in range(images):
            for r in range(2 * SIDE):
                grid_ref[image, 8 * r : 8 * r + SW, cols] = tokens[
                    half, pl.ds(r * SW * images + image, SW, stride=images), :
                ]


def from_grid(value, tokens, image, images):
    for half in range(2):
        for r in range(2 * SIDE):
            tokens[half, pl.ds(r * SW * images + image, SW, stride=images), :] = value[
                8 * r : 8 * r + SW, half * 128 : (half + 1) * 128
            ]


def prepare_group(n_dp, stages, sc):
    n = 2 * n_dp
    gflat, buffer = sc["gflat"], sc["gweights"]
    grows = buffer.shape[1]
    gflat[...] = jnp.zeros_like(gflat)
    for k in range(n):
        at = first_row(GROUP_PARAMS, n_dp, k // 2)
        size = grows - CARRIED
        gflat[k % 2, at : at + size] += buffer[place_of(stages, k), 0:size].astype(f32)
    carried = buffer[place_of(stages, n - 1)].astype(f32)[grows - CARRIED :]
    for c in range(2):
        cols = slice(c * 128, (c + 1) * 128)
        sc["vecs"][1:2, cols] = carried[c : c + 1]
        sc["vecs"][2:3, cols] = carried[2 + c : 3 + c]
    for j in range(2):
        for c in range(3):
            cols = slice(j * 384 + c * 128, j * 384 + (c + 1) * 128)
            sc["wq"][:, cols] = gflat[j, pl.ds(c, D, stride=3), :].astype(bf16)
        for c in range(2):
            cols = slice(c * 128, (c + 1) * 128)
            sc["ow"][j * 128 : (j + 1) * 128, cols] = gflat[
                j, pl.ds(770 + c, HALF, stride=2), :
            ].astype(bf16)
        sc["qbias"][:, j * 384 : j * 384 + 128] = gflat[j, 768:769, :]
        sc["qbias"][:, j * 384 + 128 : j * 384 + 256] = jnp.zeros((1, 128), f32)
        sc["qbias"][:, j * 384 + 256 : j * 384 + 384] = gflat[j, 769:770, :]
        for half in range(2):
            cols = slice(half * 128, (half + 1) * 128)
            sc["conv"][j, 0:10, cols] = gflat[j, 1026:1036, :]


def prepare_shared(n_dp, stages, sc):
    n = 2 * n_dp
    flat, buffer = sc["flat"], sc["sweights"]
    srows = buffer.shape[1]
    flat[...] = jnp.zeros_like(flat)
    for k in range(n):
        at = first_row(SHARED_PARAMS, n, k)
        flat[at : at + srows] += buffer[place_of(stages, k)].astype(f32)
    for c in range(8):
        cols = slice(c * 128, (c + 1) * 128)
        sc["uw"][:, cols] = flat[pl.ds(c, D, stride=8), :].astype(bf16)
        sc["ubias"][:, cols] = flat[2048 + c : 2049 + c, :]
    for c in range(2):
        cols = slice(c * 128, (c + 1) * 128)
        sc["dw"][:, cols] = flat[pl.ds(2056 + c, FF, stride=2), :].astype(bf16)
        for i in (0, 3, 4, 5):
            sc["vecs"][i : i + 1, cols] = flat[4104 + 2 * i + c : 4105 + 2 * i + c, :]


def place_shared(sc):
    flat = sc["flat"]
    for c in range(8):
        cols = slice(c * 128, (c + 1) * 128)
        flat[pl.ds(c, D, stride=8), :] = sc["a_uw"][:, cols]
        flat[2048 + c : 2049 + c, :] = column_sum(sc["a_ub"][:, cols])
    for q in range(4):
        turned = sc["a_dwt"][:, q * 256 : (q + 1) * 256].T
        for c in range(2):
            flat[pl.ds(2056 + 512 * q + c, 256, stride=2), :] = turned[
                :, c * 128 : (c + 1) * 128
            ]
    for c in range(2):
        cols = slice(c * 128, (c + 1) * 128)
        for i in (0, 3, 4, 5):
            flat[4104 + 2 * i + c : 4105 + 2 * i + c, :] = column_sum(
                sc["a_vec"][i, :, cols]
            )
    flat[GAIN_ROW : GAIN_ROW + CARRIED, :] = jnp.zeros((CARRIED, 128), f32)


def place_group(sc):
    gflat = sc["gflat"]
    for j in range(2):
        for c in range(3):
            cols = slice(j * 384 + c * 128, j * 384 + (c + 1) * 128)
            gflat[j, pl.ds(c, D, stride=3), :] = sc["a_wq"][:, cols]
        for c in range(2):
            cols = slice(c * 128, (c + 1) * 128)
            gflat[j, pl.ds(770 + c, HALF, stride=2), :] = sc["a_ow"][
                j * 128 : (j + 1) * 128, cols
            ]
        gflat[j, 768:769, :] = column_sum(sc["a_pb"][:, j * 384 : j * 384 + 128])
        gflat[j, 769:770, :] = column_sum(sc["a_pb"][:, j * 384 + 256 : j * 384 + 384])
        for i in range(10):
            both = column_sum(sc["a_conv"][j, i])
            gflat[j, 1026 + i : 1027 + i, :] = both[:, :HALF] + both[:, HALF:]


def first_norm(images, sc):
    for image in images:
        sc["unit"][image], sc["inverse"][image] = norm_parts(sc["x"][image])


def attention_forward(images, sc):
    scale = HD ** (-0.5)
    masks = head_masks(bf16)
    inside = row_mask()
    key_row = lax.broadcasted_iota(jnp.int32, (1, SIDE, 8, D), 2)
    gain_one, shift_one = sc["vecs"][1:2], sc["vecs"][2:3]
    qkv_ref, conv = sc["qkv"], sc["conv"]
    many = len(images)
    for image in images:
        sc["normed"][image] = (sc["unit"][image] * gain_one + shift_one).astype(bf16)
    normed = sc["normed"][pl.ds(images[0], many)].reshape(many * GRID, D)
    triples = nn(normed, sc["wq"][...]) + sc["qbias"][...]
    for i, image in enumerate(images):
        triple = triples[i * GRID : (i + 1) * GRID] * inside
        qkv_ref[image, 0] = triple[:, :384].astype(bf16)
        qkv_ref[image, 1] = to_stripes(triple[:, 384:]).astype(bf16)
    for j in range(2):
        for image in images:
            query = diagonal(qkv_ref[image, j, :, 0:128])
            keys = spread_heads(beside(qkv_ref[image, j, :, 128:256]), masks)
            value = beside(qkv_ref[image, j, :, 256:384])
            scores = nt(keys, query).reshape(HEADS, SIDE, 8, D) * scale
            scores = jnp.where(key_row < SW, scores, -jnp.inf)
            scores = scores.reshape(HEADS, STRIPE, D)
            weights = jnp.exp(scores - jnp.max(scores, axis=1, keepdims=True))
            probs = weights * (1.0 / jnp.sum(weights, axis=1, keepdims=True))
            probs = probs.reshape(HEADS * STRIPE, D)
            sc["probs"][image, j] = probs
            values = diagonal(qkv_ref[image, j, :, 256:384])
            total = pick_heads(nn(turn_heads(probs.astype(bf16)), values)) + conv[j, 9:10]
            near = neighbours(value.astype(f32), j)
            for outer in range(3):
                part = None
                for inner in range(3):
                    k = tap(j, outer, inner)
                    term = near[inner] * conv[j, k : k + 1]
                    part = term if part is None else part + term
                total = total + row_shift(part, SHIFT[j] * (outer - 1))
            both = above(total) if j == 0 else from_stripes(total)
            sc["heads"][image, :, j * 128 : (j + 1) * 128] = both.astype(bf16)


def mlp_output(images, count, drop_ref, sc):
    many = len(images)
    active = sc["active"][pl.ds(images[0], many)].reshape(many * GRID, FF)
    mlp = nn(active, sc["dw"][...]) + sc["vecs"][0:1]
    for i, image in enumerate(images):
        scale_two = drop_ref[1, image].astype(f32) / keep_prob
        value = sc["x"][image] + scale_two * mlp[i * GRID : (i + 1) * GRID]
        from_grid(value, sc["outs"], image, count)


def mlp_both(images, drop_ref, sc):
    gain_two, shift_two, out_bias = sc["vecs"][3:4], sc["vecs"][4:5], sc["vecs"][5:6]
    a_vec = sc["a_vec"]
    uw, dw, ubias = sc["uw"], sc["dw"], sc["ubias"]
    many = len(images)

    def join(parts):
        return jnp.concatenate(parts, axis=0)

    def part_of(joined, i):
        return joined[i * GRID : (i + 1) * GRID]

    heads = sc["heads"][pl.ds(images[0], many)].reshape(many * GRID, D)
    branch = nn(heads, sc["ow"][...])
    state = []
    for i, image in enumerate(images):
        scale_one = drop_ref[0, image].astype(f32) / keep_prob
        scale_two = drop_ref[1, image].astype(f32) / keep_prob
        middle = sc["x"][image] + scale_one * (part_of(branch, i) + out_bias)
        unit_two, inverse_two = norm_parts(middle)
        grad_output = sc["co"][image]
        grad_mlp_f = scale_two * grad_output
        a_vec[0] += tile_sum(grad_mlp_f)
        state.append((scale_one, scale_two, middle, unit_two, inverse_two, grad_output, grad_mlp_f))
    normed_two = join([(st[3] * gain_two + shift_two).astype(bf16) for st in state])
    grad_mlp = join([st[6].astype(bf16) for st in state])
    grad_normed = None
    for c in range(4):
        cols = slice(c * 256, (c + 1) * 256)
        hidden = nn(normed_two, uw[:, cols]) + ubias[:, cols]
        density = jnp.exp(hidden * hidden * -0.5) * (1.0 / math.sqrt(2.0 * math.pi))
        phi = 0.5 + 0.5 * lax.erf(hidden * math.sqrt(0.5))
        active = (hidden * phi).astype(bf16)
        sc["active"][pl.ds(images[0], many), :, cols] = active.reshape(many, GRID, 256)
        sc["a_dwt"][:, cols] += tn(grad_mlp, active)
        grad_active = nt(grad_mlp, dw[cols, :])
        grad_hidden = (grad_active * (phi + hidden * density)).astype(bf16)
        sc["a_ub"][:, cols] += tile_sum(grad_hidden.astype(f32))
        sc["a_uw"][:, cols] += tn(normed_two, grad_hidden)
        part = nt(grad_hidden, uw[:, cols])
        grad_normed = part if grad_normed is None else grad_normed + part
    grad_branch = []
    for i, image in enumerate(images):
        scale_one, _, middle, unit_two, inverse_two, grad_output, _ = state[i]
        sc["x"][image] = middle
        grad = part_of(grad_normed, i)
        a_vec[3] += tile_sum(grad * unit_two)
        a_vec[4] += tile_sum(grad)
        grad_middle = grad_output + norm_back(grad, unit_two, inverse_two, gain_two)
        sc["gmid"][image] = grad_middle
        grad_branch_f = scale_one * grad_middle
        a_vec[5] += tile_sum(grad_branch_f)
        grad_branch.append(grad_branch_f.astype(bf16))
    grad_branch = join(grad_branch)
    sc["a_ow"][...] += tn(heads, grad_branch)
    grad_heads = nt(grad_branch, sc["ow"][...])
    for i, image in enumerate(images):
        grad = part_of(grad_heads, i)
        sc["gheads"][image, :, :128] = grad[:, :128].astype(bf16)
        sc["gheads"][image, :, 128:] = to_stripes(grad[:, 128:]).astype(bf16)


def attention_back(images, sc, now, between):
    scale = HD ** (-0.5)
    masks = head_masks(bf16)
    inside = row_mask()[:STRIPE]
    many = len(images)
    a_conv = sc["a_conv"]
    qkv_ref, conv = sc["qkv"], sc["conv"]
    for j in range(2):
        if j == 1:
            pl.when(now)(between)
        for image in images:
            grad = sc["gheads"][image, :, j * 128 : (j + 1) * 128]
            grad_square = diagonal(grad)
            grad_f = beside(grad).astype(f32)
            query = diagonal(qkv_ref[image, j, :, 0:128])
            value = beside(qkv_ref[image, j, :, 256:384])
            probs = sc["probs"][image, j]
            grad_probs = nt(spread_heads(value, masks), grad_square)
            product = (probs * grad_probs).reshape(HEADS, STRIPE, D)
            inner = jnp.sum(product, axis=1, keepdims=True)
            grad_scores = product - probs.reshape(HEADS, STRIPE, D) * inner
            grad_scores = grad_scores.reshape(HEADS * STRIPE, D).astype(bf16)
            keys = diagonal(qkv_ref[image, j, :, 128:256])
            grad_query = pick_heads(nn(turn_heads(grad_scores), keys)) * scale
            grad_key = pick_heads(nn(grad_scores, query)) * scale
            grad_value = pick_heads(nn(probs.astype(bf16), grad_square))
            near = neighbours(grad_f, j)
            for outer in range(3):
                part = None
                for inner in range(3):
                    k = tap(j, outer, inner)
                    term = near[2 - inner] * conv[j, k : k + 1]
                    part = term if part is None else part + term
                grad_value = grad_value + row_shift(part, SHIFT[j] * (1 - outer))
            grad_value = grad_value * inside
            near = neighbours(value.astype(f32), j)
            step = SHIFT[j]
            for inner in range(3):
                a_conv[j, tap(j, 0, inner)] += tile_sum(grad_f[step:] * near[inner][:-step])
                a_conv[j, tap(j, 1, inner)] += tile_sum(grad_f * near[inner])
                a_conv[j, tap(j, 2, inner)] += tile_sum(grad_f[:-step] * near[inner][step:])
            a_conv[j, 9] += tile_sum(grad_f)
            order = above if j == 0 else from_stripes
            both = jnp.concatenate(
                [order(part) for part in (grad_query, grad_key, grad_value)], axis=1
            ).astype(bf16)
            sc["gtriple"][image, :, j * 384 : (j + 1) * 384] = both
    grad_triple = sc["gtriple"][pl.ds(images[0], many)].reshape(many * GRID, 768)
    normed = sc["normed"][pl.ds(images[0], many)].reshape(many * GRID, D)
    sc["a_pb"][...] += tile_sum(grad_triple.astype(f32))
    sc["a_wq"][...] += tn(normed, grad_triple)


def input_gradient(images, count, sc):
    many = len(images)
    gain_one = sc["vecs"][1:2]
    a_vec = sc["a_vec"]
    grad_triple = sc["gtriple"][pl.ds(images[0], many)].reshape(many * GRID, 768)
    grads = nt(grad_triple, sc["wq"][...])
    for i, image in enumerate(images):
        grad_normed = grads[i * GRID : (i + 1) * GRID]
        unit, inverse = sc["unit"][image], sc["inverse"][image]
        a_vec[1] += tile_sum(grad_normed * unit)
        a_vec[2] += tile_sum(grad_normed)
        grad = sc["gmid"][image] + norm_back(grad_normed, unit, inverse, gain_one)
        from_grid(grad, sc["tokens"], image, count)


def scratch_shapes(n_dp, srows, grows, count):
    n = 2 * n_dp
    flat_rows = max(4120, first_row(SHARED_PARAMS, n, n - 1) + srows)
    gflat_rows = max(1040, first_row(GROUP_PARAMS, n_dp, n_dp - 1) + grows)
    shapes = dict(
        flat=((flat_rows, 128), f32),
        gflat=((2, gflat_rows, 128), f32),
        sweights=((n, srows, 128), bf16),
        gweights=((n, grows, 128), bf16),
        raw=((grows, 128), f32),
        sraw=((srows, 128), f32),
        sown=((SHARED_PARAMS // n,), f32),
        gown=((1, GROUP_PARAMS // n_dp), f32),
        wq=((D, 768), bf16),
        ow=((D, D), bf16),
        uw=((D, FF), bf16),
        dw=((FF, D), bf16),
        qbias=((1, 768), f32),
        ubias=((1, FF), f32),
        vecs=((8, D), f32),
        conv=((2, 16, D), f32),
        a_wq=((D, 768), f32),
        a_ow=((D, D), f32),
        a_uw=((D, FF), f32),
        a_dwt=((D, FF), f32),
        a_pb=((8, 768), f32),
        a_ub=((8, FF), f32),
        a_vec=((6, 8, D), f32),
        a_conv=((2, 10, 8, D), f32),
        x_in=((TOK * count, D), bf16),
        tokens=((2, TOK * count, 128), f32),
        outs=((2, TOK * count, 128), f32),
        x=((count, GRID, D), f32),
        co=((count, GRID, D), f32),
        unit=((count, GRID, D), f32),
        inverse=((count, GRID, 1), f32),
        normed=((count, GRID, D), bf16),
        qkv=((count, 2, GRID, 384), bf16),
        probs=((count, 2, HEADS * STRIPE, D), f32),
        heads=((count, GRID, D), bf16),
        gmid=((count, GRID, D), f32),
        active=((count, GRID, FF), bf16),
        gheads=((count, GRID, D), bf16),
        gtriple=((count, GRID, 768), bf16),
    )
    stages = exchange_stages(n_dp)
    first, second = group_halves(grows)
    for name, rows in (("s", srows), ("g", first), ("h", second)):
        outgoing, sums = scatter_shapes(stages, rows)
        for g, shape in enumerate(outgoing):
            shapes[f"{name}out{g}"] = (shape, bf16)
            shapes[f"{name}in{g}"] = (shape, bf16)
            shapes[f"{name}sum{g}"] = (sums[g], f32)
    fast = min(1 << FAST_BITS, n_dp)
    shapes["near_stat"] = ((2 * fast, 8, 128), f32)
    shapes["far_stat"] = ((n_dp // fast, 8, 128), f32)
    made = {name: pltpu.VMEM(*shape) for name, shape in shapes.items()}
    dma = pltpu.SemaphoreType.DMA
    for name in ("sgather", "ggather", "sscatter", "gscatter", "hscatter"):
        made[name + "_send"] = dma((len(stages),))
        made[name + "_recv"] = dma((len(stages),))
    for name in ("near", "far"):
        made[name + "_send"] = dma((1,))
        made[name + "_recv"] = dma((1,))
    made["local"] = dma((5,))
    made["drops"] = pltpu.SMEM((2, count), jnp.int32)
    return made


ACCUMULATORS = ("a_wq", "a_ow", "a_uw", "a_dwt", "a_pb", "a_ub", "a_vec", "a_conv")
TOGETHER = 2
FORWARD_TOGETHER = 4
BACK_TOGETHER = 4
MLP_TOGETHER = 4
GATHER_STEP = 1
CORE_STEP = 1
OUT_STEP = 1
BACK_IMAGE = 0
OUT_TOGETHER = 4


def own_windows(n_dp, sown_ref, gown_ref, soff, goff, stages, sc):
    n = 2 * n_dp
    mine = sum((1 << t) * bit for t, bit in enumerate(own_bits(stages)))
    raw = sc["sraw"]
    share = sown_ref.shape[0]
    whole = share // UNIT * UNIT
    raw[...] = jnp.zeros_like(raw)
    raw[0 : whole // 128, :] = sown_ref[0:whole].reshape(whole // 128, 128)
    for r in range(whole // 128, -(-share // 128)):
        size = min(128, share - 128 * r)
        raw[r : r + 1, 0:size] = sown_ref[128 * r : 128 * r + size].reshape(1, size)
    window = shift_on(raw[...], soff)
    sc["sweights"][mine] = window.astype(bf16)
    raw = sc["raw"]
    grows = raw.shape[0]
    share = gown_ref.shape[1]
    raw[...] = jnp.zeros_like(raw)
    for r in range(-(-share // 128)):
        size = min(128, share - 128 * r)
        raw[r : r + 1, 0:size] = gown_ref[0:1, 128 * r : 128 * r + size]
    at = GAIN_ROW - first_row(SHARED_PARAMS, n, n - 1)
    raw[...] = shift_on(raw[...], goff)
    raw[grows - CARRIED :, :] = window[at : at + CARRIED]
    sc["gweights"][mine] = raw[...].astype(bf16)


def finish(n_dp, soff, goff, ssum, gsum, smine_ref, gmine_ref, norm_ref, near, far, sc):
    n = 2 * n_dp
    srows, grows = ssum.shape[0], gsum.shape[0]
    sshare, gshare = SHARED_PARAMS // n, GROUP_PARAMS // n_dp
    place = lax.broadcasted_iota(jnp.int32, (srows, 128), 0) * 128
    place = place + lax.broadcasted_iota(jnp.int32, (srows, 128), 1)
    shared = jnp.where((place >= soff) & (place < soff + sshare), ssum, 0.0)
    place = lax.broadcasted_iota(jnp.int32, (grows, 128), 0) * 128
    place = place + lax.broadcasted_iota(jnp.int32, (grows, 128), 1)
    grouped = jnp.where((place >= goff) & (place < goff + gshare), gsum, 0.0)
    near_me, near_peers = near
    far_me, far_peers = far
    squares = column_sum(tile_sum(shared * shared) + tile_sum(grouped * grouped))
    sums = [
        column_sum(sc["a_vec"][i, :, c * 128 : (c + 1) * 128]) for i in (1, 2) for c in range(2)
    ]
    tile = jnp.concatenate([*sums, squares, jnp.zeros((3, 128), f32)], axis=0)
    sc["near_stat"][near_me] = tile
    tile = all_share(near_me, near_peers, sc["near_stat"], sc["near_send"], sc["near_recv"])
    sc["far_stat"][far_me] = tile
    tile = all_share(far_me, far_peers, sc["far_stat"], sc["far_send"], sc["far_recv"])
    carried = tile[:CARRIED]
    total = column_sum(carried * carried) + tile[CARRIED : CARRIED + 1]
    total = jnp.sum(total, axis=1, keepdims=True)
    last = jnp.where(own_number() == n - 1, 1.0, 0.0)
    at = GAIN_ROW - first_row(SHARED_PARAMS, n, n - 1)
    smine_ref[...] = shared
    smine_ref[at : at + CARRIED, :] += carried * last
    shared = smine_ref[...]
    norm = jnp.sqrt(total)
    norm_ref[...] = jnp.broadcast_to(norm, (8, 128))
    threshold = math.sqrt(2 * GROUP_PARAMS + SHARED_PARAMS)
    factor = jnp.minimum(1.0, threshold / (norm + 1e-06))
    smine_ref[...] = shift_back(shared * factor, soff)
    grouped = shift_back(grouped * factor, goff)
    for r in range(-(-gshare // 128)):
        size = min(128, gshare - 128 * r)
        gmine_ref[0:1, 128 * r : 128 * r + size] = grouped[r : r + 1, 0:size]


def step_kernel(
    n_dp,
    count,
    names,
    drop_in,
    x_ref,
    co_ref,
    sown_ref,
    gown_ref,
    out_ref,
    gin_ref,
    smine_ref,
    gmine_ref,
    norm_ref,
    *scratch,
):
    sc = dict(zip(names, scratch))
    n = 2 * n_dp
    stages = exchange_stages(n_dp)
    near, far = group_peers(n_dp)
    devices = [device for _, device in near[1] + far[1]]
    barrier = pltpu.get_barrier_semaphore()
    for device in devices:
        pl.semaphore_signal(barrier, inc=1, device_id=device)
    load_x = pltpu.make_async_copy(x_ref, sc["x_in"], sc["local"].at[0])
    load_co = pltpu.make_async_copy(co_ref, sc["x_in"], sc["local"].at[1])
    loads = [
        pltpu.make_async_copy(source, sc[name], sc["local"].at[2 + i])
        for i, (source, name) in enumerate(
            ((sown_ref, "sown"), (gown_ref, "gown"), (drop_in, "drops"))
        )
    ]
    for load in (*loads, load_x):
        load.start()
    drop_ref = sc["drops"]
    soff = (own_number() * (SHARED_PARAMS // n)) % UNIT
    goff = (lax.axis_index("dp") * (GROUP_PARAMS // n_dp)) % UNIT
    for load in loads:
        load.wait()
    own_windows(n_dp, sc["sown"], sc["gown"], soff, goff, stages, sc)
    load_x.wait()
    to_grid(sc["x_in"], sc["tokens"], sc["x"])
    load_co.start()
    pl.semaphore_wait(barrier, len(devices))
    ggather = Gather(stages, sc["gweights"], sc["ggather_send"], sc["ggather_recv"])
    sgather = Gather(stages, sc["sweights"], sc["sgather_send"], sc["sgather_recv"])

    def run(phase, extra=None, together=TOGETHER):
        def body(i, carry):
            if extra is not None:
                for at, action in extra.items():
                    pl.when(i == at)(action)
            phase([i * together + k for k in range(together)])
            return carry

        lax.fori_loop(0, count // together, body, 0)

    last = len(stages) - 1
    ggather.start(0)
    sgather.start(0)
    for g in range(last):
        if g == last - 1:
            run(lambda images: first_norm(images, sc))
        ggather.wait(g)
        ggather.start(g + 1)
        if g < last - 1:
            sgather.wait(g)
            sgather.start(g + 1)
    for name in ACCUMULATORS:
        sc[name][...] = jnp.zeros_like(sc[name])
    load_co.wait()
    to_grid(sc["x_in"], sc["tokens"], sc["co"])
    ggather.wait(last)
    prepare_group(n_dp, stages, sc)

    def spread_cores():
        sgather.wait(last - 1)
        sgather.start(last)

    steps = count // FORWARD_TOGETHER
    run(
        lambda images: attention_forward(images, sc),
        {min(GATHER_STEP, steps - 1): spread_cores},
        FORWARD_TOGETHER,
    )
    sgather.wait(last)
    prepare_shared(n_dp, stages, sc)
    run(lambda images: mlp_both(images, drop_ref, sc), None, MLP_TOGETHER)
    place_shared(sc)

    srows, grows = sc["sweights"].shape[1], sc["gweights"].shape[1]

    def swindow(place):
        k = device_at(stages, place)
        row = (k * (SHARED_PARAMS // n)) // UNIT * 8
        return sc["flat"][pl.ds(pl.multiple_of(row, 8), srows), :]

    first, second = group_halves(grows)

    def gwindow(begin, size):
        def window(place):
            k = device_at(stages, place)
            row = ((k // 2) * (GROUP_PARAMS // n_dp)) // UNIT * 8 + begin
            return sc["gflat"][k % 2, pl.ds(pl.multiple_of(row, 8), size), :]

        return window

    def scatter(name, window):
        parts = [[sc[f"{name}{kind}{g}"] for g in range(last + 1)] for kind in ("out", "in", "sum")]
        return Scatter(
            stages, window, *parts, sc[name + "scatter_send"], sc[name + "scatter_recv"]
        )

    sscatter = scatter("s", swindow)
    gscatters = (scatter("g", gwindow(0, first)), scatter("h", gwindow(first, second)))
    sscatter.start(last)
    def advance(scatters, g):
        def action():
            for scatter in scatters:
                scatter.wait(g)
                scatter.start(g - 1)

        return action

    run(
        lambda images: attention_back(
            images, sc, images[0] == BACK_IMAGE, advance((sscatter,), last)
        ),
        None,
        BACK_TOGETHER,
    )
    place_group(sc)
    for half in gscatters:
        half.start(last)
    stores = []

    def store(held, target):
        for half in range(2):
            cols = slice(half * 128, (half + 1) * 128)
            copy = pltpu.make_async_copy(
                sc[held].at[half], target.at[:, cols], sc["local"].at[len(stores)]
            )
            copy.start()
            stores.append(copy)

    for g in range(last - 1, 0, -1):
        advance((sscatter,), g)()
    run(lambda images: input_gradient(images, count, sc), {CORE_STEP: advance(gscatters, last)})
    store("tokens", gin_ref)
    for g in range(last - 1, 1, -1):
        advance(gscatters, g)()
    run(
        lambda images: mlp_output(images, count, drop_ref, sc),
        {OUT_STEP: advance(gscatters, 1)} if last > 1 else None,
        OUT_TOGETHER,
    )
    store("outs", out_ref)
    sscatter.wait(0)
    for half in gscatters:
        half.wait(0)
    finish(
        n_dp,
        soff,
        goff,
        sc["ssum0"][0],
        jnp.concatenate([sc["gsum0"][0], sc["hsum0"][0]], axis=0),
        smine_ref,
        gmine_ref,
        norm_ref,
        near,
        far,
        sc,
    )
    for copy in stores:
        copy.wait()


def step(n_dp, drops, images, cotangent, state):
    count = images.shape[0]
    gown, _, _, sown, _, _ = state
    srows = window_rows(SHARED_PARAMS, 2 * n_dp)
    grows = window_rows(GROUP_PARAMS, n_dp, CARRIED)
    shapes = scratch_shapes(n_dp, srows, grows, count)
    vmem = pl.BlockSpec(memory_space=pltpu.VMEM)
    anywhere = pl.BlockSpec(memory_space=pl.ANY)

    def rows(array):
        return jnp.swapaxes(array, 0, 1).reshape(TOK * count, D)

    def unrows(array):
        return jnp.swapaxes(array.reshape(TOK, count, D), 0, 1)

    out, gin, smine, gmine, norm = pl.pallas_call(
        partial(step_kernel, n_dp, count, tuple(shapes)),
        in_specs=[anywhere] * 5,
        out_specs=[anywhere, anywhere, vmem, vmem, vmem],
        out_shape=[jax.ShapeDtypeStruct((TOK * count, D), f32)] * 2
        + [
            jax.ShapeDtypeStruct((srows, 128), f32),
            jax.ShapeDtypeStruct(gown.shape, f32),
            jax.ShapeDtypeStruct((8, 128), f32),
        ],
        scratch_shapes=list(shapes.values()),
        compiler_params=pltpu.CompilerParams(
            collective_id=0, has_side_effects=True, vmem_limit_bytes=62 * 1024 * 1024
        ),
        name="step",
    )(drops.T, rows(images), rows(cotangent), sown, gown)
    first, second, *updated = update(out, gin, smine.reshape(-1), gmine, norm, *state)
    return (unrows(first), unrows(second), *updated)


def adam_step(master, gradient, first, second):
    first_new = beta_one * first + (1.0 - beta_one) * gradient
    second_new = beta_two * second + (1.0 - beta_two) * gradient * gradient
    first_hat = first_new / (1.0 - beta_one**STEP)
    second_hat = second_new / (1.0 - beta_two**STEP)
    master_new = master - learn_rate * (
        first_hat / (jnp.sqrt(second_hat) + adam_eps) + decay_rate * master
    )
    return (master_new, first_new, second_new)


CHUNKS = 1


def update_kernel(*refs):
    big_in, small_in, refs = refs[:2], refs[2:11], refs[11:]
    big_out, small_out, refs = refs[:2], refs[2:13], refs[13:]
    big_buf, refs = refs[:2], refs[2:]
    held_in, held_out, sems = refs[:9], refs[9:20], refs[20:]
    big_load, big_store, small_load, small_store = sems
    size = big_in[0].shape[0] // CHUNKS

    def small_loads():
        for i in range(9):
            yield pltpu.make_async_copy(small_in[i], held_in[i], small_load.at[i])

    loads, stores = [], []
    for i in range(CHUNKS):
        rows = pl.ds(i * size, size)
        for k in range(2):
            held = big_buf[k].at[rows]
            loads.append(pltpu.make_async_copy(big_in[k].at[rows], held, big_load.at[k, i]))
            stores.append(pltpu.make_async_copy(held, big_out[k].at[rows], big_store.at[k, i]))
    small = list(small_loads())
    for load in (*small, *loads):
        load.start()
    for load in small:
        load.wait()
    smine, gmine, norm = held_in[:3]
    states = (held_in[3:6], held_in[6:9])
    held_out[0][...] = norm[0:1, 0:1]
    for gradient, (master, first, second), new in (
        (gmine[...], states[0], held_out[1:6]),
        (smine[0 : states[1][0].shape[0]], states[1], held_out[6:11]),
    ):
        new[0][...] = gradient
        new[1][...], new[2][...], new[3][...] = adam_step(
            master[...], gradient, first[...], second[...]
        )
        new[4][...] = new[1][...].astype(bf16)
    small = [
        pltpu.make_async_copy(held_out[i], small_out[i], small_store.at[i]) for i in range(11)
    ]
    for load, store in zip(loads, stores):
        load.wait()
        store.start()
    for store in small:
        store.start()
    for store in (*stores, *small):
        store.wait()


def update(out, gin, smine, gmine, norm, *state):
    anywhere = pl.BlockSpec(memory_space=pl.ANY)
    like = jax.ShapeDtypeStruct
    news = [like((1, 1), f32)]
    for master in (state[0], state[3]):
        news += [like(master.shape, f32)] * 4 + [like(master.shape, bf16)]
    small = (smine, gmine, norm, *state)
    dma = pltpu.SemaphoreType.DMA
    return pl.pallas_call(
        update_kernel,
        in_specs=[anywhere] * (2 + len(small)),
        out_specs=[anywhere] * (2 + len(news)),
        out_shape=[like(out.shape, f32)] * 2 + news,
        scratch_shapes=[pltpu.VMEM(out.shape, f32)] * 2
        + [pltpu.VMEM(array.shape, array.dtype) for array in (*small, *news)]
        + [dma((2, CHUNKS))] * 2
        + [dma((len(small),)), dma((len(news),))],
        compiler_params=pltpu.CompilerParams(vmem_limit_bytes=62 * 1024 * 1024),
        name="update",
    )(out, gin, *small)


def on_device(
    n_dp,
    images,
    cotangent,
    drop_masks,
    group_master,
    group_m1,
    group_m2,
    shared_master,
    shared_m1,
    shared_m2,
):
    state = (group_master, group_m1, group_m2, shared_master, shared_m1, shared_m2)
    output, input_grad, norm, *updated = step(n_dp, drop_masks, images, cotangent, state)
    return (output, input_grad, norm.reshape(1), *updated)


def solution(mesh):
    both = P(("dp", "heads"))
    rows = P(("dp", "heads"), None, None)
    split = P("heads", "dp")
    in_specs = (rows, rows, P(("dp", "heads"), None), split, split, split, both, both, both)
    out_specs = (rows, rows, P(), split, split, split, split, split, both, both, both, both, both)
    return jax.shard_map(
        partial(on_device, mesh.shape["dp"]),
        mesh=mesh,
        in_specs=in_specs,
        out_specs=out_specs,
        check_vma=False,
    )
```
